32 devices in a mesh: dp: 4 (over y, core), expert: 8 (over z, x).
Axes of the slice: x: 2, y: 2, z: 4, core: 2. Of those that a mesh axis runs over, the one named last changes fastest.
Arguments:
- tokens: bfloat16 [37824, 512], P(('dp', 'expert')), may hold values from -6 to 6
- ln1_gain: bfloat16 [512], P('dp'), may hold values from 0.5 to 1.5
- ln1_bias: bfloat16 [512], P('dp'), may hold values from -0.59765625 to 0.59765625
- qkv_weight: bfloat16 [512, 1536], P('dp'), may hold values from -0.25 to 0.25
- out_weight: bfloat16 [512, 512], P('dp'), may hold values from -2 to 2
- ln2_gain: bfloat16 [512], P('dp'), may hold values from 0.5 to 1.5
- ln2_bias: bfloat16 [512], P('dp'), may hold values from -0.59765625 to 0.59765625
- router_weight: bfloat16 [512, 8], P('dp'), may hold values from -0.125 to 0.125
- expert_in: bfloat16 [8, 512, 2048], P('expert'), may hold values from -0.25 to 0.25
- expert_out: bfloat16 [8, 2048, 512], P('expert'), may hold values from -1 to 1
- routes: int32 [37824, 2], P(('dp', 'expert')), may hold values from 0 to 7, as said below
- priority: int32 [37824], P(('dp', 'expert')), may hold values from 0 to 590, as said below
- capacity: int32 [8], replicated, may hold values from 112 to 224, as said below
- cotangent: bfloat16 [37824, 512], P(('dp', 'expert')), may hold values from -6 to 6
Outputs:
- block_out: bfloat16 [37824, 512], P(('dp', 'expert'))
- grad_tokens: bfloat16 [37824, 512], P(('dp', 'expert'))
- grad_ln1_gain: float32 [512], P('dp')
- grad_ln1_bias: float32 [512], P('dp')
- grad_qkv: float32 [512, 1536], P('dp')
- grad_out_proj: float32 [512, 512], P('dp')
- grad_ln2_gain: float32 [512], P('dp')
- grad_ln2_bias: float32 [512], P('dp')
- grad_router: float32 [512, 8], P('dp')
- grad_expert_in: float32 [8, 512, 2048], P('expert', None, 'dp')
- grad_expert_out: float32 [8, 2048, 512], P('expert', 'dp')
The draws below stay inside these ranges and needn't reach their ends.
Inputs may be any that keep to these rules, and one draw needn't show every extreme that they name: `routes`: each row names two different experts. In every aligned block of 591 rows, the first 224 rows name as first choice the expert whose capacity is 224. `priority`: every aligned block of 591 rows holds each value once. At least one expert has capacity 224.
All inputs are finite; a program needn't handle non-finite values.
Results may differ from the reference program's by a relative error of at most 0.024.
Values may be sent and summed in bfloat16 or wider, within the bound.
No kernel may reach another device: no remote copies, remote signals or barrier semaphores. Data moves between devices by JAX's collectives and lax.ppermute only.
A program may use at most 192 MiB of HBM per device.

```python
import jax
import jax.numpy as jnp
from jax import lax

D = 512
HEADS = 8
HEAD_DIM = 64
FF = 2048
TOP = 2
SEQ = 197
IMG_MB = 3
MICRO = 2
EXPERTS = 8
CAP = 224
TOKENS = 37824


def busy_expert(key):
    return jax.random.randint(jax.random.fold_in(key, 7), (), 0, EXPERTS)


def draw_capacity(key, part):
    values = jax.random.randint(jax.random.fold_in(key, 11), (EXPERTS,), CAP // 2, CAP + 1)
    labels = jnp.arange(EXPERTS)
    return jnp.where(labels == busy_expert(key), CAP, values).astype(jnp.int32)


def draw_routes(key, part):
    block_rows = IMG_MB * SEQ
    blocks = TOKENS // block_rows
    shuffled = jax.random.permutation(jax.random.fold_in(key, 13), EXPERTS)
    first_draw = jax.random.randint(jax.random.fold_in(key, 17), (blocks, block_rows), 0, EXPERTS)
    second_draw = jax.random.randint(jax.random.fold_in(key, 19), (blocks, block_rows), 0, EXPERTS)
    first = shuffled[jnp.minimum(first_draw, second_draw)]
    position = jnp.arange(block_rows)[None, :]
    first = jnp.where(position < CAP, busy_expert(key), first)
    offset = jax.random.randint(jax.random.fold_in(key, 23), (blocks, block_rows), 1, EXPERTS)
    second = (first + offset) % EXPERTS
    return jnp.stack([first, second], -1).reshape(TOKENS, TOP).astype(jnp.int32)


def draw_priority(key, part):
    block_rows = IMG_MB * SEQ
    blocks = TOKENS // block_rows
    block_keys = jax.random.split(jax.random.fold_in(key, 29), blocks)
    orders = jax.vmap(lambda single: jax.random.permutation(single, block_rows))(block_keys)
    return orders.reshape(TOKENS).astype(jnp.int32)


def steps_of(own_key, dims, cuts, low, largest):
    def one(dim, blocks):
        heights = jax.random.uniform(jax.random.fold_in(jax.random.fold_in(own_key, 6), dim), (blocks,), jnp.float32, low / len(cuts), largest / len(cuts))
        return jnp.repeat(jnp.exp(heights), dims[dim] // blocks).reshape((-1,) + (1,) * (len(dims) - dim - 1))

    level = one(*cuts[0])
    for cut in cuts[1:]:
        level = level * one(*cut)
    return level


def gaussian(stream_key, extent, width, reach, cuts=(), kind=jnp.bfloat16):
    level = steps_of(stream_key, extent, cuts, -0.22, 0.18) if cuts else 1.0
    values = jax.random.normal(stream_key, extent, jnp.float32) * width * level
    return jnp.minimum(jnp.maximum(values, -reach), reach).astype(kind)


def setup_inputs(seed: int = 0) -> dict:
    seeds = jax.random.split(jax.random.key(seed), 15)
    tokens = gaussian(seeds[0], (TOKENS, D), 1.0, 6.0, ((0, 32),))
    ln1_gain = jnp.clip(1.0 + 0.1 * jax.random.normal(seeds[1], (D,), jnp.float32), 0.5, 1.5).astype(jnp.bfloat16)
    ln1_bias = gaussian(seeds[2], (D,), 0.1, 0.59765625, ((0, 4),))
    qkv_weight = gaussian(seeds[3], (D, 3 * D), D ** -0.5, 0.25, ((0, 4),))
    out_weight = gaussian(seeds[4], (D, D), (max(D // 64, 1)) ** -0.5, 2.0, ((0, 4),))
    ln2_gain = jnp.clip(1.0 + 0.1 * jax.random.normal(seeds[5], (D,), jnp.float32), 0.5, 1.5).astype(jnp.bfloat16)
    ln2_bias = gaussian(seeds[6], (D,), 0.1, 0.59765625, ((0, 4),))
    router_weight = gaussian(seeds[7], (D, EXPERTS), (4 * D) ** -0.5, 0.125, ((0, 4),))
    expert_in = gaussian(seeds[8], (EXPERTS, D, FF), D ** -0.5, 0.25, ((0, 8),))
    expert_out = gaussian(seeds[9], (EXPERTS, FF, D), (max(FF // (EXPERTS * EXPERTS), 1)) ** -0.5, 1.0, ((0, 8),))
    routes = draw_routes(jax.random.fold_in(seeds[14], 71), 0)
    priority = draw_priority(jax.random.fold_in(seeds[14], 71), 0)
    capacity = draw_capacity(jax.random.fold_in(seeds[14], 71), 0)
    cotangent = gaussian(seeds[13], (TOKENS, D), 1.0, 6.0, ((0, 32),))
    return dict(tokens=tokens, ln1_gain=ln1_gain, ln1_bias=ln1_bias, qkv_weight=qkv_weight, out_weight=out_weight, ln2_gain=ln2_gain, ln2_bias=ln2_bias, router_weight=router_weight, expert_in=expert_in, expert_out=expert_out, routes=routes, priority=priority, capacity=capacity, cotangent=cotangent)


EPSILON = 1e-06
SCALING = 0.125

@jax.custom_vjp
def low(v):
    return lax.optimization_barrier(v.astype(jnp.bfloat16)).astype(jnp.float32)

@jax.custom_vjp
def low_back(v):
    return v

def low_keep(v):
    return (low(v), None)

def low_pass(kept, grad):
    return (grad,)

def back_keep(v):
    return (v, None)

def back_low(kept, grad):
    return (low(grad),)
low.defvjp(low_keep, low_pass)
low_back.defvjp(back_keep, back_low)

def matmul_hi(left, right):
    return jnp.dot(left, right, precision=lax.Precision.HIGHEST)

def layer_norm(values, gain, offset):
    center = values - lax.optimization_barrier(jnp.mean(values, -1, keepdims=True))
    spread = lax.optimization_barrier(jnp.mean(center * center, -1, keepdims=True))
    return center * lax.rsqrt(spread + EPSILON) * gain + offset

def block_ranks(route_rows, order_keys, capacity):
    count = order_keys.shape[0]
    expert_count = capacity.shape[0]
    chosen = jnp.concatenate([route_rows[:, 0], route_rows[:, 1]]).astype(jnp.int32)
    sort_keys = jnp.concatenate([order_keys, order_keys + count]).astype(jnp.int32)
    positions = jnp.arange(2 * count, dtype=jnp.int32)
    inverse = jnp.zeros((2 * count,), jnp.int32).at[sort_keys].set(positions)
    ordered = chosen[inverse]
    labels = jnp.arange(expert_count, dtype=jnp.int32)
    onehot = (ordered[:, None] == labels[None, :]).astype(jnp.int32)
    before = jnp.cumsum(onehot, 0).astype(jnp.int32) - onehot
    rank_sorted = lax.optimization_barrier(jnp.sum(before * onehot, 1)).astype(jnp.int32)
    ranking = jnp.zeros((2 * count,), jnp.int32).at[inverse].set(rank_sorted)
    limit = lax.optimization_barrier(jnp.sum((chosen[:, None] == labels[None, :]).astype(jnp.int32) * capacity[None, :], 1)).astype(jnp.int32)
    return (chosen, ranking, ranking < limit)

def attend(block):
    queries = block[:, :, 0]
    key_rows = block[:, :, 1]
    values = block[:, :, 2]
    scores = low_back(SCALING * jnp.einsum('gqhd,gkhd->ghqk', queries, key_rows, precision=lax.Precision.HIGHEST))
    weights = low(jax.nn.softmax(scores, -1))
    return jnp.einsum('ghqk,gkhd->gqhd', weights, values, precision=lax.Precision.HIGHEST)

def expert_apply(items):
    weight_in, weight_out, inputs = items
    hidden = low_back(matmul_hi(inputs, weight_in))
    active = low(jax.nn.gelu(hidden, approximate=False))
    return low_back(low(matmul_hi(active, weight_out)))

def forward(inputs, gain_one, offset_one, weight_qkv, weight_out, gain_two, offset_two, weight_router, expert_in, expert_out, chosen, ranking, kept):
    token_total = inputs.shape[0]
    features = inputs.shape[1]
    block_rows = IMG_MB * SEQ
    blocks = token_total // block_rows
    normed = low(layer_norm(inputs, gain_one, offset_one))
    projected = low_back(low(matmul_hi(normed, weight_qkv)))
    groups = projected.reshape(token_total // (MICRO * block_rows), MICRO * IMG_MB, SEQ, 3, HEADS, HEAD_DIM)
    attended = lax.map(jax.checkpoint(attend), groups).reshape(token_total, features)
    attended = low_back(low(attended))
    middle = inputs + low_back(matmul_hi(attended, weight_out))
    normed_two = low(layer_norm(middle, gain_two, offset_two))
    logits = low_back(matmul_hi(normed_two, weight_router))
    probs = jax.nn.softmax(logits, -1)
    base = jnp.arange(blocks, dtype=jnp.int32)[:, None] * block_rows
    within = jnp.arange(block_rows, dtype=jnp.int32)
    token_of = base + jnp.concatenate([within, within])[None, :]
    slot_of = jnp.arange(blocks, dtype=jnp.int32)[:, None] * CAP + jnp.where(kept, ranking, 0)
    mask = kept.astype(jnp.float32)[:, :, None]
    buffer = jnp.zeros((EXPERTS, blocks * CAP, features), jnp.float32).at[chosen, slot_of].add(normed_two[token_of] * mask)
    buffer = low_back(buffer)
    returned = lax.map(jax.checkpoint(expert_apply), (expert_in, expert_out, buffer))
    pieces = returned[chosen, slot_of] * mask
    gate_pair = jnp.take_along_axis(probs[token_of], chosen[:, :, None], -1)
    mixed = (pieces * gate_pair).reshape(blocks, 2, block_rows, features).sum(1).reshape(token_total, features)
    return middle + mixed

def reference(tokens, ln1_gain, ln1_bias, qkv_weight, out_weight, ln2_gain, ln2_bias, router_weight, expert_in, expert_out, routes, priority, capacity, cotangent):
    block_rows = IMG_MB * SEQ
    blocks = tokens.shape[0] // block_rows
    chosen, ranking, kept = jax.vmap(block_ranks, in_axes=(0, 0, None))(routes.reshape(blocks, block_rows, TOP), priority.reshape(blocks, block_rows), capacity)
    params = tuple((item.astype(jnp.float32) for item in (tokens, ln1_gain, ln1_bias, qkv_weight, out_weight, ln2_gain, ln2_bias, router_weight, expert_in, expert_out)))

    def run(*weights):
        return forward(*weights, chosen, ranking, kept)
    result, pull = jax.vjp(run, *params)
    grads = pull(cotangent.astype(jnp.float32))
    return (result.astype(jnp.bfloat16), grads[0].astype(jnp.bfloat16), grads[1], grads[2], grads[3], grads[4], grads[5], grads[6], grads[7], grads[8], grads[9])
```

```python
import functools
import jax
import jax.numpy as jnp
from jax import lax
from jax.experimental import pallas as pl
from jax.experimental.pallas import tpu as pltpu
from jax.sharding import Mesh
from jax.sharding import PartitionSpec as P

HEADS = 8
HEAD_DIM = 64
TOP = 2
SEQ = 197
IMG_MB = 3
MICRO = 2
EPSILON = 1e-06
SCALING = 0.125
ROOT_HALF = 0.7071067811865476
INV_ROOT_TWO_PI = 0.3989422804014327
PAD = 16 * ((SEQ + 15) // 16)
ROWS = IMG_MB * PAD
IMAGES = MICRO * IMG_MB
f32 = jnp.float32
bf16 = jnp.bfloat16
NN = (((1,), (0,)), ((), ()))
NT = (((1,), (1,)), ((), ()))
TN = (((0,), (0,)), ((), ()))


def mm(a, b, dims=NN):
    return lax.dot_general(a, b, dims, preferred_element_type=f32)


def whole(shape):
    zeros = (0,) * len(shape)
    return pl.BlockSpec(shape, lambda *_: zeros)


def params(mb=56):
    return pltpu.CompilerParams(vmem_limit_bytes=mb << 20)


def prepare_kernel(tok_ref, cot_ref, prow_ref, pcol_ref, r0_ref, r1_ref, lab_ref, cap_ref, tokp_ref, cotp_ref, slot_ref, slotc_ref, buf):
    total = tok_ref.shape[0]
    for src, dst in ((tok_ref, tokp_ref), (cot_ref, cotp_ref)):
        buf[pl.ds(0, total), :] = src[...].astype(f32)
        for image in range(IMAGES):
            piece = buf[pl.ds(image * SEQ, PAD), :]
            row = lax.broadcasted_iota(jnp.int32, piece.shape, 0)
            dst[image] = jnp.where(row < SEQ, piece, 0.0).astype(bf16)
    labels = lab_ref[...]
    limit = cap_ref[...]
    experts = labels.shape[0]
    for block in range(MICRO):
        below = jnp.where(pcol_ref[block] < prow_ref[block], 1.0, 0.0).astype(bf16)
        first = labels == r0_ref[block]
        second = labels == r1_ref[block]
        hot = jnp.concatenate([jnp.where(first, 1.0, 0.0), jnp.where(second, 1.0, 0.0)], 0)
        counts = mm(hot.astype(bf16), below)
        total_first = jnp.sum(hot[:experts], 1, keepdims=True)
        rank = jnp.where(
            first, counts[:experts], jnp.where(second, counts[experts:] + total_first, 1e6)
        )
        slot = jnp.where(rank < limit, rank, -1.0)
        slot_ref[block] = slot
        wide = jnp.concatenate([slot, jnp.full((128 - experts, ROWS), -1.0, f32)], 0)
        slotc_ref[block] = jnp.transpose(wide)[:, :experts]


def prepare(tokens, cotangent, prow, pcol, r0, r1, labels, limit):
    features = tokens.shape[1]
    experts = labels.shape[0]
    total = tokens.shape[0]
    return pl.pallas_call(
        prepare_kernel,
        out_shape=(
            jax.ShapeDtypeStruct((IMAGES, PAD, features), bf16),
            jax.ShapeDtypeStruct((IMAGES, PAD, features), bf16),
            jax.ShapeDtypeStruct((MICRO, experts, ROWS), f32),
            jax.ShapeDtypeStruct((MICRO, ROWS, experts), f32),
        ),
        scratch_shapes=[pltpu.VMEM((8 * ((total + PAD) // 8), features), f32)],
        compiler_params=params(),
        name="prepare",
    )(tokens, cotangent, prow, pcol, r0, r1, labels, limit)


def norm(values, gain, offset):
    center = values - jnp.mean(values, -1, keepdims=True)
    inverse = lax.rsqrt(jnp.mean(center * center, -1, keepdims=True) + EPSILON)
    normal = center * inverse
    return normal * gain + offset, normal, inverse


def vectors(w_ref):
    quarters = w_ref.shape[0]
    width = w_ref.shape[1] - 16
    row = [w_ref[q, pl.ds(width, 1), :] for q in range(quarters)]

    def pick(index):
        return jnp.concatenate([r[:, index * width : (index + 1) * width] for r in row], 1)

    return pick, width


def dense_weights(w_ref, features):
    width = w_ref.shape[1] - 16
    qkv = w_ref[:, :width, : 3 * features].reshape(features, 3 * features)
    out = w_ref[:, :width, 3 * features : 4 * features].reshape(features, features)
    return qkv, out


def router_rows(pick, labels):
    experts = labels.shape[0]
    table = jnp.concatenate([pick(4 + e) for e in range(experts)], 0)
    order = labels == lax.broadcasted_iota(jnp.int32, (experts, experts), 1)
    return mm(jnp.where(order, 1.0, 0.0).astype(bf16), table).astype(bf16), order


def half_mask(index, value):
    lane = lax.broadcasted_iota(jnp.int32, (1, 2 * HEAD_DIM), 1)
    return jnp.where((lane < HEAD_DIM) == (index == 0), value, 0.0).astype(bf16)


def forward_kernel(tok_ref, w_ref, lab_ref, proj_ref, prob_ref, att_ref, mid_ref, n2_ref, gate_ref):
    features = tok_ref.shape[2]
    pick, _ = vectors(w_ref)
    qkv, out = dense_weights(w_ref, features)
    inputs = tok_ref[0].astype(f32)
    pre, _, _ = norm(inputs, pick(0).astype(f32), pick(1).astype(f32))
    projected = mm(pre.astype(bf16), qkv).astype(bf16)
    proj_ref[0] = projected
    column = lax.broadcasted_iota(jnp.int32, (1, PAD), 1)
    pair = 2 * HEAD_DIM
    parts = []
    for group in range(HEADS // 2):
        q2 = projected[:, group * pair : (group + 1) * pair]
        k2 = projected[:, features + group * pair : features + (group + 1) * pair]
        v2 = projected[:, 2 * features + group * pair : 2 * features + (group + 1) * pair]
        total = None
        for half in range(2):
            scores = mm(q2 * half_mask(half, SCALING), k2, NT)
            scores = jnp.where(column < SEQ, scores, -1e30)
            expos = jnp.exp(scores - jnp.max(scores, -1, keepdims=True))
            probs = (expos * (1.0 / jnp.sum(expos, -1, keepdims=True))).astype(bf16)
            prob_ref[0, 2 * group + half] = probs
            piece = mm(probs, v2 * half_mask(half, 1.0))
            total = piece if total is None else total + piece
        parts.append(total.astype(bf16))
    attended = jnp.concatenate(parts, 1)
    att_ref[0] = attended
    middle = inputs + mm(attended, out)
    mid_ref[0] = middle
    pre_two, _, _ = norm(middle, pick(2).astype(f32), pick(3).astype(f32))
    normed_two = pre_two.astype(bf16)
    n2_ref[0] = normed_two
    router, _ = router_rows(pick, lab_ref[...])
    logits = mm(router, normed_two, NT)
    expos = jnp.exp(logits - jnp.max(logits, 0, keepdims=True))
    gate_ref[0] = expos / jnp.sum(expos, 0, keepdims=True)


def image(*tail):
    zeros = (0,) * len(tail)
    return pl.BlockSpec((1, *tail), lambda i: (i, *zeros))


def forward_images(tokp, weights, labels):
    count, _, features = tokp.shape
    experts = labels.shape[0]
    flops = 2 * count * PAD * (4 * features * features + 2 * PAD * 256 * HEADS)
    return pl.pallas_call(
        forward_kernel,
        grid=(count,),
        in_specs=[image(PAD, features), whole(weights.shape), whole(labels.shape)],
        out_specs=(
            image(PAD, 3 * features),
            image(HEADS, PAD, PAD),
            image(PAD, features),
            image(PAD, features),
            image(PAD, features),
            image(experts, PAD),
        ),
        out_shape=(
            jax.ShapeDtypeStruct((count, PAD, 3 * features), bf16),
            jax.ShapeDtypeStruct((count, HEADS, PAD, PAD), bf16),
            jax.ShapeDtypeStruct((count, PAD, features), bf16),
            jax.ShapeDtypeStruct((count, PAD, features), f32),
            jax.ShapeDtypeStruct((count, PAD, features), bf16),
            jax.ShapeDtypeStruct((count, experts, PAD), f32),
        ),
        compiler_params=params(),
        cost_estimate=pl.CostEstimate(flops=flops, bytes_accessed=count * 3_000_000, transcendentals=0),
        name="forward",
    )(tokp, weights, labels)


def gelu_pair(field):
    cdf = 0.5 * (1.0 + lax.erf(field * ROOT_HALF))
    return field * cdf, cdf + field * (jnp.exp(-0.5 * field * field) * INV_ROOT_TWO_PI)


def expert_kernel(blocks, *refs):
    n2_refs = refs[:blocks]
    cot_refs = refs[blocks : 2 * blocks]
    slot_ref, gate_ref, w_ref, res_ref, dx_ref, grad_ref, dg_ref = refs[2 * blocks : 2 * blocks + 7]
    x_s, g_s, raw_s, xt_s, gt_s, gs_s, r_acc, dx_acc, h_s, da_s, act_s, dh_s = refs[2 * blocks + 7 :]
    step = pl.program_id(0)
    slots = x_s.shape[0] // blocks
    row = lax.broadcasted_iota(jnp.int32, (slots, ROWS), 0).astype(f32)

    @pl.when(step == 0)
    def _():
        for b in range(blocks):
            span = pl.ds(b * slots, slots)
            hit = row == slot_ref[pl.ds(b, 1), :]
            pick = jnp.where(hit, 1.0, 0.0)
            gate = jnp.sum(jnp.where(hit, gate_ref[pl.ds(b, 1), :], 0.0), 1, keepdims=True)
            pick = pick.astype(bf16)
            x = mm(pick, n2_refs[b][...])
            raw = mm(pick, cot_refs[b][...])
            x_s[span, :] = x.astype(bf16)
            raw_s[span, :] = raw.astype(bf16)
            g = gate * raw
            g_s[span, :] = g.astype(bf16)
            gs_s[span, :] = jnp.broadcast_to(gate, (slots, 128))
        xt_s[...] = jnp.transpose(x_s[...])
        gt_s[...] = jnp.transpose(g_s[...])
        r_acc[...] = jnp.zeros_like(r_acc)
        dx_acc[...] = jnp.zeros_like(dx_acc)

    w_in = w_ref[0, 0]
    w_out = w_ref[0, 1]
    h_s[...] = mm(x_s[...], w_in)
    da_s[...] = mm(g_s[...], w_out, NT)
    tile = 16

    @pl.loop(0, x_s.shape[0] // tile)
    def _(r):
        span = pl.ds(pl.multiple_of(r * tile, tile), tile)
        act, slope = gelu_pair(h_s[span, :])
        act_s[span, :] = act.astype(bf16)
        dh_s[span, :] = (da_s[span, :] * slope).astype(bf16)

    r_acc[...] += mm(act_s[...], w_out)
    dx_acc[...] += mm(dh_s[...], w_in, NT)
    grad_ref[0, 0] = mm(xt_s[...], dh_s[...]).astype(bf16)
    grad_ref[0, 1] = mm(gt_s[...], act_s[...]).astype(bf16)

    @pl.when(step == pl.num_programs(0) - 1)
    def _():
        dx_ref[...] = dx_acc[...].astype(bf16).reshape(dx_ref.shape)
        for b in range(blocks):
            span = pl.ds(b * slots, slots)
            res = r_acc[span, :].astype(bf16).astype(f32)
            dgate = jnp.sum(res * raw_s[span, :].astype(f32), 1, keepdims=True)
            res_ref[b] = (res * gs_s[span, 0:1]).astype(bf16)
            hit = row == slot_ref[pl.ds(b, 1), :]
            dg_ref[pl.ds(b, 1), :] = jnp.sum(jnp.where(hit, dgate, 0.0), 0, keepdims=True)


def expert_apply(n2, cot, slot, gate, weights, slots):
    blocks = len(n2)
    features = n2[0].shape[1]
    quarters, _, _, width = weights.shape
    rows = blocks * slots
    return pl.pallas_call(
        functools.partial(expert_kernel, blocks),
        grid=(quarters,),
        in_specs=[whole(piece.shape) for piece in (*n2, *cot)]
        + [
            whole(slot.shape),
            whole(gate.shape),
            pl.BlockSpec((1, 2, features, width), lambda i: (i, 0, 0, 0)),
        ],
        out_specs=(
            whole((blocks, slots, features)),
            whole((blocks, slots, features)),
            pl.BlockSpec((1, 2, features, width), lambda i: (i, 0, 0, 0)),
            whole((blocks, ROWS)),
        ),
        out_shape=(
            jax.ShapeDtypeStruct((blocks, slots, features), bf16),
            jax.ShapeDtypeStruct((blocks, slots, features), bf16),
            jax.ShapeDtypeStruct((quarters, 2, features, width), bf16),
            jax.ShapeDtypeStruct((blocks, ROWS), f32),
        ),
        scratch_shapes=[
            pltpu.VMEM((rows, features), bf16),
            pltpu.VMEM((rows, features), bf16),
            pltpu.VMEM((rows, features), bf16),
            pltpu.VMEM((features, rows), bf16),
            pltpu.VMEM((features, rows), bf16),
            pltpu.VMEM((rows, 128), f32),
            pltpu.VMEM((rows, features), f32),
            pltpu.VMEM((rows, features), f32),
            pltpu.VMEM((rows, width), f32),
            pltpu.VMEM((rows, width), f32),
            pltpu.VMEM((rows, width), bf16),
            pltpu.VMEM((rows, width), bf16),
        ],
        compiler_params=params(),
        cost_estimate=pl.CostEstimate(
            flops=12 * rows * features * width * quarters, bytes_accessed=16_000_000, transcendentals=0
        ),
        name="expert",
    )(*n2, *cot, slot, gate, weights)


def selector(columns, slots):
    count = columns.shape[1]
    lane = lax.broadcasted_iota(jnp.int32, (columns.shape[0], slots), 1).astype(f32)
    pieces = [jnp.where(columns[:, k : k + 1] == lane, 1.0, 0.0).astype(bf16) for k in range(count)]
    return jnp.concatenate(pieces, 1)


def combine_kernel(count, slotr_ref, *refs):
    res_refs = refs[:count]
    dx_refs = refs[count : 2 * count]
    mixed_ref, dn2_ref = refs[2 * count :]
    slots = res_refs[0].shape[1]
    wide = jnp.concatenate([slotr_ref[0], jnp.full((128 - count, ROWS), -1.0, f32)], 0)
    pick = selector(jnp.transpose(wide)[:, :count], slots)
    mixed_ref[0] = mm(pick, jnp.concatenate([r[0] for r in res_refs], 0)).astype(bf16)
    dn2_ref[0] = mm(pick, jnp.concatenate([r[0] for r in dx_refs], 0)).astype(bf16)


def combine(slotr, results, dxs, first):
    count = len(results)
    _, slots, features = results[0].shape
    blocks = slotr.shape[0]
    piece = pl.BlockSpec((1, slots, features), lambda i: (i + first, 0, 0))
    return pl.pallas_call(
        functools.partial(combine_kernel, count),
        grid=(blocks,),
        in_specs=[pl.BlockSpec((1, count, ROWS), lambda i: (i, 0, 0))] + [piece] * (2 * count),
        out_specs=(image(ROWS, features), image(ROWS, features)),
        out_shape=(jax.ShapeDtypeStruct((blocks, ROWS, features), bf16),) * 2,
        compiler_params=params(),
        cost_estimate=pl.CostEstimate(
            flops=4 * blocks * ROWS * features * slots * count, bytes_accessed=10_000_000, transcendentals=0
        ),
        name="combine",
    )(slotr, *results, *dxs)


def norm_back(grad, normal, inverse, gain):
    scaled = grad * gain
    return inverse * (
        scaled
        - jnp.mean(scaled, -1, keepdims=True)
        - normal * jnp.mean(scaled * normal, -1, keepdims=True)
    )


def backward_kernel(count, tok_ref, cot_ref, proj_ref, prob_ref, att_ref, mid_ref, n2_ref, gate_ref, dg_ref, slotc_ref, mixp_ref, dn2p_ref, w_ref, lab_ref, *refs):
    res_refs = refs[:count]
    dx_refs = refs[count : 2 * count]
    out_ref, dtok_ref, gq_ref, go_ref, gr_ref, gv_ref = refs[2 * count :]
    step = pl.program_id(0)
    features = tok_ref.shape[2]

    @pl.when(step == 0)
    def _():
        gq_ref[...] = jnp.zeros_like(gq_ref)
        go_ref[...] = jnp.zeros_like(go_ref)
        gr_ref[...] = jnp.zeros_like(gr_ref)
        gv_ref[...] = jnp.zeros_like(gv_ref)

    pick, _ = vectors(w_ref)
    qkv, out = dense_weights(w_ref, features)
    slots = res_refs[0].shape[1]
    choose = selector(slotc_ref[0], slots)
    middle = mid_ref[0]
    mixed = mm(choose, jnp.concatenate([r[0] for r in res_refs], 0)) + mixp_ref[0].astype(f32)
    out_ref[0] = (middle + mixed).astype(bf16)
    gates = gate_ref[0]
    dgates = dg_ref[0]
    dlogits = gates * (dgates - jnp.sum(gates * dgates, 0, keepdims=True))
    dlogits = dlogits.astype(bf16)
    router, order = router_rows(pick, lab_ref[...])
    normed_two = n2_ref[0]
    turn = jnp.where(order, 1.0, 0.0).astype(bf16)
    gr_ref[...] += mm(dlogits, normed_two)
    dn2 = (
        mm(dlogits, router, TN)
        + mm(choose, jnp.concatenate([r[0] for r in dx_refs], 0))
        + dn2p_ref[0].astype(f32)
    )
    gain_two = pick(2).astype(f32)
    _, normal_two, inverse_two = norm(middle, gain_two, 0.0)
    gv_ref[2:3, :] += jnp.sum(dn2 * normal_two, 0, keepdims=True)
    gv_ref[3:4, :] += jnp.sum(dn2, 0, keepdims=True)
    dmiddle = cot_ref[0].astype(f32) + norm_back(dn2, normal_two, inverse_two, gain_two)
    dbranch = dmiddle.astype(bf16)
    go_ref[...] += mm(att_ref[0], dbranch, TN)
    dattended = mm(dbranch, out, NT).astype(bf16)
    pair = 2 * HEAD_DIM
    dqs, dks, dvs = [], [], []
    for group in range(HEADS // 2):
        q2 = proj_ref[0, :, group * pair : (group + 1) * pair]
        k2 = proj_ref[0, :, features + group * pair : features + (group + 1) * pair]
        v2 = proj_ref[0, :, 2 * features + group * pair : 2 * features + (group + 1) * pair]
        d2 = dattended[:, group * pair : (group + 1) * pair]
        dq = dk = dv = None
        for half in range(2):
            probs = prob_ref[0, 2 * group + half]
            wide = probs.astype(f32)
            dm = d2 * half_mask(half, 1.0)
            dweights = mm(dm, v2, NT)
            inner = jnp.sum(dweights * wide, -1, keepdims=True)
            dscores = (wide * (dweights - inner)).astype(bf16)
            part_q = mm(dscores, k2 * half_mask(half, SCALING))
            part_k = mm(dscores, q2 * half_mask(half, SCALING), TN)
            part_v = mm(probs, dm, TN)
            dq = part_q if dq is None else dq + part_q
            dk = part_k if dk is None else dk + part_k
            dv = part_v if dv is None else dv + part_v
        dqs.append(dq.astype(bf16))
        dks.append(dk.astype(bf16))
        dvs.append(dv.astype(bf16))
    dprojected = jnp.concatenate(dqs + dks + dvs, 1)
    gain_one = pick(0).astype(f32)
    pre, normal_one, inverse_one = norm(tok_ref[0].astype(f32), gain_one, pick(1).astype(f32))
    gq_ref[...] += mm(pre.astype(bf16), dprojected, TN)
    dnormed = mm(dprojected, qkv, NT)
    gv_ref[0:1, :] += jnp.sum(dnormed * normal_one, 0, keepdims=True)
    gv_ref[1:2, :] += jnp.sum(dnormed, 0, keepdims=True)
    dtok_ref[0] = (dmiddle + norm_back(dnormed, normal_one, inverse_one, gain_one)).astype(bf16)


def backward_images(first, tokp, cotp, saved, dgates, slotc, mixed_part, dn2_part, weights, labels, results, dxs):
    projected, probs, attended, middle, n2, gates = saved
    count = len(results)
    images = projected.shape[0]
    features = tokp.shape[2]
    experts = labels.shape[0]
    slots = results[0].shape[1]

    def late(*tail):
        zeros = (0,) * len(tail)
        return pl.BlockSpec((1, *tail), lambda i: (i + first, *zeros))

    block = pl.BlockSpec((1, slots, features), lambda i: (lax.div(i + first, IMG_MB), 0, 0))
    return pl.pallas_call(
        functools.partial(backward_kernel, count),
        grid=(images,),
        in_specs=[
            late(PAD, features),
            late(PAD, features),
            image(PAD, 3 * features),
            image(HEADS, PAD, PAD),
            image(PAD, features),
            image(PAD, features),
            image(PAD, features),
            image(experts, PAD),
            late(experts, PAD),
            late(PAD, count),
            late(PAD, features),
            late(PAD, features),
            whole(weights.shape),
            whole(labels.shape),
        ]
        + [block] * (2 * count),
        out_specs=(
            image(PAD, features),
            image(PAD, features),
            whole((features, 3 * features)),
            whole((features, features)),
            whole((experts, features)),
            whole((8, features)),
        ),
        out_shape=(
            jax.ShapeDtypeStruct((images, PAD, features), bf16),
            jax.ShapeDtypeStruct((images, PAD, features), bf16),
            jax.ShapeDtypeStruct((features, 3 * features), f32),
            jax.ShapeDtypeStruct((features, features), f32),
            jax.ShapeDtypeStruct((experts, features), f32),
            jax.ShapeDtypeStruct((8, features), f32),
        ),
        compiler_params=params(),
        cost_estimate=pl.CostEstimate(
            flops=5 * 2 * images * PAD * 4 * features * features, bytes_accessed=images * 5_000_000, transcendentals=0
        ),
        name="backward",
    )(tokp, cotp, projected, probs, attended, middle, n2, gates, dgates, slotc, mixed_part, dn2_part, weights, labels, *results, *dxs)


def norm_forward(values, gain, offset):
    center = values - jnp.mean(values, -1, keepdims=True)
    inverse = lax.rsqrt(jnp.mean(center * center, -1, keepdims=True) + EPSILON)
    normal = center * inverse
    return (normal * gain + offset, normal, inverse)


def norm_backward(grad, normal, inverse, gain):
    scaled = grad * gain
    return inverse * (
        scaled
        - jnp.mean(scaled, -1, keepdims=True)
        - normal * jnp.mean(scaled * normal, -1, keepdims=True)
    )


def gelu_value(field):
    return 0.5 * field * (1.0 + lax.erf(field * ROOT_HALF))


def gelu_slope(field):
    return (
        0.5 * (1.0 + lax.erf(field * ROOT_HALF))
        + field * jnp.exp(-0.5 * field * field) * INV_ROOT_TWO_PI
    )


def block_ranks(route_rows, order_keys, capacity):
    count = order_keys.shape[0]
    expert_count = capacity.shape[0]
    chosen = jnp.concatenate([route_rows[:, 0], route_rows[:, 1]])
    sort_keys = jnp.concatenate([order_keys, order_keys + count])
    positions = jnp.arange(2 * count, dtype=jnp.int32)
    inverse = jnp.zeros((2 * count,), jnp.int32).at[sort_keys].set(positions)
    ordered = chosen[inverse]
    labels = jnp.arange(expert_count, dtype=jnp.int32)
    onehot = (ordered[:, None] == labels[None, :]).astype(jnp.int32)
    before = jnp.cumsum(onehot, 0) - onehot
    rank_sorted = jnp.sum(before * onehot, 1)
    ranking = jnp.zeros((2 * count,), jnp.int32).at[inverse].set(rank_sorted)
    pair_onehot = chosen[:, None] == labels[None, :]
    limit = jnp.sum(pair_onehot.astype(jnp.int32) * capacity[None, :], 1)
    return (chosen, ranking, ranking < limit, pair_onehot.astype(jnp.float32))


def exchanged(
    tokens,
    ln1_gain,
    ln1_bias,
    qkv_weight,
    out_weight,
    ln2_gain,
    ln2_bias,
    router_weight,
    expert_in,
    expert_out,
    routes,
    priority,
    capacity,
    cotangent,
):
    f32 = jnp.float32
    bf16 = jnp.bfloat16
    gathered = (
        lax.all_gather(ln1_gain, "dp", axis=0, tiled=True),
        lax.all_gather(ln1_bias, "dp", axis=0, tiled=True),
        lax.all_gather(qkv_weight, "dp", axis=0, tiled=True),
        lax.all_gather(out_weight, "dp", axis=0, tiled=True),
        lax.all_gather(ln2_gain, "dp", axis=0, tiled=True),
        lax.all_gather(ln2_bias, "dp", axis=0, tiled=True),
        lax.all_gather(router_weight, "dp", axis=0, tiled=True),
    )
    gain_one = gathered[0].astype(f32)
    offset_one = gathered[1].astype(f32)
    weight_qkv = gathered[2]
    weight_out = gathered[3]
    gain_two = gathered[4].astype(f32)
    offset_two = gathered[5].astype(f32)
    weight_router = gathered[6]
    features = tokens.shape[1]
    owners = lax.axis_size("expert")
    per_owner = expert_in.shape[0]
    experts = owners * per_owner
    slots = 8 * (3 * TOP * IMG_MB * SEQ // (16 * experts) + 1)
    row_count = IMG_MB * SEQ
    sum_gain_one = jnp.zeros((features,), f32)
    sum_offset_one = jnp.zeros((features,), f32)
    sum_qkv = jnp.zeros(weight_qkv.shape, f32)
    sum_out = jnp.zeros(weight_out.shape, f32)
    sum_gain_two = jnp.zeros((features,), f32)
    sum_offset_two = jnp.zeros((features,), f32)
    sum_router = jnp.zeros(weight_router.shape, f32)
    sum_expert_in = jnp.zeros(expert_in.shape, f32)
    sum_expert_out = jnp.zeros(expert_out.shape, f32)
    outputs = []
    input_grads = []
    for micro in range(MICRO):
        start = micro * row_count
        inputs = tokens[start : start + row_count].astype(f32)
        pre_one, normal_one, inverse_one = norm_forward(inputs, gain_one, offset_one)
        normed = pre_one.astype(bf16)
        projected = jnp.dot(normed, weight_qkv, preferred_element_type=f32).astype(bf16)
        projected = projected.reshape(IMG_MB, SEQ, 3, HEADS, HEAD_DIM)
        queries = projected[:, :, 0]
        key_rows = projected[:, :, 1]
        values = projected[:, :, 2]
        scores = (
            jnp.einsum("gqhd,gkhd->ghqk", queries, key_rows, preferred_element_type=f32) * SCALING
        )
        highest = jnp.max(scores, -1, keepdims=True)
        expos = jnp.exp(scores - highest)
        totals = jnp.sum(expos, -1, keepdims=True)
        log_total = highest + jnp.log(totals)
        attn_weights = (expos / totals).astype(bf16)
        attended = jnp.einsum(
            "ghqk,gkhd->gqhd", attn_weights, values, preferred_element_type=f32
        ).astype(bf16)
        attended = attended.reshape(row_count, features)
        middle = inputs + jnp.dot(attended, weight_out, preferred_element_type=f32)
        pre_two, normal_two, inverse_two = norm_forward(middle, gain_two, offset_two)
        normed_two = pre_two.astype(bf16)
        logits = jnp.dot(normed_two, weight_router, preferred_element_type=f32)
        gates = jax.nn.softmax(logits, -1)
        route_rows = routes[start : start + row_count]
        chosen, ranking, kept, pair_onehot = block_ranks(
            route_rows, priority[start : start + row_count], capacity
        )
        keep_float = kept.astype(f32)
        slot_send = jnp.where(kept, ranking, slots)
        slot_read = jnp.where(kept, ranking, 0)
        doubled = jnp.concatenate([normed_two, normed_two], 0)
        send = (
            jnp.zeros((experts, slots, features), bf16)
            .at[chosen, slot_send]
            .set(doubled, mode="drop")
        )
        received = lax.all_to_all(
            send.reshape(owners, per_owner, slots, features),
            "expert",
            split_axis=0,
            concat_axis=0,
            tiled=True,
        )
        hidden = jnp.einsum("sjcd,jdf->sjcf", received, expert_in, preferred_element_type=f32)
        active = gelu_value(hidden).astype(bf16)
        result = jnp.einsum(
            "sjcf,jfd->sjcd", active, expert_out, preferred_element_type=f32
        ).astype(bf16)
        back = lax.all_to_all(result, "expert", split_axis=0, concat_axis=0, tiled=True).reshape(
            experts, slots, features
        )
        pieces = back[chosen, slot_read].astype(f32) * keep_float[:, None]
        picked = jnp.take_along_axis(gates, route_rows, 1)
        gate_pair = jnp.concatenate([picked[:, 0], picked[:, 1]])
        mixed = pieces[:row_count] * picked[:, 0:1] + pieces[row_count:] * picked[:, 1:2]
        outputs.append((middle + mixed).astype(bf16))
        grad_out = cotangent[start : start + row_count].astype(f32)
        grad_doubled = jnp.concatenate([grad_out, grad_out], 0)
        dgate = jnp.sum(grad_doubled * pieces, -1)
        dpieces = (grad_doubled * (gate_pair * keep_float)[:, None]).astype(bf16)
        dgates = (
            pair_onehot[:row_count] * dgate[:row_count, None]
            + pair_onehot[row_count:] * dgate[row_count:, None]
        )
        dlogits = (gates * (dgates - jnp.sum(gates * dgates, -1, keepdims=True))).astype(bf16)
        grad_send = (
            jnp.zeros((experts, slots, features), bf16)
            .at[chosen, slot_send]
            .set(dpieces, mode="drop")
        )
        grad_received = lax.all_to_all(
            grad_send.reshape(owners, per_owner, slots, features),
            "expert",
            split_axis=0,
            concat_axis=0,
            tiled=True,
        )
        dactive = jnp.einsum(
            "sjcd,jfd->sjcf", grad_received, expert_out, preferred_element_type=f32
        )
        dhidden = (dactive * gelu_slope(hidden)).astype(bf16)
        grad_w_out = jnp.einsum("sjcf,sjcd->jfd", active, grad_received, preferred_element_type=f32)
        grad_w_in = jnp.einsum("sjcd,sjcf->jdf", received, dhidden, preferred_element_type=f32)
        sum_expert_in = sum_expert_in + grad_w_in
        sum_expert_out = sum_expert_out + grad_w_out
        dsent = jnp.einsum("sjcf,jdf->sjcd", dhidden, expert_in, preferred_element_type=f32).astype(
            bf16
        )
        dreturn = lax.all_to_all(dsent, "expert", split_axis=0, concat_axis=0, tiled=True).reshape(
            experts, slots, features
        )
        dpair = dreturn[chosen, slot_read].astype(f32) * keep_float[:, None]
        dnormed_two = (
            jnp.dot(dlogits, weight_router.T, preferred_element_type=f32)
            + dpair[:row_count]
            + dpair[row_count:]
        )
        sum_router = sum_router + jnp.dot(normed_two.T, dlogits, preferred_element_type=f32)
        sum_gain_two = sum_gain_two + jnp.sum(dnormed_two * normal_two, 0)
        sum_offset_two = sum_offset_two + jnp.sum(dnormed_two, 0)
        dmiddle = grad_out + norm_backward(dnormed_two, normal_two, inverse_two, gain_two)
        dbranch = dmiddle.astype(bf16)
        sum_out = sum_out + jnp.dot(attended.T, dbranch, preferred_element_type=f32)
        dattended = jnp.dot(dbranch, weight_out.T, preferred_element_type=f32).astype(bf16)
        dattended = dattended.reshape(IMG_MB, SEQ, HEADS, HEAD_DIM)
        again = (
            jnp.einsum("gqhd,gkhd->ghqk", queries, key_rows, preferred_element_type=f32) * SCALING
        )
        probs_again = jnp.exp(again - log_total)
        dvalues = jnp.einsum(
            "ghqk,gqhd->gkhd", probs_again.astype(bf16), dattended, preferred_element_type=f32
        )
        dweights = jnp.einsum("gqhd,gkhd->ghqk", dattended, values, preferred_element_type=f32)
        inner = jnp.sum(dweights * probs_again, -1, keepdims=True)
        dscores = (probs_again * (dweights - inner)).astype(bf16)
        dqueries = (
            jnp.einsum("ghqk,gkhd->gqhd", dscores, key_rows, preferred_element_type=f32) * SCALING
        )
        dkeys = (
            jnp.einsum("ghqk,gqhd->gkhd", dscores, queries, preferred_element_type=f32) * SCALING
        )
        dprojected = (
            jnp.stack([dqueries, dkeys, dvalues], 2).astype(bf16).reshape(row_count, 3 * features)
        )
        sum_qkv = sum_qkv + jnp.dot(normed.T, dprojected, preferred_element_type=f32)
        dnormed = jnp.dot(dprojected, weight_qkv.T, preferred_element_type=f32)
        sum_gain_one = sum_gain_one + jnp.sum(dnormed * normal_one, 0)
        sum_offset_one = sum_offset_one + jnp.sum(dnormed, 0)
        input_grads.append(
            (dmiddle + norm_backward(dnormed, normal_one, inverse_one, gain_one)).astype(bf16)
        )
    grad_expert_in, grad_expert_out = (
        lax.psum_scatter(
            sum_expert_in.astype(jnp.bfloat16), "dp", scatter_dimension=2, tiled=True
        ).astype(jnp.float32),
        lax.psum_scatter(
            sum_expert_out.astype(jnp.bfloat16), "dp", scatter_dimension=1, tiled=True
        ).astype(jnp.float32),
    )
    dense = (
        sum_gain_one,
        sum_offset_one,
        sum_qkv,
        sum_out,
        sum_gain_two,
        sum_offset_two,
        sum_router,
    )
    totals_all = (
        lax.psum(dense[0].astype(jnp.bfloat16), "expert").astype(jnp.float32),
        lax.psum(dense[1].astype(jnp.bfloat16), "expert").astype(jnp.float32),
        lax.psum(dense[2].astype(jnp.bfloat16), "expert").astype(jnp.float32),
        lax.psum(dense[3].astype(jnp.bfloat16), "expert").astype(jnp.float32),
        lax.psum(dense[4].astype(jnp.bfloat16), "expert").astype(jnp.float32),
        lax.psum(dense[5].astype(jnp.bfloat16), "expert").astype(jnp.float32),
        lax.psum(dense[6].astype(jnp.bfloat16), "expert").astype(jnp.float32),
    )
    owned = (
        lax.psum_scatter(
            totals_all[0].astype(jnp.bfloat16), "dp", scatter_dimension=0, tiled=True
        ).astype(jnp.float32),
        lax.psum_scatter(
            totals_all[1].astype(jnp.bfloat16), "dp", scatter_dimension=0, tiled=True
        ).astype(jnp.float32),
        lax.psum_scatter(
            totals_all[2].astype(jnp.bfloat16), "dp", scatter_dimension=0, tiled=True
        ).astype(jnp.float32),
        lax.psum_scatter(
            totals_all[3].astype(jnp.bfloat16), "dp", scatter_dimension=0, tiled=True
        ).astype(jnp.float32),
        lax.psum_scatter(
            totals_all[4].astype(jnp.bfloat16), "dp", scatter_dimension=0, tiled=True
        ).astype(jnp.float32),
        lax.psum_scatter(
            totals_all[5].astype(jnp.bfloat16), "dp", scatter_dimension=0, tiled=True
        ).astype(jnp.float32),
        lax.psum_scatter(
            totals_all[6].astype(jnp.bfloat16), "dp", scatter_dimension=0, tiled=True
        ).astype(jnp.float32),
    )
    block_out = jnp.concatenate(outputs, 0)
    grad_tokens = jnp.concatenate(input_grads, 0)
    return (
        block_out,
        grad_tokens,
        owned[0],
        owned[1],
        owned[2],
        owned[3],
        owned[4],
        owned[5],
        owned[6],
        grad_expert_in,
        grad_expert_out,
    )


SWAP = [(0, 1), (1, 0)]
OUTWARD = [(1, 0), (2, 3)]
INWARD = [(0, 1), (3, 2)]
MIDDLE = [(1, 2), (2, 1)]
ALONG = ((0, 1, 2, 3), (1, 2, 0, 3), (2, 1, 3, 0), (3, 2, 1, 0))


def add(*pieces):
    total = pieces[0].astype(f32)
    for piece in pieces[1:]:
        total = total + piece.astype(f32)
    return total.astype(bf16)


def gather_experts(expert_in, expert_out, y, core):
    width = expert_in.shape[2] // 4

    def quarter(index):
        return jnp.stack(
            [
                lax.dynamic_slice_in_dim(expert_in[0], index * width, width, 1),
                lax.dynamic_slice_in_dim(expert_out[0], index * width, width, 0),
            ]
        )

    own = [quarter(2 * (y ^ (j & 1)) + (core ^ (j >> 1))) for j in range(4)]
    one = own[0]
    near = lax.ppermute(one, "z", OUTWARD) + lax.ppermute(one, "z", MIDDLE)
    inward = lax.ppermute(one, "z", INWARD)
    second = inward + lax.ppermute(near, "z", OUTWARD)
    third = lax.ppermute(inward, "z", MIDDLE)
    third = third + lax.ppermute(third, "z", OUTWARD)
    held = [own]
    for piece in (near, second, third):
        across = lax.ppermute(piece, "y", SWAP)
        held.append(
            [piece, across, lax.ppermute(piece, "core", SWAP), lax.ppermute(across, "core", SWAP)]
        )
    return [jnp.stack(pieces) for pieces in held]


def reduce_expert(grad):
    half = add(grad[:2], lax.ppermute(grad[2:], "core", SWAP))
    return add(half[0], lax.ppermute(half[1], "y", SWAP))


def reduce_along(pieces):
    own, near, second, third = pieces
    first_in = lax.ppermute(third, "z", INWARD)
    second_in = lax.ppermute(second, "z", INWARD)
    second_mid = lax.ppermute(add(third, first_in), "z", MIDDLE)
    third_in = lax.ppermute(near, "z", INWARD)
    third_mid = lax.ppermute(add(near, second_in), "z", MIDDLE)
    third_out = lax.ppermute(add(second, second_mid), "z", OUTWARD)
    total = own.astype(f32) + third_in.astype(f32) + third_mid.astype(f32) + third_out.astype(f32)
    return total


def paired(
    tokens,
    ln1_gain,
    ln1_bias,
    qkv_weight,
    out_weight,
    ln2_gain,
    ln2_bias,
    router_weight,
    expert_in,
    expert_out,
    routes,
    priority,
    capacity,
    cotangent,
):
    y, core, z, x = (lax.axis_index(name) for name in ("y", "core", "z", "x"))
    features = tokens.shape[1]
    experts = capacity.shape[0]
    width = qkv_weight.shape[0]
    count = experts // 2
    slots = 8 * (3 * TOP * IMG_MB * SEQ // (16 * experts) + 1)
    lanes = 4 * features
    extra = jnp.concatenate([ln1_gain, ln1_bias, ln2_gain, ln2_bias, router_weight.T.reshape(-1)])
    extra = jnp.pad(extra[None], ((0, 15), (0, lanes - extra.shape[0])))
    packed = jnp.concatenate([jnp.concatenate([qkv_weight, out_weight], 1), extra], 0)
    weights = lax.all_gather(packed, ("y", "core"), axis=0)

    along = jnp.array(ALONG, jnp.int32)[z]
    labels = jnp.concatenate([2 * along + x, 2 * along + (1 - x)])
    limit = jnp.sum(
        jnp.where(labels[:, None] == jnp.arange(experts)[None, :], capacity[None, :], 0), 1
    ).astype(f32)

    def rows_of(values, fill):
        cut = jnp.pad(
            values.reshape(MICRO, IMG_MB, SEQ), ((0, 0), (0, 0), (0, PAD - SEQ)), constant_values=fill
        )
        return cut.reshape(MICRO, 1, ROWS)

    prow = rows_of(priority, 1 << 20)
    tokp, cotp, slot, slotc = prepare(
        tokens,
        cotangent,
        prow,
        prow.reshape(MICRO, ROWS, 1),
        rows_of(routes[:, 0], -1),
        rows_of(routes[:, 1], -1),
        labels[:, None],
        limit[:, None],
    )
    held = gather_experts(expert_in, expert_out, y, core)
    cot_other = lax.ppermute(cotp, "x", SWAP)
    slot_other = lax.ppermute(slot[:, count:], "x", SWAP)
    saved = []
    n2_other = []
    labels_column = labels[:, None]
    for micro in range(MICRO):
        start = micro * IMG_MB
        saved.append(forward_images(tokp[start : start + IMG_MB], weights, labels_column))
        n2_other.append(lax.ppermute(saved[-1][4], "x", SWAP))
    gates = jnp.stack([piece[5] for piece in saved])
    gates = gates.transpose(0, 2, 1, 3).reshape(MICRO, experts, ROWS)
    gates_other = lax.ppermute(gates[:, count:], "x", SWAP)

    n2 = [piece[4].reshape(ROWS, features) for piece in saved]
    n2 += [piece.reshape(ROWS, features) for piece in n2_other]
    cot = [piece[m * IMG_MB : (m + 1) * IMG_MB].reshape(ROWS, features) for piece in (cotp, cot_other) for m in range(MICRO)]
    slot_all = jnp.concatenate([slot[:, :count], slot_other], 0)
    gate_all = jnp.concatenate([gates[:, :count], gates_other], 0)
    results, dxs, grads, dgs = [], [], [], []
    for k in range(count):
        res, dx, grad, dg = expert_apply(n2, cot, slot_all[:, k], gate_all[:, k], held[k], slots)
        results.append(res)
        dxs.append(dx)
        grads.append(grad)
        dgs.append(dg)
    mixed, dn2 = combine(slot_other, results, dxs, MICRO)
    mixed = lax.ppermute(mixed, "x", SWAP).reshape(IMAGES, PAD, features)
    dn2 = lax.ppermute(dn2, "x", SWAP).reshape(IMAGES, PAD, features)
    dg = jnp.stack(dgs, 1)
    dgates = jnp.concatenate([dg[:MICRO], lax.ppermute(dg[MICRO:], "x", SWAP)], 1)
    dgates = dgates.reshape(MICRO, experts, IMG_MB, PAD).transpose(0, 2, 1, 3)
    dgates = dgates.reshape(IMAGES, experts, PAD)
    columns = slotc[:, :, :count].reshape(IMAGES, PAD, count)
    back = []
    for micro in range(MICRO):
        back.append(
            backward_images(
                micro * IMG_MB, tokp, cotp, saved[micro], dgates, columns, mixed, dn2, weights, labels_column, results, dxs
            )
        )
    total = reduce_along([reduce_expert(grad) for grad in grads])
    grad_in = total[0][None]
    grad_out = total[1].T[None]

    gq, go, gr, gv = (sum(piece[i] for piece in back) for i in range(2, 6))
    gr = jnp.sum(jnp.where((jnp.arange(experts)[:, None] == labels[None, :])[:, :, None], gr[None], 0.0), 1)
    body = jnp.concatenate([gq, go], 1).reshape(4, width, lanes)
    tail = jnp.concatenate([gv[:4], gr], 0).reshape(4 + experts, 4, width).transpose(1, 0, 2).reshape(4, 1, -1)
    tail = jnp.pad(tail, ((0, 0), (0, 15), (0, lanes - tail.shape[2])))
    dense = jnp.concatenate([body, tail], 1).astype(bf16)
    dense = lax.psum_scatter(dense, ("y", "core"), scatter_dimension=0, tiled=False)
    dense = lax.psum(dense, ("z", "x")).astype(f32)
    row = dense[width]

    def flat(index):
        joined = jnp.concatenate([piece[index] for piece in back], 0)
        return joined[:, :SEQ].reshape(tokens.shape)

    return (
        flat(0),
        flat(1),
        row[:width],
        row[width : 2 * width],
        dense[:width, : 3 * features],
        dense[:width, 3 * features :],
        row[2 * width : 3 * width],
        row[3 * width : 4 * width],
        row[4 * width : (4 + experts) * width].reshape(experts, width).T,
        grad_in,
        grad_out,
    )


def solution(mesh):
    if mesh.shape["dp"] == 4 and mesh.shape["expert"] == 8:
        mesh = Mesh(mesh.devices.reshape(2, 2, 4, 2), ("y", "core", "z", "x"))
        body, dp, expert = paired, ("y", "core"), ("z", "x")
    else:
        body, dp, expert = exchanged, ("dp",), ("expert",)
    rows = P((*dp, *expert), None)
    return jax.shard_map(
        body,
        mesh=mesh,
        in_specs=(
            rows,
            P(dp),
            P(dp),
            P(dp, None),
            P(dp, None),
            P(dp),
            P(dp),
            P(dp, None),
            P(expert, None, None),
            P(expert, None, None),
            rows,
            P((*dp, *expert)),
            P(),
            rows,
        ),
        out_specs=(
            rows,
            rows,
            P(dp),
            P(dp),
            P(dp, None),
            P(dp, None),
            P(dp),
            P(dp),
            P(dp, None),
            P(expert, None, dp),
            P(expert, dp, None),
        ),
        check_vma=False,
    )
```

```python
import functools
import jax
import jax.numpy as jnp
from jax import lax
from jax.experimental import pallas as pl
from jax.experimental.pallas import tpu as pltpu
from jax.sharding import Mesh
from jax.sharding import PartitionSpec as P

HEADS = 8
HEAD_DIM = 64
TOP = 2
SEQ = 197
IMG_MB = 3
MICRO = 2
EPSILON = 1e-06
SCALING = 0.125
ROOT_HALF = 0.7071067811865476
INV_ROOT_TWO_PI = 0.3989422804014327
PAD = 16 * ((SEQ + 15) // 16)
ROWS = IMG_MB * PAD
IMAGES = MICRO * IMG_MB
f32 = jnp.float32
bf16 = jnp.bfloat16
NN = (((1,), (0,)), ((), ()))
NT = (((1,), (1,)), ((), ()))
TN = (((0,), (0,)), ((), ()))


def mm(a, b, dims=NN):
    return lax.dot_general(a, b, dims, preferred_element_type=f32)


def whole(shape):
    zeros = (0,) * len(shape)
    return pl.BlockSpec(shape, lambda *_: zeros)


def params(mb=60):
    return pltpu.CompilerParams(vmem_limit_bytes=mb << 20)


SHARE = 1.0


def cost(flops, moved):
    return pl.CostEstimate(flops=int(flops * SHARE), bytes_accessed=int(moved * SHARE), transcendentals=0)


Z_AT, X_AT, Y_AT, CORE_AT = 4, 5, 6, 7


def expert_of(place_ref, index):
    return 2 * (place_ref[Z_AT] ^ (index & 3)) + (place_ref[X_AT] ^ (index >> 2))


def label_column(place_ref, experts):
    index = lax.broadcasted_iota(jnp.int32, (experts, 1), 0)
    label = jnp.zeros((experts, 1), jnp.int32)
    for r in range(experts):
        label = jnp.where(index == r, expert_of(place_ref, r), label)
    return label


def wide_transpose(rows, fill):
    pad = jnp.full((128 - rows.shape[0], rows.shape[1]), fill, f32)
    return jnp.transpose(jnp.concatenate([rows, pad], 0))


def pack_kernel(place_ref, g1_ref, b1_ref, g2_ref, b2_ref, qkv_ref, out_ref, router_ref, in_ref, back_ref, packed_ref, one_ref, sem):
    width = qkv_ref.shape[0]
    span = one_ref.shape[1]
    start = pl.multiple_of(place_ref[0] * span, span)
    copies = (
        pltpu.make_async_copy(in_ref.at[0, :, pl.ds(start, span)], one_ref.at[0], sem.at[0]),
        pltpu.make_async_copy(back_ref.at[0, pl.ds(start, span), :], one_ref.at[1], sem.at[1]),
    )
    for copy in copies:
        copy.start()
    packed_ref[0, :width, : qkv_ref.shape[1]] = qkv_ref[...]
    packed_ref[0, :width, qkv_ref.shape[1] :] = out_ref[...]
    experts = router_ref.shape[1]
    router = router_ref[...].astype(f32)
    router = jnp.concatenate([router, jnp.zeros((width, 128 - experts), f32)], 1)
    router = jnp.transpose(router)
    pieces = [ref[...].astype(f32) for ref in (g1_ref, b1_ref, g2_ref, b2_ref)]
    pieces += [router[e : e + 1, :] for e in range(experts)]
    rest = packed_ref.shape[2] - width * len(pieces)
    row = jnp.concatenate(pieces + [jnp.zeros((1, rest), f32)], 1)
    row = jnp.concatenate([row, jnp.zeros((15, row.shape[1]), f32)], 0)
    packed_ref[0, width:, :] = row.astype(bf16)
    for copy in copies:
        copy.wait()


def pack(place, vectors_in, qkv, out, router, expert_in, expert_out):
    width, columns = qkv.shape
    features = out.shape[1]
    span = expert_in.shape[2] // 4
    rows = [vector.reshape(1, width) for vector in vectors_in]
    packed = (1, width + 16, columns + features)
    return pl.pallas_call(
        pack_kernel,
        grid_spec=pltpu.PrefetchScalarGridSpec(
            num_scalar_prefetch=1,
            grid=(1,),
            in_specs=[whole(row.shape) for row in rows]
            + [whole(qkv.shape), whole(out.shape), whole(router.shape)]
            + [pl.BlockSpec(memory_space=pl.ANY)] * 2,
            out_specs=(whole(packed), whole((2, features, span))),
            scratch_shapes=[pltpu.SemaphoreType.DMA((2,))],
        ),
        out_shape=(
            jax.ShapeDtypeStruct(packed, bf16),
            jax.ShapeDtypeStruct((2, features, span), bf16),
        ),
        compiler_params=params(),
        cost_estimate=cost(0, 4_000_000),
        name="pack",
    )(place, *rows, qkv, out, router, expert_in, expert_out)


def prepare_kernel(place_ref, cap_ref, tok_ref, cot_ref, route_ref, prio_ref, tokp_ref, cotp_ref, slot_ref, slotc_ref, buf, keys):
    total = tok_ref.shape[0]
    experts = slot_ref.shape[1]
    for src, dst in ((tok_ref, tokp_ref), (cot_ref, cotp_ref)):
        buf[pl.ds(0, total), :] = src[...].astype(f32)
        for image in range(IMAGES):
            piece = buf[pl.ds(image * SEQ, PAD), :]
            row = lax.broadcasted_iota(jnp.int32, piece.shape, 0)
            dst[image] = jnp.where(row < SEQ, piece, 0.0).astype(bf16)
    keys[...] = jnp.full_like(keys, -1.0)
    keys[pl.ds(0, total), 0:2] = route_ref[...].astype(f32)
    keys[pl.ds(0, total), 2:3] = prio_ref[...].astype(f32)
    labels = label_column(place_ref, experts)
    limit = jnp.zeros((experts, 1), f32)
    for e in range(experts):
        limit = jnp.where(labels == e, cap_ref[e].astype(f32), limit)
    labels = labels.astype(f32)
    for block in range(MICRO):
        columns = []
        for image in range(IMG_MB):
            piece = keys[pl.ds((block * IMG_MB + image) * SEQ, PAD), :]
            row = lax.broadcasted_iota(jnp.int32, piece.shape, 0)
            columns.append(jnp.where(row < SEQ, piece, -1.0))
        column = jnp.concatenate(columns, 0)
        turned = jnp.transpose(column)
        key_column = jnp.where(column[:, 2:3] < 0.0, 1e6, column[:, 2:3])
        below = jnp.where(key_column < turned[2:3, :], 1.0, 0.0).astype(bf16)
        first = labels == turned[0:1, :]
        second = labels == turned[1:2, :]
        hot = jnp.concatenate([jnp.where(first, 1.0, 0.0), jnp.where(second, 1.0, 0.0)], 0)
        counts = mm(hot.astype(bf16), below)
        total_first = jnp.sum(hot[:experts], 1, keepdims=True)
        rank = jnp.where(
            first, counts[:experts], jnp.where(second, counts[experts:] + total_first, 1e6)
        )
        slot = jnp.where(rank < limit, rank, -1.0)
        slot_ref[block] = slot
        slotc_ref[block] = wide_transpose(slot, -1.0)[:, :experts]


def prepare(place, capacity, tokens, cotangent, routes, priority):
    total, features = tokens.shape
    experts = capacity.shape[0]
    tall = 8 * ((total + PAD) // 8)
    priority = priority.reshape(total, 1)
    padded = (IMAGES, PAD, features)
    return pl.pallas_call(
        prepare_kernel,
        grid_spec=pltpu.PrefetchScalarGridSpec(
            num_scalar_prefetch=2,
            grid=(1,),
            in_specs=[whole(tokens.shape)] * 2 + [whole(routes.shape), whole(priority.shape)],
            out_specs=(
                whole(padded),
                whole(padded),
                whole((MICRO, experts, ROWS)),
                whole((MICRO, ROWS, experts)),
            ),
            scratch_shapes=[pltpu.VMEM((tall, features), f32), pltpu.VMEM((tall, 128), f32)],
        ),
        out_shape=(
            jax.ShapeDtypeStruct(padded, bf16),
            jax.ShapeDtypeStruct(padded, bf16),
            jax.ShapeDtypeStruct((MICRO, experts, ROWS), f32),
            jax.ShapeDtypeStruct((MICRO, ROWS, experts), f32),
        ),
        compiler_params=params(),
        cost_estimate=cost(0, 8_000_000),
        name="prepare",
    )(place, capacity, tokens, cotangent, routes, priority)


def norm(values, gain, offset):
    center = values - jnp.mean(values, -1, keepdims=True)
    inverse = lax.rsqrt(jnp.mean(center * center, -1, keepdims=True) + EPSILON)
    normal = center * inverse
    return normal * gain + offset, normal, inverse


def load_dense(place_ref, two_ref, more_ref, w_s, sem):
    copies = [
        pltpu.make_async_copy((two_ref, more_ref)[j // 2].at[j % 2], w_s.at[place_ref[j]], sem.at[j])
        for j in range(4)
    ]
    for copy in copies:
        copy.start()
    for copy in copies:
        copy.wait()


def vectors(w_s):
    quarters = w_s.shape[0]
    width = w_s.shape[1] - 16
    row = [w_s[q, pl.ds(width, 1), :] for q in range(quarters)]

    def pick(index):
        return jnp.concatenate([r[:, index * width : (index + 1) * width] for r in row], 1)

    return pick


def dense_weights(w_s, features):
    width = w_s.shape[1] - 16
    qkv = w_s[:, :width, : 3 * features].reshape(features, 3 * features)
    out = w_s[:, :width, 3 * features :].reshape(features, features)
    return qkv, out


def router_rows(pick, place_ref, experts):
    table = jnp.concatenate([pick(4 + e) for e in range(experts)], 0)
    labels = label_column(place_ref, experts)
    order = labels == lax.broadcasted_iota(jnp.int32, (experts, experts), 1)
    return mm(jnp.where(order, 1.0, 0.0).astype(bf16), table).astype(bf16)


def half_mask(index, value):
    lane = lax.broadcasted_iota(jnp.int32, (1, 2 * HEAD_DIM), 1)
    return jnp.where((lane < HEAD_DIM) == (index == 0), value, 0.0).astype(bf16)


def forward_kernel(place_ref, tok_ref, two_ref, more_ref, proj_ref, prob_ref, att_ref, mid_ref, n2_ref, gate_ref, w_s, sem):
    features = tok_ref.shape[2]
    step = pl.program_id(0)

    @pl.when(step == 0)
    def _():
        load_dense(place_ref, two_ref, more_ref, w_s, sem)

    pick = vectors(w_s)
    qkv, out = dense_weights(w_s, features)
    inputs = tok_ref[0].astype(f32)
    pre, _, _ = norm(inputs, pick(0).astype(f32), pick(1).astype(f32))
    projected = mm(pre.astype(bf16), qkv).astype(bf16)
    proj_ref[0] = projected
    column = lax.broadcasted_iota(jnp.int32, (1, PAD), 1)
    pair = 2 * HEAD_DIM
    parts = []
    for group in range(HEADS // 2):
        q2 = projected[:, group * pair : (group + 1) * pair]
        k2 = projected[:, features + group * pair : features + (group + 1) * pair]
        v2 = projected[:, 2 * features + group * pair : 2 * features + (group + 1) * pair]
        total = None
        for half in range(2):
            scores = mm(q2 * half_mask(half, SCALING), k2, NT)
            scores = jnp.where(column < SEQ, scores, -1e30)
            expos = jnp.exp(scores - jnp.max(scores, -1, keepdims=True))
            probs = (expos * (1.0 / jnp.sum(expos, -1, keepdims=True))).astype(bf16)
            prob_ref[0, 2 * group + half] = probs
            piece = mm(probs, v2 * half_mask(half, 1.0))
            total = piece if total is None else total + piece
        parts.append(total.astype(bf16))
    attended = jnp.concatenate(parts, 1)
    att_ref[0] = attended
    middle = inputs + mm(attended, out)
    mid_ref[0] = middle
    pre_two, _, _ = norm(middle, pick(2).astype(f32), pick(3).astype(f32))
    normed_two = pre_two.astype(bf16)
    n2_ref[0] = normed_two
    router = router_rows(pick, place_ref, gate_ref.shape[0])
    logits = mm(router, normed_two, NT)
    expos = jnp.exp(logits - jnp.max(logits, 0, keepdims=True))
    gates = expos / jnp.sum(expos, 0, keepdims=True)
    for i in range(IMG_MB):

        @pl.when(step == i)
        def _():
            gate_ref[:, i * PAD : (i + 1) * PAD] = gates


def image(*tail):
    zeros = (0,) * len(tail)
    return pl.BlockSpec((1, *tail), lambda i, *_: (i, *zeros))


def forward_images(first, place, tokp, dense, experts):
    features = tokp.shape[2]
    count = IMG_MB
    flops = 2 * count * PAD * (4 * features * features + 2 * PAD * 256 * HEADS)
    return pl.pallas_call(
        forward_kernel,
        grid_spec=pltpu.PrefetchScalarGridSpec(
            num_scalar_prefetch=1,
            grid=(count,),
            in_specs=[pl.BlockSpec((1, PAD, features), lambda i, _: (i + first, 0, 0))]
            + [pl.BlockSpec(memory_space=pl.ANY)] * 2,
            out_specs=(
                image(PAD, 3 * features),
                image(HEADS, PAD, PAD),
                image(PAD, features),
                image(PAD, features),
                image(PAD, features),
                whole((experts, ROWS)),
            ),
            scratch_shapes=[
                pltpu.VMEM((4, *dense[0].shape[1:]), bf16),
                pltpu.SemaphoreType.DMA((4,)),
            ],
        ),
        out_shape=(
            jax.ShapeDtypeStruct((count, PAD, 3 * features), bf16),
            jax.ShapeDtypeStruct((count, HEADS, PAD, PAD), bf16),
            jax.ShapeDtypeStruct((count, PAD, features), bf16),
            jax.ShapeDtypeStruct((count, PAD, features), f32),
            jax.ShapeDtypeStruct((count, PAD, features), bf16),
            jax.ShapeDtypeStruct((experts, ROWS), f32),
        ),
        compiler_params=params(),
        cost_estimate=cost(flops, count * 3_000_000),
        name="forward",
    )(place, tokp, *dense)


def gelu_pair(field):
    cdf = 0.5 * (1.0 + lax.erf(field * ROOT_HALF))
    return field * cdf, cdf + field * (jnp.exp(-0.5 * field * field) * INV_ROOT_TWO_PI)


def expert_kernel(index, own, place_ref, *refs):
    blocks = 2 * MICRO
    n2_refs = refs[:blocks]
    cot_refs = refs[blocks : blocks + 2]
    slot_ref, gate0_ref, gate1_ref, other_ref = refs[blocks + 2 : blocks + 6]
    refs = refs[blocks + 6 :]
    sources = 2 if own else 3
    w_refs = refs[:sources]
    refs = refs[sources:]
    res_ref, dx_ref, keep_ref, send_ref, dg_ref, dgo_ref = refs[:6]
    w_s, sem, n2_s, cot_s, in_sem, x_s, g_s, raw_s, xt_s, gt_s, gs_s, r_acc, dx_acc, act_s, dh_s = refs[6:]
    step = pl.program_id(0)
    quarters, _, _, width = w_s.shape
    slots = x_s.shape[0] // blocks
    row = lax.broadcasted_iota(jnp.int32, (slots, ROWS), 0).astype(f32)

    def copies(j):
        if own:
            start = pl.multiple_of(place_ref[j] * width, width)
            return (
                pltpu.make_async_copy(w_refs[0].at[0, :, pl.ds(start, width)], w_s.at[j, 0], sem.at[2 * j]),
                pltpu.make_async_copy(w_refs[1].at[0, pl.ds(start, width), :], w_s.at[j, 1], sem.at[2 * j + 1]),
            )
        source = w_refs[j] if j < 2 else w_refs[2].at[j - 2]
        return (pltpu.make_async_copy(source, w_s.at[j], sem.at[j]),)

    def slot_row(b):
        if b < MICRO:
            return slot_ref[b, pl.ds(index, 1), :]
        return other_ref[b - MICRO, pl.ds(index + 4, 1), :]

    def gate_row(b):
        if b < MICRO:
            return (gate0_ref, gate1_ref)[b][pl.ds(index, 1), :]
        return other_ref[b, pl.ds(index + 4, 1), :]

    def rows_in(b):
        return (
            pltpu.make_async_copy(n2_refs[b], n2_s.at[b], in_sem.at[2 * b]),
            pltpu.make_async_copy(cot_refs[b // MICRO].at[b % MICRO], cot_s.at[b], in_sem.at[2 * b + 1]),
        )

    @pl.when(step == 0)
    def _():
        for b in range(blocks):
            for copy in rows_in(b):
                copy.start()
        for j in range(quarters):
            for copy in copies(j):
                copy.start()
        r_acc[...] = jnp.zeros_like(r_acc)
        dx_acc[...] = jnp.zeros_like(dx_acc)
        for b in range(blocks):
            for copy in rows_in(b):
                copy.wait()
            span = pl.ds(b * slots, slots)
            hit = row == slot_row(b)
            pick = jnp.where(hit, 1.0, 0.0)
            gate = jnp.sum(jnp.where(hit, gate_row(b), 0.0), 1, keepdims=True)
            pick = pick.astype(bf16)
            x = mm(pick, n2_s[b])
            raw = mm(pick, cot_s[b])
            x_s[span, :] = x.astype(bf16)
            raw_s[span, :] = raw.astype(bf16)
            g = gate * raw
            g_s[span, :] = g.astype(bf16)
            gs_s[span, :] = jnp.broadcast_to(gate, (slots, 128))
        xt_s[...] = jnp.transpose(x_s[...])
        gt_s[...] = jnp.transpose(g_s[...])

    for j in range(quarters):

        @pl.when(step == j)
        def _():
            for copy in copies(j):
                copy.wait()

    w_in = w_s[step, 0]
    w_out = w_s[step, 1]
    rows = x_s.shape[0] // 2
    for r in range(2):
        span = pl.ds(r * rows, rows)
        act, slope = gelu_pair(mm(x_s[span, :], w_in))
        act = act.astype(bf16)
        dh = (mm(g_s[span, :], w_out, NT) * slope).astype(bf16)
        act_s[span, :] = act
        dh_s[span, :] = dh
        r_acc[span, :] += mm(act, w_out)
        dx_acc[span, :] += mm(dh, w_in, NT)
    grad_in = mm(xt_s[...], dh_s[...]).astype(bf16)
    grad_out = mm(gt_s[...], act_s[...]).astype(bf16)

    @pl.when(step < quarters // 2)
    def _():
        keep_ref[0, 0] = grad_in
        keep_ref[0, 1] = grad_out

    @pl.when(step >= quarters // 2)
    def _():
        send_ref[0, 0] = grad_in
        send_ref[0, 1] = grad_out

    @pl.when(step == quarters - 1)
    def _():
        dx_ref[...] = dx_acc[...].astype(bf16).reshape(dx_ref.shape)
        for b in range(blocks):
            span = pl.ds(b * slots, slots)
            res = r_acc[span, :].astype(bf16).astype(f32)
            dgate = jnp.sum(res * raw_s[span, :].astype(f32), 1, keepdims=True)
            res_ref[b] = (res * gs_s[span, 0:1]).astype(bf16)
            hit = row == slot_row(b)
            line = jnp.sum(jnp.where(hit, dgate, 0.0), 0, keepdims=True)
            for i in range(IMG_MB):
                to = (dg_ref, dgo_ref)[b // MICRO]
                to[pl.ds((b % MICRO) * IMG_MB + i, 1), :] = line[:, i * PAD : (i + 1) * PAD]


def expert_apply(index, place, n2, cot, tables, weights, slots):
    blocks = 2 * MICRO
    features = n2[0].shape[1]
    own = len(weights) == 2
    quarters = 4
    width = weights[0].shape[2] // (4 if own else 1)
    rows = blocks * slots

    def fixed(shape):
        zeros = (0,) * len(shape)
        return pl.BlockSpec(shape, lambda *_: zeros)

    half = quarters // 2
    pieces = jax.ShapeDtypeStruct((half, 2, features, width), bf16)
    return pl.pallas_call(
        functools.partial(expert_kernel, index, own),
        grid_spec=pltpu.PrefetchScalarGridSpec(
            num_scalar_prefetch=1,
            grid=(quarters,),
            in_specs=[pl.BlockSpec(memory_space=pl.ANY)] * (blocks + 2)
            + [fixed(piece.shape) for piece in tables]
            + [pl.BlockSpec(memory_space=pl.ANY)] * len(weights),
            out_specs=(
                fixed((blocks, slots, features)),
                fixed((blocks, slots, features)),
                pl.BlockSpec((1, 2, features, width), lambda i, _: (jnp.minimum(i, half - 1), 0, 0, 0)),
                pl.BlockSpec((1, 2, features, width), lambda i, _: (jnp.maximum(i - half, 0), 0, 0, 0)),
                fixed((IMAGES, PAD)),
                fixed((IMAGES, PAD)),
            ),
            scratch_shapes=[
                pltpu.VMEM((quarters, 2, features, width), bf16),
                pltpu.SemaphoreType.DMA((2 * quarters,)),
                pltpu.VMEM((blocks, ROWS, features), bf16),
                pltpu.VMEM((blocks, ROWS, features), bf16),
                pltpu.SemaphoreType.DMA((2 * blocks,)),
                pltpu.VMEM((rows, features), bf16),
                pltpu.VMEM((rows, features), bf16),
                pltpu.VMEM((rows, features), bf16),
                pltpu.VMEM((features, rows), bf16),
                pltpu.VMEM((features, rows), bf16),
                pltpu.VMEM((rows, 128), f32),
                pltpu.VMEM((rows, features), f32),
                pltpu.VMEM((rows, features), f32),
                pltpu.VMEM((rows, width), bf16),
                pltpu.VMEM((rows, width), bf16),
            ],
        ),
        out_shape=(
            jax.ShapeDtypeStruct((blocks, slots, features), bf16),
            jax.ShapeDtypeStruct((blocks, slots, features), bf16),
            pieces,
            pieces,
            jax.ShapeDtypeStruct((IMAGES, PAD), f32),
            jax.ShapeDtypeStruct((IMAGES, PAD), f32),
        ),
        compiler_params=params(),
        cost_estimate=cost(12 * rows * features * width * quarters, 16_000_000),
        name="expert",
    )(place, *n2, *cot, *tables, *weights)


def selector(columns, slots):
    count = columns.shape[1]
    lane = lax.broadcasted_iota(jnp.int32, (columns.shape[0], slots), 1).astype(f32)
    pieces = [jnp.where(columns[:, k : k + 1] == lane, 1.0, 0.0).astype(bf16) for k in range(count)]
    return jnp.concatenate(pieces, 1)


def combine_kernel(count, slot_ref, *refs):
    slots = refs[0].shape[1]
    pick = selector(wide_transpose(slot_ref[0, count:, :], -1.0)[:, :count], slots)
    refs[count][0] = mm(pick, jnp.concatenate([r[0] for r in refs[:count]], 0)).astype(bf16)


def combine(slot, pieces, block, blocks):
    count = len(pieces)
    _, slots, features = pieces[0].shape
    piece = pl.BlockSpec((1, slots, features), lambda i: (i + block + MICRO, 0, 0))
    return pl.pallas_call(
        functools.partial(combine_kernel, count),
        grid=(blocks,),
        in_specs=[pl.BlockSpec((1, 2 * count, ROWS), lambda i: (i + block, 0, 0))] + [piece] * count,
        out_specs=image(ROWS, features),
        out_shape=jax.ShapeDtypeStruct((blocks, ROWS, features), bf16),
        compiler_params=params(),
        cost_estimate=cost(2 * blocks * ROWS * features * slots * count, 5_000_000),
        name="combine",
    )(slot, *pieces)


def finish_kernel(count, mid0_ref, mid1_ref, part_ref, slotc_ref, dtok0_ref, dtok1_ref, *refs):
    out_ref, dout_ref, buf, dbuf = refs[count:]
    slots = refs[0].shape[1]
    step = pl.program_id(0)
    choose = selector(slotc_ref[0, :, :count], slots)
    mixed = mm(choose, jnp.concatenate([r[0] for r in refs[:count]], 0)) + part_ref[0].astype(f32)
    early = step < IMG_MB
    middle = jnp.where(early, mid0_ref[0], mid1_ref[0])
    value = middle + mixed
    grad = jnp.where(early, dtok0_ref[0].astype(f32), dtok1_ref[0].astype(f32))
    for i in range(IMAGES):

        @pl.when(step == i)
        def _():
            buf[pl.ds(i * SEQ, SEQ), :] = value[:SEQ]
            dbuf[pl.ds(i * SEQ, SEQ), :] = grad[:SEQ]

    @pl.when(step == IMAGES - 1)
    def _():
        out_ref[...] = buf[pl.ds(0, out_ref.shape[0]), :].astype(bf16)
        dout_ref[...] = dbuf[pl.ds(0, out_ref.shape[0]), :].astype(bf16)


def finish(middles, part, slotc, dtoks, results):
    count = len(results)
    _, slots, features = results[0].shape
    experts = slotc.shape[2]
    piece = pl.BlockSpec((1, slots, features), lambda i: (lax.div(i, IMG_MB), 0, 0))
    total = IMAGES * SEQ
    tall = 8 * ((total + 7) // 8)
    early = pl.BlockSpec((1, PAD, features), lambda i: (jnp.minimum(i, IMG_MB - 1), 0, 0))
    later = pl.BlockSpec((1, PAD, features), lambda i: (jnp.maximum(i - IMG_MB, 0), 0, 0))
    return pl.pallas_call(
        functools.partial(finish_kernel, count),
        grid=(IMAGES,),
        in_specs=[early, later, image(PAD, features), image(PAD, experts), early, later] + [piece] * count,
        out_specs=(whole((total, features)), whole((total, features))),
        out_shape=(jax.ShapeDtypeStruct((total, features), bf16),) * 2,
        scratch_shapes=[pltpu.VMEM((tall, features), f32)] * 2,
        compiler_params=params(),
        cost_estimate=cost(4 * ROWS * features * slots * count, 15_000_000),
        name="finish",
    )(*middles, part, slotc, *dtoks, *results)


def norm_back(grad, normal, inverse, gain):
    scaled = grad * gain
    return inverse * (
        scaled
        - jnp.mean(scaled, -1, keepdims=True)
        - normal * jnp.mean(scaled * normal, -1, keepdims=True)
    )


def backward_kernel(first, count, place_ref, tok_ref, cot_ref, proj_ref, prob_ref, att_ref, mid_ref, n2_ref, gate_ref, slotc_ref, dn2p_ref, dgo_ref, two_ref, more_ref, *refs):
    dx_refs = refs[:count]
    dg_refs = refs[count : 2 * count]
    refs = refs[2 * count :]
    chained = first > 0
    if chained:
        before_ref, before_row_ref = refs[:2]
        dtok_ref, keep_ref, send_ref, w_s, sem, acc_ref, row_ref = refs[2:]
    else:
        dtok_ref, acc_ref, row_ref, w_s, sem = refs
    step = pl.program_id(0)
    features = tok_ref.shape[2]
    experts = 2 * count

    @pl.when(step == 0)
    def _():
        load_dense(place_ref, two_ref, more_ref, w_s, sem)
        if chained:
            acc_ref[...] = before_ref[...]
            row_ref[...] = before_row_ref[...]
        else:
            acc_ref[...] = jnp.zeros_like(acc_ref)
            row_ref[...] = jnp.zeros_like(row_ref)

    pick = vectors(w_s)
    qkv, out = dense_weights(w_s, features)
    slots = dx_refs[0].shape[1]
    choose = selector(slotc_ref[0, :, :count], slots)
    middle = mid_ref[0]
    gates = gate_ref[:, 0:PAD]
    for i in range(1, IMG_MB):
        gates = jnp.where(step == i, gate_ref[:, i * PAD : (i + 1) * PAD], gates)
    dgates = jnp.concatenate(
        [ref[pl.ds(first + step, 1), :] for ref in dg_refs] + [dgo_ref[k, pl.ds(first + step, 1), :] for k in range(count)], 0
    )
    dlogits = gates * (dgates - jnp.sum(gates * dgates, 0, keepdims=True))
    dlogits = dlogits.astype(bf16)
    router = router_rows(pick, place_ref, experts)
    row_ref[8 : 8 + experts, :] += mm(dlogits, n2_ref[0])
    dn2 = (
        mm(dlogits, router, TN)
        + mm(choose, jnp.concatenate([r[0] for r in dx_refs], 0))
        + dn2p_ref[0].astype(f32)
    )
    gain_two = pick(2).astype(f32)
    _, normal_two, inverse_two = norm(middle, gain_two, 0.0)
    row_ref[2:3, :] += jnp.sum(dn2 * normal_two, 0, keepdims=True)
    row_ref[3:4, :] += jnp.sum(dn2, 0, keepdims=True)
    dmiddle = cot_ref[0].astype(f32) + norm_back(dn2, normal_two, inverse_two, gain_two)
    dbranch = dmiddle.astype(bf16)
    acc_ref[:, 3 * features :] += mm(att_ref[0], dbranch, TN)
    dattended = mm(dbranch, out, NT).astype(bf16)
    pair = 2 * HEAD_DIM
    dqs, dks, dvs = [], [], []
    for group in range(HEADS // 2):
        q2 = proj_ref[0, :, group * pair : (group + 1) * pair]
        k2 = proj_ref[0, :, features + group * pair : features + (group + 1) * pair]
        v2 = proj_ref[0, :, 2 * features + group * pair : 2 * features + (group + 1) * pair]
        d2 = dattended[:, group * pair : (group + 1) * pair]
        dq = dk = dv = None
        for half in range(2):
            probs = prob_ref[0, 2 * group + half]
            wide = probs.astype(f32)
            dm = d2 * half_mask(half, 1.0)
            dweights = mm(dm, v2, NT)
            inner = jnp.sum(dweights * wide, -1, keepdims=True)
            dscores = (wide * (dweights - inner)).astype(bf16)
            part_q = mm(dscores, k2 * half_mask(half, SCALING))
            part_k = mm(dscores, q2 * half_mask(half, SCALING), TN)
            part_v = mm(probs, dm, TN)
            dq = part_q if dq is None else dq + part_q
            dk = part_k if dk is None else dk + part_k
            dv = part_v if dv is None else dv + part_v
        dqs.append(dq.astype(bf16))
        dks.append(dk.astype(bf16))
        dvs.append(dv.astype(bf16))
    dprojected = jnp.concatenate(dqs + dks + dvs, 1)
    gain_one = pick(0).astype(f32)
    pre, normal_one, inverse_one = norm(tok_ref[0].astype(f32), gain_one, pick(1).astype(f32))
    acc_ref[:, : 3 * features] += mm(pre.astype(bf16), dprojected, TN)
    dnormed = mm(dprojected, qkv, NT)
    row_ref[0:1, :] += jnp.sum(dnormed * normal_one, 0, keepdims=True)
    row_ref[1:2, :] += jnp.sum(dnormed, 0, keepdims=True)
    dtok_ref[0] = (dmiddle + norm_back(dnormed, normal_one, inverse_one, gain_one)).astype(bf16)
    if chained:

        @pl.when(step == pl.num_programs(0) - 1)
        def _():
            width = keep_ref.shape[1] - 16
            lines = [row_ref[i : i + 1, :] for i in range(4)]
            for e in range(experts):
                line = jnp.zeros((1, features), f32)
                for r in range(experts):
                    line = jnp.where(expert_of(place_ref, r) == e, row_ref[8 + r : 9 + r, :], line)
                lines.append(line)
            blank = jnp.zeros((1, 4 * features - (4 + experts) * width), f32)
            tails = []
            for q in range(4):
                parts = [line[:, q * width : (q + 1) * width] for line in lines]
                tails.append(jnp.concatenate(parts + [blank], 1))
            for j in range(4):
                quarter = place_ref[j]
                to = (keep_ref, send_ref)[j // 2]
                to[j % 2, :width, :] = acc_ref[pl.ds(pl.multiple_of(quarter * width, width), width), :].astype(bf16)
                tail = tails[0]
                for q in range(1, 4):
                    tail = jnp.where(quarter == q, tails[q], tail)
                tail = jnp.concatenate([tail, jnp.zeros((15, tail.shape[1]), f32)], 0)
                to[j % 2, width:, :] = tail.astype(bf16)


def backward_images(first, place, tokp, cotp, saved, dgs, dg_other, slotc, dn2_part, dense, dxs, before):
    projected, probs, attended, middle, n2, gates = saved
    count = len(dxs)
    images = projected.shape[0]
    features = tokp.shape[2]
    experts = 2 * count
    slots = dxs[0].shape[1]

    def late(*tail):
        zeros = (0,) * len(tail)
        return pl.BlockSpec((1, *tail), lambda i, _: (i + first, *zeros))

    block = pl.BlockSpec((1, slots, features), lambda i, _: (first // IMG_MB, 0, 0))
    totals = ((features, 4 * features), (8 + experts, features))
    packed = (2, *dense[0].shape[1:])
    scratch = [pltpu.VMEM((4, *dense[0].shape[1:]), bf16), pltpu.SemaphoreType.DMA((4,))]
    out_specs = [image(PAD, features)]
    out_shape = [jax.ShapeDtypeStruct((images, PAD, features), bf16)]
    if before:
        out_specs += [whole(packed)] * 2
        out_shape += [jax.ShapeDtypeStruct(packed, bf16)] * 2
        scratch += [pltpu.VMEM(shape, f32) for shape in totals]
    else:
        out_specs += [whole(shape) for shape in totals]
        out_shape += [jax.ShapeDtypeStruct(shape, f32) for shape in totals]
    return pl.pallas_call(
        functools.partial(backward_kernel, first, count),
        grid_spec=pltpu.PrefetchScalarGridSpec(
            num_scalar_prefetch=1,
            grid=(images,),
            in_specs=[
                late(PAD, features),
                late(PAD, features),
                image(PAD, 3 * features),
                image(HEADS, PAD, PAD),
                image(PAD, features),
                image(PAD, features),
                image(PAD, features),
                whole(gates.shape),
                late(PAD, experts),
                image(PAD, features),
                whole(dg_other.shape),
            ]
            + [pl.BlockSpec(memory_space=pl.ANY)] * 2
            + [block] * count
            + [whole(piece.shape) for piece in dgs]
            + [whole(piece.shape) for piece in before],
            out_specs=tuple(out_specs),
            scratch_shapes=scratch,
        ),
        out_shape=tuple(out_shape),
        compiler_params=params(),
        cost_estimate=cost(10 * images * PAD * 4 * features * features, images * 5_000_000),
        name="backward",
    )(place, tokp, cotp, projected, probs, attended, middle, n2, gates, slotc, dn2_part, dg_other, *dense, *dxs, *dgs, *before)


def norm_forward(values, gain, offset):
    center = values - jnp.mean(values, -1, keepdims=True)
    inverse = lax.rsqrt(jnp.mean(center * center, -1, keepdims=True) + EPSILON)
    normal = center * inverse
    return (normal * gain + offset, normal, inverse)


def norm_backward(grad, normal, inverse, gain):
    scaled = grad * gain
    return inverse * (
        scaled
        - jnp.mean(scaled, -1, keepdims=True)
        - normal * jnp.mean(scaled * normal, -1, keepdims=True)
    )


def gelu_value(field):
    return 0.5 * field * (1.0 + lax.erf(field * ROOT_HALF))


def gelu_slope(field):
    return (
        0.5 * (1.0 + lax.erf(field * ROOT_HALF))
        + field * jnp.exp(-0.5 * field * field) * INV_ROOT_TWO_PI
    )


def block_ranks(route_rows, order_keys, capacity):
    count = order_keys.shape[0]
    expert_count = capacity.shape[0]
    chosen = jnp.concatenate([route_rows[:, 0], route_rows[:, 1]])
    sort_keys = jnp.concatenate([order_keys, order_keys + count])
    positions = jnp.arange(2 * count, dtype=jnp.int32)
    inverse = jnp.zeros((2 * count,), jnp.int32).at[sort_keys].set(positions)
    ordered = chosen[inverse]
    labels = jnp.arange(expert_count, dtype=jnp.int32)
    onehot = (ordered[:, None] == labels[None, :]).astype(jnp.int32)
    before = jnp.cumsum(onehot, 0) - onehot
    rank_sorted = jnp.sum(before * onehot, 1)
    ranking = jnp.zeros((2 * count,), jnp.int32).at[inverse].set(rank_sorted)
    pair_onehot = chosen[:, None] == labels[None, :]
    limit = jnp.sum(pair_onehot.astype(jnp.int32) * capacity[None, :], 1)
    return (chosen, ranking, ranking < limit, pair_onehot.astype(jnp.float32))


def exchanged(
    tokens,
    ln1_gain,
    ln1_bias,
    qkv_weight,
    out_weight,
    ln2_gain,
    ln2_bias,
    router_weight,
    expert_in,
    expert_out,
    routes,
    priority,
    capacity,
    cotangent,
):
    f32 = jnp.float32
    bf16 = jnp.bfloat16
    gathered = (
        lax.all_gather(ln1_gain, "dp", axis=0, tiled=True),
        lax.all_gather(ln1_bias, "dp", axis=0, tiled=True),
        lax.all_gather(qkv_weight, "dp", axis=0, tiled=True),
        lax.all_gather(out_weight, "dp", axis=0, tiled=True),
        lax.all_gather(ln2_gain, "dp", axis=0, tiled=True),
        lax.all_gather(ln2_bias, "dp", axis=0, tiled=True),
        lax.all_gather(router_weight, "dp", axis=0, tiled=True),
    )
    gain_one = gathered[0].astype(f32)
    offset_one = gathered[1].astype(f32)
    weight_qkv = gathered[2]
    weight_out = gathered[3]
    gain_two = gathered[4].astype(f32)
    offset_two = gathered[5].astype(f32)
    weight_router = gathered[6]
    features = tokens.shape[1]
    owners = lax.axis_size("expert")
    per_owner = expert_in.shape[0]
    experts = owners * per_owner
    slots = 8 * (3 * TOP * IMG_MB * SEQ // (16 * experts) + 1)
    row_count = IMG_MB * SEQ
    sum_gain_one = jnp.zeros((features,), f32)
    sum_offset_one = jnp.zeros((features,), f32)
    sum_qkv = jnp.zeros(weight_qkv.shape, f32)
    sum_out = jnp.zeros(weight_out.shape, f32)
    sum_gain_two = jnp.zeros((features,), f32)
    sum_offset_two = jnp.zeros((features,), f32)
    sum_router = jnp.zeros(weight_router.shape, f32)
    sum_expert_in = jnp.zeros(expert_in.shape, f32)
    sum_expert_out = jnp.zeros(expert_out.shape, f32)
    outputs = []
    input_grads = []
    for micro in range(MICRO):
        start = micro * row_count
        inputs = tokens[start : start + row_count].astype(f32)
        pre_one, normal_one, inverse_one = norm_forward(inputs, gain_one, offset_one)
        normed = pre_one.astype(bf16)
        projected = jnp.dot(normed, weight_qkv, preferred_element_type=f32).astype(bf16)
        projected = projected.reshape(IMG_MB, SEQ, 3, HEADS, HEAD_DIM)
        queries = projected[:, :, 0]
        key_rows = projected[:, :, 1]
        values = projected[:, :, 2]
        scores = (
            jnp.einsum("gqhd,gkhd->ghqk", queries, key_rows, preferred_element_type=f32) * SCALING
        )
        highest = jnp.max(scores, -1, keepdims=True)
        expos = jnp.exp(scores - highest)
        totals = jnp.sum(expos, -1, keepdims=True)
        log_total = highest + jnp.log(totals)
        attn_weights = (expos / totals).astype(bf16)
        attended = jnp.einsum(
            "ghqk,gkhd->gqhd", attn_weights, values, preferred_element_type=f32
        ).astype(bf16)
        attended = attended.reshape(row_count, features)
        middle = inputs + jnp.dot(attended, weight_out, preferred_element_type=f32)
        pre_two, normal_two, inverse_two = norm_forward(middle, gain_two, offset_two)
        normed_two = pre_two.astype(bf16)
        logits = jnp.dot(normed_two, weight_router, preferred_element_type=f32)
        gates = jax.nn.softmax(logits, -1)
        route_rows = routes[start : start + row_count]
        chosen, ranking, kept, pair_onehot = block_ranks(
            route_rows, priority[start : start + row_count], capacity
        )
        keep_float = kept.astype(f32)
        slot_send = jnp.where(kept, ranking, slots)
        slot_read = jnp.where(kept, ranking, 0)
        doubled = jnp.concatenate([normed_two, normed_two], 0)
        send = (
            jnp.zeros((experts, slots, features), bf16)
            .at[chosen, slot_send]
            .set(doubled, mode="drop")
        )
        received = lax.all_to_all(
            send.reshape(owners, per_owner, slots, features),
            "expert",
            split_axis=0,
            concat_axis=0,
            tiled=True,
        )
        hidden = jnp.einsum("sjcd,jdf->sjcf", received, expert_in, preferred_element_type=f32)
        active = gelu_value(hidden).astype(bf16)
        result = jnp.einsum(
            "sjcf,jfd->sjcd", active, expert_out, preferred_element_type=f32
        ).astype(bf16)
        back = lax.all_to_all(result, "expert", split_axis=0, concat_axis=0, tiled=True).reshape(
            experts, slots, features
        )
        pieces = back[chosen, slot_read].astype(f32) * keep_float[:, None]
        picked = jnp.take_along_axis(gates, route_rows, 1)
        gate_pair = jnp.concatenate([picked[:, 0], picked[:, 1]])
        mixed = pieces[:row_count] * picked[:, 0:1] + pieces[row_count:] * picked[:, 1:2]
        outputs.append((middle + mixed).astype(bf16))
        grad_out = cotangent[start : start + row_count].astype(f32)
        grad_doubled = jnp.concatenate([grad_out, grad_out], 0)
        dgate = jnp.sum(grad_doubled * pieces, -1)
        dpieces = (grad_doubled * (gate_pair * keep_float)[:, None]).astype(bf16)
        dgates = (
            pair_onehot[:row_count] * dgate[:row_count, None]
            + pair_onehot[row_count:] * dgate[row_count:, None]
        )
        dlogits = (gates * (dgates - jnp.sum(gates * dgates, -1, keepdims=True))).astype(bf16)
        grad_send = (
            jnp.zeros((experts, slots, features), bf16)
            .at[chosen, slot_send]
            .set(dpieces, mode="drop")
        )
        grad_received = lax.all_to_all(
            grad_send.reshape(owners, per_owner, slots, features),
            "expert",
            split_axis=0,
            concat_axis=0,
            tiled=True,
        )
        dactive = jnp.einsum(
            "sjcd,jfd->sjcf", grad_received, expert_out, preferred_element_type=f32
        )
        dhidden = (dactive * gelu_slope(hidden)).astype(bf16)
        grad_w_out = jnp.einsum("sjcf,sjcd->jfd", active, grad_received, preferred_element_type=f32)
        grad_w_in = jnp.einsum("sjcd,sjcf->jdf", received, dhidden, preferred_element_type=f32)
        sum_expert_in = sum_expert_in + grad_w_in
        sum_expert_out = sum_expert_out + grad_w_out
        dsent = jnp.einsum("sjcf,jdf->sjcd", dhidden, expert_in, preferred_element_type=f32).astype(
            bf16
        )
        dreturn = lax.all_to_all(dsent, "expert", split_axis=0, concat_axis=0, tiled=True).reshape(
            experts, slots, features
        )
        dpair = dreturn[chosen, slot_read].astype(f32) * keep_float[:, None]
        dnormed_two = (
            jnp.dot(dlogits, weight_router.T, preferred_element_type=f32)
            + dpair[:row_count]
            + dpair[row_count:]
        )
        sum_router = sum_router + jnp.dot(normed_two.T, dlogits, preferred_element_type=f32)
        sum_gain_two = sum_gain_two + jnp.sum(dnormed_two * normal_two, 0)
        sum_offset_two = sum_offset_two + jnp.sum(dnormed_two, 0)
        dmiddle = grad_out + norm_backward(dnormed_two, normal_two, inverse_two, gain_two)
        dbranch = dmiddle.astype(bf16)
        sum_out = sum_out + jnp.dot(attended.T, dbranch, preferred_element_type=f32)
        dattended = jnp.dot(dbranch, weight_out.T, preferred_element_type=f32).astype(bf16)
        dattended = dattended.reshape(IMG_MB, SEQ, HEADS, HEAD_DIM)
        again = (
            jnp.einsum("gqhd,gkhd->ghqk", queries, key_rows, preferred_element_type=f32) * SCALING
        )
        probs_again = jnp.exp(again - log_total)
        dvalues = jnp.einsum(
            "ghqk,gqhd->gkhd", probs_again.astype(bf16), dattended, preferred_element_type=f32
        )
        dweights = jnp.einsum("gqhd,gkhd->ghqk", dattended, values, preferred_element_type=f32)
        inner = jnp.sum(dweights * probs_again, -1, keepdims=True)
        dscores = (probs_again * (dweights - inner)).astype(bf16)
        dqueries = (
            jnp.einsum("ghqk,gkhd->gqhd", dscores, key_rows, preferred_element_type=f32) * SCALING
        )
        dkeys = (
            jnp.einsum("ghqk,gqhd->gkhd", dscores, queries, preferred_element_type=f32) * SCALING
        )
        dprojected = (
            jnp.stack([dqueries, dkeys, dvalues], 2).astype(bf16).reshape(row_count, 3 * features)
        )
        sum_qkv = sum_qkv + jnp.dot(normed.T, dprojected, preferred_element_type=f32)
        dnormed = jnp.dot(dprojected, weight_qkv.T, preferred_element_type=f32)
        sum_gain_one = sum_gain_one + jnp.sum(dnormed * normal_one, 0)
        sum_offset_one = sum_offset_one + jnp.sum(dnormed, 0)
        input_grads.append(
            (dmiddle + norm_backward(dnormed, normal_one, inverse_one, gain_one)).astype(bf16)
        )
    grad_expert_in, grad_expert_out = (
        lax.psum_scatter(
            sum_expert_in.astype(jnp.bfloat16), "dp", scatter_dimension=2, tiled=True
        ).astype(jnp.float32),
        lax.psum_scatter(
            sum_expert_out.astype(jnp.bfloat16), "dp", scatter_dimension=1, tiled=True
        ).astype(jnp.float32),
    )
    dense = (
        sum_gain_one,
        sum_offset_one,
        sum_qkv,
        sum_out,
        sum_gain_two,
        sum_offset_two,
        sum_router,
    )
    totals_all = (
        lax.psum(dense[0].astype(jnp.bfloat16), "expert").astype(jnp.float32),
        lax.psum(dense[1].astype(jnp.bfloat16), "expert").astype(jnp.float32),
        lax.psum(dense[2].astype(jnp.bfloat16), "expert").astype(jnp.float32),
        lax.psum(dense[3].astype(jnp.bfloat16), "expert").astype(jnp.float32),
        lax.psum(dense[4].astype(jnp.bfloat16), "expert").astype(jnp.float32),
        lax.psum(dense[5].astype(jnp.bfloat16), "expert").astype(jnp.float32),
        lax.psum(dense[6].astype(jnp.bfloat16), "expert").astype(jnp.float32),
    )
    owned = (
        lax.psum_scatter(
            totals_all[0].astype(jnp.bfloat16), "dp", scatter_dimension=0, tiled=True
        ).astype(jnp.float32),
        lax.psum_scatter(
            totals_all[1].astype(jnp.bfloat16), "dp", scatter_dimension=0, tiled=True
        ).astype(jnp.float32),
        lax.psum_scatter(
            totals_all[2].astype(jnp.bfloat16), "dp", scatter_dimension=0, tiled=True
        ).astype(jnp.float32),
        lax.psum_scatter(
            totals_all[3].astype(jnp.bfloat16), "dp", scatter_dimension=0, tiled=True
        ).astype(jnp.float32),
        lax.psum_scatter(
            totals_all[4].astype(jnp.bfloat16), "dp", scatter_dimension=0, tiled=True
        ).astype(jnp.float32),
        lax.psum_scatter(
            totals_all[5].astype(jnp.bfloat16), "dp", scatter_dimension=0, tiled=True
        ).astype(jnp.float32),
        lax.psum_scatter(
            totals_all[6].astype(jnp.bfloat16), "dp", scatter_dimension=0, tiled=True
        ).astype(jnp.float32),
    )
    block_out = jnp.concatenate(outputs, 0)
    grad_tokens = jnp.concatenate(input_grads, 0)
    return (
        block_out,
        grad_tokens,
        owned[0],
        owned[1],
        owned[2],
        owned[3],
        owned[4],
        owned[5],
        owned[6],
        grad_expert_in,
        grad_expert_out,
    )


SWAP = [(0, 1), (1, 0)]
OUTWARD = [(1, 0), (2, 3)]
INWARD = [(0, 1), (3, 2)]
MIDDLE = [(1, 2), (2, 1)]


def flip(bit):
    return [(i, i ^ bit) for i in range(4)]


def add(*pieces):
    total = pieces[0].astype(f32)
    for piece in pieces[1:]:
        total = total + piece.astype(f32)
    return total.astype(bf16)


def stage(*values):
    return lax.optimization_barrier(values)


def after(value, *others):
    return lax.optimization_barrier((value, *others))[0]


def paired(
    tokens,
    ln1_gain,
    ln1_bias,
    qkv_weight,
    out_weight,
    ln2_gain,
    ln2_bias,
    router_weight,
    expert_in,
    expert_out,
    routes,
    priority,
    capacity,
    cotangent,
):
    y, core, z, x = (lax.axis_index(name) for name in ("y", "core", "z", "x"))
    features = tokens.shape[1]
    experts = capacity.shape[0]
    width = qkv_weight.shape[0]
    count = experts // 2
    slots = 8 * (3 * TOP * IMG_MB * SEQ // (16 * experts) + 1)
    lanes = 4 * features

    order = jnp.arange(8, dtype=jnp.int32)
    place = (((order & 1) ^ y) << 1) | (((order >> 1) & 1) ^ core)
    for at, value in ((Z_AT, z), (X_AT, x), (Y_AT, y), (CORE_AT, core)):
        place = jnp.where(order == at, value, place)

    def swap(value, axis, pairs=SWAP):
        return lax.ppermute(value, axis, pairs)

    gains = (ln1_gain, ln1_bias, ln2_gain, ln2_bias)
    packed, one = pack(place, gains, qkv_weight, out_weight, router_weight, expert_in, expert_out)
    from_y = swap(packed, "y")
    near = swap(one, "z", flip(1))
    centre = swap(one, "z", MIDDLE)
    tokp, cotp, slot, slotc = prepare(place, capacity, tokens, cotangent, routes, priority)
    two = jnp.concatenate([packed, after(from_y, slot)], 0)
    dense = (two, swap(two, "core"))

    place, near, centre = stage(place, near, centre)
    cot_other = swap(cotp, "x")
    second_mid = swap(near, "z", MIDDLE)
    second_out = swap(centre, "z", OUTWARD)
    across = [swap(near, "y")]
    saved = [forward_images(0, place, tokp, dense, experts)]
    place, cot_other, first_n2 = stage(place, cot_other, saved[0][4])
    n2_other = [swap(first_n2, "x")]
    saved.append(forward_images(IMG_MB, place, tokp, dense, experts))
    place, last_n2, last_gates, second_mid, second_out, side, n2_back = stage(
        place, saved[1][4], saved[1][5], second_mid, second_out, across[0], n2_other[0]
    )
    across, n2_other = [side], [n2_back]
    n2_other.append(swap(last_n2, "x"))
    tables = jnp.concatenate([slot, saved[0][5][None], last_gates[None]], 0)
    other = swap(tables, "x")
    second = second_mid + second_out
    outer = swap(second, "z", OUTWARD)
    across.append(swap(second, "y"))
    corner = [swap(jnp.stack([near, across[0]]), "core")]

    n2 = [piece[4].reshape(ROWS, features) for piece in saved]
    n2 += [piece.reshape(ROWS, features) for piece in n2_other]
    cot = [piece.reshape(MICRO, ROWS, features) for piece in (cotp, cot_other)]
    tables = (slot, saved[0][5], saved[1][5], other)
    out0 = expert_apply(0, place, n2, cot, tables, (expert_in, expert_out), slots)
    place, outer, side, last_corner, *out0 = stage(place, outer, across[1], corner[0], *out0)
    across[1], corner[0] = side, last_corner
    third = centre + outer
    across.append(swap(third, "y"))
    corner.append(swap(jnp.stack([second, across[1]]), "core"))
    core0 = swap(out0[3], "core")
    out1 = expert_apply(1, place, n2, cot, tables, (near, across[0], corner[0]), slots)
    place, side, last_corner, core0, *out1 = stage(place, across[2], corner[1], core0, *out1)
    across[2], corner[1] = side, last_corner
    corner.append(swap(jnp.stack([third, across[2]]), "core"))
    core1 = swap(out1[3], "core")
    side0 = swap(add(out0[2][1], core0[1]), "y")
    out2 = expert_apply(2, place, n2, cot, tables, (second, across[1], corner[1]), slots)
    place, last_corner, core1, side0, *out2 = stage(place, corner[2], core1, side0, *out2)
    corner[2] = last_corner
    core2 = swap(out2[3], "core")
    side1 = swap(add(out1[2][1], core1[1]), "y")
    out3 = expert_apply(3, place, n2, cot, tables, (third, across[2], corner[2]), slots)
    place, core2, side1, *out3 = stage(place, core2, side1, *out3)

    outs = (out0, out1, out2, out3)
    results, dxs, keeps, _, dgs, dgos = ([piece[i] for piece in outs] for i in range(6))
    core3 = swap(out3[3], "core")
    side2 = swap(add(out2[2][1], core2[1]), "y")
    dg_other = swap(jnp.stack(dgos), "x")
    dn2_mine = [combine(other, dxs, 0, 1)]
    dn2 = [swap(dn2_mine[0], "x").reshape(IMG_MB, PAD, features)]
    dn2_mine.append(combine(after(other, dn2_mine[0]), dxs, 1, 1))
    mixed_mine = combine(after(other, *dn2_mine), results, 0, MICRO)
    place, mixed_mine, core3, back, last = stage(place, mixed_mine, core3, dn2[0], dn2_mine[1])
    dn2 = [back, swap(last, "x").reshape(IMG_MB, PAD, features)]
    columns = slotc.reshape(IMAGES, PAD, experts)

    near_sum = add(out1[2][0], core1[0], side1)
    own_sum = add(out0[2][0], core0[0], side0)

    def back_images(micro, place, before):
        return backward_images(
            micro * IMG_MB, place, tokp, cotp, saved[micro], dgs, dg_other, columns, dn2[micro], dense, dxs, before
        )

    first = back_images(0, place, ())
    place, side2, back, *first = stage(place, side2, dn2[1], *first)
    dn2[1] = back
    second_sum = add(out2[2][0], core2[0], side2)
    side3 = swap(add(out3[2][1], core3[1]), "y")
    second_in = swap(second_sum, "z", INWARD)
    mixed = swap(mixed_mine, "x").reshape(IMAGES, PAD, features)
    keep_send = back_images(1, place, tuple(first[1:]))
    place, side3, second_in, mixed, *keep_send = stage(place, side3, second_in, mixed, *keep_send)
    dtok = [first[0], keep_send[0]]
    keep, send = keep_send[1:]
    third_sum = add(out3[2][0], core3[0], side3)
    third_in = swap(third_sum, "z", INWARD)
    third_mid = swap(add(third_sum, second_in), "z", MIDDLE)
    block_out, grad_tokens = finish([piece[3] for piece in saved], mixed, columns, dtok, results)

    from_near = swap(send, "core")
    part = swap(add(keep[1], from_near[1]), "y")
    part, third_in, third_mid = stage(part, third_in, third_mid)
    second_mid = swap(add(second_sum, third_in), "z", MIDDLE)
    first_swap = swap(add(near_sum, second_mid), "z", flip(1))
    part = add(keep[0], from_near[0], part)
    cut = part.reshape(width + 16, 8, lanes // 8).transpose(1, 0, 2)
    cut = lax.all_to_all(cut, ("z", "x"), split_axis=0, concat_axis=0, tiled=True)
    cut = jnp.sum(cut.astype(f32), 0).astype(bf16)
    part = lax.all_gather(cut, ("z", "x"), axis=0)
    part = part.transpose(1, 0, 2).reshape(width + 16, lanes).astype(f32)
    row = part[width]

    total = own_sum.astype(f32) + first_swap.astype(f32) + third_mid.astype(f32)

    return (
        block_out,
        grad_tokens,
        row[:width],
        row[width : 2 * width],
        part[:width, : 3 * features],
        part[:width, 3 * features :],
        row[2 * width : 3 * width],
        row[3 * width : 4 * width],
        row[4 * width : (4 + experts) * width].reshape(experts, width).T,
        total[0][None],
        total[1].T[None],
    )


def solution(mesh):
    if mesh.shape["dp"] == 4 and mesh.shape["expert"] == 8:
        mesh = Mesh(mesh.devices.reshape(2, 2, 4, 2), ("y", "core", "z", "x"))
        body, dp, expert = paired, ("y", "core"), ("z", "x")
    else:
        body, dp, expert = exchanged, ("dp",), ("expert",)
    rows = P((*dp, *expert), None)
    return jax.shard_map(
        body,
        mesh=mesh,
        in_specs=(
            rows,
            P(dp),
            P(dp),
            P(dp, None),
            P(dp, None),
            P(dp),
            P(dp),
            P(dp, None),
            P(expert, None, None),
            P(expert, None, None),
            rows,
            P((*dp, *expert)),
            P(),
            rows,
        ),
        out_specs=(
            rows,
            rows,
            P(dp),
            P(dp),
            P(dp, None),
            P(dp, None),
            P(dp),
            P(dp),
            P(dp, None),
            P(expert, None, dp),
            P(expert, dp, None),
        ),
        check_vma=False,
    )
```

```python
import functools
import jax
import jax.numpy as jnp
from jax import lax
from jax.experimental import pallas as pl
from jax.experimental.pallas import tpu as pltpu
from jax.sharding import Mesh
from jax.sharding import PartitionSpec as P

HEADS = 8
HEAD_DIM = 64
TOP = 2
SEQ = 197
IMG_MB = 3
MICRO = 2
EPSILON = 1e-06
SCALING = 0.125
ROOT_HALF = 0.7071067811865476
INV_ROOT_TWO_PI = 0.3989422804014327
PAD = 16 * ((SEQ + 15) // 16)
ROWS = IMG_MB * PAD
IMAGES = MICRO * IMG_MB
f32 = jnp.float32
bf16 = jnp.bfloat16
NN = (((1,), (0,)), ((), ()))
NT = (((1,), (1,)), ((), ()))
TN = (((0,), (0,)), ((), ()))


def mm(a, b, dims=NN):
    return lax.dot_general(a, b, dims, preferred_element_type=f32)


def whole(shape):
    zeros = (0,) * len(shape)
    return pl.BlockSpec(shape, lambda *_: zeros)


def params(mb=60):
    return pltpu.CompilerParams(vmem_limit_bytes=mb << 20)


SHARE = 1.0


def cost(flops, moved):
    return pl.CostEstimate(flops=int(flops * SHARE), bytes_accessed=int(moved * SHARE), transcendentals=0)


Z_AT, X_AT, Y_AT, CORE_AT = 4, 5, 6, 7


def expert_of(place_ref, index):
    return 2 * (place_ref[Z_AT] ^ (index & 3)) + (place_ref[X_AT] ^ (index >> 2))


def label_column(place_ref, experts):
    index = lax.broadcasted_iota(jnp.int32, (experts, 1), 0)
    label = jnp.zeros((experts, 1), jnp.int32)
    for r in range(experts):
        label = jnp.where(index == r, expert_of(place_ref, r), label)
    return label


def wide_transpose(rows, fill):
    pad = jnp.full((128 - rows.shape[0], rows.shape[1]), fill, f32)
    return jnp.transpose(jnp.concatenate([rows, pad], 0))


def pack_kernel(g1_ref, b1_ref, g2_ref, b2_ref, qkv_ref, out_ref, router_ref, packed_ref):
    width, columns = qkv_ref.shape
    packed_ref[0, :width, :columns] = qkv_ref[...]
    packed_ref[0, :width, columns:] = out_ref[...]
    pieces = [ref[...].astype(f32) for ref in (g1_ref, b1_ref, g2_ref, b2_ref)]
    router = router_ref[...].astype(f32)
    pieces += [router[e : e + 1, :] for e in range(router.shape[0])]
    rest = packed_ref.shape[2] - width * len(pieces)
    row = jnp.concatenate(pieces + [jnp.zeros((1, rest), f32)], 1)
    row = jnp.concatenate([row, jnp.zeros((15, row.shape[1]), f32)], 0)
    packed_ref[0, width:, :] = row.astype(bf16)


def pack(vectors_in, qkv, out, router):
    width, columns = qkv.shape
    rows = [vector.reshape(1, width) for vector in vectors_in]
    packed = (1, width + 16, columns + out.shape[1])
    inputs = (*rows, qkv, out, router)
    return pl.pallas_call(
        pack_kernel,
        grid=(1,),
        in_specs=[whole(value.shape) for value in inputs],
        out_specs=whole(packed),
        out_shape=jax.ShapeDtypeStruct(packed, bf16),
        compiler_params=params(60),
        cost_estimate=cost(0, 2_000_000),
        name="pack",
    )(*inputs)


def quarter_kernel(place_ref, in_ref, back_ref, one_ref, sem):
    span = one_ref.shape[1]
    start = pl.multiple_of(place_ref[0] * span, span)
    copies = (
        pltpu.make_async_copy(in_ref.at[0, :, pl.ds(start, span)], one_ref.at[0], sem.at[0]),
        pltpu.make_async_copy(back_ref.at[0, pl.ds(start, span), :], one_ref.at[1], sem.at[1]),
    )
    for copy in copies:
        copy.start()
    for copy in copies:
        copy.wait()


def quarter_of(place, expert_in, expert_out):
    shape = (2, expert_in.shape[1], expert_in.shape[2] // 4)
    return pl.pallas_call(
        quarter_kernel,
        grid_spec=pltpu.PrefetchScalarGridSpec(
            num_scalar_prefetch=1,
            grid=(1,),
            in_specs=[pl.BlockSpec(memory_space=pl.ANY)] * 2,
            out_specs=whole(shape),
            scratch_shapes=[pltpu.SemaphoreType.DMA((2,))],
        ),
        out_shape=jax.ShapeDtypeStruct(shape, bf16),
        compiler_params=params(60),
        cost_estimate=cost(0, 2_000_000),
        name="quarter",
    )(place, expert_in, expert_out)


def pad_rows(src_ref, dst_ref, buf):
    buf[pl.ds(0, src_ref.shape[0]), :] = src_ref[...].astype(f32)
    for image in range(IMAGES):
        piece = buf[pl.ds(image * SEQ, PAD), :]
        row = lax.broadcasted_iota(jnp.int32, piece.shape, 0)
        dst_ref[image] = jnp.where(row < SEQ, piece, 0.0).astype(bf16)


def pad_images(values):
    total, features = values.shape
    padded = (IMAGES, PAD, features)
    return pl.pallas_call(
        pad_rows,
        grid=(1,),
        in_specs=[whole(values.shape)],
        out_specs=whole(padded),
        out_shape=jax.ShapeDtypeStruct(padded, bf16),
        scratch_shapes=[pltpu.VMEM((8 * ((total + PAD) // 8), features), f32)],
        compiler_params=params(60),
        cost_estimate=cost(0, 4_000_000),
        name="pad",
    )(values)


def prepare_kernel(place_ref, cap_ref, tok_ref, route_ref, prio_ref, tokp_ref, slot_ref, slotc_ref, buf, keys):
    total = tok_ref.shape[0]
    experts = slot_ref.shape[1]
    pad_rows(tok_ref, tokp_ref, buf)
    keys[...] = jnp.full_like(keys, -1.0)
    keys[pl.ds(0, total), 0:2] = route_ref[...].astype(f32)
    keys[pl.ds(0, total), 2:3] = prio_ref[...].astype(f32)
    labels = label_column(place_ref, experts)
    limit = jnp.zeros((experts, 1), f32)
    for e in range(experts):
        limit = jnp.where(labels == e, cap_ref[e].astype(f32), limit)
    labels = labels.astype(f32)
    for block in range(MICRO):
        columns = []
        for image in range(IMG_MB):
            piece = keys[pl.ds((block * IMG_MB + image) * SEQ, PAD), :]
            row = lax.broadcasted_iota(jnp.int32, piece.shape, 0)
            columns.append(jnp.where(row < SEQ, piece, -1.0))
        column = jnp.concatenate(columns, 0)
        turned = jnp.transpose(column)
        key_column = jnp.where(column[:, 2:3] < 0.0, 1e6, column[:, 2:3])
        below = jnp.where(key_column < turned[2:3, :], 1.0, 0.0).astype(bf16)
        first = labels == turned[0:1, :]
        second = labels == turned[1:2, :]
        hot = jnp.concatenate([jnp.where(first, 1.0, 0.0), jnp.where(second, 1.0, 0.0)], 0)
        counts = mm(hot.astype(bf16), below)
        total_first = jnp.sum(hot[:experts], 1, keepdims=True)
        rank = jnp.where(
            first, counts[:experts], jnp.where(second, counts[experts:] + total_first, 1e6)
        )
        slot = jnp.where(rank < limit, rank, -1.0)
        slot_ref[block] = slot
        slotc_ref[block] = wide_transpose(slot, -1.0)[:, :experts]


def prepare(place, capacity, tokens, routes, priority):
    total, features = tokens.shape
    experts = capacity.shape[0]
    tall = 8 * ((total + PAD) // 8)
    priority = priority.reshape(total, 1)
    padded = (IMAGES, PAD, features)
    return pl.pallas_call(
        prepare_kernel,
        grid_spec=pltpu.PrefetchScalarGridSpec(
            num_scalar_prefetch=2,
            grid=(1,),
            in_specs=[whole(tokens.shape), whole(routes.shape), whole(priority.shape)],
            out_specs=(
                whole(padded),
                whole((MICRO, experts, ROWS)),
                whole((MICRO, ROWS, experts)),
            ),
            scratch_shapes=[pltpu.VMEM((tall, features), f32), pltpu.VMEM((tall, 128), f32)],
        ),
        out_shape=(
            jax.ShapeDtypeStruct(padded, bf16),
            jax.ShapeDtypeStruct((MICRO, experts, ROWS), f32),
            jax.ShapeDtypeStruct((MICRO, ROWS, experts), f32),
        ),
        compiler_params=params(60),
        cost_estimate=cost(0, 8_000_000),
        name="prepare",
    )(place, capacity, tokens, routes, priority)


def norm(values, gain, offset):
    center = values - jnp.mean(values, -1, keepdims=True)
    inverse = lax.rsqrt(jnp.mean(center * center, -1, keepdims=True) + EPSILON)
    normal = center * inverse
    return normal * gain + offset, normal, inverse


def load_dense(place_ref, two_ref, more_ref, w_s, sem):
    copies = [
        pltpu.make_async_copy((two_ref, more_ref)[j // 2].at[j % 2], w_s.at[place_ref[j]], sem.at[j])
        for j in range(4)
    ]
    for copy in copies:
        copy.start()
    return copies


def vectors(w_s):
    quarters = w_s.shape[0]
    width = w_s.shape[1] - 16
    row = [w_s[q, pl.ds(width, 1), :] for q in range(quarters)]

    def pick(index):
        return jnp.concatenate([r[:, index * width : (index + 1) * width] for r in row], 1)

    return pick


def dense_weights(w_s, features):
    width = w_s.shape[1] - 16
    qkv = w_s[:, :width, : 3 * features].reshape(features, 3 * features)
    out = w_s[:, :width, 3 * features :].reshape(features, features)
    return qkv, out


def router_rows(pick, place_ref, experts):
    table = jnp.concatenate([pick(4 + e) for e in range(experts)], 0)
    labels = label_column(place_ref, experts)
    order = labels == lax.broadcasted_iota(jnp.int32, (experts, experts), 1)
    return mm(jnp.where(order, 1.0, 0.0).astype(bf16), table).astype(bf16)


def half_mask(index, value):
    lane = lax.broadcasted_iota(jnp.int32, (1, 2 * HEAD_DIM), 1)
    return jnp.where((lane < HEAD_DIM) == (index == 0), value, 0.0).astype(bf16)


def forward_kernel(first, place_ref, tok_ref, two_ref, more_ref, proj_ref, prob_ref, att_ref, mid_ref, n2_ref, gate_ref, w_s, sem, in_sem, out_sem, tok_s, n1_s, proj_s, prob_s, att_s, mid_s, n2_s):
    features = tok_s.shape[1]
    copy_in = pltpu.make_async_copy(tok_ref.at[first // IMG_MB], tok_s, in_sem.at[0])
    copy_in.start()
    waits = load_dense(place_ref, two_ref, more_ref, w_s, sem)
    out_copies = [
        pltpu.make_async_copy(src, dst, out_sem.at[i])
        for i, (src, dst) in enumerate(
            ((proj_s, proj_ref), (prob_s, prob_ref), (att_s, att_ref), (mid_s, mid_ref), (n2_s, n2_ref))
        )
    ]
    copy_in.wait()
    for copy in waits:
        copy.wait()
    pick = vectors(w_s)
    qkv, out = dense_weights(w_s, features)
    gain, offset = pick(0).astype(f32), pick(1).astype(f32)

    @pl.loop(0, IMG_MB)
    def _(i):
        span = pl.ds(pl.multiple_of(i * PAD, PAD), PAD)
        pre, _, _ = norm(tok_s[span, :].astype(f32), gain, offset)
        n1_s[span, :] = pre.astype(bf16)

    proj_s[...] = mm(n1_s[...], qkv).astype(bf16)
    out_copies[0].start()
    column = lax.broadcasted_iota(jnp.int32, (1, PAD), 1)
    pair = 2 * HEAD_DIM

    @pl.loop(0, IMG_MB)
    def _(i):
        span = pl.ds(pl.multiple_of(i * PAD, PAD), PAD)
        for group in range(HEADS // 2):
            q2 = proj_s[span, group * pair : (group + 1) * pair]
            k2 = proj_s[span, features + group * pair : features + (group + 1) * pair]
            v2 = proj_s[span, 2 * features + group * pair : 2 * features + (group + 1) * pair]
            total = None
            for half in range(2):
                scores = mm(q2 * half_mask(half, SCALING), k2, NT)
                scores = jnp.where(column < SEQ, scores, -1e30)
                expos = jnp.exp(scores - jnp.max(scores, -1, keepdims=True))
                probs = (expos * (1.0 / jnp.sum(expos, -1, keepdims=True))).astype(bf16)
                prob_s[i, 2 * group + half] = probs
                piece = mm(probs, v2 * half_mask(half, 1.0))
                total = piece if total is None else total + piece
            att_s[span, group * pair : (group + 1) * pair] = total.astype(bf16)

    out_copies[1].start()
    out_copies[2].start()
    mid_s[...] = mm(att_s[...], out)
    gain_two, offset_two = pick(2).astype(f32), pick(3).astype(f32)

    @pl.loop(0, IMG_MB)
    def _(i):
        span = pl.ds(pl.multiple_of(i * PAD, PAD), PAD)
        middle = tok_s[span, :].astype(f32) + mid_s[span, :]
        mid_s[span, :] = middle
        pre, _, _ = norm(middle, gain_two, offset_two)
        n2_s[span, :] = pre.astype(bf16)

    out_copies[4].start()
    out_copies[3].start()
    router = router_rows(pick, place_ref, gate_ref.shape[0])
    logits = mm(router, n2_s[...], NT)
    expos = jnp.exp(logits - jnp.max(logits, 0, keepdims=True))
    gate_ref[...] = expos / jnp.sum(expos, 0, keepdims=True)
    for copy in out_copies:
        copy.wait()


def image(*tail):
    zeros = (0,) * len(tail)
    return pl.BlockSpec((1, *tail), lambda i, *_: (i, *zeros))


def forward_images(first, place, tokp, dense, experts):
    features = tokp.shape[2]
    count = IMG_MB
    flops = 2 * count * PAD * (4 * features * features + 2 * PAD * 256 * HEADS)
    shapes = (
        ((ROWS, 3 * features), bf16),
        ((count, HEADS, PAD, PAD), bf16),
        ((ROWS, features), bf16),
        ((ROWS, features), f32),
        ((ROWS, features), bf16),
    )
    scratch = [((ROWS, features), bf16), ((ROWS, features), bf16), *shapes]
    return pl.pallas_call(
        functools.partial(forward_kernel, first),
        grid_spec=pltpu.PrefetchScalarGridSpec(
            num_scalar_prefetch=1,
            grid=(1,),
            in_specs=[pl.BlockSpec(memory_space=pl.ANY)] * 3,
            out_specs=(*[pl.BlockSpec(memory_space=pl.ANY)] * 5, whole((experts, ROWS))),
            scratch_shapes=[
                pltpu.VMEM((4, *dense[0].shape[1:]), bf16),
                pltpu.SemaphoreType.DMA((4,)),
                pltpu.SemaphoreType.DMA((1,)),
                pltpu.SemaphoreType.DMA((5,)),
            ]
            + [pltpu.VMEM(*shape) for shape in scratch],
        ),
        out_shape=(
            *[jax.ShapeDtypeStruct(*shape) for shape in shapes],
            jax.ShapeDtypeStruct((experts, ROWS), f32),
        ),
        compiler_params=params(60),
        cost_estimate=cost(flops, count * 3_000_000),
        name="forward",
    )(place, tokp.reshape(MICRO, ROWS, features), *dense)


def gelu_pair(field):
    cdf = 0.5 * (1.0 + lax.erf(field * ROOT_HALF))
    return field * cdf, cdf + field * (jnp.exp(-0.5 * field * field) * INV_ROOT_TWO_PI)


def expert_kernel(index, own, place_ref, *refs):
    blocks = 2 * MICRO
    n2_refs = refs[:blocks]
    cot_refs = refs[blocks : blocks + 2]
    slot_ref, gate0_ref, gate1_ref, other_ref = refs[blocks + 2 : blocks + 6]
    refs = refs[blocks + 6 :]
    sources = 2 if own else 4
    w_refs = refs[:sources]
    refs = refs[sources:]
    res_ref, dx_ref, keep_ref, send_ref, dg_ref, dgo_ref = refs[:6]
    w_s, sem, n2_s, cot_s, in_sem, x_s, g_s, raw_s, xt_s, gt_s, gs_s, r_acc, dx_acc, act_s, dh_s = refs[6:]
    step = pl.program_id(0)
    quarters, _, _, width = w_s.shape
    slots = x_s.shape[0] // blocks
    row = lax.broadcasted_iota(jnp.int32, (slots, ROWS), 0).astype(f32)

    def copies(j):
        if own:
            start = pl.multiple_of(place_ref[j] * width, width)
            return (
                pltpu.make_async_copy(w_refs[0].at[0, :, pl.ds(start, width)], w_s.at[j, 0], sem.at[2 * j]),
                pltpu.make_async_copy(w_refs[1].at[0, pl.ds(start, width), :], w_s.at[j, 1], sem.at[2 * j + 1]),
            )
        return (pltpu.make_async_copy(w_refs[j], w_s.at[j], sem.at[j]),)

    def slot_row(b):
        if b < MICRO:
            return slot_ref[b, pl.ds(index, 1), :]
        return other_ref[b - MICRO, pl.ds(index + 4, 1), :]

    def gate_row(b):
        if b < MICRO:
            return (gate0_ref, gate1_ref)[b][pl.ds(index, 1), :]
        return other_ref[b, pl.ds(index + 4, 1), :]

    def rows_in(b):
        return (
            pltpu.make_async_copy(n2_refs[b], n2_s.at[b], in_sem.at[2 * b]),
            pltpu.make_async_copy(cot_refs[b // MICRO].at[b % MICRO], cot_s.at[b], in_sem.at[2 * b + 1]),
        )

    @pl.when(step == 0)
    def _():
        for b in range(blocks):
            for copy in rows_in(b):
                copy.start()
        for j in range(quarters):
            for copy in copies(j):
                copy.start()
        r_acc[...] = jnp.zeros_like(r_acc)
        dx_acc[...] = jnp.zeros_like(dx_acc)
        for b in range(blocks):
            for copy in rows_in(b):
                copy.wait()
            span = pl.ds(b * slots, slots)
            hit = row == slot_row(b)
            pick = jnp.where(hit, 1.0, 0.0)
            gate = jnp.sum(jnp.where(hit, gate_row(b), 0.0), 1, keepdims=True)
            pick = pick.astype(bf16)
            x = mm(pick, n2_s[b])
            raw = mm(pick, cot_s[b])
            x_s[span, :] = x.astype(bf16)
            raw_s[span, :] = raw.astype(bf16)
            g = gate * raw
            g_s[span, :] = g.astype(bf16)
            gs_s[span, :] = jnp.broadcast_to(gate, (slots, 128))
        xt_s[...] = jnp.transpose(x_s[...])
        gt_s[...] = jnp.transpose(g_s[...])

    for j in range(quarters):

        @pl.when(step == j)
        def _():
            for copy in copies(j):
                copy.wait()

    w_in = w_s[step, 0]
    w_out = w_s[step, 1]
    rows = x_s.shape[0] // 2
    for r in range(2):
        span = pl.ds(r * rows, rows)
        act, slope = gelu_pair(mm(x_s[span, :], w_in))
        act = act.astype(bf16)
        dh = (mm(g_s[span, :], w_out, NT) * slope).astype(bf16)
        act_s[span, :] = act
        dh_s[span, :] = dh
        r_acc[span, :] += mm(act, w_out)
        dx_acc[span, :] += mm(dh, w_in, NT)
    grad_in = mm(xt_s[...], dh_s[...]).astype(bf16)
    grad_out = mm(gt_s[...], act_s[...]).astype(bf16)

    @pl.when(step < quarters // 2)
    def _():
        keep_ref[0, 0] = grad_in
        keep_ref[0, 1] = grad_out

    @pl.when(step >= quarters // 2)
    def _():
        send_ref[0, 0] = grad_in
        send_ref[0, 1] = grad_out

    @pl.when(step == quarters - 1)
    def _():
        dx_ref[...] = dx_acc[...].astype(bf16).reshape(dx_ref.shape)
        for b in range(blocks):
            span = pl.ds(b * slots, slots)
            res = r_acc[span, :].astype(bf16).astype(f32)
            dgate = jnp.sum(res * raw_s[span, :].astype(f32), 1, keepdims=True)
            res_ref[b] = (res * gs_s[span, 0:1]).astype(bf16)
            hit = row == slot_row(b)
            line = jnp.sum(jnp.where(hit, dgate, 0.0), 0, keepdims=True)
            to = (dg_ref, dgo_ref)[b // MICRO]
            to[pl.ds(b % MICRO, 1), :] = line


def expert_apply(index, place, n2, cot, tables, weights, slots):
    blocks = 2 * MICRO
    features = n2[0].shape[1]
    own = len(weights) == 2
    quarters = 4
    width = weights[0].shape[2] // (4 if own else 1)
    rows = blocks * slots

    def fixed(shape):
        zeros = (0,) * len(shape)
        return pl.BlockSpec(shape, lambda *_: zeros)

    half = quarters // 2
    pieces = jax.ShapeDtypeStruct((half, 2, features, width), bf16)
    return pl.pallas_call(
        functools.partial(expert_kernel, index, own),
        grid_spec=pltpu.PrefetchScalarGridSpec(
            num_scalar_prefetch=1,
            grid=(quarters,),
            in_specs=[pl.BlockSpec(memory_space=pl.ANY)] * (blocks + 2)
            + [fixed(piece.shape) for piece in tables]
            + [pl.BlockSpec(memory_space=pl.ANY)] * len(weights),
            out_specs=(
                fixed((blocks, slots, features)),
                fixed((blocks, slots, features)),
                pl.BlockSpec((1, 2, features, width), lambda i, _: (jnp.minimum(i, half - 1), 0, 0, 0)),
                pl.BlockSpec((1, 2, features, width), lambda i, _: (jnp.maximum(i - half, 0), 0, 0, 0)),
                fixed((MICRO, ROWS)),
                fixed((MICRO, ROWS)),
            ),
            scratch_shapes=[
                pltpu.VMEM((quarters, 2, features, width), bf16),
                pltpu.SemaphoreType.DMA((2 * quarters,)),
                pltpu.VMEM((blocks, ROWS, features), bf16),
                pltpu.VMEM((blocks, ROWS, features), bf16),
                pltpu.SemaphoreType.DMA((2 * blocks,)),
                pltpu.VMEM((rows, features), bf16),
                pltpu.VMEM((rows, features), bf16),
                pltpu.VMEM((rows, features), bf16),
                pltpu.VMEM((features, rows), bf16),
                pltpu.VMEM((features, rows), bf16),
                pltpu.VMEM((rows, 128), f32),
                pltpu.VMEM((rows, features), f32),
                pltpu.VMEM((rows, features), f32),
                pltpu.VMEM((rows, width), bf16),
                pltpu.VMEM((rows, width), bf16),
            ],
        ),
        out_shape=(
            jax.ShapeDtypeStruct((blocks, slots, features), bf16),
            jax.ShapeDtypeStruct((blocks, slots, features), bf16),
            pieces,
            pieces,
            jax.ShapeDtypeStruct((MICRO, ROWS), f32),
            jax.ShapeDtypeStruct((MICRO, ROWS), f32),
        ),
        compiler_params=params(60),
        cost_estimate=cost(12 * rows * features * width * quarters, 16_000_000),
        name="expert",
    )(place, *n2, *cot, *tables, *weights)


def selector(columns, slots):
    count = columns.shape[1]
    lane = lax.broadcasted_iota(jnp.int32, (columns.shape[0], slots), 1).astype(f32)
    pieces = [jnp.where(columns[:, k : k + 1] == lane, 1.0, 0.0).astype(bf16) for k in range(count)]
    return jnp.concatenate(pieces, 1)


def combine_kernel(count, slot_ref, *refs):
    slots = refs[0].shape[1]
    pick = selector(wide_transpose(slot_ref[0, count:, :], -1.0)[:, :count], slots)
    refs[count][0] = mm(pick, jnp.concatenate([r[0] for r in refs[:count]], 0)).astype(bf16)


def combine(slot, pieces, block, blocks):
    count = len(pieces)
    _, slots, features = pieces[0].shape
    piece = pl.BlockSpec((1, slots, features), lambda i: (i + block + MICRO, 0, 0))
    return pl.pallas_call(
        functools.partial(combine_kernel, count),
        grid=(blocks,),
        in_specs=[pl.BlockSpec((1, 2 * count, ROWS), lambda i: (i + block, 0, 0))] + [piece] * count,
        out_specs=image(ROWS, features),
        out_shape=jax.ShapeDtypeStruct((blocks, ROWS, features), bf16),
        compiler_params=params(24),
        cost_estimate=cost(2 * blocks * ROWS * features * slots * count, 5_000_000),
        name="combine",
    )(slot, *pieces)


def finish_kernel(count, mid0_ref, mid1_ref, part_ref, slotc_ref, dtok0_ref, dtok1_ref, *refs):
    out_ref, dout_ref, buf, dbuf = refs[count:]
    slots = refs[0].shape[1]
    step = pl.program_id(0)
    choose = selector(slotc_ref[0, :, :count], slots)
    mixed = mm(choose, jnp.concatenate([r[0] for r in refs[:count]], 0)) + part_ref[0].astype(f32)
    early = step < IMG_MB
    middle = jnp.where(early, mid0_ref[...], mid1_ref[...])
    value = middle + mixed
    grad = jnp.where(early, dtok0_ref[...].astype(f32), dtok1_ref[...].astype(f32))
    for i in range(IMAGES):

        @pl.when(step == i)
        def _():
            buf[pl.ds(i * SEQ, SEQ), :] = value[:SEQ]
            dbuf[pl.ds(i * SEQ, SEQ), :] = grad[:SEQ]

    @pl.when(step == IMAGES - 1)
    def _():
        out_ref[...] = buf[pl.ds(0, out_ref.shape[0]), :].astype(bf16)
        dout_ref[...] = dbuf[pl.ds(0, out_ref.shape[0]), :].astype(bf16)


def finish(middles, part, slotc, dtoks, results):
    count = len(results)
    _, slots, features = results[0].shape
    experts = slotc.shape[2]
    piece = pl.BlockSpec((1, slots, features), lambda i: (lax.div(i, IMG_MB), 0, 0))
    total = IMAGES * SEQ
    tall = 8 * ((total + 7) // 8)
    early = pl.BlockSpec((PAD, features), lambda i: (jnp.minimum(i, IMG_MB - 1), 0))
    later = pl.BlockSpec((PAD, features), lambda i: (jnp.maximum(i - IMG_MB, 0), 0))
    return pl.pallas_call(
        functools.partial(finish_kernel, count),
        grid=(IMAGES,),
        in_specs=[early, later, image(PAD, features), image(PAD, experts), early, later] + [piece] * count,
        out_specs=(whole((total, features)), whole((total, features))),
        out_shape=(jax.ShapeDtypeStruct((total, features), bf16),) * 2,
        scratch_shapes=[pltpu.VMEM((tall, features), f32)] * 2,
        compiler_params=params(24),
        cost_estimate=cost(4 * ROWS * features * slots * count, 15_000_000),
        name="finish",
    )(*middles, part, slotc, *dtoks, *results)


def norm_back(grad, normal, inverse, gain):
    scaled = grad * gain
    return inverse * (
        scaled
        - jnp.mean(scaled, -1, keepdims=True)
        - normal * jnp.mean(scaled * normal, -1, keepdims=True)
    )


def backward_kernel(first, count, place_ref, gate_ref, slotc_ref, dgo_ref, *refs):
    dg_refs = refs[:count]
    sources = refs[count : count + 8]
    refs = refs[count + 8 :]
    two_ref, more_ref = refs[:2]
    dx_refs = refs[2 : 2 + count]
    refs = refs[2 + count :]
    chained = first > 0
    if chained:
        before_ref, before_row_ref = refs[:2]
        dtok_ref, keep_ref, send_ref = refs[2:5]
        acc_s, acc_sem, row_ref = refs[5:8]
        refs = refs[8:]
    else:
        dtok_ref, acc_ref, row_ref = refs[:3]
        acc_s, acc_sem = refs[3:5]
        refs = refs[5:]
    w_s, sem, in_sem, dx_sem = refs[:4]
    tok_s, cot_s, proj_s, prob_s, att_s, mid_s, n2_s, dn2_s = stores = refs[4:12]
    dx_s, dbr_s, datt_s, dproj_s, n1_s, sum_s = refs[12:]
    micro = first // IMG_MB
    features = tok_s.shape[1]
    experts = 2 * count
    slots = dx_s.shape[0] // count
    copies = []
    for i, (src, dst) in enumerate(zip(sources, stores)):
        copies.append(pltpu.make_async_copy(src.at[micro] if i < 2 else src, dst, in_sem.at[i]))
    tok_in, cot_in, proj_in, prob_in, att_in, mid_in, n2_in, dn2_in = copies
    dx_in = [
        pltpu.make_async_copy(dx_refs[k].at[micro], dx_s.at[pl.ds(k * slots, slots), :], dx_sem.at[k])
        for k in range(count)
    ]
    for copy in (*dx_in, dn2_in, n2_in):
        copy.start()
    dense_in = load_dense(place_ref, two_ref, more_ref, w_s, sem)
    for copy in (mid_in, cot_in, att_in, proj_in, prob_in, tok_in):
        copy.start()
    if chained:
        acc_in = pltpu.make_async_copy(before_ref, acc_s, acc_sem.at[0])
        acc_in.start()
        row_ref[...] = before_row_ref[...]
    else:
        row_ref[...] = jnp.zeros_like(row_ref)
    choose = selector(slotc_ref[0, :, :count], slots)
    gates = gate_ref[...]
    dgates = [ref[pl.ds(micro, 1), :] for ref in dg_refs] + [dgo_ref[k, pl.ds(micro, 1), :] for k in range(count)]
    dgates = jnp.concatenate(dgates, 0)
    dlogits = (gates * (dgates - jnp.sum(gates * dgates, 0, keepdims=True))).astype(bf16)
    for copy in (*dx_in, dn2_in, n2_in, *dense_in):
        copy.wait()
    pick = vectors(w_s)
    qkv, out = dense_weights(w_s, features)
    router = router_rows(pick, place_ref, experts)
    row_ref[8 : 8 + experts, :] += mm(dlogits, n2_s[...])
    sum_s[...] = mm(choose, dx_s[...]) + mm(dlogits, router, TN)
    mid_in.wait()
    cot_in.wait()
    gain_two = pick(2).astype(f32)

    @pl.loop(0, IMG_MB)
    def _(i):
        span = pl.ds(pl.multiple_of(i * PAD, PAD), PAD)
        dn2 = sum_s[span, :] + dn2_s[span, :].astype(f32)
        _, normal_two, inverse_two = norm(mid_s[span, :], gain_two, 0.0)
        row_ref[2:3, :] += jnp.sum(dn2 * normal_two, 0, keepdims=True)
        row_ref[3:4, :] += jnp.sum(dn2, 0, keepdims=True)
        dmiddle = cot_s[span, :].astype(f32) + norm_back(dn2, normal_two, inverse_two, gain_two)
        mid_s[span, :] = dmiddle
        dbr_s[span, :] = dmiddle.astype(bf16)

    att_in.wait()
    if chained:
        acc_in.wait()
    grad_out = mm(att_s[...], dbr_s[...], TN)
    if chained:
        acc_s[:, 3 * features :] += grad_out
    else:
        acc_s[:, 3 * features :] = grad_out
    datt_s[...] = mm(dbr_s[...], out, NT).astype(bf16)
    proj_in.wait()
    prob_in.wait()
    tok_in.wait()
    pair = 2 * HEAD_DIM
    gain_one, offset_one = pick(0).astype(f32), pick(1).astype(f32)

    @pl.loop(0, IMG_MB)
    def _(i):
        span = pl.ds(pl.multiple_of(i * PAD, PAD), PAD)
        pre, _, _ = norm(tok_s[span, :].astype(f32), gain_one, offset_one)
        n1_s[span, :] = pre.astype(bf16)
        for group in range(HEADS // 2):
            at = [part * features + group * pair for part in range(3)]
            q2, k2, v2 = (proj_s[span, start : start + pair] for start in at)
            d2 = datt_s[span, group * pair : (group + 1) * pair]
            dq = dk = dv = None
            for half in range(2):
                probs = prob_s[i, 2 * group + half]
                wide = probs.astype(f32)
                dm = d2 * half_mask(half, 1.0)
                dweights = mm(dm, v2, NT)
                inner = jnp.sum(dweights * wide, -1, keepdims=True)
                dscores = (wide * (dweights - inner)).astype(bf16)
                part_q = mm(dscores, k2 * half_mask(half, SCALING))
                part_k = mm(dscores, q2 * half_mask(half, SCALING), TN)
                part_v = mm(probs, dm, TN)
                dq = part_q if dq is None else dq + part_q
                dk = part_k if dk is None else dk + part_k
                dv = part_v if dv is None else dv + part_v
            for start, value in zip(at, (dq, dk, dv)):
                dproj_s[span, start : start + pair] = value.astype(bf16)

    grad_qkv = mm(n1_s[...], dproj_s[...], TN)
    if chained:
        acc_s[:, : 3 * features] += grad_qkv
    else:
        acc_s[:, : 3 * features] = grad_qkv
        acc_out = pltpu.make_async_copy(acc_s, acc_ref, acc_sem.at[0])
        acc_out.start()
    sum_s[...] = mm(dproj_s[...], qkv, NT)

    @pl.loop(0, IMG_MB)
    def _(i):
        span = pl.ds(pl.multiple_of(i * PAD, PAD), PAD)
        dnormed = sum_s[span, :]
        _, normal_one, inverse_one = norm(tok_s[span, :].astype(f32), gain_one, offset_one)
        row_ref[0:1, :] += jnp.sum(dnormed * normal_one, 0, keepdims=True)
        row_ref[1:2, :] += jnp.sum(dnormed, 0, keepdims=True)
        dtok_ref[span, :] = (mid_s[span, :] + norm_back(dnormed, normal_one, inverse_one, gain_one)).astype(bf16)

    if not chained:
        acc_out.wait()
        return
    width = keep_ref.shape[1] - 16
    lines = [row_ref[i : i + 1, :] for i in range(4)]
    for e in range(experts):
        line = jnp.zeros((1, features), f32)
        for r in range(experts):
            line = jnp.where(expert_of(place_ref, r) == e, row_ref[8 + r : 9 + r, :], line)
        lines.append(line)
    blank = jnp.zeros((1, 4 * features - (4 + experts) * width), f32)
    tails = []
    for q in range(4):
        parts = [line[:, q * width : (q + 1) * width] for line in lines]
        tails.append(jnp.concatenate(parts + [blank], 1))
    for j in range(4):
        quarter = place_ref[j]
        to = (keep_ref, send_ref)[j // 2]
        to[j % 2, :width, :] = acc_s[pl.ds(pl.multiple_of(quarter * width, width), width), :].astype(bf16)
        tail = tails[0]
        for q in range(1, 4):
            tail = jnp.where(quarter == q, tails[q], tail)
        tail = jnp.concatenate([tail, jnp.zeros((15, tail.shape[1]), f32)], 0)
        to[j % 2, width:, :] = tail.astype(bf16)


def backward_images(first, place, tokp, cotp, saved, dgs, dg_other, slotc, dn2_part, dense, dxs, before):
    projected, probs, attended, middle, n2, gates = saved
    count = len(dxs)
    features = tokp.shape[2]
    experts = 2 * count
    slots = dxs[0].shape[1]
    totals = ((features, 4 * features), (8 + experts, features))
    packed = (2, *dense[0].shape[1:])
    anywhere = pl.BlockSpec(memory_space=pl.ANY)
    flat = (MICRO, ROWS, features)
    sources = (tokp.reshape(flat), cotp.reshape(flat), projected, probs, attended, middle, n2, dn2_part)
    out_specs = [whole((ROWS, features))]
    out_shape = [jax.ShapeDtypeStruct((ROWS, features), bf16)]
    scratch = [pltpu.VMEM(totals[0], f32), pltpu.SemaphoreType.DMA((1,))]
    if before:
        out_specs += [whole(packed)] * 2
        out_shape += [jax.ShapeDtypeStruct(packed, bf16)] * 2
        scratch.append(pltpu.VMEM(totals[1], f32))
        extra = [anywhere, whole(totals[1])]
    else:
        out_specs += [anywhere, whole(totals[1])]
        out_shape += [jax.ShapeDtypeStruct(shape, f32) for shape in totals]
        extra = []
    scratch += [
        pltpu.VMEM((4, *dense[0].shape[1:]), bf16),
        pltpu.SemaphoreType.DMA((4,)),
        pltpu.SemaphoreType.DMA((8,)),
        pltpu.SemaphoreType.DMA((count,)),
    ]
    scratch += [pltpu.VMEM((ROWS, features), bf16)] * 2
    scratch += [pltpu.VMEM(piece.shape, piece.dtype) for piece in sources[2:]]
    scratch += [
        pltpu.VMEM((count * slots, features), bf16),
        pltpu.VMEM((ROWS, features), bf16),
        pltpu.VMEM((ROWS, features), bf16),
        pltpu.VMEM((ROWS, 3 * features), bf16),
        pltpu.VMEM((ROWS, features), bf16),
        pltpu.VMEM((ROWS, features), f32),
    ]
    micro = first // IMG_MB
    return pl.pallas_call(
        functools.partial(backward_kernel, first, count),
        grid_spec=pltpu.PrefetchScalarGridSpec(
            num_scalar_prefetch=1,
            grid=(1,),
            in_specs=[
                whole(gates.shape),
                pl.BlockSpec((1, ROWS, experts), lambda i, _: (micro, 0, 0)),
                whole(dg_other.shape),
            ]
            + [whole(piece.shape) for piece in dgs]
            + [anywhere] * (10 + count)
            + extra,
            out_specs=tuple(out_specs),
            scratch_shapes=scratch,
        ),
        out_shape=tuple(out_shape),
        compiler_params=params(40),
        cost_estimate=cost(40 * ROWS * features * features, 15_000_000),
        name="backward",
    )(place, gates, slotc, dg_other, *dgs, *sources, *dense, *dxs, *before)


def settle_kernel(place_ref, far_ref, *refs):
    in_ref, back_ref = refs[-2:]
    z = place_ref[Z_AT]
    outer = jnp.where((z == 0) | (z == 3), 1.0, 0.0)

    def total(i):
        value = far_ref[i].astype(f32) * outer + refs[i - 4][...].astype(f32)
        for ref in refs[:-4]:
            piece = ref[0, i] if len(ref.shape) == 4 else ref[i]
            value = value + piece.astype(f32)
        return value

    in_ref[0] = total(0)
    back_ref[0] = jnp.transpose(total(1))


def settle(place, *pieces):
    features, span = pieces[-1].shape

    def spec(piece):
        shape = (1, *piece.shape[1:]) if len(piece.shape) == 4 else piece.shape
        return whole(shape)

    return pl.pallas_call(
        settle_kernel,
        grid_spec=pltpu.PrefetchScalarGridSpec(
            num_scalar_prefetch=1,
            grid=(1,),
            in_specs=[spec(piece) for piece in pieces],
            out_specs=(whole((1, features, span)), whole((1, span, features))),
        ),
        out_shape=(
            jax.ShapeDtypeStruct((1, features, span), f32),
            jax.ShapeDtypeStruct((1, span, features), f32),
        ),
        compiler_params=params(24),
        cost_estimate=cost(0, 5_000_000),
        name="settle",
    )(place, *pieces)


def unpack_kernel(part_ref, qkv_ref, out_ref, router_ref, g1_ref, b1_ref, g2_ref, b2_ref):
    width, columns = qkv_ref.shape
    pieces, _, lanes = part_ref.shape
    for i in range(pieces):
        value = part_ref[i, :width, :].astype(f32)
        at = i * lanes
        if at < columns:
            qkv_ref[:, at : at + lanes] = value
        else:
            out_ref[:, at - columns : at - columns + lanes] = value
    row = jnp.concatenate([part_ref[i, width:, :].astype(f32)[0:1] for i in range(pieces)], 1)
    for i, ref in enumerate((g1_ref, b1_ref, g2_ref, b2_ref)):
        ref[...] = row[:, i * width : (i + 1) * width]
    lines = [row[:, (4 + e) * width : (5 + e) * width] for e in range(router_ref.shape[0])]
    router_ref[...] = jnp.concatenate(lines, 0)


def unpack(part, columns, experts):
    pieces, height, lanes = part.shape
    width = height - 16
    line = (1, width)
    shapes = ((width, columns), (width, pieces * lanes - columns), (experts, width), line, line, line, line)
    return pl.pallas_call(
        unpack_kernel,
        grid=(1,),
        in_specs=[whole(part.shape)],
        out_specs=tuple(whole(shape) for shape in shapes),
        out_shape=tuple(jax.ShapeDtypeStruct(shape, f32) for shape in shapes),
        compiler_params=params(24),
        cost_estimate=cost(0, 3_000_000),
        name="unpack",
    )(part)


def norm_forward(values, gain, offset):
    center = values - jnp.mean(values, -1, keepdims=True)
    inverse = lax.rsqrt(jnp.mean(center * center, -1, keepdims=True) + EPSILON)
    normal = center * inverse
    return (normal * gain + offset, normal, inverse)


def norm_backward(grad, normal, inverse, gain):
    scaled = grad * gain
    return inverse * (
        scaled
        - jnp.mean(scaled, -1, keepdims=True)
        - normal * jnp.mean(scaled * normal, -1, keepdims=True)
    )


def gelu_value(field):
    return 0.5 * field * (1.0 + lax.erf(field * ROOT_HALF))


def gelu_slope(field):
    return (
        0.5 * (1.0 + lax.erf(field * ROOT_HALF))
        + field * jnp.exp(-0.5 * field * field) * INV_ROOT_TWO_PI
    )


def block_ranks(route_rows, order_keys, capacity):
    count = order_keys.shape[0]
    expert_count = capacity.shape[0]
    chosen = jnp.concatenate([route_rows[:, 0], route_rows[:, 1]])
    sort_keys = jnp.concatenate([order_keys, order_keys + count])
    positions = jnp.arange(2 * count, dtype=jnp.int32)
    inverse = jnp.zeros((2 * count,), jnp.int32).at[sort_keys].set(positions)
    ordered = chosen[inverse]
    labels = jnp.arange(expert_count, dtype=jnp.int32)
    onehot = (ordered[:, None] == labels[None, :]).astype(jnp.int32)
    before = jnp.cumsum(onehot, 0) - onehot
    rank_sorted = jnp.sum(before * onehot, 1)
    ranking = jnp.zeros((2 * count,), jnp.int32).at[inverse].set(rank_sorted)
    pair_onehot = chosen[:, None] == labels[None, :]
    limit = jnp.sum(pair_onehot.astype(jnp.int32) * capacity[None, :], 1)
    return (chosen, ranking, ranking < limit, pair_onehot.astype(jnp.float32))


def exchanged(
    tokens,
    ln1_gain,
    ln1_bias,
    qkv_weight,
    out_weight,
    ln2_gain,
    ln2_bias,
    router_weight,
    expert_in,
    expert_out,
    routes,
    priority,
    capacity,
    cotangent,
):
    f32 = jnp.float32
    bf16 = jnp.bfloat16
    gathered = (
        lax.all_gather(ln1_gain, "dp", axis=0, tiled=True),
        lax.all_gather(ln1_bias, "dp", axis=0, tiled=True),
        lax.all_gather(qkv_weight, "dp", axis=0, tiled=True),
        lax.all_gather(out_weight, "dp", axis=0, tiled=True),
        lax.all_gather(ln2_gain, "dp", axis=0, tiled=True),
        lax.all_gather(ln2_bias, "dp", axis=0, tiled=True),
        lax.all_gather(router_weight, "dp", axis=0, tiled=True),
    )
    gain_one = gathered[0].astype(f32)
    offset_one = gathered[1].astype(f32)
    weight_qkv = gathered[2]
    weight_out = gathered[3]
    gain_two = gathered[4].astype(f32)
    offset_two = gathered[5].astype(f32)
    weight_router = gathered[6]
    features = tokens.shape[1]
    owners = lax.axis_size("expert")
    per_owner = expert_in.shape[0]
    experts = owners * per_owner
    slots = 8 * (3 * TOP * IMG_MB * SEQ // (16 * experts) + 1)
    row_count = IMG_MB * SEQ
    sum_gain_one = jnp.zeros((features,), f32)
    sum_offset_one = jnp.zeros((features,), f32)
    sum_qkv = jnp.zeros(weight_qkv.shape, f32)
    sum_out = jnp.zeros(weight_out.shape, f32)
    sum_gain_two = jnp.zeros((features,), f32)
    sum_offset_two = jnp.zeros((features,), f32)
    sum_router = jnp.zeros(weight_router.shape, f32)
    sum_expert_in = jnp.zeros(expert_in.shape, f32)
    sum_expert_out = jnp.zeros(expert_out.shape, f32)
    outputs = []
    input_grads = []
    for micro in range(MICRO):
        start = micro * row_count
        inputs = tokens[start : start + row_count].astype(f32)
        pre_one, normal_one, inverse_one = norm_forward(inputs, gain_one, offset_one)
        normed = pre_one.astype(bf16)
        projected = jnp.dot(normed, weight_qkv, preferred_element_type=f32).astype(bf16)
        projected = projected.reshape(IMG_MB, SEQ, 3, HEADS, HEAD_DIM)
        queries = projected[:, :, 0]
        key_rows = projected[:, :, 1]
        values = projected[:, :, 2]
        scores = (
            jnp.einsum("gqhd,gkhd->ghqk", queries, key_rows, preferred_element_type=f32) * SCALING
        )
        highest = jnp.max(scores, -1, keepdims=True)
        expos = jnp.exp(scores - highest)
        totals = jnp.sum(expos, -1, keepdims=True)
        log_total = highest + jnp.log(totals)
        attn_weights = (expos / totals).astype(bf16)
        attended = jnp.einsum(
            "ghqk,gkhd->gqhd", attn_weights, values, preferred_element_type=f32
        ).astype(bf16)
        attended = attended.reshape(row_count, features)
        middle = inputs + jnp.dot(attended, weight_out, preferred_element_type=f32)
        pre_two, normal_two, inverse_two = norm_forward(middle, gain_two, offset_two)
        normed_two = pre_two.astype(bf16)
        logits = jnp.dot(normed_two, weight_router, preferred_element_type=f32)
        gates = jax.nn.softmax(logits, -1)
        route_rows = routes[start : start + row_count]
        chosen, ranking, kept, pair_onehot = block_ranks(
            route_rows, priority[start : start + row_count], capacity
        )
        keep_float = kept.astype(f32)
        slot_send = jnp.where(kept, ranking, slots)
        slot_read = jnp.where(kept, ranking, 0)
        doubled = jnp.concatenate([normed_two, normed_two], 0)
        send = (
            jnp.zeros((experts, slots, features), bf16)
            .at[chosen, slot_send]
            .set(doubled, mode="drop")
        )
        received = lax.all_to_all(
            send.reshape(owners, per_owner, slots, features),
            "expert",
            split_axis=0,
            concat_axis=0,
            tiled=True,
        )
        hidden = jnp.einsum("sjcd,jdf->sjcf", received, expert_in, preferred_element_type=f32)
        active = gelu_value(hidden).astype(bf16)
        result = jnp.einsum(
            "sjcf,jfd->sjcd", active, expert_out, preferred_element_type=f32
        ).astype(bf16)
        back = lax.all_to_all(result, "expert", split_axis=0, concat_axis=0, tiled=True).reshape(
            experts, slots, features
        )
        pieces = back[chosen, slot_read].astype(f32) * keep_float[:, None]
        picked = jnp.take_along_axis(gates, route_rows, 1)
        gate_pair = jnp.concatenate([picked[:, 0], picked[:, 1]])
        mixed = pieces[:row_count] * picked[:, 0:1] + pieces[row_count:] * picked[:, 1:2]
        outputs.append((middle + mixed).astype(bf16))
        grad_out = cotangent[start : start + row_count].astype(f32)
        grad_doubled = jnp.concatenate([grad_out, grad_out], 0)
        dgate = jnp.sum(grad_doubled * pieces, -1)
        dpieces = (grad_doubled * (gate_pair * keep_float)[:, None]).astype(bf16)
        dgates = (
            pair_onehot[:row_count] * dgate[:row_count, None]
            + pair_onehot[row_count:] * dgate[row_count:, None]
        )
        dlogits = (gates * (dgates - jnp.sum(gates * dgates, -1, keepdims=True))).astype(bf16)
        grad_send = (
            jnp.zeros((experts, slots, features), bf16)
            .at[chosen, slot_send]
            .set(dpieces, mode="drop")
        )
        grad_received = lax.all_to_all(
            grad_send.reshape(owners, per_owner, slots, features),
            "expert",
            split_axis=0,
            concat_axis=0,
            tiled=True,
        )
        dactive = jnp.einsum(
            "sjcd,jfd->sjcf", grad_received, expert_out, preferred_element_type=f32
        )
        dhidden = (dactive * gelu_slope(hidden)).astype(bf16)
        grad_w_out = jnp.einsum("sjcf,sjcd->jfd", active, grad_received, preferred_element_type=f32)
        grad_w_in = jnp.einsum("sjcd,sjcf->jdf", received, dhidden, preferred_element_type=f32)
        sum_expert_in = sum_expert_in + grad_w_in
        sum_expert_out = sum_expert_out + grad_w_out
        dsent = jnp.einsum("sjcf,jdf->sjcd", dhidden, expert_in, preferred_element_type=f32).astype(
            bf16
        )
        dreturn = lax.all_to_all(dsent, "expert", split_axis=0, concat_axis=0, tiled=True).reshape(
            experts, slots, features
        )
        dpair = dreturn[chosen, slot_read].astype(f32) * keep_float[:, None]
        dnormed_two = (
            jnp.dot(dlogits, weight_router.T, preferred_element_type=f32)
            + dpair[:row_count]
            + dpair[row_count:]
        )
        sum_router = sum_router + jnp.dot(normed_two.T, dlogits, preferred_element_type=f32)
        sum_gain_two = sum_gain_two + jnp.sum(dnormed_two * normal_two, 0)
        sum_offset_two = sum_offset_two + jnp.sum(dnormed_two, 0)
        dmiddle = grad_out + norm_backward(dnormed_two, normal_two, inverse_two, gain_two)
        dbranch = dmiddle.astype(bf16)
        sum_out = sum_out + jnp.dot(attended.T, dbranch, preferred_element_type=f32)
        dattended = jnp.dot(dbranch, weight_out.T, preferred_element_type=f32).astype(bf16)
        dattended = dattended.reshape(IMG_MB, SEQ, HEADS, HEAD_DIM)
        again = (
            jnp.einsum("gqhd,gkhd->ghqk", queries, key_rows, preferred_element_type=f32) * SCALING
        )
        probs_again = jnp.exp(again - log_total)
        dvalues = jnp.einsum(
            "ghqk,gqhd->gkhd", probs_again.astype(bf16), dattended, preferred_element_type=f32
        )
        dweights = jnp.einsum("gqhd,gkhd->ghqk", dattended, values, preferred_element_type=f32)
        inner = jnp.sum(dweights * probs_again, -1, keepdims=True)
        dscores = (probs_again * (dweights - inner)).astype(bf16)
        dqueries = (
            jnp.einsum("ghqk,gkhd->gqhd", dscores, key_rows, preferred_element_type=f32) * SCALING
        )
        dkeys = (
            jnp.einsum("ghqk,gqhd->gkhd", dscores, queries, preferred_element_type=f32) * SCALING
        )
        dprojected = (
            jnp.stack([dqueries, dkeys, dvalues], 2).astype(bf16).reshape(row_count, 3 * features)
        )
        sum_qkv = sum_qkv + jnp.dot(normed.T, dprojected, preferred_element_type=f32)
        dnormed = jnp.dot(dprojected, weight_qkv.T, preferred_element_type=f32)
        sum_gain_one = sum_gain_one + jnp.sum(dnormed * normal_one, 0)
        sum_offset_one = sum_offset_one + jnp.sum(dnormed, 0)
        input_grads.append(
            (dmiddle + norm_backward(dnormed, normal_one, inverse_one, gain_one)).astype(bf16)
        )
    grad_expert_in, grad_expert_out = (
        lax.psum_scatter(
            sum_expert_in.astype(jnp.bfloat16), "dp", scatter_dimension=2, tiled=True
        ).astype(jnp.float32),
        lax.psum_scatter(
            sum_expert_out.astype(jnp.bfloat16), "dp", scatter_dimension=1, tiled=True
        ).astype(jnp.float32),
    )
    dense = (
        sum_gain_one,
        sum_offset_one,
        sum_qkv,
        sum_out,
        sum_gain_two,
        sum_offset_two,
        sum_router,
    )
    totals_all = (
        lax.psum(dense[0].astype(jnp.bfloat16), "expert").astype(jnp.float32),
        lax.psum(dense[1].astype(jnp.bfloat16), "expert").astype(jnp.float32),
        lax.psum(dense[2].astype(jnp.bfloat16), "expert").astype(jnp.float32),
        lax.psum(dense[3].astype(jnp.bfloat16), "expert").astype(jnp.float32),
        lax.psum(dense[4].astype(jnp.bfloat16), "expert").astype(jnp.float32),
        lax.psum(dense[5].astype(jnp.bfloat16), "expert").astype(jnp.float32),
        lax.psum(dense[6].astype(jnp.bfloat16), "expert").astype(jnp.float32),
    )
    owned = (
        lax.psum_scatter(
            totals_all[0].astype(jnp.bfloat16), "dp", scatter_dimension=0, tiled=True
        ).astype(jnp.float32),
        lax.psum_scatter(
            totals_all[1].astype(jnp.bfloat16), "dp", scatter_dimension=0, tiled=True
        ).astype(jnp.float32),
        lax.psum_scatter(
            totals_all[2].astype(jnp.bfloat16), "dp", scatter_dimension=0, tiled=True
        ).astype(jnp.float32),
        lax.psum_scatter(
            totals_all[3].astype(jnp.bfloat16), "dp", scatter_dimension=0, tiled=True
        ).astype(jnp.float32),
        lax.psum_scatter(
            totals_all[4].astype(jnp.bfloat16), "dp", scatter_dimension=0, tiled=True
        ).astype(jnp.float32),
        lax.psum_scatter(
            totals_all[5].astype(jnp.bfloat16), "dp", scatter_dimension=0, tiled=True
        ).astype(jnp.float32),
        lax.psum_scatter(
            totals_all[6].astype(jnp.bfloat16), "dp", scatter_dimension=0, tiled=True
        ).astype(jnp.float32),
    )
    block_out = jnp.concatenate(outputs, 0)
    grad_tokens = jnp.concatenate(input_grads, 0)
    return (
        block_out,
        grad_tokens,
        owned[0],
        owned[1],
        owned[2],
        owned[3],
        owned[4],
        owned[5],
        owned[6],
        grad_expert_in,
        grad_expert_out,
    )


SWAP = [(0, 1), (1, 0)]
OUTWARD = [(1, 0), (2, 3)]
SECOND = [(0, 1), (3, 2), (1, 3), (2, 0)]
MIDDLE = [(1, 2), (2, 1)]


def flip(bit):
    return [(i, i ^ bit) for i in range(4)]


def add(*pieces):
    total = pieces[0].astype(f32)
    for piece in pieces[1:]:
        total = total + piece.astype(f32)
    return total.astype(bf16)


def stage(*values):
    return lax.optimization_barrier(values)


def after(value, *others):
    return lax.optimization_barrier((value, *others))[0]


def paired(
    tokens,
    ln1_gain,
    ln1_bias,
    qkv_weight,
    out_weight,
    ln2_gain,
    ln2_bias,
    router_weight,
    expert_in,
    expert_out,
    routes,
    priority,
    capacity,
    cotangent,
):
    y, core, z, x = (lax.axis_index(name) for name in ("y", "core", "z", "x"))
    features = tokens.shape[1]
    experts = capacity.shape[0]
    width = qkv_weight.shape[0]
    count = experts // 2
    slots = 8 * (3 * TOP * IMG_MB * SEQ // (16 * experts) + 1)
    lanes = 4 * features

    order = jnp.arange(8, dtype=jnp.int32)
    place = (((order & 1) ^ y) << 1) | (((order >> 1) & 1) ^ core)
    for at, value in ((Z_AT, z), (X_AT, x), (Y_AT, y), (CORE_AT, core)):
        place = jnp.where(order == at, value, place)

    def swap(value, axis, pairs=SWAP):
        return lax.ppermute(value, axis, pairs)

    gains = (ln1_gain, ln1_bias, ln2_gain, ln2_bias)
    packed = pack(gains, qkv_weight, out_weight, router_weight.T)
    from_y = swap(packed, "y")
    one = quarter_of(after(place, packed), expert_in, expert_out)
    near = swap(one, "z", flip(1))
    centre = swap(one, "z", MIDDLE)
    cotp = pad_images(after(cotangent, one))
    cot_other = swap(cotp, "x")
    place, cotp = stage(place, cotp)
    tokp, slot, slotc = prepare(place, capacity, tokens, routes, priority)
    place, from_y, tokp, slot = stage(place, from_y, tokp, slot)
    two = jnp.concatenate([packed, from_y], 0)
    dense = (two, swap(two, "core"))

    place, near, centre = stage(place, near, centre)
    second_mid = swap(near, "z", MIDDLE)
    second_out = swap(centre, "z", OUTWARD)
    across = [swap(near, "y")]
    saved = [forward_images(0, place, tokp, dense, experts)]
    place, cot_other, first_n2 = stage(place, cot_other, saved[0][4])
    n2_other = [swap(first_n2, "x")]
    saved.append(forward_images(IMG_MB, place, tokp, dense, experts))
    place, last_n2, last_gates, second_mid, second_out, across[0], n2_other[0] = stage(
        place, saved[1][4], saved[1][5], second_mid, second_out, across[0], n2_other[0]
    )
    n2_other.append(swap(last_n2, "x"))
    tables = jnp.concatenate([slot, saved[0][5][None], last_gates[None]], 0)
    other = swap(tables, "x")
    second = second_mid + second_out
    outer = swap(second, "z", OUTWARD)
    across.append(swap(second, "y"))
    corner = [swap(piece, "core") for piece in (near, across[0])]

    n2 = [piece[4] for piece in saved] + n2_other
    cot = [piece.reshape(MICRO, ROWS, features) for piece in (cotp, cot_other)]
    tables = (slot, saved[0][5], saved[1][5], other)
    place, *corner = stage(place, *corner)
    pieces = (near, across[0], *corner)
    out1 = expert_apply(1, place, n2, cot, tables, pieces, slots)
    place, outer, across[1], *out1 = stage(place, outer, across[1], *out1)
    third = centre + outer
    across.append(swap(third, "y"))
    corner = [swap(piece, "core") for piece in (second, across[1])]
    core1 = swap(out1[3], "core")
    place, *corner = stage(place, *corner)
    pieces = (second, across[1], *corner)
    out2 = expert_apply(2, place, n2, cot, tables, pieces, slots)
    place, across[2], core1, *out2 = stage(place, across[2], core1, *out2)
    corner = [swap(piece, "core") for piece in (third, across[2])]
    core2 = swap(out2[3], "core")
    side1 = swap(add(out1[2][1], core1[1]), "y")
    place, *corner = stage(place, *corner)
    pieces = (third, across[2], *corner)
    out3 = expert_apply(3, place, n2, cot, tables, pieces, slots)
    place, core2, side1, *out3 = stage(place, core2, side1, *out3)
    core3 = swap(out3[3], "core")
    side2 = swap(add(out2[2][1], core2[1]), "y")
    first_swap = swap(add(out1[2][0], core1[0], side1), "z", flip(1))
    out0 = expert_apply(0, place, n2, cot, tables, (expert_in, expert_out), slots)
    place, core3, side2, first_swap, *out0 = stage(place, core3, side2, first_swap, *out0)

    outs = (out0, out1, out2, out3)
    results, dxs, keeps, _, dgs, dgos = ([piece[i] for piece in outs] for i in range(6))
    dn2_mine = [combine(other, dxs, 0, 1)]
    rest, core_send, dn2_send, *dgos = stage(other, out0[3], dn2_mine[0], *dgos)
    dn2 = [swap(dn2_send, "x")]
    dg_other = swap(jnp.stack(dgos), "x")
    side3 = swap(add(out3[2][1], core3[1]), "y")
    second_swap = swap(add(out2[2][0], core2[0], side2), "z", SECOND)
    core0 = swap(core_send, "core")
    dn2_mine.append(combine(rest, dxs, 1, 1))
    mixed_mine = combine(after(rest, dn2_mine[1]), results, 0, MICRO)
    place, mixed_mine, core0, dn2[0], last, dg_other = stage(
        place, mixed_mine, core0, dn2[0], dn2_mine[1], dg_other
    )
    dn2.append(swap(last, "x"))

    columns = slotc.reshape(IMAGES, PAD, experts)

    def back_images(micro, place, before):
        rows = dn2[micro].reshape(ROWS, features)
        return backward_images(
            micro * IMG_MB, place, tokp, cotp, saved[micro], dgs, dg_other, slotc, rows, dense, dxs, before
        )

    first = back_images(0, place, ())
    place, second_swap, side3, dn2[1], *first = stage(place, second_swap, side3, dn2[1], *first)
    inner = (z == 1) | (z == 2)
    third_sum = add(out3[2][0], core3[0], side3, jnp.where(inner, second_swap, 0.0))
    third_swap = [swap(third_sum[0], "z", flip(3))]
    side0 = swap(add(out0[2][1], core0[1]), "y")
    mixed = swap(mixed_mine, "x")
    keep_send = back_images(1, place, tuple(first[1:]))
    place, third_swap[0], side0, mixed, *keep_send = stage(place, third_swap[0], side0, mixed, *keep_send)
    third_swap.append(swap(third_sum[1], "z", flip(3)))
    mixed = mixed.reshape(IMAGES, PAD, features)
    dtok = [first[0], keep_send[0]]
    keep, send = keep_send[1:]

    from_near = swap(send, "core")
    part = swap(add(keep[1], from_near[1]), "y")
    block_out, grad_tokens = finish([piece[3] for piece in saved], mixed, columns, dtok, results)
    part, third_swap[1], block_out, grad_tokens = stage(part, third_swap[1], block_out, grad_tokens)
    part = add(keep[0], from_near[0], part)
    cut = part.reshape(width + 16, 8, lanes // 8).transpose(1, 0, 2)
    cut = lax.all_to_all(cut, ("z", "x"), split_axis=0, concat_axis=0, tiled=True)
    cut = jnp.sum(cut.astype(f32), 0).astype(bf16)
    part = jnp.broadcast_to(cut[None], (8, *cut.shape))
    part = lax.all_to_all(part, ("z", "x"), split_axis=0, concat_axis=0, tiled=True)
    gq, go, gr, *lines = unpack(part, 3 * features, experts)
    lines = [line.reshape(width) for line in lines]
    grad_in, grad_back = settle(place, second_swap, out0[2], core0, side0, first_swap, *third_swap)

    return (block_out, grad_tokens, lines[0], lines[1], gq, go, lines[2], lines[3], gr.T, grad_in, grad_back)


def solution(mesh):
    if mesh.shape["dp"] == 4 and mesh.shape["expert"] == 8:
        mesh = Mesh(mesh.devices.reshape(2, 2, 4, 2), ("y", "core", "z", "x"))
        body, dp, expert = paired, ("y", "core"), ("z", "x")
    else:
        body, dp, expert = exchanged, ("dp",), ("expert",)
    rows = P((*dp, *expert), None)
    return jax.shard_map(
        body,
        mesh=mesh,
        in_specs=(
            rows,
            P(dp),
            P(dp),
            P(dp, None),
            P(dp, None),
            P(dp),
            P(dp),
            P(dp, None),
            P(expert, None, None),
            P(expert, None, None),
            rows,
            P((*dp, *expert)),
            P(),
            rows,
        ),
        out_specs=(
            rows,
            rows,
            P(dp),
            P(dp),
            P(dp, None),
            P(dp, None),
            P(dp),
            P(dp),
            P(dp, None),
            P(expert, None, dp),
            P(expert, dp, None),
        ),
        check_vma=False,
    )
```

```python
import functools
import jax
import jax.numpy as jnp
from jax import lax
from jax.experimental import pallas as pl
from jax.experimental.pallas import tpu as pltpu
from jax.sharding import Mesh
from jax.sharding import PartitionSpec as P

HEADS = 8
HEAD_DIM = 64
TOP = 2
SEQ = 197
IMG_MB = 3
MICRO = 2
EPSILON = 1e-06
SCALING = 0.125
ROOT_HALF = 0.7071067811865476
INV_ROOT_TWO_PI = 0.3989422804014327
PAD = 16 * ((SEQ + 15) // 16)
ROWS = IMG_MB * PAD
IMAGES = MICRO * IMG_MB
f32 = jnp.float32
bf16 = jnp.bfloat16
NN = (((1,), (0,)), ((), ()))
NT = (((1,), (1,)), ((), ()))
TN = (((0,), (0,)), ((), ()))


def mm(a, b, dims=NN):
    return lax.dot_general(a, b, dims, preferred_element_type=f32)


def whole(shape):
    zeros = (0,) * len(shape)
    return pl.BlockSpec(shape, lambda *_: zeros)


def params(mb=60):
    return pltpu.CompilerParams(vmem_limit_bytes=mb << 20)


SHARE = 1.0


def cost(flops, moved):
    return pl.CostEstimate(flops=int(flops * SHARE), bytes_accessed=int(moved * SHARE), transcendentals=0)


Z_AT, X_AT, Y_AT, CORE_AT = 4, 5, 6, 7


def expert_of(place_ref, index):
    return 2 * (place_ref[Z_AT] ^ (index & 3)) + (place_ref[X_AT] ^ (index >> 2))


def label_column(place_ref, experts):
    index = lax.broadcasted_iota(jnp.int32, (experts, 1), 0)
    label = jnp.zeros((experts, 1), jnp.int32)
    for r in range(experts):
        label = jnp.where(index == r, expert_of(place_ref, r), label)
    return label


def wide_transpose(rows, fill):
    pad = jnp.full((128 - rows.shape[0], rows.shape[1]), fill, f32)
    return jnp.transpose(jnp.concatenate([rows, pad], 0))


def pack_kernel(g1_ref, b1_ref, g2_ref, b2_ref, qkv_ref, out_ref, router_ref, packed_ref):
    width, columns = qkv_ref.shape
    packed_ref[0, :width, :columns] = qkv_ref[...]
    packed_ref[0, :width, columns:] = out_ref[...]
    pieces = [ref[...].astype(f32) for ref in (g1_ref, b1_ref, g2_ref, b2_ref)]
    router = router_ref[...].astype(f32)
    pieces += [router[e : e + 1, :] for e in range(router.shape[0])]
    rest = packed_ref.shape[2] - width * len(pieces)
    row = jnp.concatenate(pieces + [jnp.zeros((1, rest), f32)], 1)
    row = jnp.concatenate([row, jnp.zeros((15, row.shape[1]), f32)], 0)
    packed_ref[0, width:, :] = row.astype(bf16)


def pack(vectors_in, qkv, out, router):
    width, columns = qkv.shape
    rows = [vector.reshape(1, width) for vector in vectors_in]
    packed = (1, width + 16, columns + out.shape[1])
    inputs = (*rows, qkv, out, router)
    return pl.pallas_call(
        pack_kernel,
        grid=(1,),
        in_specs=[whole(value.shape) for value in inputs],
        out_specs=whole(packed),
        out_shape=jax.ShapeDtypeStruct(packed, bf16),
        compiler_params=params(60),
        cost_estimate=cost(0, 2_000_000),
        name="pack",
    )(*inputs)


def quarter_kernel(place_ref, in_ref, back_ref, one_ref, sem):
    span = one_ref.shape[1]
    start = pl.multiple_of(place_ref[0] * span, span)
    copies = (
        pltpu.make_async_copy(in_ref.at[0, :, pl.ds(start, span)], one_ref.at[0], sem.at[0]),
        pltpu.make_async_copy(back_ref.at[0, pl.ds(start, span), :], one_ref.at[1], sem.at[1]),
    )
    for copy in copies:
        copy.start()
    for copy in copies:
        copy.wait()


def quarter_of(place, expert_in, expert_out):
    shape = (2, expert_in.shape[1], expert_in.shape[2] // 4)
    return pl.pallas_call(
        quarter_kernel,
        grid_spec=pltpu.PrefetchScalarGridSpec(
            num_scalar_prefetch=1,
            grid=(1,),
            in_specs=[pl.BlockSpec(memory_space=pl.ANY)] * 2,
            out_specs=whole(shape),
            scratch_shapes=[pltpu.SemaphoreType.DMA((2,))],
        ),
        out_shape=jax.ShapeDtypeStruct(shape, bf16),
        compiler_params=params(60),
        cost_estimate=cost(0, 2_000_000),
        name="quarter",
    )(place, expert_in, expert_out)


def pad_rows(src_ref, dst_ref, buf):
    buf[pl.ds(0, src_ref.shape[0]), :] = src_ref[...].astype(f32)
    for image in range(IMAGES):
        piece = buf[pl.ds(image * SEQ, PAD), :]
        row = lax.broadcasted_iota(jnp.int32, piece.shape, 0)
        dst_ref[image] = jnp.where(row < SEQ, piece, 0.0).astype(bf16)


def pad_images(values):
    total, features = values.shape
    padded = (IMAGES, PAD, features)
    return pl.pallas_call(
        pad_rows,
        grid=(1,),
        in_specs=[whole(values.shape)],
        out_specs=whole(padded),
        out_shape=jax.ShapeDtypeStruct(padded, bf16),
        scratch_shapes=[pltpu.VMEM((8 * ((total + PAD) // 8), features), f32)],
        compiler_params=params(60),
        cost_estimate=cost(0, 4_000_000),
        name="pad",
    )(values)


def prepare_kernel(place_ref, cap_ref, tok_ref, route_ref, prio_ref, tokp_ref, slot_ref, slotc_ref, buf, keys):
    total = tok_ref.shape[0]
    experts = slot_ref.shape[1]
    pad_rows(tok_ref, tokp_ref, buf)
    keys[...] = jnp.full_like(keys, -1.0)
    keys[pl.ds(0, total), 0:2] = route_ref[...].astype(f32)
    keys[pl.ds(0, total), 2:3] = prio_ref[...].astype(f32)
    labels = label_column(place_ref, experts)
    limit = jnp.zeros((experts, 1), f32)
    for e in range(experts):
        limit = jnp.where(labels == e, cap_ref[e].astype(f32), limit)
    labels = labels.astype(f32)
    for block in range(MICRO):
        columns = []
        for image in range(IMG_MB):
            piece = keys[pl.ds((block * IMG_MB + image) * SEQ, PAD), :]
            row = lax.broadcasted_iota(jnp.int32, piece.shape, 0)
            columns.append(jnp.where(row < SEQ, piece, -1.0))
        column = jnp.concatenate(columns, 0)
        turned = jnp.transpose(column)
        key_column = jnp.where(column[:, 2:3] < 0.0, 1e6, column[:, 2:3])
        below = jnp.where(key_column < turned[2:3, :], 1.0, 0.0).astype(bf16)
        first = labels == turned[0:1, :]
        second = labels == turned[1:2, :]
        hot = jnp.concatenate([jnp.where(first, 1.0, 0.0), jnp.where(second, 1.0, 0.0)], 0)
        counts = mm(hot.astype(bf16), below)
        total_first = jnp.sum(hot[:experts], 1, keepdims=True)
        rank = jnp.where(
            first, counts[:experts], jnp.where(second, counts[experts:] + total_first, 1e6)
        )
        slot = jnp.where(rank < limit, rank, -1.0)
        slot_ref[block] = slot
        slotc_ref[block] = wide_transpose(slot, -1.0)[:, :experts]


def prepare(place, capacity, tokens, routes, priority):
    total, features = tokens.shape
    experts = capacity.shape[0]
    tall = 8 * ((total + PAD) // 8)
    priority = priority.reshape(total, 1)
    padded = (IMAGES, PAD, features)
    return pl.pallas_call(
        prepare_kernel,
        grid_spec=pltpu.PrefetchScalarGridSpec(
            num_scalar_prefetch=2,
            grid=(1,),
            in_specs=[whole(tokens.shape), whole(routes.shape), whole(priority.shape)],
            out_specs=(
                whole(padded),
                whole((MICRO, experts, ROWS)),
                whole((MICRO, ROWS, experts)),
            ),
            scratch_shapes=[pltpu.VMEM((tall, features), f32), pltpu.VMEM((tall, 128), f32)],
        ),
        out_shape=(
            jax.ShapeDtypeStruct(padded, bf16),
            jax.ShapeDtypeStruct((MICRO, experts, ROWS), f32),
            jax.ShapeDtypeStruct((MICRO, ROWS, experts), f32),
        ),
        compiler_params=params(60),
        cost_estimate=cost(0, 8_000_000),
        name="prepare",
    )(place, capacity, tokens, routes, priority)


def norm(values, gain, offset):
    center = values - jnp.mean(values, -1, keepdims=True)
    inverse = lax.rsqrt(jnp.mean(center * center, -1, keepdims=True) + EPSILON)
    normal = center * inverse
    return normal * gain + offset, normal, inverse


def load_dense(place_ref, two_ref, more_ref, w_s, sem):
    copies = [
        pltpu.make_async_copy((two_ref, more_ref)[j // 2].at[j % 2], w_s.at[place_ref[j]], sem.at[j])
        for j in range(4)
    ]
    for copy in copies:
        copy.start()
    return copies


def vectors(w_s):
    quarters = w_s.shape[0]
    width = w_s.shape[1] - 16
    row = [w_s[q, pl.ds(width, 1), :] for q in range(quarters)]

    def pick(index):
        return jnp.concatenate([r[:, index * width : (index + 1) * width] for r in row], 1)

    return pick


def dense_weights(w_s, features):
    width = w_s.shape[1] - 16
    qkv = w_s[:, :width, : 3 * features].reshape(features, 3 * features)
    out = w_s[:, :width, 3 * features :].reshape(features, features)
    return qkv, out


def router_rows(pick, place_ref, experts):
    table = jnp.concatenate([pick(4 + e) for e in range(experts)], 0)
    labels = label_column(place_ref, experts)
    order = labels == lax.broadcasted_iota(jnp.int32, (experts, experts), 1)
    return mm(jnp.where(order, 1.0, 0.0).astype(bf16), table).astype(bf16)


def half_mask(index, value):
    lane = lax.broadcasted_iota(jnp.int32, (1, 2 * HEAD_DIM), 1)
    return jnp.where((lane < HEAD_DIM) == (index == 0), value, 0.0).astype(bf16)


def forward_kernel(first, place_ref, tok_ref, two_ref, more_ref, proj_ref, prob_ref, att_ref, mid_ref, n2_ref, gate_ref, w_s, sem, in_sem, out_sem, tok_s, n1_s, proj_s, prob_s, att_s, mid_s, n2_s):
    features = tok_s.shape[1]
    copy_in = pltpu.make_async_copy(tok_ref.at[first // IMG_MB], tok_s, in_sem.at[0])
    copy_in.start()
    waits = load_dense(place_ref, two_ref, more_ref, w_s, sem)
    out_copies = [
        pltpu.make_async_copy(src, dst, out_sem.at[i])
        for i, (src, dst) in enumerate(
            ((proj_s, proj_ref), (prob_s, prob_ref), (att_s, att_ref), (mid_s, mid_ref), (n2_s, n2_ref))
        )
    ]
    copy_in.wait()
    for copy in waits:
        copy.wait()
    pick = vectors(w_s)
    qkv, out = dense_weights(w_s, features)
    gain, offset = pick(0).astype(f32), pick(1).astype(f32)

    @pl.loop(0, IMG_MB)
    def _(i):
        span = pl.ds(pl.multiple_of(i * PAD, PAD), PAD)
        pre, _, _ = norm(tok_s[span, :].astype(f32), gain, offset)
        n1_s[span, :] = pre.astype(bf16)

    proj_s[...] = mm(n1_s[...], qkv).astype(bf16)
    out_copies[0].start()
    column = lax.broadcasted_iota(jnp.int32, (1, PAD), 1)
    pair = 2 * HEAD_DIM

    @pl.loop(0, IMG_MB)
    def _(i):
        span = pl.ds(pl.multiple_of(i * PAD, PAD), PAD)
        for group in range(HEADS // 2):
            q2 = proj_s[span, group * pair : (group + 1) * pair]
            k2 = proj_s[span, features + group * pair : features + (group + 1) * pair]
            v2 = proj_s[span, 2 * features + group * pair : 2 * features + (group + 1) * pair]
            total = None
            for half in range(2):
                scores = mm(q2 * half_mask(half, SCALING), k2, NT)
                scores = jnp.where(column < SEQ, scores, -1e30)
                expos = jnp.exp(scores - jnp.max(scores, -1, keepdims=True))
                probs = (expos * (1.0 / jnp.sum(expos, -1, keepdims=True))).astype(bf16)
                prob_s[i, 2 * group + half] = probs
                piece = mm(probs, v2 * half_mask(half, 1.0))
                total = piece if total is None else total + piece
            att_s[span, group * pair : (group + 1) * pair] = total.astype(bf16)

    out_copies[1].start()
    out_copies[2].start()
    mid_s[...] = mm(att_s[...], out)
    gain_two, offset_two = pick(2).astype(f32), pick(3).astype(f32)

    @pl.loop(0, IMG_MB)
    def _(i):
        span = pl.ds(pl.multiple_of(i * PAD, PAD), PAD)
        middle = tok_s[span, :].astype(f32) + mid_s[span, :]
        mid_s[span, :] = middle
        pre, _, _ = norm(middle, gain_two, offset_two)
        n2_s[span, :] = pre.astype(bf16)

    out_copies[4].start()
    out_copies[3].start()
    router = router_rows(pick, place_ref, gate_ref.shape[0])
    logits = mm(router, n2_s[...], NT)
    expos = jnp.exp(logits - jnp.max(logits, 0, keepdims=True))
    gate_ref[...] = expos / jnp.sum(expos, 0, keepdims=True)
    for copy in out_copies:
        copy.wait()


def image(*tail):
    zeros = (0,) * len(tail)
    return pl.BlockSpec((1, *tail), lambda i, *_: (i, *zeros))


def forward_images(first, place, tokp, dense, experts):
    features = tokp.shape[2]
    count = IMG_MB
    flops = 2 * count * PAD * (4 * features * features + 2 * PAD * 256 * HEADS)
    shapes = (
        ((ROWS, 3 * features), bf16),
        ((count, HEADS, PAD, PAD), bf16),
        ((ROWS, features), bf16),
        ((ROWS, features), f32),
        ((ROWS, features), bf16),
    )
    scratch = [((ROWS, features), bf16), ((ROWS, features), bf16), *shapes]
    return pl.pallas_call(
        functools.partial(forward_kernel, first),
        grid_spec=pltpu.PrefetchScalarGridSpec(
            num_scalar_prefetch=1,
            grid=(1,),
            in_specs=[pl.BlockSpec(memory_space=pl.ANY)] * 3,
            out_specs=(*[pl.BlockSpec(memory_space=pl.ANY)] * 5, whole((experts, ROWS))),
            scratch_shapes=[
                pltpu.VMEM((4, *dense[0].shape[1:]), bf16),
                pltpu.SemaphoreType.DMA((4,)),
                pltpu.SemaphoreType.DMA((1,)),
                pltpu.SemaphoreType.DMA((5,)),
            ]
            + [pltpu.VMEM(*shape) for shape in scratch],
        ),
        out_shape=(
            *[jax.ShapeDtypeStruct(*shape) for shape in shapes],
            jax.ShapeDtypeStruct((experts, ROWS), f32),
        ),
        compiler_params=params(32),
        cost_estimate=cost(flops, count * 3_000_000),
        name="forward",
    )(place, tokp.reshape(MICRO, ROWS, features), *dense)


def gelu_pair(field):
    cdf = 0.5 * (1.0 + lax.erf(field * ROOT_HALF))
    return field * cdf, cdf + field * (jnp.exp(-0.5 * field * field) * INV_ROOT_TWO_PI)


def expert_kernel(index, own, part, place_ref, *refs):
    low, high = {"all": (0, 2 * MICRO), "own": (0, MICRO), "other": (MICRO, 2 * MICRO)}[part]
    blocks = high - low
    n2_refs = refs[:blocks]
    refs = refs[blocks:]
    cot_refs = refs[: blocks // MICRO]
    refs = refs[blocks // MICRO :]
    if low == 0:
        slot_ref, gate0_ref, gate1_ref = refs[:3]
        refs = refs[3:]
    if high > MICRO:
        other_ref = refs[0]
        refs = refs[1:]
    sources = 2 if own else 4
    w_refs = refs[:sources]
    refs = refs[sources:]
    if part == "other":
        keep_in_ref, send_in_ref = refs[:2]
        refs = refs[2:]
    res_ref, dx_ref, keep_ref, send_ref = refs[:4]
    refs = refs[4:]
    lines = {}
    for first in range(low, high, MICRO):
        lines[first] = refs[0]
        refs = refs[1:]
    w_s, sem, n2_s, cot_s, in_sem, x_s, g_s, raw_s, xt_s, gt_s, gs_s, r_acc, dx_acc, act_s, dh_s = refs
    step = pl.program_id(0)
    quarters, _, _, width = w_s.shape
    slots = x_s.shape[0] // blocks
    row = lax.broadcasted_iota(jnp.int32, (slots, ROWS), 0).astype(f32)

    def copies(j):
        if own:
            start = pl.multiple_of(place_ref[j] * width, width)
            return (
                pltpu.make_async_copy(w_refs[0].at[0, :, pl.ds(start, width)], w_s.at[j, 0], sem.at[2 * j]),
                pltpu.make_async_copy(w_refs[1].at[0, pl.ds(start, width), :], w_s.at[j, 1], sem.at[2 * j + 1]),
            )
        return (pltpu.make_async_copy(w_refs[j], w_s.at[j], sem.at[j]),)

    def slot_row(local):
        b = low + local
        if b < MICRO:
            return slot_ref[b, pl.ds(index, 1), :]
        return other_ref[b - MICRO, pl.ds(index + 4, 1), :]

    def gate_row(local):
        b = low + local
        if b < MICRO:
            return (gate0_ref, gate1_ref)[b][pl.ds(index, 1), :]
        return other_ref[b, pl.ds(index + 4, 1), :]

    def rows_in(b):
        return (
            pltpu.make_async_copy(n2_refs[b], n2_s.at[b], in_sem.at[2 * b]),
            pltpu.make_async_copy(cot_refs[b // MICRO].at[b % MICRO], cot_s.at[b], in_sem.at[2 * b + 1]),
        )

    @pl.when(step == 0)
    def _():
        for b in range(blocks):
            for copy in rows_in(b):
                copy.start()
        for j in range(quarters):
            for copy in copies(j):
                copy.start()
        r_acc[...] = jnp.zeros_like(r_acc)
        dx_acc[...] = jnp.zeros_like(dx_acc)
        for b in range(blocks):
            for copy in rows_in(b):
                copy.wait()
            span = pl.ds(b * slots, slots)
            hit = row == slot_row(b)
            pick = jnp.where(hit, 1.0, 0.0)
            gate = jnp.sum(jnp.where(hit, gate_row(b), 0.0), 1, keepdims=True)
            pick = pick.astype(bf16)
            x = mm(pick, n2_s[b])
            raw = mm(pick, cot_s[b])
            x_s[span, :] = x.astype(bf16)
            raw_s[span, :] = raw.astype(bf16)
            g = gate * raw
            g_s[span, :] = g.astype(bf16)
            gs_s[span, :] = jnp.broadcast_to(gate, (slots, 128))
        xt_s[...] = jnp.transpose(x_s[...])
        gt_s[...] = jnp.transpose(g_s[...])

    for j in range(quarters):

        @pl.when(step == j)
        def _():
            for copy in copies(j):
                copy.wait()

    w_in = w_s[step, 0]
    w_out = w_s[step, 1]
    rows = MICRO * slots
    for r in range(blocks // MICRO):
        span = pl.ds(r * rows, rows)
        act, slope = gelu_pair(mm(x_s[span, :], w_in))
        act = act.astype(bf16)
        dh = (mm(g_s[span, :], w_out, NT) * slope).astype(bf16)
        act_s[span, :] = act
        dh_s[span, :] = dh
        r_acc[span, :] += mm(act, w_out)
        dx_acc[span, :] += mm(dh, w_in, NT)
    grad_in = mm(xt_s[...], dh_s[...])
    grad_out = mm(gt_s[...], act_s[...])
    if part == "other":
        early = step < quarters // 2
        grad_in += jnp.where(early, keep_in_ref[0, 0].astype(f32), send_in_ref[0, 0].astype(f32))
        grad_out += jnp.where(early, keep_in_ref[0, 1].astype(f32), send_in_ref[0, 1].astype(f32))

    @pl.when(step < quarters // 2)
    def _():
        keep_ref[0, 0] = grad_in.astype(bf16)
        keep_ref[0, 1] = grad_out.astype(bf16)

    @pl.when(step >= quarters // 2)
    def _():
        send_ref[0, 0] = grad_in.astype(bf16)
        send_ref[0, 1] = grad_out.astype(bf16)

    @pl.when(step == quarters - 1)
    def _():
        dx_ref[...] = dx_acc[...].astype(bf16).reshape(dx_ref.shape)
        for b in range(blocks):
            span = pl.ds(b * slots, slots)
            res = r_acc[span, :].astype(bf16).astype(f32)
            dgate = jnp.sum(res * raw_s[span, :].astype(f32), 1, keepdims=True)
            res_ref[b] = (res * gs_s[span, 0:1]).astype(bf16)
            hit = row == slot_row(b)
            line = jnp.sum(jnp.where(hit, dgate, 0.0), 0, keepdims=True)
            lines[low + b - b % MICRO][pl.ds(b % MICRO, 1), :] = line


def expert_apply(index, place, n2, cot, tables, weights, slots, part="all", before=()):
    blocks = len(n2)
    features = n2[0].shape[1]
    own = len(weights) == 2
    quarters = 4
    width = weights[0].shape[2] // (4 if own else 1)
    rows = blocks * slots

    def fixed(shape):
        zeros = (0,) * len(shape)
        return pl.BlockSpec(shape, lambda *_: zeros)

    half = quarters // 2
    keep = pl.BlockSpec((1, 2, features, width), lambda i, _: (jnp.minimum(i, half - 1), 0, 0, 0))
    send = pl.BlockSpec((1, 2, features, width), lambda i, _: (jnp.maximum(i - half, 0), 0, 0, 0))
    groups = blocks // MICRO
    return pl.pallas_call(
        functools.partial(expert_kernel, index, own, part),
        grid_spec=pltpu.PrefetchScalarGridSpec(
            num_scalar_prefetch=1,
            grid=(quarters,),
            in_specs=[pl.BlockSpec(memory_space=pl.ANY)] * (blocks + len(cot))
            + [fixed(piece.shape) for piece in tables]
            + [pl.BlockSpec(memory_space=pl.ANY)] * len(weights)
            + [keep, send][: len(before)],
            out_specs=(
                fixed((blocks, slots, features)),
                fixed((blocks, slots, features)),
                keep,
                send,
                *[fixed((MICRO, ROWS))] * groups,
            ),
            scratch_shapes=[
                pltpu.VMEM((quarters, 2, features, width), bf16),
                pltpu.SemaphoreType.DMA((2 * quarters,)),
                pltpu.VMEM((blocks, ROWS, features), bf16),
                pltpu.VMEM((blocks, ROWS, features), bf16),
                pltpu.SemaphoreType.DMA((2 * blocks,)),
                pltpu.VMEM((rows, features), bf16),
                pltpu.VMEM((rows, features), bf16),
                pltpu.VMEM((rows, features), bf16),
                pltpu.VMEM((features, rows), bf16),
                pltpu.VMEM((features, rows), bf16),
                pltpu.VMEM((rows, 128), f32),
                pltpu.VMEM((rows, features), f32),
                pltpu.VMEM((rows, features), f32),
                pltpu.VMEM((rows, width), bf16),
                pltpu.VMEM((rows, width), bf16),
            ],
        ),
        out_shape=(
            pltpu.HBM((blocks, slots, features), bf16),
            pltpu.HBM((blocks, slots, features), bf16),
            pltpu.HBM((half, 2, features, width), bf16),
            pltpu.HBM((half, 2, features, width), bf16),
            *[jax.ShapeDtypeStruct((MICRO, ROWS), f32)] * groups,
        ),
        compiler_params=params(40),
        cost_estimate=cost(12 * rows * features * width * quarters, 4_000_000 + 3_000_000 * blocks),
        name="expert",
    )(place, *n2, *cot, *tables, *weights, *before)


def selector(columns, slots):
    count = columns.shape[1]
    lane = lax.broadcasted_iota(jnp.int32, (columns.shape[0], slots), 1).astype(f32)
    pieces = [jnp.where(columns[:, k : k + 1] == lane, 1.0, 0.0).astype(bf16) for k in range(count)]
    return jnp.concatenate(pieces, 1)


def combine_kernel(count, slot_ref, *refs):
    slots = refs[0].shape[1]
    pick = selector(wide_transpose(slot_ref[0, count:, :], -1.0)[:, :count], slots)
    refs[count][0] = mm(pick, jnp.concatenate([r[0] for r in refs[:count]], 0)).astype(bf16)


def combine(slot, pieces, block, blocks):
    count = len(pieces)
    _, slots, features = pieces[0].shape
    late = pl.BlockSpec((1, slots, features), lambda i: (i + block + MICRO, 0, 0))
    short = pl.BlockSpec((1, slots, features), lambda i: (i + block, 0, 0))
    return pl.pallas_call(
        functools.partial(combine_kernel, count),
        grid=(blocks,),
        in_specs=[pl.BlockSpec((1, 2 * count, ROWS), lambda i: (i + block, 0, 0))]
        + [late if piece.shape[0] > MICRO else short for piece in pieces],
        out_specs=image(ROWS, features),
        out_shape=jax.ShapeDtypeStruct((blocks, ROWS, features), bf16),
        compiler_params=params(24),
        cost_estimate=cost(2 * blocks * ROWS * features * slots * count, 5_000_000),
        name="combine",
    )(slot, *pieces)


def finish_kernel(count, mid0_ref, mid1_ref, part_ref, slotc_ref, dtok0_ref, dtok1_ref, *refs):
    out_ref, dout_ref, buf, dbuf = refs[count:]
    slots = refs[0].shape[1]
    step = pl.program_id(0)
    choose = selector(slotc_ref[0, :, :count], slots)
    mixed = mm(choose, jnp.concatenate([r[0] for r in refs[:count]], 0)) + part_ref[0].astype(f32)
    early = step < IMG_MB
    middle = jnp.where(early, mid0_ref[...], mid1_ref[...])
    value = middle + mixed
    grad = jnp.where(early, dtok0_ref[...].astype(f32), dtok1_ref[...].astype(f32))
    for i in range(IMAGES):

        @pl.when(step == i)
        def _():
            buf[pl.ds(i * SEQ, SEQ), :] = value[:SEQ]
            dbuf[pl.ds(i * SEQ, SEQ), :] = grad[:SEQ]

    @pl.when(step == IMAGES - 1)
    def _():
        out_ref[...] = buf[pl.ds(0, out_ref.shape[0]), :].astype(bf16)
        dout_ref[...] = dbuf[pl.ds(0, out_ref.shape[0]), :].astype(bf16)


def finish(middles, part, slotc, dtoks, results):
    count = len(results)
    _, slots, features = results[0].shape
    experts = slotc.shape[2]
    piece = pl.BlockSpec((1, slots, features), lambda i: (lax.div(i, IMG_MB), 0, 0))
    total = IMAGES * SEQ
    tall = 8 * ((total + 7) // 8)
    early = pl.BlockSpec((PAD, features), lambda i: (jnp.minimum(i, IMG_MB - 1), 0))
    later = pl.BlockSpec((PAD, features), lambda i: (jnp.maximum(i - IMG_MB, 0), 0))
    return pl.pallas_call(
        functools.partial(finish_kernel, count),
        grid=(IMAGES,),
        in_specs=[early, later, image(PAD, features), image(PAD, experts), early, later] + [piece] * count,
        out_specs=(whole((total, features)), whole((total, features))),
        out_shape=(jax.ShapeDtypeStruct((total, features), bf16),) * 2,
        scratch_shapes=[pltpu.VMEM((tall, features), f32)] * 2,
        compiler_params=params(24),
        cost_estimate=cost(4 * ROWS * features * slots * count, 15_000_000),
        name="finish",
    )(*middles, part, slotc, *dtoks, *results)


def norm_back(grad, normal, inverse, gain):
    scaled = grad * gain
    return inverse * (
        scaled
        - jnp.mean(scaled, -1, keepdims=True)
        - normal * jnp.mean(scaled * normal, -1, keepdims=True)
    )


def backward_kernel(first, count, place_ref, gate_ref, slotc_ref, dgo_ref, *refs):
    dg_refs = refs[:count]
    sources = refs[count : count + 8]
    refs = refs[count + 8 :]
    two_ref, more_ref = refs[:2]
    dx_refs = refs[2 : 2 + count]
    refs = refs[2 + count :]
    chained = first > 0
    if chained:
        before_ref, before_row_ref = refs[:2]
        dtok_ref, keep_ref, send_ref = refs[2:5]
        acc_s, acc_sem, row_ref = refs[5:8]
        refs = refs[8:]
    else:
        dtok_ref, acc_ref, row_ref = refs[:3]
        acc_s, acc_sem = refs[3:5]
        refs = refs[5:]
    w_s, sem, in_sem, dx_sem = refs[:4]
    tok_s, cot_s, proj_s, prob_s, att_s, mid_s, n2_s, dn2_s = stores = refs[4:12]
    dx_s, dbr_s, datt_s, dproj_s, n1_s, sum_s = refs[12:]
    micro = first // IMG_MB
    features = tok_s.shape[1]
    experts = 2 * count
    slots = dx_s.shape[0] // count
    copies = []
    for i, (src, dst) in enumerate(zip(sources, stores)):
        copies.append(pltpu.make_async_copy(src.at[micro] if i < 2 else src, dst, in_sem.at[i]))
    tok_in, cot_in, proj_in, prob_in, att_in, mid_in, n2_in, dn2_in = copies
    dx_in = [
        pltpu.make_async_copy(dx_refs[k].at[micro], dx_s.at[pl.ds(k * slots, slots), :], dx_sem.at[k])
        for k in range(count)
    ]
    for copy in (*dx_in, dn2_in, n2_in):
        copy.start()
    dense_in = load_dense(place_ref, two_ref, more_ref, w_s, sem)
    for copy in (mid_in, cot_in, att_in, proj_in, prob_in, tok_in):
        copy.start()
    if chained:
        acc_in = pltpu.make_async_copy(before_ref, acc_s, acc_sem.at[0])
        acc_in.start()
        row_ref[...] = before_row_ref[...]
    else:
        row_ref[...] = jnp.zeros_like(row_ref)
    choose = selector(slotc_ref[0, :, :count], slots)
    gates = gate_ref[...]
    dgates = [ref[pl.ds(micro, 1), :] for ref in dg_refs] + [dgo_ref[k, pl.ds(micro, 1), :] for k in range(count)]
    dgates = jnp.concatenate(dgates, 0)
    dlogits = (gates * (dgates - jnp.sum(gates * dgates, 0, keepdims=True))).astype(bf16)
    for copy in (*dx_in, dn2_in, n2_in, *dense_in):
        copy.wait()
    pick = vectors(w_s)
    qkv, out = dense_weights(w_s, features)
    router = router_rows(pick, place_ref, experts)
    row_ref[8 : 8 + experts, :] += mm(dlogits, n2_s[...])
    sum_s[...] = mm(choose, dx_s[...]) + mm(dlogits, router, TN)
    mid_in.wait()
    cot_in.wait()
    gain_two = pick(2).astype(f32)

    @pl.loop(0, IMG_MB)
    def _(i):
        span = pl.ds(pl.multiple_of(i * PAD, PAD), PAD)
        dn2 = sum_s[span, :] + dn2_s[span, :].astype(f32)
        _, normal_two, inverse_two = norm(mid_s[span, :], gain_two, 0.0)
        row_ref[2:3, :] += jnp.sum(dn2 * normal_two, 0, keepdims=True)
        row_ref[3:4, :] += jnp.sum(dn2, 0, keepdims=True)
        dmiddle = cot_s[span, :].astype(f32) + norm_back(dn2, normal_two, inverse_two, gain_two)
        mid_s[span, :] = dmiddle
        dbr_s[span, :] = dmiddle.astype(bf16)

    att_in.wait()
    if chained:
        acc_in.wait()
    grad_out = mm(att_s[...], dbr_s[...], TN)
    if chained:
        acc_s[:, 3 * features :] += grad_out
    else:
        acc_s[:, 3 * features :] = grad_out
    datt_s[...] = mm(dbr_s[...], out, NT).astype(bf16)
    proj_in.wait()
    prob_in.wait()
    tok_in.wait()
    pair = 2 * HEAD_DIM
    gain_one, offset_one = pick(0).astype(f32), pick(1).astype(f32)

    @pl.loop(0, IMG_MB)
    def _(i):
        span = pl.ds(pl.multiple_of(i * PAD, PAD), PAD)
        pre, _, _ = norm(tok_s[span, :].astype(f32), gain_one, offset_one)
        n1_s[span, :] = pre.astype(bf16)
        for group in range(HEADS // 2):
            at = [part * features + group * pair for part in range(3)]
            q2, k2, v2 = (proj_s[span, start : start + pair] for start in at)
            d2 = datt_s[span, group * pair : (group + 1) * pair]
            dq = dk = dv = None
            for half in range(2):
                probs = prob_s[i, 2 * group + half]
                wide = probs.astype(f32)
                dm = d2 * half_mask(half, 1.0)
                dweights = mm(dm, v2, NT)
                inner = jnp.sum(dweights * wide, -1, keepdims=True)
                dscores = (wide * (dweights - inner)).astype(bf16)
                part_q = mm(dscores, k2 * half_mask(half, SCALING))
                part_k = mm(dscores, q2 * half_mask(half, SCALING), TN)
                part_v = mm(probs, dm, TN)
                dq = part_q if dq is None else dq + part_q
                dk = part_k if dk is None else dk + part_k
                dv = part_v if dv is None else dv + part_v
            for start, value in zip(at, (dq, dk, dv)):
                dproj_s[span, start : start + pair] = value.astype(bf16)

    grad_qkv = mm(n1_s[...], dproj_s[...], TN)
    if chained:
        acc_s[:, : 3 * features] += grad_qkv
    else:
        acc_s[:, : 3 * features] = grad_qkv
        acc_out = pltpu.make_async_copy(acc_s, acc_ref, acc_sem.at[0])
        acc_out.start()
    sum_s[...] = mm(dproj_s[...], qkv, NT)

    @pl.loop(0, IMG_MB)
    def _(i):
        span = pl.ds(pl.multiple_of(i * PAD, PAD), PAD)
        dnormed = sum_s[span, :]
        _, normal_one, inverse_one = norm(tok_s[span, :].astype(f32), gain_one, offset_one)
        row_ref[0:1, :] += jnp.sum(dnormed * normal_one, 0, keepdims=True)
        row_ref[1:2, :] += jnp.sum(dnormed, 0, keepdims=True)
        dtok_ref[span, :] = (mid_s[span, :] + norm_back(dnormed, normal_one, inverse_one, gain_one)).astype(bf16)

    if not chained:
        acc_out.wait()
        return
    width = keep_ref.shape[1] - 16
    lines = [row_ref[i : i + 1, :] for i in range(4)]
    for e in range(experts):
        line = jnp.zeros((1, features), f32)
        for r in range(experts):
            line = jnp.where(expert_of(place_ref, r) == e, row_ref[8 + r : 9 + r, :], line)
        lines.append(line)
    blank = jnp.zeros((1, 4 * features - (4 + experts) * width), f32)
    tails = []
    for q in range(4):
        parts = [line[:, q * width : (q + 1) * width] for line in lines]
        tails.append(jnp.concatenate(parts + [blank], 1))
    for j in range(4):
        quarter = place_ref[j]
        to = (keep_ref, send_ref)[j // 2]
        to[j % 2, :width, :] = acc_s[pl.ds(pl.multiple_of(quarter * width, width), width), :].astype(bf16)
        tail = tails[0]
        for q in range(1, 4):
            tail = jnp.where(quarter == q, tails[q], tail)
        tail = jnp.concatenate([tail, jnp.zeros((15, tail.shape[1]), f32)], 0)
        to[j % 2, width:, :] = tail.astype(bf16)


def backward_images(first, place, tokp, cotp, saved, dgs, dg_other, slotc, dn2_part, dense, dxs, before):
    projected, probs, attended, middle, n2, gates = saved
    count = len(dxs)
    features = tokp.shape[2]
    experts = 2 * count
    slots = dxs[0].shape[1]
    totals = ((features, 4 * features), (8 + experts, features))
    packed = (2, *dense[0].shape[1:])
    anywhere = pl.BlockSpec(memory_space=pl.ANY)
    flat = (MICRO, ROWS, features)
    sources = (tokp.reshape(flat), cotp.reshape(flat), projected, probs, attended, middle, n2, dn2_part)
    out_specs = [whole((ROWS, features))]
    out_shape = [jax.ShapeDtypeStruct((ROWS, features), bf16)]
    scratch = [pltpu.VMEM(totals[0], f32), pltpu.SemaphoreType.DMA((1,))]
    if before:
        out_specs += [whole(packed)] * 2
        out_shape += [jax.ShapeDtypeStruct(packed, bf16)] * 2
        scratch.append(pltpu.VMEM(totals[1], f32))
        extra = [anywhere, whole(totals[1])]
    else:
        out_specs += [anywhere, whole(totals[1])]
        out_shape += [jax.ShapeDtypeStruct(shape, f32) for shape in totals]
        extra = []
    scratch += [
        pltpu.VMEM((4, *dense[0].shape[1:]), bf16),
        pltpu.SemaphoreType.DMA((4,)),
        pltpu.SemaphoreType.DMA((8,)),
        pltpu.SemaphoreType.DMA((count,)),
    ]
    scratch += [pltpu.VMEM((ROWS, features), bf16)] * 2
    scratch += [pltpu.VMEM(piece.shape, piece.dtype) for piece in sources[2:]]
    scratch += [
        pltpu.VMEM((count * slots, features), bf16),
        pltpu.VMEM((ROWS, features), bf16),
        pltpu.VMEM((ROWS, features), bf16),
        pltpu.VMEM((ROWS, 3 * features), bf16),
        pltpu.VMEM((ROWS, features), bf16),
        pltpu.VMEM((ROWS, features), f32),
    ]
    micro = first // IMG_MB
    return pl.pallas_call(
        functools.partial(backward_kernel, first, count),
        grid_spec=pltpu.PrefetchScalarGridSpec(
            num_scalar_prefetch=1,
            grid=(1,),
            in_specs=[
                whole(gates.shape),
                pl.BlockSpec((1, ROWS, experts), lambda i, _: (micro, 0, 0)),
                whole(dg_other.shape),
            ]
            + [whole(piece.shape) for piece in dgs]
            + [anywhere] * (10 + count)
            + extra,
            out_specs=tuple(out_specs),
            scratch_shapes=scratch,
        ),
        out_shape=tuple(out_shape),
        compiler_params=params(40),
        cost_estimate=cost(40 * ROWS * features * features, 15_000_000),
        name="backward",
    )(place, gates, slotc, dg_other, *dgs, *sources, *dense, *dxs, *before)


def settle_kernel(place_ref, far_ref, *refs):
    in_ref, back_ref = refs[-2:]
    z = place_ref[Z_AT]
    outer = jnp.where((z == 0) | (z == 3), 1.0, 0.0)

    def total(i):
        value = far_ref[i].astype(f32) * outer + refs[i - 4][...].astype(f32)
        for ref in refs[:-4]:
            piece = ref[0, i] if len(ref.shape) == 4 else ref[i]
            value = value + piece.astype(f32)
        return value

    in_ref[0] = total(0)
    back_ref[0] = jnp.transpose(total(1))


def settle(place, *pieces):
    features, span = pieces[-1].shape

    def spec(piece):
        shape = (1, *piece.shape[1:]) if len(piece.shape) == 4 else piece.shape
        return whole(shape)

    return pl.pallas_call(
        settle_kernel,
        grid_spec=pltpu.PrefetchScalarGridSpec(
            num_scalar_prefetch=1,
            grid=(1,),
            in_specs=[spec(piece) for piece in pieces],
            out_specs=(whole((1, features, span)), whole((1, span, features))),
        ),
        out_shape=(
            jax.ShapeDtypeStruct((1, features, span), f32),
            jax.ShapeDtypeStruct((1, span, features), f32),
        ),
        compiler_params=params(24),
        cost_estimate=cost(0, 5_000_000),
        name="settle",
    )(place, *pieces)


def unpack_kernel(part_ref, qkv_ref, out_ref, router_ref, g1_ref, b1_ref, g2_ref, b2_ref):
    width, columns = qkv_ref.shape
    pieces, _, lanes = part_ref.shape
    for i in range(pieces):
        value = part_ref[i, :width, :].astype(f32)
        at = i * lanes
        if at < columns:
            qkv_ref[:, at : at + lanes] = value
        else:
            out_ref[:, at - columns : at - columns + lanes] = value
    row = jnp.concatenate([part_ref[i, width:, :].astype(f32)[0:1] for i in range(pieces)], 1)
    for i, ref in enumerate((g1_ref, b1_ref, g2_ref, b2_ref)):
        ref[...] = row[:, i * width : (i + 1) * width]
    lines = [row[:, (4 + e) * width : (5 + e) * width] for e in range(router_ref.shape[0])]
    router_ref[...] = jnp.concatenate(lines, 0)


def unpack(part, columns, experts):
    pieces, height, lanes = part.shape
    width = height - 16
    line = (1, width)
    shapes = ((width, columns), (width, pieces * lanes - columns), (experts, width), line, line, line, line)
    return pl.pallas_call(
        unpack_kernel,
        grid=(1,),
        in_specs=[whole(part.shape)],
        out_specs=tuple(whole(shape) for shape in shapes),
        out_shape=tuple(jax.ShapeDtypeStruct(shape, f32) for shape in shapes),
        compiler_params=params(24),
        cost_estimate=cost(0, 3_000_000),
        name="unpack",
    )(part)


def norm_forward(values, gain, offset):
    center = values - jnp.mean(values, -1, keepdims=True)
    inverse = lax.rsqrt(jnp.mean(center * center, -1, keepdims=True) + EPSILON)
    normal = center * inverse
    return (normal * gain + offset, normal, inverse)


def norm_backward(grad, normal, inverse, gain):
    scaled = grad * gain
    return inverse * (
        scaled
        - jnp.mean(scaled, -1, keepdims=True)
        - normal * jnp.mean(scaled * normal, -1, keepdims=True)
    )


def gelu_value(field):
    return 0.5 * field * (1.0 + lax.erf(field * ROOT_HALF))


def gelu_slope(field):
    return (
        0.5 * (1.0 + lax.erf(field * ROOT_HALF))
        + field * jnp.exp(-0.5 * field * field) * INV_ROOT_TWO_PI
    )


def block_ranks(route_rows, order_keys, capacity):
    count = order_keys.shape[0]
    expert_count = capacity.shape[0]
    chosen = jnp.concatenate([route_rows[:, 0], route_rows[:, 1]])
    sort_keys = jnp.concatenate([order_keys, order_keys + count])
    positions = jnp.arange(2 * count, dtype=jnp.int32)
    inverse = jnp.zeros((2 * count,), jnp.int32).at[sort_keys].set(positions)
    ordered = chosen[inverse]
    labels = jnp.arange(expert_count, dtype=jnp.int32)
    onehot = (ordered[:, None] == labels[None, :]).astype(jnp.int32)
    before = jnp.cumsum(onehot, 0) - onehot
    rank_sorted = jnp.sum(before * onehot, 1)
    ranking = jnp.zeros((2 * count,), jnp.int32).at[inverse].set(rank_sorted)
    pair_onehot = chosen[:, None] == labels[None, :]
    limit = jnp.sum(pair_onehot.astype(jnp.int32) * capacity[None, :], 1)
    return (chosen, ranking, ranking < limit, pair_onehot.astype(jnp.float32))


def exchanged(
    tokens,
    ln1_gain,
    ln1_bias,
    qkv_weight,
    out_weight,
    ln2_gain,
    ln2_bias,
    router_weight,
    expert_in,
    expert_out,
    routes,
    priority,
    capacity,
    cotangent,
):
    f32 = jnp.float32
    bf16 = jnp.bfloat16
    gathered = (
        lax.all_gather(ln1_gain, "dp", axis=0, tiled=True),
        lax.all_gather(ln1_bias, "dp", axis=0, tiled=True),
        lax.all_gather(qkv_weight, "dp", axis=0, tiled=True),
        lax.all_gather(out_weight, "dp", axis=0, tiled=True),
        lax.all_gather(ln2_gain, "dp", axis=0, tiled=True),
        lax.all_gather(ln2_bias, "dp", axis=0, tiled=True),
        lax.all_gather(router_weight, "dp", axis=0, tiled=True),
    )
    gain_one = gathered[0].astype(f32)
    offset_one = gathered[1].astype(f32)
    weight_qkv = gathered[2]
    weight_out = gathered[3]
    gain_two = gathered[4].astype(f32)
    offset_two = gathered[5].astype(f32)
    weight_router = gathered[6]
    features = tokens.shape[1]
    owners = lax.axis_size("expert")
    per_owner = expert_in.shape[0]
    experts = owners * per_owner
    slots = 8 * (3 * TOP * IMG_MB * SEQ // (16 * experts) + 1)
    row_count = IMG_MB * SEQ
    sum_gain_one = jnp.zeros((features,), f32)
    sum_offset_one = jnp.zeros((features,), f32)
    sum_qkv = jnp.zeros(weight_qkv.shape, f32)
    sum_out = jnp.zeros(weight_out.shape, f32)
    sum_gain_two = jnp.zeros((features,), f32)
    sum_offset_two = jnp.zeros((features,), f32)
    sum_router = jnp.zeros(weight_router.shape, f32)
    sum_expert_in = jnp.zeros(expert_in.shape, f32)
    sum_expert_out = jnp.zeros(expert_out.shape, f32)
    outputs = []
    input_grads = []
    for micro in range(MICRO):
        start = micro * row_count
        inputs = tokens[start : start + row_count].astype(f32)
        pre_one, normal_one, inverse_one = norm_forward(inputs, gain_one, offset_one)
        normed = pre_one.astype(bf16)
        projected = jnp.dot(normed, weight_qkv, preferred_element_type=f32).astype(bf16)
        projected = projected.reshape(IMG_MB, SEQ, 3, HEADS, HEAD_DIM)
        queries = projected[:, :, 0]
        key_rows = projected[:, :, 1]
        values = projected[:, :, 2]
        scores = (
            jnp.einsum("gqhd,gkhd->ghqk", queries, key_rows, preferred_element_type=f32) * SCALING
        )
        highest = jnp.max(scores, -1, keepdims=True)
        expos = jnp.exp(scores - highest)
        totals = jnp.sum(expos, -1, keepdims=True)
        log_total = highest + jnp.log(totals)
        attn_weights = (expos / totals).astype(bf16)
        attended = jnp.einsum(
            "ghqk,gkhd->gqhd", attn_weights, values, preferred_element_type=f32
        ).astype(bf16)
        attended = attended.reshape(row_count, features)
        middle = inputs + jnp.dot(attended, weight_out, preferred_element_type=f32)
        pre_two, normal_two, inverse_two = norm_forward(middle, gain_two, offset_two)
        normed_two = pre_two.astype(bf16)
        logits = jnp.dot(normed_two, weight_router, preferred_element_type=f32)
        gates = jax.nn.softmax(logits, -1)
        route_rows = routes[start : start + row_count]
        chosen, ranking, kept, pair_onehot = block_ranks(
            route_rows, priority[start : start + row_count], capacity
        )
        keep_float = kept.astype(f32)
        slot_send = jnp.where(kept, ranking, slots)
        slot_read = jnp.where(kept, ranking, 0)
        doubled = jnp.concatenate([normed_two, normed_two], 0)
        send = (
            jnp.zeros((experts, slots, features), bf16)
            .at[chosen, slot_send]
            .set(doubled, mode="drop")
        )
        received = lax.all_to_all(
            send.reshape(owners, per_owner, slots, features),
            "expert",
            split_axis=0,
            concat_axis=0,
            tiled=True,
        )
        hidden = jnp.einsum("sjcd,jdf->sjcf", received, expert_in, preferred_element_type=f32)
        active = gelu_value(hidden).astype(bf16)
        result = jnp.einsum(
            "sjcf,jfd->sjcd", active, expert_out, preferred_element_type=f32
        ).astype(bf16)
        back = lax.all_to_all(result, "expert", split_axis=0, concat_axis=0, tiled=True).reshape(
            experts, slots, features
        )
        pieces = back[chosen, slot_read].astype(f32) * keep_float[:, None]
        picked = jnp.take_along_axis(gates, route_rows, 1)
        gate_pair = jnp.concatenate([picked[:, 0], picked[:, 1]])
        mixed = pieces[:row_count] * picked[:, 0:1] + pieces[row_count:] * picked[:, 1:2]
        outputs.append((middle + mixed).astype(bf16))
        grad_out = cotangent[start : start + row_count].astype(f32)
        grad_doubled = jnp.concatenate([grad_out, grad_out], 0)
        dgate = jnp.sum(grad_doubled * pieces, -1)
        dpieces = (grad_doubled * (gate_pair * keep_float)[:, None]).astype(bf16)
        dgates = (
            pair_onehot[:row_count] * dgate[:row_count, None]
            + pair_onehot[row_count:] * dgate[row_count:, None]
        )
        dlogits = (gates * (dgates - jnp.sum(gates * dgates, -1, keepdims=True))).astype(bf16)
        grad_send = (
            jnp.zeros((experts, slots, features), bf16)
            .at[chosen, slot_send]
            .set(dpieces, mode="drop")
        )
        grad_received = lax.all_to_all(
            grad_send.reshape(owners, per_owner, slots, features),
            "expert",
            split_axis=0,
            concat_axis=0,
            tiled=True,
        )
        dactive = jnp.einsum(
            "sjcd,jfd->sjcf", grad_received, expert_out, preferred_element_type=f32
        )
        dhidden = (dactive * gelu_slope(hidden)).astype(bf16)
        grad_w_out = jnp.einsum("sjcf,sjcd->jfd", active, grad_received, preferred_element_type=f32)
        grad_w_in = jnp.einsum("sjcd,sjcf->jdf", received, dhidden, preferred_element_type=f32)
        sum_expert_in = sum_expert_in + grad_w_in
        sum_expert_out = sum_expert_out + grad_w_out
        dsent = jnp.einsum("sjcf,jdf->sjcd", dhidden, expert_in, preferred_element_type=f32).astype(
            bf16
        )
        dreturn = lax.all_to_all(dsent, "expert", split_axis=0, concat_axis=0, tiled=True).reshape(
            experts, slots, features
        )
        dpair = dreturn[chosen, slot_read].astype(f32) * keep_float[:, None]
        dnormed_two = (
            jnp.dot(dlogits, weight_router.T, preferred_element_type=f32)
            + dpair[:row_count]
            + dpair[row_count:]
        )
        sum_router = sum_router + jnp.dot(normed_two.T, dlogits, preferred_element_type=f32)
        sum_gain_two = sum_gain_two + jnp.sum(dnormed_two * normal_two, 0)
        sum_offset_two = sum_offset_two + jnp.sum(dnormed_two, 0)
        dmiddle = grad_out + norm_backward(dnormed_two, normal_two, inverse_two, gain_two)
        dbranch = dmiddle.astype(bf16)
        sum_out = sum_out + jnp.dot(attended.T, dbranch, preferred_element_type=f32)
        dattended = jnp.dot(dbranch, weight_out.T, preferred_element_type=f32).astype(bf16)
        dattended = dattended.reshape(IMG_MB, SEQ, HEADS, HEAD_DIM)
        again = (
            jnp.einsum("gqhd,gkhd->ghqk", queries, key_rows, preferred_element_type=f32) * SCALING
        )
        probs_again = jnp.exp(again - log_total)
        dvalues = jnp.einsum(
            "ghqk,gqhd->gkhd", probs_again.astype(bf16), dattended, preferred_element_type=f32
        )
        dweights = jnp.einsum("gqhd,gkhd->ghqk", dattended, values, preferred_element_type=f32)
        inner = jnp.sum(dweights * probs_again, -1, keepdims=True)
        dscores = (probs_again * (dweights - inner)).astype(bf16)
        dqueries = (
            jnp.einsum("ghqk,gkhd->gqhd", dscores, key_rows, preferred_element_type=f32) * SCALING
        )
        dkeys = (
            jnp.einsum("ghqk,gqhd->gkhd", dscores, queries, preferred_element_type=f32) * SCALING
        )
        dprojected = (
            jnp.stack([dqueries, dkeys, dvalues], 2).astype(bf16).reshape(row_count, 3 * features)
        )
        sum_qkv = sum_qkv + jnp.dot(normed.T, dprojected, preferred_element_type=f32)
        dnormed = jnp.dot(dprojected, weight_qkv.T, preferred_element_type=f32)
        sum_gain_one = sum_gain_one + jnp.sum(dnormed * normal_one, 0)
        sum_offset_one = sum_offset_one + jnp.sum(dnormed, 0)
        input_grads.append(
            (dmiddle + norm_backward(dnormed, normal_one, inverse_one, gain_one)).astype(bf16)
        )
    grad_expert_in, grad_expert_out = (
        lax.psum_scatter(
            sum_expert_in.astype(jnp.bfloat16), "dp", scatter_dimension=2, tiled=True
        ).astype(jnp.float32),
        lax.psum_scatter(
            sum_expert_out.astype(jnp.bfloat16), "dp", scatter_dimension=1, tiled=True
        ).astype(jnp.float32),
    )
    dense = (
        sum_gain_one,
        sum_offset_one,
        sum_qkv,
        sum_out,
        sum_gain_two,
        sum_offset_two,
        sum_router,
    )
    totals_all = (
        lax.psum(dense[0].astype(jnp.bfloat16), "expert").astype(jnp.float32),
        lax.psum(dense[1].astype(jnp.bfloat16), "expert").astype(jnp.float32),
        lax.psum(dense[2].astype(jnp.bfloat16), "expert").astype(jnp.float32),
        lax.psum(dense[3].astype(jnp.bfloat16), "expert").astype(jnp.float32),
        lax.psum(dense[4].astype(jnp.bfloat16), "expert").astype(jnp.float32),
        lax.psum(dense[5].astype(jnp.bfloat16), "expert").astype(jnp.float32),
        lax.psum(dense[6].astype(jnp.bfloat16), "expert").astype(jnp.float32),
    )
    owned = (
        lax.psum_scatter(
            totals_all[0].astype(jnp.bfloat16), "dp", scatter_dimension=0, tiled=True
        ).astype(jnp.float32),
        lax.psum_scatter(
            totals_all[1].astype(jnp.bfloat16), "dp", scatter_dimension=0, tiled=True
        ).astype(jnp.float32),
        lax.psum_scatter(
            totals_all[2].astype(jnp.bfloat16), "dp", scatter_dimension=0, tiled=True
        ).astype(jnp.float32),
        lax.psum_scatter(
            totals_all[3].astype(jnp.bfloat16), "dp", scatter_dimension=0, tiled=True
        ).astype(jnp.float32),
        lax.psum_scatter(
            totals_all[4].astype(jnp.bfloat16), "dp", scatter_dimension=0, tiled=True
        ).astype(jnp.float32),
        lax.psum_scatter(
            totals_all[5].astype(jnp.bfloat16), "dp", scatter_dimension=0, tiled=True
        ).astype(jnp.float32),
        lax.psum_scatter(
            totals_all[6].astype(jnp.bfloat16), "dp", scatter_dimension=0, tiled=True
        ).astype(jnp.float32),
    )
    block_out = jnp.concatenate(outputs, 0)
    grad_tokens = jnp.concatenate(input_grads, 0)
    return (
        block_out,
        grad_tokens,
        owned[0],
        owned[1],
        owned[2],
        owned[3],
        owned[4],
        owned[5],
        owned[6],
        grad_expert_in,
        grad_expert_out,
    )


SWAP = [(0, 1), (1, 0)]
OUTWARD = [(1, 0), (2, 3)]
SECOND = [(0, 1), (3, 2), (1, 3), (2, 0)]
MIDDLE = [(1, 2), (2, 1)]


def flip(bit):
    return [(i, i ^ bit) for i in range(4)]


def add(*pieces):
    total = pieces[0].astype(f32)
    for piece in pieces[1:]:
        total = total + piece.astype(f32)
    return total.astype(bf16)


def stage(*values):
    return lax.optimization_barrier(values)


def after(value, *others):
    return lax.optimization_barrier((value, *others))[0]


def paired(
    tokens,
    ln1_gain,
    ln1_bias,
    qkv_weight,
    out_weight,
    ln2_gain,
    ln2_bias,
    router_weight,
    expert_in,
    expert_out,
    routes,
    priority,
    capacity,
    cotangent,
):
    y, core, z, x = (lax.axis_index(name) for name in ("y", "core", "z", "x"))
    features = tokens.shape[1]
    experts = capacity.shape[0]
    width = qkv_weight.shape[0]
    count = experts // 2
    slots = 8 * (3 * TOP * IMG_MB * SEQ // (16 * experts) + 1)
    lanes = 4 * features

    order = jnp.arange(8, dtype=jnp.int32)
    place = (((order & 1) ^ y) << 1) | (((order >> 1) & 1) ^ core)
    for at, value in ((Z_AT, z), (X_AT, x), (Y_AT, y), (CORE_AT, core)):
        place = jnp.where(order == at, value, place)

    def swap(value, axis, pairs=SWAP):
        return lax.ppermute(value, axis, pairs)

    gains = (ln1_gain, ln1_bias, ln2_gain, ln2_bias)
    packed = pack(gains, qkv_weight, out_weight, router_weight.T)
    from_y = swap(packed, "y")
    one = quarter_of(after(place, packed), expert_in, expert_out)
    near = swap(one, "z", flip(1))
    centre = swap(one, "z", MIDDLE)
    cotp = pad_images(after(cotangent, one))
    cot_other = swap(cotp, "x")
    place, cotp = stage(place, cotp)
    tokp, slot, slotc = prepare(place, capacity, tokens, routes, priority)
    place, from_y, tokp, slot = stage(place, from_y, tokp, slot)
    two = jnp.concatenate([packed, from_y], 0)
    dense = (two, swap(two, "core"))

    place, near, centre = stage(place, near, centre)
    second_mid = swap(near, "z", MIDDLE)
    second_out = swap(centre, "z", OUTWARD)
    across = [swap(near, "y")]
    saved = [forward_images(0, place, tokp, dense, experts)]
    place, cot_other, first_n2 = stage(place, cot_other, saved[0][4])
    n2_other = [swap(first_n2, "x")]
    saved.append(forward_images(IMG_MB, place, tokp, dense, experts))
    place, last_n2, last_gates, second_mid, second_out, across[0], n2_other[0] = stage(
        place, saved[1][4], saved[1][5], second_mid, second_out, across[0], n2_other[0]
    )
    n2_other.append(swap(last_n2, "x"))
    tables = jnp.concatenate([slot, saved[0][5][None], last_gates[None]], 0)
    other = swap(tables, "x")
    second = second_mid + second_out
    outer = swap(second, "z", OUTWARD)
    across.append(swap(second, "y"))
    corner = [swap(piece, "core") for piece in (near, across[0])]

    n2 = [piece[4] for piece in saved] + n2_other
    cot = [piece.reshape(MICRO, ROWS, features) for piece in (cotp, cot_other)]
    tables = (slot, saved[0][5], saved[1][5], other)
    place, *corner = stage(place, *corner)
    pieces = (near, across[0], *corner)
    half1 = expert_apply(1, place, n2[:MICRO], cot[:1], tables[:3], pieces, slots, "own")
    place, *half1 = stage(place, *half1)
    out1 = expert_apply(1, place, n2[MICRO:], cot[1:], tables[3:], pieces, slots, "other", half1[2:4])
    place, outer, across[1], *out1 = stage(place, outer, across[1], *out1)
    third = centre + outer
    across.append(swap(third, "y"))
    corner = [swap(piece, "core") for piece in (second, across[1])]
    core1 = swap(out1[3], "core")
    place, *corner = stage(place, *corner)
    pieces = (second, across[1], *corner)
    out2 = expert_apply(2, place, n2, cot, tables, pieces, slots)
    place, across[2], core1, *out2 = stage(place, across[2], core1, *out2)
    corner = [swap(piece, "core") for piece in (third, across[2])]
    core2 = swap(out2[3], "core")
    side1 = swap(add(out1[2][1], core1[1]), "y")
    place, *corner = stage(place, *corner)
    pieces = (third, across[2], *corner)
    out3 = expert_apply(3, place, n2, cot, tables, pieces, slots)
    place, core2, side1, *out3 = stage(place, core2, side1, *out3)
    core3 = swap(out3[3], "core")
    side2 = swap(add(out2[2][1], core2[1]), "y")
    first_swap = swap(add(out1[2][0], core1[0], side1), "z", flip(1))
    out0 = expert_apply(0, place, n2, cot, tables, (expert_in, expert_out), slots)
    place, core3, side2, first_swap, *out0 = stage(place, core3, side2, first_swap, *out0)

    outs = (out0, half1, out2, out3)
    results, dxs, _, _, dgs = ([piece[i] for piece in outs] for i in range(5))
    outs = (out0, out1, out2, out3)
    other_results, other_dxs, _, _ = ([piece[i] for piece in outs] for i in range(4))
    dgos = [piece[-1] for piece in outs]
    dn2_mine = [combine(other, other_dxs, 0, 1)]
    rest, core_send, dn2_send, *dgos = stage(other, out0[3], dn2_mine[0], *dgos)
    dn2 = [swap(dn2_send, "x")]
    dg_other = swap(jnp.stack(dgos), "x")
    side3 = swap(add(out3[2][1], core3[1]), "y")
    second_swap = swap(add(out2[2][0], core2[0], side2), "z", SECOND)
    core0 = swap(core_send, "core")
    dn2_mine.append(combine(rest, other_dxs, 1, 1))
    mixed_mine = combine(after(rest, dn2_mine[1]), other_results, 0, MICRO)
    place, mixed_mine, core0, dn2[0], last, dg_other = stage(
        place, mixed_mine, core0, dn2[0], dn2_mine[1], dg_other
    )
    dn2.append(swap(last, "x"))

    columns = slotc.reshape(IMAGES, PAD, experts)

    def back_images(micro, place, before):
        rows = dn2[micro].reshape(ROWS, features)
        return backward_images(
            micro * IMG_MB, place, tokp, cotp, saved[micro], dgs, dg_other, slotc, rows, dense, dxs, before
        )

    first = back_images(0, place, ())
    place, second_swap, side3, dn2[1], *first = stage(place, second_swap, side3, dn2[1], *first)
    inner = (z == 1) | (z == 2)
    third_sum = add(out3[2][0], core3[0], side3, jnp.where(inner, second_swap, 0.0))
    third_swap = [swap(third_sum[0], "z", flip(3))]
    side0 = swap(add(out0[2][1], core0[1]), "y")
    mixed = swap(mixed_mine, "x")
    keep_send = back_images(1, place, tuple(first[1:]))
    place, third_swap[0], side0, mixed, *keep_send = stage(place, third_swap[0], side0, mixed, *keep_send)
    third_swap.append(swap(third_sum[1], "z", flip(3)))
    mixed = mixed.reshape(IMAGES, PAD, features)
    dtok = [first[0], keep_send[0]]
    keep, send = keep_send[1:]

    from_near = swap(send, "core")
    part = swap(add(keep[1], from_near[1]), "y")
    block_out, grad_tokens = finish([piece[3] for piece in saved], mixed, columns, dtok, results)
    part, third_swap[1], block_out, grad_tokens = stage(part, third_swap[1], block_out, grad_tokens)
    part = add(keep[0], from_near[0], part)
    cut = part.reshape(width + 16, 8, lanes // 8).transpose(1, 0, 2)
    cut = lax.all_to_all(cut, ("z", "x"), split_axis=0, concat_axis=0, tiled=True)
    cut = jnp.sum(cut.astype(f32), 0).astype(bf16)
    part = jnp.broadcast_to(cut[None], (8, *cut.shape))
    part = lax.all_to_all(part, ("z", "x"), split_axis=0, concat_axis=0, tiled=True)
    gq, go, gr, *lines = unpack(part, 3 * features, experts)
    lines = [line.reshape(width) for line in lines]
    grad_in, grad_back = settle(place, second_swap, out0[2], core0, side0, first_swap, *third_swap)

    return (block_out, grad_tokens, lines[0], lines[1], gq, go, lines[2], lines[3], gr.T, grad_in, grad_back)


def solution(mesh):
    if mesh.shape["dp"] == 4 and mesh.shape["expert"] == 8:
        mesh = Mesh(mesh.devices.reshape(2, 2, 4, 2), ("y", "core", "z", "x"))
        body, dp, expert = paired, ("y", "core"), ("z", "x")
    else:
        body, dp, expert = exchanged, ("dp",), ("expert",)
    rows = P((*dp, *expert), None)
    return jax.shard_map(
        body,
        mesh=mesh,
        in_specs=(
            rows,
            P(dp),
            P(dp),
            P(dp, None),
            P(dp, None),
            P(dp),
            P(dp),
            P(dp, None),
            P(expert, None, None),
            P(expert, None, None),
            rows,
            P((*dp, *expert)),
            P(),
            rows,
        ),
        out_specs=(
            rows,
            rows,
            P(dp),
            P(dp),
            P(dp, None),
            P(dp, None),
            P(dp),
            P(dp),
            P(dp, None),
            P(expert, None, dp),
            P(expert, dp, None),
        ),
        check_vma=False,
    )
```

```python
import functools
import jax
import jax.numpy as jnp
from jax import lax
from jax.experimental import pallas as pl
from jax.experimental.pallas import tpu as pltpu
from jax.sharding import Mesh
from jax.sharding import PartitionSpec as P

HEADS = 8
HEAD_DIM = 64
TOP = 2
SEQ = 197
IMG_MB = 3
MICRO = 2
EPSILON = 1e-06
SCALING = 0.125
ROOT_HALF = 0.7071067811865476
INV_ROOT_TWO_PI = 0.3989422804014327
PAD = 16 * ((SEQ + 15) // 16)
ROWS = IMG_MB * PAD
IMAGES = MICRO * IMG_MB
f32 = jnp.float32
bf16 = jnp.bfloat16
NN = (((1,), (0,)), ((), ()))
NT = (((1,), (1,)), ((), ()))
TN = (((0,), (0,)), ((), ()))


def mm(a, b, dims=NN):
    return lax.dot_general(a, b, dims, preferred_element_type=f32)


def whole(shape):
    zeros = (0,) * len(shape)
    return pl.BlockSpec(shape, lambda *_: zeros)


def pinned(value):
    return pltpu.with_memory_space_constraint(value, pltpu.HBM)


def params(mb=60):
    return pltpu.CompilerParams(vmem_limit_bytes=mb << 20)


SHARE = 1.0


def cost(flops, moved):
    return pl.CostEstimate(flops=int(flops * SHARE), bytes_accessed=int(moved * SHARE), transcendentals=0)


Z_AT, X_AT, Y_AT, CORE_AT = 4, 5, 6, 7


def expert_of(place_ref, index):
    return 2 * (place_ref[Z_AT] ^ (index & 3)) + (place_ref[X_AT] ^ (index >> 2))


def label_column(place_ref, experts):
    index = lax.broadcasted_iota(jnp.int32, (experts, 1), 0)
    label = jnp.zeros((experts, 1), jnp.int32)
    for r in range(experts):
        label = jnp.where(index == r, expert_of(place_ref, r), label)
    return label


def wide_transpose(rows, fill):
    pad = jnp.full((128 - rows.shape[0], rows.shape[1]), fill, f32)
    return jnp.transpose(jnp.concatenate([rows, pad], 0))


def pack_kernel(g1_ref, b1_ref, g2_ref, b2_ref, qkv_ref, out_ref, router_ref, packed_ref):
    width, columns = qkv_ref.shape
    packed_ref[0, :width, :columns] = qkv_ref[...]
    packed_ref[0, :width, columns:] = out_ref[...]
    pieces = [ref[...].astype(f32) for ref in (g1_ref, b1_ref, g2_ref, b2_ref)]
    router = router_ref[...].astype(f32)
    pieces += [router[e : e + 1, :] for e in range(router.shape[0])]
    rest = packed_ref.shape[2] - width * len(pieces)
    row = jnp.concatenate(pieces + [jnp.zeros((1, rest), f32)], 1)
    row = jnp.concatenate([row, jnp.zeros((15, row.shape[1]), f32)], 0)
    packed_ref[0, width:, :] = row.astype(bf16)


def pack(vectors_in, qkv, out, router):
    width, columns = qkv.shape
    rows = [vector.reshape(1, width) for vector in vectors_in]
    packed = (1, width + 16, columns + out.shape[1])
    inputs = (*rows, qkv, out, router)
    return pl.pallas_call(
        pack_kernel,
        grid=(1,),
        in_specs=[whole(value.shape) for value in inputs],
        out_specs=whole(packed),
        out_shape=jax.ShapeDtypeStruct(packed, bf16),
        compiler_params=params(60),
        cost_estimate=cost(0, 2_000_000),
        name="pack",
    )(*inputs)


def quarter_kernel(place_ref, in_ref, back_ref, one_ref, sem):
    span = one_ref.shape[1]
    start = pl.multiple_of(place_ref[0] * span, span)
    copies = (
        pltpu.make_async_copy(in_ref.at[0, :, pl.ds(start, span)], one_ref.at[0], sem.at[0]),
        pltpu.make_async_copy(back_ref.at[0, pl.ds(start, span), :], one_ref.at[1], sem.at[1]),
    )
    for copy in copies:
        copy.start()
    for copy in copies:
        copy.wait()


def quarter_of(place, expert_in, expert_out):
    shape = (2, expert_in.shape[1], expert_in.shape[2] // 4)
    return pl.pallas_call(
        quarter_kernel,
        grid_spec=pltpu.PrefetchScalarGridSpec(
            num_scalar_prefetch=1,
            grid=(1,),
            in_specs=[pl.BlockSpec(memory_space=pl.ANY)] * 2,
            out_specs=whole(shape),
            scratch_shapes=[pltpu.SemaphoreType.DMA((2,))],
        ),
        out_shape=jax.ShapeDtypeStruct(shape, bf16),
        compiler_params=params(60),
        cost_estimate=cost(0, 2_000_000),
        name="quarter",
    )(place, expert_in, expert_out)


def pad_rows(src_ref, dst_ref, buf):
    buf[pl.ds(0, src_ref.shape[0]), :] = src_ref[...].astype(f32)
    for image in range(IMAGES):
        piece = buf[pl.ds(image * SEQ, PAD), :]
        row = lax.broadcasted_iota(jnp.int32, piece.shape, 0)
        dst_ref[image] = jnp.where(row < SEQ, piece, 0.0).astype(bf16)


def pad_images(values):
    total, features = values.shape
    padded = (IMAGES, PAD, features)
    return pl.pallas_call(
        pad_rows,
        grid=(1,),
        in_specs=[whole(values.shape)],
        out_specs=whole(padded),
        out_shape=jax.ShapeDtypeStruct(padded, bf16),
        scratch_shapes=[pltpu.VMEM((8 * ((total + PAD) // 8), features), f32)],
        compiler_params=params(60),
        cost_estimate=cost(0, 4_000_000),
        name="pad",
    )(values)


def prepare_kernel(place_ref, cap_ref, tok_ref, route_ref, prio_ref, tokp_ref, slot_ref, slotc_ref, buf, keys):
    total = tok_ref.shape[0]
    experts = slot_ref.shape[1]
    pad_rows(tok_ref, tokp_ref, buf)
    keys[...] = jnp.full_like(keys, -1.0)
    keys[pl.ds(0, total), 0:2] = route_ref[...].astype(f32)
    keys[pl.ds(0, total), 2:3] = prio_ref[...].astype(f32)
    labels = label_column(place_ref, experts)
    limit = jnp.zeros((experts, 1), f32)
    for e in range(experts):
        limit = jnp.where(labels == e, cap_ref[e].astype(f32), limit)
    labels = labels.astype(f32)
    for block in range(MICRO):
        columns = []
        for image in range(IMG_MB):
            piece = keys[pl.ds((block * IMG_MB + image) * SEQ, PAD), :]
            row = lax.broadcasted_iota(jnp.int32, piece.shape, 0)
            columns.append(jnp.where(row < SEQ, piece, -1.0))
        column = jnp.concatenate(columns, 0)
        turned = jnp.transpose(column)
        key_column = jnp.where(column[:, 2:3] < 0.0, 1e6, column[:, 2:3])
        below = jnp.where(key_column < turned[2:3, :], 1.0, 0.0).astype(bf16)
        first = labels == turned[0:1, :]
        second = labels == turned[1:2, :]
        hot = jnp.concatenate([jnp.where(first, 1.0, 0.0), jnp.where(second, 1.0, 0.0)], 0)
        counts = mm(hot.astype(bf16), below)
        total_first = jnp.sum(hot[:experts], 1, keepdims=True)
        rank = jnp.where(
            first, counts[:experts], jnp.where(second, counts[experts:] + total_first, 1e6)
        )
        slot = jnp.where(rank < limit, rank, -1.0)
        slot_ref[block] = slot
        slotc_ref[block] = wide_transpose(slot, -1.0)[:, :experts]


def prepare(place, capacity, tokens, routes, priority):
    total, features = tokens.shape
    experts = capacity.shape[0]
    tall = 8 * ((total + PAD) // 8)
    priority = priority.reshape(total, 1)
    padded = (IMAGES, PAD, features)
    return pl.pallas_call(
        prepare_kernel,
        grid_spec=pltpu.PrefetchScalarGridSpec(
            num_scalar_prefetch=2,
            grid=(1,),
            in_specs=[whole(tokens.shape), whole(routes.shape), whole(priority.shape)],
            out_specs=(
                whole(padded),
                whole((MICRO, experts, ROWS)),
                whole((MICRO, ROWS, experts)),
            ),
            scratch_shapes=[pltpu.VMEM((tall, features), f32), pltpu.VMEM((tall, 128), f32)],
        ),
        out_shape=(
            jax.ShapeDtypeStruct(padded, bf16),
            jax.ShapeDtypeStruct((MICRO, experts, ROWS), f32),
            jax.ShapeDtypeStruct((MICRO, ROWS, experts), f32),
        ),
        compiler_params=params(60),
        cost_estimate=cost(0, 8_000_000),
        name="prepare",
    )(place, capacity, tokens, routes, priority)


def norm(values, gain, offset):
    center = values - jnp.mean(values, -1, keepdims=True)
    inverse = lax.rsqrt(jnp.mean(center * center, -1, keepdims=True) + EPSILON)
    normal = center * inverse
    return normal * gain + offset, normal, inverse


def load_dense(place_ref, two_ref, more_ref, w_s, sem):
    copies = [
        pltpu.make_async_copy((two_ref, more_ref)[j // 2].at[j % 2], w_s.at[place_ref[j]], sem.at[j])
        for j in range(4)
    ]
    for copy in copies:
        copy.start()
    return copies


def vectors(w_s):
    quarters = w_s.shape[0]
    width = w_s.shape[1] - 16
    row = [w_s[q, pl.ds(width, 1), :] for q in range(quarters)]

    def pick(index):
        return jnp.concatenate([r[:, index * width : (index + 1) * width] for r in row], 1)

    return pick


def dense_weights(w_s, features):
    width = w_s.shape[1] - 16
    qkv = w_s[:, :width, : 3 * features].reshape(features, 3 * features)
    out = w_s[:, :width, 3 * features :].reshape(features, features)
    return qkv, out


def router_rows(pick, place_ref, experts):
    table = jnp.concatenate([pick(4 + e) for e in range(experts)], 0)
    labels = label_column(place_ref, experts)
    order = labels == lax.broadcasted_iota(jnp.int32, (experts, experts), 1)
    return mm(jnp.where(order, 1.0, 0.0).astype(bf16), table).astype(bf16)


def half_mask(index, value):
    lane = lax.broadcasted_iota(jnp.int32, (1, 2 * HEAD_DIM), 1)
    return jnp.where((lane < HEAD_DIM) == (index == 0), value, 0.0).astype(bf16)


def forward_kernel(first, place_ref, tok_ref, two_ref, more_ref, proj_ref, prob_ref, att_ref, mid_ref, n2_ref, gate_ref, w_s, sem, in_sem, out_sem, tok_s, n1_s, proj_s, prob_s, att_s, mid_s, n2_s):
    features = tok_s.shape[1]
    copy_in = pltpu.make_async_copy(tok_ref.at[first // IMG_MB], tok_s, in_sem.at[0])
    copy_in.start()
    waits = load_dense(place_ref, two_ref, more_ref, w_s, sem)
    out_copies = [
        pltpu.make_async_copy(src, dst, out_sem.at[i])
        for i, (src, dst) in enumerate(
            ((proj_s, proj_ref), (prob_s, prob_ref), (att_s, att_ref), (mid_s, mid_ref), (n2_s, n2_ref))
        )
    ]
    copy_in.wait()
    for copy in waits:
        copy.wait()
    pick = vectors(w_s)
    qkv, out = dense_weights(w_s, features)
    gain, offset = pick(0).astype(f32), pick(1).astype(f32)

    @pl.loop(0, IMG_MB)
    def _(i):
        span = pl.ds(pl.multiple_of(i * PAD, PAD), PAD)
        pre, _, _ = norm(tok_s[span, :].astype(f32), gain, offset)
        n1_s[span, :] = pre.astype(bf16)

    proj_s[...] = mm(n1_s[...], qkv).astype(bf16)
    out_copies[0].start()
    column = lax.broadcasted_iota(jnp.int32, (1, PAD), 1)
    pair = 2 * HEAD_DIM

    @pl.loop(0, IMG_MB)
    def _(i):
        span = pl.ds(pl.multiple_of(i * PAD, PAD), PAD)
        for group in range(HEADS // 2):
            q2 = proj_s[span, group * pair : (group + 1) * pair]
            k2 = proj_s[span, features + group * pair : features + (group + 1) * pair]
            v2 = proj_s[span, 2 * features + group * pair : 2 * features + (group + 1) * pair]
            total = None
            for half in range(2):
                scores = mm(q2 * half_mask(half, SCALING), k2, NT)
                scores = jnp.where(column < SEQ, scores, -1e30)
                expos = jnp.exp(scores - jnp.max(scores, -1, keepdims=True))
                probs = (expos * (1.0 / jnp.sum(expos, -1, keepdims=True))).astype(bf16)
                prob_s[i, 2 * group + half] = probs
                piece = mm(probs, v2 * half_mask(half, 1.0))
                total = piece if total is None else total + piece
            att_s[span, group * pair : (group + 1) * pair] = total.astype(bf16)

    out_copies[1].start()
    out_copies[2].start()
    mid_s[...] = mm(att_s[...], out)
    gain_two, offset_two = pick(2).astype(f32), pick(3).astype(f32)

    @pl.loop(0, IMG_MB)
    def _(i):
        span = pl.ds(pl.multiple_of(i * PAD, PAD), PAD)
        middle = tok_s[span, :].astype(f32) + mid_s[span, :]
        mid_s[span, :] = middle
        pre, _, _ = norm(middle, gain_two, offset_two)
        n2_s[span, :] = pre.astype(bf16)

    out_copies[4].start()
    out_copies[3].start()
    router = router_rows(pick, place_ref, gate_ref.shape[0])
    logits = mm(router, n2_s[...], NT)
    expos = jnp.exp(logits - jnp.max(logits, 0, keepdims=True))
    gate_ref[...] = expos / jnp.sum(expos, 0, keepdims=True)
    for copy in out_copies:
        copy.wait()


def image(*tail):
    zeros = (0,) * len(tail)
    return pl.BlockSpec((1, *tail), lambda i, *_: (i, *zeros))


def forward_images(first, place, tokp, dense, experts):
    features = tokp.shape[2]
    count = IMG_MB
    flops = 2 * count * PAD * (4 * features * features + 2 * PAD * 256 * HEADS)
    shapes = (
        ((ROWS, 3 * features), bf16),
        ((count, HEADS, PAD, PAD), bf16),
        ((ROWS, features), bf16),
        ((ROWS, features), f32),
        ((ROWS, features), bf16),
    )
    scratch = [((ROWS, features), bf16), ((ROWS, features), bf16), *shapes]
    return pl.pallas_call(
        functools.partial(forward_kernel, first),
        grid_spec=pltpu.PrefetchScalarGridSpec(
            num_scalar_prefetch=1,
            grid=(1,),
            in_specs=[pl.BlockSpec(memory_space=pl.ANY)] * 3,
            out_specs=(*[pl.BlockSpec(memory_space=pl.ANY)] * 5, whole((experts, ROWS))),
            scratch_shapes=[
                pltpu.VMEM((4, *dense[0].shape[1:]), bf16),
                pltpu.SemaphoreType.DMA((4,)),
                pltpu.SemaphoreType.DMA((1,)),
                pltpu.SemaphoreType.DMA((5,)),
            ]
            + [pltpu.VMEM(*shape) for shape in scratch],
        ),
        out_shape=(
            *[pltpu.HBM(*shape) for shape in shapes],
            jax.ShapeDtypeStruct((experts, ROWS), f32),
        ),
        compiler_params=params(32),
        cost_estimate=cost(flops, count * 3_000_000),
        name="forward",
    )(place, tokp.reshape(MICRO, ROWS, features), *dense)


def gelu_pair(field):
    cdf = 0.5 * (1.0 + lax.erf(field * ROOT_HALF))
    return field * cdf, cdf + field * (jnp.exp(-0.5 * field * field) * INV_ROOT_TWO_PI)


def expert_kernel(index, own, part, place_ref, *refs):
    low, high = {"all": (0, 2 * MICRO), "own": (0, MICRO), "other": (MICRO, 2 * MICRO)}[part]
    blocks = high - low
    n2_refs = refs[:blocks]
    refs = refs[blocks:]
    cot_refs = refs[: blocks // MICRO]
    refs = refs[blocks // MICRO :]
    if low == 0:
        slot_ref, gate0_ref, gate1_ref = refs[:3]
        refs = refs[3:]
    if high > MICRO:
        other_ref = refs[0]
        refs = refs[1:]
    sources = 2 if own else 4
    w_refs = refs[:sources]
    refs = refs[sources:]
    if part == "other":
        keep_in_ref, send_in_ref = refs[:2]
        refs = refs[2:]
    res_ref, dx_ref, keep_ref, send_ref = refs[:4]
    refs = refs[4:]
    lines = {}
    for first in range(low, high, MICRO):
        lines[first] = refs[0]
        refs = refs[1:]
    w_s, sem, n2_s, cot_s, in_sem, x_s, g_s, raw_s, xt_s, gt_s, gs_s, r_acc, dx_acc, act_s, dh_s = refs
    step = pl.program_id(0)
    quarters, _, _, width = w_s.shape
    slots = x_s.shape[0] // blocks
    row = lax.broadcasted_iota(jnp.int32, (slots, ROWS), 0).astype(f32)

    def copies(j):
        if own:
            start = pl.multiple_of(place_ref[j] * width, width)
            return (
                pltpu.make_async_copy(w_refs[0].at[0, :, pl.ds(start, width)], w_s.at[j, 0], sem.at[2 * j]),
                pltpu.make_async_copy(w_refs[1].at[0, pl.ds(start, width), :], w_s.at[j, 1], sem.at[2 * j + 1]),
            )
        return (pltpu.make_async_copy(w_refs[j], w_s.at[j], sem.at[j]),)

    def slot_row(local):
        b = low + local
        if b < MICRO:
            return slot_ref[b, pl.ds(index, 1), :]
        return other_ref[b - MICRO, pl.ds(index + 4, 1), :]

    def gate_row(local):
        b = low + local
        if b < MICRO:
            return (gate0_ref, gate1_ref)[b][pl.ds(index, 1), :]
        return other_ref[b, pl.ds(index + 4, 1), :]

    def rows_in(b):
        return (
            pltpu.make_async_copy(n2_refs[b], n2_s.at[b], in_sem.at[2 * b]),
            pltpu.make_async_copy(cot_refs[b // MICRO].at[b % MICRO], cot_s.at[b], in_sem.at[2 * b + 1]),
        )

    @pl.when(step == 0)
    def _():
        for b in range(blocks):
            for copy in rows_in(b):
                copy.start()
        for j in range(quarters):
            for copy in copies(j):
                copy.start()
        r_acc[...] = jnp.zeros_like(r_acc)
        dx_acc[...] = jnp.zeros_like(dx_acc)
        for b in range(blocks):
            for copy in rows_in(b):
                copy.wait()
            span = pl.ds(b * slots, slots)
            hit = row == slot_row(b)
            pick = jnp.where(hit, 1.0, 0.0)
            gate = jnp.sum(jnp.where(hit, gate_row(b), 0.0), 1, keepdims=True)
            pick = pick.astype(bf16)
            x = mm(pick, n2_s[b])
            raw = mm(pick, cot_s[b])
            x_s[span, :] = x.astype(bf16)
            raw_s[span, :] = raw.astype(bf16)
            g = gate * raw
            g_s[span, :] = g.astype(bf16)
            gs_s[span, :] = jnp.broadcast_to(gate, (slots, 128))
        xt_s[...] = jnp.transpose(x_s[...])
        gt_s[...] = jnp.transpose(g_s[...])

    for j in range(quarters):

        @pl.when(step == j)
        def _():
            for copy in copies(j):
                copy.wait()

    w_in = w_s[step, 0]
    w_out = w_s[step, 1]
    rows = MICRO * slots
    for r in range(blocks // MICRO):
        span = pl.ds(r * rows, rows)
        act, slope = gelu_pair(mm(x_s[span, :], w_in))
        act = act.astype(bf16)
        dh = (mm(g_s[span, :], w_out, NT) * slope).astype(bf16)
        act_s[span, :] = act
        dh_s[span, :] = dh
        r_acc[span, :] += mm(act, w_out)
        dx_acc[span, :] += mm(dh, w_in, NT)
    grad_in = mm(xt_s[...], dh_s[...])
    grad_out = mm(gt_s[...], act_s[...])
    if part == "other":
        early = step < quarters // 2
        grad_in += jnp.where(early, keep_in_ref[0, 0].astype(f32), send_in_ref[0, 0].astype(f32))
        grad_out += jnp.where(early, keep_in_ref[0, 1].astype(f32), send_in_ref[0, 1].astype(f32))

    @pl.when(step < quarters // 2)
    def _():
        keep_ref[0, 0] = grad_in.astype(bf16)
        keep_ref[0, 1] = grad_out.astype(bf16)

    @pl.when(step >= quarters // 2)
    def _():
        send_ref[0, 0] = grad_in.astype(bf16)
        send_ref[0, 1] = grad_out.astype(bf16)

    @pl.when(step == quarters - 1)
    def _():
        dx_ref[...] = dx_acc[...].astype(bf16).reshape(dx_ref.shape)
        for b in range(blocks):
            span = pl.ds(b * slots, slots)
            res = r_acc[span, :].astype(bf16).astype(f32)
            dgate = jnp.sum(res * raw_s[span, :].astype(f32), 1, keepdims=True)
            res_ref[b] = (res * gs_s[span, 0:1]).astype(bf16)
            hit = row == slot_row(b)
            line = jnp.sum(jnp.where(hit, dgate, 0.0), 0, keepdims=True)
            lines[low + b - b % MICRO][pl.ds(b % MICRO, 1), :] = line


def expert_apply(index, place, n2, cot, tables, weights, slots, part="all", before=()):
    blocks = len(n2)
    features = n2[0].shape[1]
    own = len(weights) == 2
    quarters = 4
    width = weights[0].shape[2] // (4 if own else 1)
    rows = blocks * slots

    def fixed(shape):
        zeros = (0,) * len(shape)
        return pl.BlockSpec(shape, lambda *_: zeros)

    half = quarters // 2
    keep = pl.BlockSpec((1, 2, features, width), lambda i, _: (jnp.minimum(i, half - 1), 0, 0, 0))
    send = pl.BlockSpec((1, 2, features, width), lambda i, _: (jnp.maximum(i - half, 0), 0, 0, 0))
    groups = blocks // MICRO
    return pl.pallas_call(
        functools.partial(expert_kernel, index, own, part),
        grid_spec=pltpu.PrefetchScalarGridSpec(
            num_scalar_prefetch=1,
            grid=(quarters,),
            in_specs=[pl.BlockSpec(memory_space=pl.ANY)] * (blocks + len(cot))
            + [fixed(piece.shape) for piece in tables]
            + [pl.BlockSpec(memory_space=pl.ANY)] * len(weights)
            + [keep, send][: len(before)],
            out_specs=(
                fixed((blocks, slots, features)),
                fixed((blocks, slots, features)),
                keep,
                send,
                *[fixed((MICRO, ROWS))] * groups,
            ),
            scratch_shapes=[
                pltpu.VMEM((quarters, 2, features, width), bf16),
                pltpu.SemaphoreType.DMA((2 * quarters,)),
                pltpu.VMEM((blocks, ROWS, features), bf16),
                pltpu.VMEM((blocks, ROWS, features), bf16),
                pltpu.SemaphoreType.DMA((2 * blocks,)),
                pltpu.VMEM((rows, features), bf16),
                pltpu.VMEM((rows, features), bf16),
                pltpu.VMEM((rows, features), bf16),
                pltpu.VMEM((features, rows), bf16),
                pltpu.VMEM((features, rows), bf16),
                pltpu.VMEM((rows, 128), f32),
                pltpu.VMEM((rows, features), f32),
                pltpu.VMEM((rows, features), f32),
                pltpu.VMEM((rows, width), bf16),
                pltpu.VMEM((rows, width), bf16),
            ],
        ),
        out_shape=(
            pltpu.HBM((blocks, slots, features), bf16),
            pltpu.HBM((blocks, slots, features), bf16),
            pltpu.HBM((half, 2, features, width), bf16),
            pltpu.HBM((half, 2, features, width), bf16),
            *[jax.ShapeDtypeStruct((MICRO, ROWS), f32)] * groups,
        ),
        compiler_params=params(40),
        cost_estimate=cost(12 * rows * features * width * quarters, 4_000_000 + 3_000_000 * blocks),
        name="expert",
    )(place, *n2, *cot, *tables, *weights, *map(pinned, before))


def selector(columns, slots):
    count = columns.shape[1]
    lane = lax.broadcasted_iota(jnp.int32, (columns.shape[0], slots), 1).astype(f32)
    pieces = [jnp.where(columns[:, k : k + 1] == lane, 1.0, 0.0).astype(bf16) for k in range(count)]
    return jnp.concatenate(pieces, 1)


def combine_kernel(count, slot_ref, *refs):
    slots = refs[0].shape[1]
    pick = selector(wide_transpose(slot_ref[0, count:, :], -1.0)[:, :count], slots)
    refs[count][0] = mm(pick, jnp.concatenate([r[0] for r in refs[:count]], 0)).astype(bf16)


def combine(slot, pieces, block, blocks):
    count = len(pieces)
    _, slots, features = pieces[0].shape
    late = pl.BlockSpec((1, slots, features), lambda i: (i + block + MICRO, 0, 0))
    short = pl.BlockSpec((1, slots, features), lambda i: (i + block, 0, 0))
    return pl.pallas_call(
        functools.partial(combine_kernel, count),
        grid=(blocks,),
        in_specs=[pl.BlockSpec((1, 2 * count, ROWS), lambda i: (i + block, 0, 0))]
        + [late if piece.shape[0] > MICRO else short for piece in pieces],
        out_specs=image(ROWS, features),
        out_shape=jax.ShapeDtypeStruct((blocks, ROWS, features), bf16),
        compiler_params=params(24),
        cost_estimate=cost(2 * blocks * ROWS * features * slots * count, 5_000_000),
        name="combine",
    )(slot, *map(pinned, pieces))


def finish_kernel(count, mid0_ref, mid1_ref, part_ref, slotc_ref, dtok0_ref, dtok1_ref, *refs):
    out_ref, dout_ref, buf, dbuf = refs[count:]
    slots = refs[0].shape[1]
    step = pl.program_id(0)
    choose = selector(slotc_ref[0, :, :count], slots)
    mixed = mm(choose, jnp.concatenate([r[0] for r in refs[:count]], 0)) + part_ref[0].astype(f32)
    early = step < IMG_MB
    middle = jnp.where(early, mid0_ref[...], mid1_ref[...])
    value = middle + mixed
    grad = jnp.where(early, dtok0_ref[...].astype(f32), dtok1_ref[...].astype(f32))
    for i in range(IMAGES):

        @pl.when(step == i)
        def _():
            buf[pl.ds(i * SEQ, SEQ), :] = value[:SEQ]
            dbuf[pl.ds(i * SEQ, SEQ), :] = grad[:SEQ]

    @pl.when(step == IMAGES - 1)
    def _():
        out_ref[...] = buf[pl.ds(0, out_ref.shape[0]), :].astype(bf16)
        dout_ref[...] = dbuf[pl.ds(0, out_ref.shape[0]), :].astype(bf16)


def finish(middles, part, slotc, dtoks, results):
    count = len(results)
    _, slots, features = results[0].shape
    experts = slotc.shape[2]
    piece = pl.BlockSpec((1, slots, features), lambda i: (lax.div(i, IMG_MB), 0, 0))
    total = IMAGES * SEQ
    tall = 8 * ((total + 7) // 8)
    early = pl.BlockSpec((PAD, features), lambda i: (jnp.minimum(i, IMG_MB - 1), 0))
    later = pl.BlockSpec((PAD, features), lambda i: (jnp.maximum(i - IMG_MB, 0), 0))
    return pl.pallas_call(
        functools.partial(finish_kernel, count),
        grid=(IMAGES,),
        in_specs=[early, later, image(PAD, features), image(PAD, experts), early, later] + [piece] * count,
        out_specs=(whole((total, features)), whole((total, features))),
        out_shape=(jax.ShapeDtypeStruct((total, features), bf16),) * 2,
        scratch_shapes=[pltpu.VMEM((tall, features), f32)] * 2,
        compiler_params=params(24),
        cost_estimate=cost(4 * ROWS * features * slots * count, 15_000_000),
        name="finish",
    )(*middles, part, slotc, *dtoks, *results)


def norm_back(grad, normal, inverse, gain):
    scaled = grad * gain
    return inverse * (
        scaled
        - jnp.mean(scaled, -1, keepdims=True)
        - normal * jnp.mean(scaled * normal, -1, keepdims=True)
    )


def backward_kernel(first, count, place_ref, gate_ref, slotc_ref, dgo_ref, *refs):
    dg_refs = refs[:count]
    sources = refs[count : count + 8]
    refs = refs[count + 8 :]
    two_ref, more_ref = refs[:2]
    dx_refs = refs[2 : 2 + count]
    refs = refs[2 + count :]
    chained = first > 0
    if chained:
        before_ref, before_row_ref = refs[:2]
        dtok_ref, keep_ref, send_ref = refs[2:5]
        acc_s, acc_sem, row_ref = refs[5:8]
        refs = refs[8:]
    else:
        dtok_ref, acc_ref, row_ref = refs[:3]
        acc_s, acc_sem = refs[3:5]
        refs = refs[5:]
    w_s, sem, in_sem, dx_sem = refs[:4]
    tok_s, cot_s, proj_s, prob_s, att_s, mid_s, n2_s, dn2_s = stores = refs[4:12]
    dx_s, dbr_s, datt_s, dproj_s, n1_s, sum_s = refs[12:]
    micro = first // IMG_MB
    features = tok_s.shape[1]
    experts = 2 * count
    slots = dx_s.shape[0] // count
    copies = []
    for i, (src, dst) in enumerate(zip(sources, stores)):
        copies.append(pltpu.make_async_copy(src.at[micro] if i < 2 else src, dst, in_sem.at[i]))
    tok_in, cot_in, proj_in, prob_in, att_in, mid_in, n2_in, dn2_in = copies
    dx_in = [
        pltpu.make_async_copy(dx_refs[k].at[micro], dx_s.at[pl.ds(k * slots, slots), :], dx_sem.at[k])
        for k in range(count)
    ]
    for copy in (*dx_in, dn2_in, n2_in):
        copy.start()
    dense_in = load_dense(place_ref, two_ref, more_ref, w_s, sem)
    for copy in (mid_in, cot_in, att_in, proj_in, prob_in, tok_in):
        copy.start()
    if chained:
        acc_in = pltpu.make_async_copy(before_ref, acc_s, acc_sem.at[0])
        acc_in.start()
        row_ref[...] = before_row_ref[...]
    else:
        row_ref[...] = jnp.zeros_like(row_ref)
    choose = selector(slotc_ref[0, :, :count], slots)
    gates = gate_ref[...]
    dgates = [ref[pl.ds(micro, 1), :] for ref in dg_refs] + [dgo_ref[k, pl.ds(micro, 1), :] for k in range(count)]
    dgates = jnp.concatenate(dgates, 0)
    dlogits = (gates * (dgates - jnp.sum(gates * dgates, 0, keepdims=True))).astype(bf16)
    for copy in (*dx_in, dn2_in, n2_in, *dense_in):
        copy.wait()
    pick = vectors(w_s)
    qkv, out = dense_weights(w_s, features)
    router = router_rows(pick, place_ref, experts)
    row_ref[8 : 8 + experts, :] += mm(dlogits, n2_s[...])
    sum_s[...] = mm(choose, dx_s[...]) + mm(dlogits, router, TN)
    mid_in.wait()
    cot_in.wait()
    gain_two = pick(2).astype(f32)

    @pl.loop(0, IMG_MB)
    def _(i):
        span = pl.ds(pl.multiple_of(i * PAD, PAD), PAD)
        dn2 = sum_s[span, :] + dn2_s[span, :].astype(f32)
        _, normal_two, inverse_two = norm(mid_s[span, :], gain_two, 0.0)
        row_ref[2:3, :] += jnp.sum(dn2 * normal_two, 0, keepdims=True)
        row_ref[3:4, :] += jnp.sum(dn2, 0, keepdims=True)
        dmiddle = cot_s[span, :].astype(f32) + norm_back(dn2, normal_two, inverse_two, gain_two)
        mid_s[span, :] = dmiddle
        dbr_s[span, :] = dmiddle.astype(bf16)

    att_in.wait()
    if chained:
        acc_in.wait()
    grad_out = mm(att_s[...], dbr_s[...], TN)
    if chained:
        acc_s[:, 3 * features :] += grad_out
    else:
        acc_s[:, 3 * features :] = grad_out
    datt_s[...] = mm(dbr_s[...], out, NT).astype(bf16)
    proj_in.wait()
    prob_in.wait()
    tok_in.wait()
    pair = 2 * HEAD_DIM
    gain_one, offset_one = pick(0).astype(f32), pick(1).astype(f32)

    @pl.loop(0, IMG_MB)
    def _(i):
        span = pl.ds(pl.multiple_of(i * PAD, PAD), PAD)
        pre, _, _ = norm(tok_s[span, :].astype(f32), gain_one, offset_one)
        n1_s[span, :] = pre.astype(bf16)
        for group in range(HEADS // 2):
            at = [part * features + group * pair for part in range(3)]
            q2, k2, v2 = (proj_s[span, start : start + pair] for start in at)
            d2 = datt_s[span, group * pair : (group + 1) * pair]
            dq = dk = dv = None
            for half in range(2):
                probs = prob_s[i, 2 * group + half]
                wide = probs.astype(f32)
                dm = d2 * half_mask(half, 1.0)
                dweights = mm(dm, v2, NT)
                inner = jnp.sum(dweights * wide, -1, keepdims=True)
                dscores = (wide * (dweights - inner)).astype(bf16)
                part_q = mm(dscores, k2 * half_mask(half, SCALING))
                part_k = mm(dscores, q2 * half_mask(half, SCALING), TN)
                part_v = mm(probs, dm, TN)
                dq = part_q if dq is None else dq + part_q
                dk = part_k if dk is None else dk + part_k
                dv = part_v if dv is None else dv + part_v
            for start, value in zip(at, (dq, dk, dv)):
                dproj_s[span, start : start + pair] = value.astype(bf16)

    grad_qkv = mm(n1_s[...], dproj_s[...], TN)
    if chained:
        acc_s[:, : 3 * features] += grad_qkv
    else:
        acc_s[:, : 3 * features] = grad_qkv
        acc_out = pltpu.make_async_copy(acc_s, acc_ref, acc_sem.at[0])
        acc_out.start()
    sum_s[...] = mm(dproj_s[...], qkv, NT)

    @pl.loop(0, IMG_MB)
    def _(i):
        span = pl.ds(pl.multiple_of(i * PAD, PAD), PAD)
        dnormed = sum_s[span, :]
        _, normal_one, inverse_one = norm(tok_s[span, :].astype(f32), gain_one, offset_one)
        row_ref[0:1, :] += jnp.sum(dnormed * normal_one, 0, keepdims=True)
        row_ref[1:2, :] += jnp.sum(dnormed, 0, keepdims=True)
        dtok_ref[span, :] = (mid_s[span, :] + norm_back(dnormed, normal_one, inverse_one, gain_one)).astype(bf16)

    if not chained:
        acc_out.wait()
        return
    width = keep_ref.shape[1] - 16
    lines = [row_ref[i : i + 1, :] for i in range(4)]
    for e in range(experts):
        line = jnp.zeros((1, features), f32)
        for r in range(experts):
            line = jnp.where(expert_of(place_ref, r) == e, row_ref[8 + r : 9 + r, :], line)
        lines.append(line)
    blank = jnp.zeros((1, 4 * features - (4 + experts) * width), f32)
    tails = []
    for q in range(4):
        parts = [line[:, q * width : (q + 1) * width] for line in lines]
        tails.append(jnp.concatenate(parts + [blank], 1))
    for j in range(4):
        quarter = place_ref[j]
        to = (keep_ref, send_ref)[j // 2]
        to[j % 2, :width, :] = acc_s[pl.ds(pl.multiple_of(quarter * width, width), width), :].astype(bf16)
        tail = tails[0]
        for q in range(1, 4):
            tail = jnp.where(quarter == q, tails[q], tail)
        tail = jnp.concatenate([tail, jnp.zeros((15, tail.shape[1]), f32)], 0)
        to[j % 2, width:, :] = tail.astype(bf16)


def backward_images(first, place, tokp, cotp, saved, dgs, dg_other, slotc, dn2_part, dense, dxs, before):
    projected, probs, attended, middle, n2, gates = saved
    count = len(dxs)
    features = tokp.shape[2]
    experts = 2 * count
    slots = dxs[0].shape[1]
    totals = ((features, 4 * features), (8 + experts, features))
    packed = (2, *dense[0].shape[1:])
    anywhere = pl.BlockSpec(memory_space=pl.ANY)
    flat = (MICRO, ROWS, features)
    sources = (tokp.reshape(flat), cotp.reshape(flat), projected, probs, attended, middle, n2, dn2_part)
    out_specs = [whole((ROWS, features))]
    out_shape = [jax.ShapeDtypeStruct((ROWS, features), bf16)]
    scratch = [pltpu.VMEM(totals[0], f32), pltpu.SemaphoreType.DMA((1,))]
    if before:
        out_specs += [whole(packed)] * 2
        out_shape += [jax.ShapeDtypeStruct(packed, bf16)] * 2
        scratch.append(pltpu.VMEM(totals[1], f32))
        extra = [anywhere, whole(totals[1])]
    else:
        out_specs += [anywhere, whole(totals[1])]
        out_shape += [jax.ShapeDtypeStruct(shape, f32) for shape in totals]
        extra = []
    scratch += [
        pltpu.VMEM((4, *dense[0].shape[1:]), bf16),
        pltpu.SemaphoreType.DMA((4,)),
        pltpu.SemaphoreType.DMA((8,)),
        pltpu.SemaphoreType.DMA((count,)),
    ]
    scratch += [pltpu.VMEM((ROWS, features), bf16)] * 2
    scratch += [pltpu.VMEM(piece.shape, piece.dtype) for piece in sources[2:]]
    scratch += [
        pltpu.VMEM((count * slots, features), bf16),
        pltpu.VMEM((ROWS, features), bf16),
        pltpu.VMEM((ROWS, features), bf16),
        pltpu.VMEM((ROWS, 3 * features), bf16),
        pltpu.VMEM((ROWS, features), bf16),
        pltpu.VMEM((ROWS, features), f32),
    ]
    micro = first // IMG_MB
    return pl.pallas_call(
        functools.partial(backward_kernel, first, count),
        grid_spec=pltpu.PrefetchScalarGridSpec(
            num_scalar_prefetch=1,
            grid=(1,),
            in_specs=[
                whole(gates.shape),
                pl.BlockSpec((1, ROWS, experts), lambda i, _: (micro, 0, 0)),
                whole(dg_other.shape),
            ]
            + [whole(piece.shape) for piece in dgs]
            + [anywhere] * (10 + count)
            + extra,
            out_specs=tuple(out_specs),
            scratch_shapes=scratch,
        ),
        out_shape=tuple(out_shape),
        compiler_params=params(40),
        cost_estimate=cost(40 * ROWS * features * features, 15_000_000),
        name="backward",
    )(place, gates, slotc, dg_other, *dgs, *sources, *dense, *dxs, *before)


def settle_kernel(place_ref, far_ref, *refs):
    in_ref, back_ref = refs[-2:]
    z = place_ref[Z_AT]
    outer = jnp.where((z == 0) | (z == 3), 1.0, 0.0)

    def total(i):
        value = far_ref[i].astype(f32) * outer + refs[i - 4][...].astype(f32)
        for ref in refs[:-4]:
            piece = ref[0, i] if len(ref.shape) == 4 else ref[i]
            value = value + piece.astype(f32)
        return value

    in_ref[0] = total(0)
    back_ref[0] = jnp.transpose(total(1))


def settle(place, *pieces):
    features, span = pieces[-1].shape

    def spec(piece):
        shape = (1, *piece.shape[1:]) if len(piece.shape) == 4 else piece.shape
        return whole(shape)

    return pl.pallas_call(
        settle_kernel,
        grid_spec=pltpu.PrefetchScalarGridSpec(
            num_scalar_prefetch=1,
            grid=(1,),
            in_specs=[spec(piece) for piece in pieces],
            out_specs=(whole((1, features, span)), whole((1, span, features))),
        ),
        out_shape=(
            jax.ShapeDtypeStruct((1, features, span), f32),
            jax.ShapeDtypeStruct((1, span, features), f32),
        ),
        compiler_params=params(24),
        cost_estimate=cost(0, 5_000_000),
        name="settle",
    )(place, *map(pinned, pieces))


def unpack_kernel(part_ref, qkv_ref, out_ref, router_ref, g1_ref, b1_ref, g2_ref, b2_ref):
    width, columns = qkv_ref.shape
    pieces, _, lanes = part_ref.shape
    for i in range(pieces):
        value = part_ref[i, :width, :].astype(f32)
        at = i * lanes
        if at < columns:
            qkv_ref[:, at : at + lanes] = value
        else:
            out_ref[:, at - columns : at - columns + lanes] = value
    row = jnp.concatenate([part_ref[i, width:, :].astype(f32)[0:1] for i in range(pieces)], 1)
    for i, ref in enumerate((g1_ref, b1_ref, g2_ref, b2_ref)):
        ref[...] = row[:, i * width : (i + 1) * width]
    lines = [row[:, (4 + e) * width : (5 + e) * width] for e in range(router_ref.shape[0])]
    router_ref[...] = jnp.concatenate(lines, 0)


def unpack(part, columns, experts):
    pieces, height, lanes = part.shape
    width = height - 16
    line = (1, width)
    shapes = ((width, columns), (width, pieces * lanes - columns), (experts, width), line, line, line, line)
    return pl.pallas_call(
        unpack_kernel,
        grid=(1,),
        in_specs=[whole(part.shape)],
        out_specs=tuple(whole(shape) for shape in shapes),
        out_shape=tuple(jax.ShapeDtypeStruct(shape, f32) for shape in shapes),
        compiler_params=params(24),
        cost_estimate=cost(0, 3_000_000),
        name="unpack",
    )(part)


def norm_forward(values, gain, offset):
    center = values - jnp.mean(values, -1, keepdims=True)
    inverse = lax.rsqrt(jnp.mean(center * center, -1, keepdims=True) + EPSILON)
    normal = center * inverse
    return (normal * gain + offset, normal, inverse)


def norm_backward(grad, normal, inverse, gain):
    scaled = grad * gain
    return inverse * (
        scaled
        - jnp.mean(scaled, -1, keepdims=True)
        - normal * jnp.mean(scaled * normal, -1, keepdims=True)
    )


def gelu_value(field):
    return 0.5 * field * (1.0 + lax.erf(field * ROOT_HALF))


def gelu_slope(field):
    return (
        0.5 * (1.0 + lax.erf(field * ROOT_HALF))
        + field * jnp.exp(-0.5 * field * field) * INV_ROOT_TWO_PI
    )


def block_ranks(route_rows, order_keys, capacity):
    count = order_keys.shape[0]
    expert_count = capacity.shape[0]
    chosen = jnp.concatenate([route_rows[:, 0], route_rows[:, 1]])
    sort_keys = jnp.concatenate([order_keys, order_keys + count])
    positions = jnp.arange(2 * count, dtype=jnp.int32)
    inverse = jnp.zeros((2 * count,), jnp.int32).at[sort_keys].set(positions)
    ordered = chosen[inverse]
    labels = jnp.arange(expert_count, dtype=jnp.int32)
    onehot = (ordered[:, None] == labels[None, :]).astype(jnp.int32)
    before = jnp.cumsum(onehot, 0) - onehot
    rank_sorted = jnp.sum(before * onehot, 1)
    ranking = jnp.zeros((2 * count,), jnp.int32).at[inverse].set(rank_sorted)
    pair_onehot = chosen[:, None] == labels[None, :]
    limit = jnp.sum(pair_onehot.astype(jnp.int32) * capacity[None, :], 1)
    return (chosen, ranking, ranking < limit, pair_onehot.astype(jnp.float32))


def exchanged(
    tokens,
    ln1_gain,
    ln1_bias,
    qkv_weight,
    out_weight,
    ln2_gain,
    ln2_bias,
    router_weight,
    expert_in,
    expert_out,
    routes,
    priority,
    capacity,
    cotangent,
):
    f32 = jnp.float32
    bf16 = jnp.bfloat16
    gathered = (
        lax.all_gather(ln1_gain, "dp", axis=0, tiled=True),
        lax.all_gather(ln1_bias, "dp", axis=0, tiled=True),
        lax.all_gather(qkv_weight, "dp", axis=0, tiled=True),
        lax.all_gather(out_weight, "dp", axis=0, tiled=True),
        lax.all_gather(ln2_gain, "dp", axis=0, tiled=True),
        lax.all_gather(ln2_bias, "dp", axis=0, tiled=True),
        lax.all_gather(router_weight, "dp", axis=0, tiled=True),
    )
    gain_one = gathered[0].astype(f32)
    offset_one = gathered[1].astype(f32)
    weight_qkv = gathered[2]
    weight_out = gathered[3]
    gain_two = gathered[4].astype(f32)
    offset_two = gathered[5].astype(f32)
    weight_router = gathered[6]
    features = tokens.shape[1]
    owners = lax.axis_size("expert")
    per_owner = expert_in.shape[0]
    experts = owners * per_owner
    slots = 8 * (3 * TOP * IMG_MB * SEQ // (16 * experts) + 1)
    row_count = IMG_MB * SEQ
    sum_gain_one = jnp.zeros((features,), f32)
    sum_offset_one = jnp.zeros((features,), f32)
    sum_qkv = jnp.zeros(weight_qkv.shape, f32)
    sum_out = jnp.zeros(weight_out.shape, f32)
    sum_gain_two = jnp.zeros((features,), f32)
    sum_offset_two = jnp.zeros((features,), f32)
    sum_router = jnp.zeros(weight_router.shape, f32)
    sum_expert_in = jnp.zeros(expert_in.shape, f32)
    sum_expert_out = jnp.zeros(expert_out.shape, f32)
    outputs = []
    input_grads = []
    for micro in range(MICRO):
        start = micro * row_count
        inputs = tokens[start : start + row_count].astype(f32)
        pre_one, normal_one, inverse_one = norm_forward(inputs, gain_one, offset_one)
        normed = pre_one.astype(bf16)
        projected = jnp.dot(normed, weight_qkv, preferred_element_type=f32).astype(bf16)
        projected = projected.reshape(IMG_MB, SEQ, 3, HEADS, HEAD_DIM)
        queries = projected[:, :, 0]
        key_rows = projected[:, :, 1]
        values = projected[:, :, 2]
        scores = (
            jnp.einsum("gqhd,gkhd->ghqk", queries, key_rows, preferred_element_type=f32) * SCALING
        )
        highest = jnp.max(scores, -1, keepdims=True)
        expos = jnp.exp(scores - highest)
        totals = jnp.sum(expos, -1, keepdims=True)
        log_total = highest + jnp.log(totals)
        attn_weights = (expos / totals).astype(bf16)
        attended = jnp.einsum(
            "ghqk,gkhd->gqhd", attn_weights, values, preferred_element_type=f32
        ).astype(bf16)
        attended = attended.reshape(row_count, features)
        middle = inputs + jnp.dot(attended, weight_out, preferred_element_type=f32)
        pre_two, normal_two, inverse_two = norm_forward(middle, gain_two, offset_two)
        normed_two = pre_two.astype(bf16)
        logits = jnp.dot(normed_two, weight_router, preferred_element_type=f32)
        gates = jax.nn.softmax(logits, -1)
        route_rows = routes[start : start + row_count]
        chosen, ranking, kept, pair_onehot = block_ranks(
            route_rows, priority[start : start + row_count], capacity
        )
        keep_float = kept.astype(f32)
        slot_send = jnp.where(kept, ranking, slots)
        slot_read = jnp.where(kept, ranking, 0)
        doubled = jnp.concatenate([normed_two, normed_two], 0)
        send = (
            jnp.zeros((experts, slots, features), bf16)
            .at[chosen, slot_send]
            .set(doubled, mode="drop")
        )
        received = lax.all_to_all(
            send.reshape(owners, per_owner, slots, features),
            "expert",
            split_axis=0,
            concat_axis=0,
            tiled=True,
        )
        hidden = jnp.einsum("sjcd,jdf->sjcf", received, expert_in, preferred_element_type=f32)
        active = gelu_value(hidden).astype(bf16)
        result = jnp.einsum(
            "sjcf,jfd->sjcd", active, expert_out, preferred_element_type=f32
        ).astype(bf16)
        back = lax.all_to_all(result, "expert", split_axis=0, concat_axis=0, tiled=True).reshape(
            experts, slots, features
        )
        pieces = back[chosen, slot_read].astype(f32) * keep_float[:, None]
        picked = jnp.take_along_axis(gates, route_rows, 1)
        gate_pair = jnp.concatenate([picked[:, 0], picked[:, 1]])
        mixed = pieces[:row_count] * picked[:, 0:1] + pieces[row_count:] * picked[:, 1:2]
        outputs.append((middle + mixed).astype(bf16))
        grad_out = cotangent[start : start + row_count].astype(f32)
        grad_doubled = jnp.concatenate([grad_out, grad_out], 0)
        dgate = jnp.sum(grad_doubled * pieces, -1)
        dpieces = (grad_doubled * (gate_pair * keep_float)[:, None]).astype(bf16)
        dgates = (
            pair_onehot[:row_count] * dgate[:row_count, None]
            + pair_onehot[row_count:] * dgate[row_count:, None]
        )
        dlogits = (gates * (dgates - jnp.sum(gates * dgates, -1, keepdims=True))).astype(bf16)
        grad_send = (
            jnp.zeros((experts, slots, features), bf16)
            .at[chosen, slot_send]
            .set(dpieces, mode="drop")
        )
        grad_received = lax.all_to_all(
            grad_send.reshape(owners, per_owner, slots, features),
            "expert",
            split_axis=0,
            concat_axis=0,
            tiled=True,
        )
        dactive = jnp.einsum(
            "sjcd,jfd->sjcf", grad_received, expert_out, preferred_element_type=f32
        )
        dhidden = (dactive * gelu_slope(hidden)).astype(bf16)
        grad_w_out = jnp.einsum("sjcf,sjcd->jfd", active, grad_received, preferred_element_type=f32)
        grad_w_in = jnp.einsum("sjcd,sjcf->jdf", received, dhidden, preferred_element_type=f32)
        sum_expert_in = sum_expert_in + grad_w_in
        sum_expert_out = sum_expert_out + grad_w_out
        dsent = jnp.einsum("sjcf,jdf->sjcd", dhidden, expert_in, preferred_element_type=f32).astype(
            bf16
        )
        dreturn = lax.all_to_all(dsent, "expert", split_axis=0, concat_axis=0, tiled=True).reshape(
            experts, slots, features
        )
        dpair = dreturn[chosen, slot_read].astype(f32) * keep_float[:, None]
        dnormed_two = (
            jnp.dot(dlogits, weight_router.T, preferred_element_type=f32)
            + dpair[:row_count]
            + dpair[row_count:]
        )
        sum_router = sum_router + jnp.dot(normed_two.T, dlogits, preferred_element_type=f32)
        sum_gain_two = sum_gain_two + jnp.sum(dnormed_two * normal_two, 0)
        sum_offset_two = sum_offset_two + jnp.sum(dnormed_two, 0)
        dmiddle = grad_out + norm_backward(dnormed_two, normal_two, inverse_two, gain_two)
        dbranch = dmiddle.astype(bf16)
        sum_out = sum_out + jnp.dot(attended.T, dbranch, preferred_element_type=f32)
        dattended = jnp.dot(dbranch, weight_out.T, preferred_element_type=f32).astype(bf16)
        dattended = dattended.reshape(IMG_MB, SEQ, HEADS, HEAD_DIM)
        again = (
            jnp.einsum("gqhd,gkhd->ghqk", queries, key_rows, preferred_element_type=f32) * SCALING
        )
        probs_again = jnp.exp(again - log_total)
        dvalues = jnp.einsum(
            "ghqk,gqhd->gkhd", probs_again.astype(bf16), dattended, preferred_element_type=f32
        )
        dweights = jnp.einsum("gqhd,gkhd->ghqk", dattended, values, preferred_element_type=f32)
        inner = jnp.sum(dweights * probs_again, -1, keepdims=True)
        dscores = (probs_again * (dweights - inner)).astype(bf16)
        dqueries = (
            jnp.einsum("ghqk,gkhd->gqhd", dscores, key_rows, preferred_element_type=f32) * SCALING
        )
        dkeys = (
            jnp.einsum("ghqk,gqhd->gkhd", dscores, queries, preferred_element_type=f32) * SCALING
        )
        dprojected = (
            jnp.stack([dqueries, dkeys, dvalues], 2).astype(bf16).reshape(row_count, 3 * features)
        )
        sum_qkv = sum_qkv + jnp.dot(normed.T, dprojected, preferred_element_type=f32)
        dnormed = jnp.dot(dprojected, weight_qkv.T, preferred_element_type=f32)
        sum_gain_one = sum_gain_one + jnp.sum(dnormed * normal_one, 0)
        sum_offset_one = sum_offset_one + jnp.sum(dnormed, 0)
        input_grads.append(
            (dmiddle + norm_backward(dnormed, normal_one, inverse_one, gain_one)).astype(bf16)
        )
    grad_expert_in, grad_expert_out = (
        lax.psum_scatter(
            sum_expert_in.astype(jnp.bfloat16), "dp", scatter_dimension=2, tiled=True
        ).astype(jnp.float32),
        lax.psum_scatter(
            sum_expert_out.astype(jnp.bfloat16), "dp", scatter_dimension=1, tiled=True
        ).astype(jnp.float32),
    )
    dense = (
        sum_gain_one,
        sum_offset_one,
        sum_qkv,
        sum_out,
        sum_gain_two,
        sum_offset_two,
        sum_router,
    )
    totals_all = (
        lax.psum(dense[0].astype(jnp.bfloat16), "expert").astype(jnp.float32),
        lax.psum(dense[1].astype(jnp.bfloat16), "expert").astype(jnp.float32),
        lax.psum(dense[2].astype(jnp.bfloat16), "expert").astype(jnp.float32),
        lax.psum(dense[3].astype(jnp.bfloat16), "expert").astype(jnp.float32),
        lax.psum(dense[4].astype(jnp.bfloat16), "expert").astype(jnp.float32),
        lax.psum(dense[5].astype(jnp.bfloat16), "expert").astype(jnp.float32),
        lax.psum(dense[6].astype(jnp.bfloat16), "expert").astype(jnp.float32),
    )
    owned = (
        lax.psum_scatter(
            totals_all[0].astype(jnp.bfloat16), "dp", scatter_dimension=0, tiled=True
        ).astype(jnp.float32),
        lax.psum_scatter(
            totals_all[1].astype(jnp.bfloat16), "dp", scatter_dimension=0, tiled=True
        ).astype(jnp.float32),
        lax.psum_scatter(
            totals_all[2].astype(jnp.bfloat16), "dp", scatter_dimension=0, tiled=True
        ).astype(jnp.float32),
        lax.psum_scatter(
            totals_all[3].astype(jnp.bfloat16), "dp", scatter_dimension=0, tiled=True
        ).astype(jnp.float32),
        lax.psum_scatter(
            totals_all[4].astype(jnp.bfloat16), "dp", scatter_dimension=0, tiled=True
        ).astype(jnp.float32),
        lax.psum_scatter(
            totals_all[5].astype(jnp.bfloat16), "dp", scatter_dimension=0, tiled=True
        ).astype(jnp.float32),
        lax.psum_scatter(
            totals_all[6].astype(jnp.bfloat16), "dp", scatter_dimension=0, tiled=True
        ).astype(jnp.float32),
    )
    block_out = jnp.concatenate(outputs, 0)
    grad_tokens = jnp.concatenate(input_grads, 0)
    return (
        block_out,
        grad_tokens,
        owned[0],
        owned[1],
        owned[2],
        owned[3],
        owned[4],
        owned[5],
        owned[6],
        grad_expert_in,
        grad_expert_out,
    )


SWAP = [(0, 1), (1, 0)]
OUTWARD = [(1, 0), (2, 3)]
SECOND = [(0, 1), (3, 2), (1, 3), (2, 0)]
MIDDLE = [(1, 2), (2, 1)]


def flip(bit):
    return [(i, i ^ bit) for i in range(4)]


def add(*pieces):
    total = pieces[0].astype(f32)
    for piece in pieces[1:]:
        total = total + piece.astype(f32)
    return total.astype(bf16)


def stage(*values):
    return lax.optimization_barrier(values)


def after(value, *others):
    return lax.optimization_barrier((value, *others))[0]


def paired(
    tokens,
    ln1_gain,
    ln1_bias,
    qkv_weight,
    out_weight,
    ln2_gain,
    ln2_bias,
    router_weight,
    expert_in,
    expert_out,
    routes,
    priority,
    capacity,
    cotangent,
):
    y, core, z, x = (lax.axis_index(name) for name in ("y", "core", "z", "x"))
    features = tokens.shape[1]
    experts = capacity.shape[0]
    width = qkv_weight.shape[0]
    count = experts // 2
    slots = 8 * (3 * TOP * IMG_MB * SEQ // (16 * experts) + 1)
    lanes = 4 * features

    order = jnp.arange(8, dtype=jnp.int32)
    place = (((order & 1) ^ y) << 1) | (((order >> 1) & 1) ^ core)
    for at, value in ((Z_AT, z), (X_AT, x), (Y_AT, y), (CORE_AT, core)):
        place = jnp.where(order == at, value, place)

    def swap(value, axis, pairs=SWAP):
        return lax.ppermute(value, axis, pairs)

    gains = (ln1_gain, ln1_bias, ln2_gain, ln2_bias)
    packed = pack(gains, qkv_weight, out_weight, router_weight.T)
    from_y = swap(packed, "y")
    one = quarter_of(after(place, packed), expert_in, expert_out)
    near = swap(one, "z", flip(1))
    centre = swap(one, "z", MIDDLE)
    cotp = pad_images(after(cotangent, one))
    cot_other = swap(cotp, "x")
    place, cotp = stage(place, cotp)
    tokp, slot, slotc = prepare(place, capacity, tokens, routes, priority)
    place, from_y, tokp, slot = stage(place, from_y, tokp, slot)
    two = jnp.concatenate([packed, from_y], 0)
    dense = (two, swap(two, "core"))

    place, near, centre = stage(place, near, centre)
    second_mid = swap(near, "z", MIDDLE)
    second_out = swap(centre, "z", OUTWARD)
    across = [swap(near, "y")]
    saved = [forward_images(0, place, tokp, dense, experts)]
    place, cot_other, first_n2 = stage(place, cot_other, saved[0][4])
    n2_other = [swap(first_n2, "x")]
    saved.append(forward_images(IMG_MB, place, tokp, dense, experts))
    place, last_n2, last_gates, second_mid, second_out, across[0], n2_other[0] = stage(
        place, saved[1][4], saved[1][5], second_mid, second_out, across[0], n2_other[0]
    )
    n2_other.append(swap(last_n2, "x"))
    tables = jnp.concatenate([slot, saved[0][5][None], last_gates[None]], 0)
    other = swap(tables, "x")
    second = second_mid + second_out
    outer = swap(second, "z", OUTWARD)
    across.append(swap(second, "y"))
    corner = [swap(piece, "core") for piece in (near, across[0])]

    n2 = [piece[4] for piece in saved] + n2_other
    cot = [piece.reshape(MICRO, ROWS, features) for piece in (cotp, cot_other)]
    tables = (slot, saved[0][5], saved[1][5], other)
    place, *corner = stage(place, *corner)
    pieces = (near, across[0], *corner)
    half1 = expert_apply(1, place, n2[:MICRO], cot[:1], tables[:3], pieces, slots, "own")
    place, *half1 = stage(place, *half1)
    out1 = expert_apply(1, place, n2[MICRO:], cot[1:], tables[3:], pieces, slots, "other", half1[2:4])
    place, outer, across[1], *out1 = stage(place, outer, across[1], *out1)
    third = centre + outer
    across.append(swap(third, "y"))
    corner = [swap(piece, "core") for piece in (second, across[1])]
    core1 = swap(out1[3], "core")
    place, *corner = stage(place, *corner)
    pieces = (second, across[1], *corner)
    out2 = expert_apply(2, place, n2, cot, tables, pieces, slots)
    place, across[2], core1, *out2 = stage(place, across[2], core1, *out2)
    corner = [swap(piece, "core") for piece in (third, across[2])]
    core2 = swap(out2[3], "core")
    side1 = swap(add(out1[2][1], core1[1]), "y")
    place, *corner = stage(place, *corner)
    pieces = (third, across[2], *corner)
    out3 = expert_apply(3, place, n2, cot, tables, pieces, slots)
    place, core2, side1, *out3 = stage(place, core2, side1, *out3)
    core3 = swap(out3[3], "core")
    side2 = swap(add(out2[2][1], core2[1]), "y")
    first_swap = swap(add(out1[2][0], core1[0], side1), "z", flip(1))
    out0 = expert_apply(0, place, n2, cot, tables, (expert_in, expert_out), slots)
    place, core3, side2, first_swap, *out0 = stage(place, core3, side2, first_swap, *out0)

    outs = (out0, half1, out2, out3)
    results, dxs, _, _, dgs = ([piece[i] for piece in outs] for i in range(5))
    outs = (out0, out1, out2, out3)
    other_results, other_dxs, _, _ = ([piece[i] for piece in outs] for i in range(4))
    dgos = [piece[-1] for piece in outs]
    dn2_mine = [combine(other, other_dxs, 0, 1)]
    rest, core_send, dn2_send, *dgos = stage(other, out0[3], dn2_mine[0], *dgos)
    dn2 = [swap(dn2_send, "x")]
    dg_other = swap(jnp.stack(dgos), "x")
    side3 = swap(add(out3[2][1], core3[1]), "y")
    second_swap = swap(add(out2[2][0], core2[0], side2), "z", SECOND)
    core0 = swap(core_send, "core")
    dn2_mine.append(combine(rest, other_dxs, 1, 1))
    mixed_mine = combine(after(rest, dn2_mine[1]), other_results, 0, MICRO)
    place, mixed_mine, core0, dn2[0], last, dg_other = stage(
        place, mixed_mine, core0, dn2[0], dn2_mine[1], dg_other
    )
    dn2.append(swap(last, "x"))

    columns = slotc.reshape(IMAGES, PAD, experts)

    def back_images(micro, place, before):
        rows = dn2[micro].reshape(ROWS, features)
        return backward_images(
            micro * IMG_MB, place, tokp, cotp, saved[micro], dgs, dg_other, slotc, rows, dense, dxs, before
        )

    first = back_images(0, place, ())
    place, second_swap, side3, dn2[1], *first = stage(place, second_swap, side3, dn2[1], *first)
    inner = (z == 1) | (z == 2)
    third_sum = add(out3[2][0], core3[0], side3, jnp.where(inner, second_swap, 0.0))
    third_swap = [swap(third_sum[0], "z", flip(3))]
    side0 = swap(add(out0[2][1], core0[1]), "y")
    mixed = swap(mixed_mine, "x")
    keep_send = back_images(1, place, tuple(first[1:]))
    place, third_swap[0], side0, mixed, *keep_send = stage(place, third_swap[0], side0, mixed, *keep_send)
    third_swap.append(swap(third_sum[1], "z", flip(3)))
    mixed = mixed.reshape(IMAGES, PAD, features)
    dtok = [first[0], keep_send[0]]
    keep, send = keep_send[1:]

    from_near = swap(send, "core")
    part = swap(add(keep[1], from_near[1]), "y")
    block_out, grad_tokens = finish([piece[3] for piece in saved], mixed, columns, dtok, results)
    part, third_swap[1], block_out, grad_tokens = stage(part, third_swap[1], block_out, grad_tokens)
    part = add(keep[0], from_near[0], part)
    cut = part.reshape(width + 16, 8, lanes // 8).transpose(1, 0, 2)
    cut = lax.all_to_all(cut, ("z", "x"), split_axis=0, concat_axis=0, tiled=True)
    cut = jnp.sum(cut.astype(f32), 0).astype(bf16)
    part = jnp.broadcast_to(cut[None], (8, *cut.shape))
    part = lax.all_to_all(part, ("z", "x"), split_axis=0, concat_axis=0, tiled=True)
    gq, go, gr, *lines = unpack(part, 3 * features, experts)
    lines = [line.reshape(width) for line in lines]
    grad_in, grad_back = settle(place, second_swap, out0[2], core0, side0, first_swap, *third_swap)

    return (block_out, grad_tokens, lines[0], lines[1], gq, go, lines[2], lines[3], gr.T, grad_in, grad_back)


def solution(mesh):
    if mesh.shape["dp"] == 4 and mesh.shape["expert"] == 8:
        mesh = Mesh(mesh.devices.reshape(2, 2, 4, 2), ("y", "core", "z", "x"))
        body, dp, expert = paired, ("y", "core"), ("z", "x")
    else:
        body, dp, expert = exchanged, ("dp",), ("expert",)
    rows = P((*dp, *expert), None)
    return jax.shard_map(
        body,
        mesh=mesh,
        in_specs=(
            rows,
            P(dp),
            P(dp),
            P(dp, None),
            P(dp, None),
            P(dp),
            P(dp),
            P(dp, None),
            P(expert, None, None),
            P(expert, None, None),
            rows,
            P((*dp, *expert)),
            P(),
            rows,
        ),
        out_specs=(
            rows,
            rows,
            P(dp),
            P(dp),
            P(dp, None),
            P(dp, None),
            P(dp),
            P(dp),
            P(dp, None),
            P(expert, None, dp),
            P(expert, dp, None),
        ),
        check_vma=False,
    )
```

```python
import functools
import jax
import jax.numpy as jnp
from jax import lax
from jax.experimental import pallas as pl
from jax.experimental.pallas import tpu as pltpu
from jax.sharding import Mesh
from jax.sharding import PartitionSpec as P

HEADS = 8
HEAD_DIM = 64
TOP = 2
SEQ = 197
IMG_MB = 3
MICRO = 2
EPSILON = 1e-06
SCALING = 0.125
ROOT_HALF = 0.7071067811865476
INV_ROOT_TWO_PI = 0.3989422804014327
PAD = 16 * ((SEQ + 15) // 16)
ROWS = IMG_MB * PAD
IMAGES = MICRO * IMG_MB
f32 = jnp.float32
bf16 = jnp.bfloat16
NN = (((1,), (0,)), ((), ()))
NT = (((1,), (1,)), ((), ()))
TN = (((0,), (0,)), ((), ()))


def mm(a, b, dims=NN):
    return lax.dot_general(a, b, dims, preferred_element_type=f32)


def whole(shape):
    zeros = (0,) * len(shape)
    return pl.BlockSpec(shape, lambda *_: zeros)


def pinned(value):
    return pltpu.with_memory_space_constraint(value, pltpu.HBM)


def params(mb=60):
    return pltpu.CompilerParams(vmem_limit_bytes=mb << 20)


SHARE = 1.0


def cost(flops, moved):
    return pl.CostEstimate(flops=int(flops * SHARE), bytes_accessed=int(moved * SHARE), transcendentals=0)


Z_AT, X_AT, Y_AT, CORE_AT = 4, 5, 6, 7


def expert_of(place_ref, index):
    return 2 * (place_ref[Z_AT] ^ (index & 3)) + (place_ref[X_AT] ^ (index >> 2))


def label_column(place_ref, experts):
    index = lax.broadcasted_iota(jnp.int32, (experts, 1), 0)
    label = jnp.zeros((experts, 1), jnp.int32)
    for r in range(experts):
        label = jnp.where(index == r, expert_of(place_ref, r), label)
    return label


def wide_transpose(rows, fill):
    pad = jnp.full((128 - rows.shape[0], rows.shape[1]), fill, f32)
    return jnp.transpose(jnp.concatenate([rows, pad], 0))


def pack_kernel(g1_ref, b1_ref, g2_ref, b2_ref, qkv_ref, out_ref, router_ref, packed_ref):
    width, columns = qkv_ref.shape
    packed_ref[0, :width, :columns] = qkv_ref[...]
    packed_ref[0, :width, columns:] = out_ref[...]
    pieces = [ref[...].astype(f32) for ref in (g1_ref, b1_ref, g2_ref, b2_ref)]
    router = router_ref[...].astype(f32)
    pieces += [router[e : e + 1, :] for e in range(router.shape[0])]
    rest = packed_ref.shape[2] - width * len(pieces)
    row = jnp.concatenate(pieces + [jnp.zeros((1, rest), f32)], 1)
    row = jnp.concatenate([row, jnp.zeros((15, row.shape[1]), f32)], 0)
    packed_ref[0, width:, :] = row.astype(bf16)


def pack(vectors_in, qkv, out, router):
    width, columns = qkv.shape
    rows = [vector.reshape(1, width) for vector in vectors_in]
    packed = (1, width + 16, columns + out.shape[1])
    inputs = (*rows, qkv, out, router)
    return pl.pallas_call(
        pack_kernel,
        grid=(1,),
        in_specs=[whole(value.shape) for value in inputs],
        out_specs=whole(packed),
        out_shape=jax.ShapeDtypeStruct(packed, bf16),
        compiler_params=params(60),
        cost_estimate=cost(0, 2_000_000),
        name="pack",
    )(*inputs)


def quarter_kernel(place_ref, in_ref, back_ref, one_ref, sem):
    span = one_ref.shape[1]
    start = pl.multiple_of(place_ref[0] * span, span)
    copies = (
        pltpu.make_async_copy(in_ref.at[0, :, pl.ds(start, span)], one_ref.at[0], sem.at[0]),
        pltpu.make_async_copy(back_ref.at[0, pl.ds(start, span), :], one_ref.at[1], sem.at[1]),
    )
    for copy in copies:
        copy.start()
    for copy in copies:
        copy.wait()


def quarter_of(place, expert_in, expert_out):
    shape = (2, expert_in.shape[1], expert_in.shape[2] // 4)
    return pl.pallas_call(
        quarter_kernel,
        grid_spec=pltpu.PrefetchScalarGridSpec(
            num_scalar_prefetch=1,
            grid=(1,),
            in_specs=[pl.BlockSpec(memory_space=pl.ANY)] * 2,
            out_specs=whole(shape),
            scratch_shapes=[pltpu.SemaphoreType.DMA((2,))],
        ),
        out_shape=jax.ShapeDtypeStruct(shape, bf16),
        compiler_params=params(60),
        cost_estimate=cost(0, 2_000_000),
        name="quarter",
    )(place, expert_in, expert_out)


def pad_rows(src_ref, dst_ref, buf):
    buf[pl.ds(0, src_ref.shape[0]), :] = src_ref[...].astype(f32)
    for image in range(IMAGES):
        piece = buf[pl.ds(image * SEQ, PAD), :]
        row = lax.broadcasted_iota(jnp.int32, piece.shape, 0)
        dst_ref[image] = jnp.where(row < SEQ, piece, 0.0).astype(bf16)


def pad_images(values):
    total, features = values.shape
    padded = (IMAGES, PAD, features)
    return pl.pallas_call(
        pad_rows,
        grid=(1,),
        in_specs=[whole(values.shape)],
        out_specs=whole(padded),
        out_shape=jax.ShapeDtypeStruct(padded, bf16),
        scratch_shapes=[pltpu.VMEM((8 * ((total + PAD) // 8), features), f32)],
        compiler_params=params(60),
        cost_estimate=cost(0, 4_000_000),
        name="pad",
    )(values)


def prepare_kernel(place_ref, cap_ref, tok_ref, route_ref, prio_ref, tokp_ref, slot_ref, slotc_ref, buf, keys):
    total = tok_ref.shape[0]
    experts = slot_ref.shape[1]
    pad_rows(tok_ref, tokp_ref, buf)
    keys[...] = jnp.full_like(keys, -1.0)
    keys[pl.ds(0, total), 0:2] = route_ref[...].astype(f32)
    keys[pl.ds(0, total), 2:3] = prio_ref[...].astype(f32)
    labels = label_column(place_ref, experts)
    limit = jnp.zeros((experts, 1), f32)
    for e in range(experts):
        limit = jnp.where(labels == e, cap_ref[e].astype(f32), limit)
    labels = labels.astype(f32)
    for block in range(MICRO):
        columns = []
        for image in range(IMG_MB):
            piece = keys[pl.ds((block * IMG_MB + image) * SEQ, PAD), :]
            row = lax.broadcasted_iota(jnp.int32, piece.shape, 0)
            columns.append(jnp.where(row < SEQ, piece, -1.0))
        column = jnp.concatenate(columns, 0)
        turned = jnp.transpose(column)
        key_column = jnp.where(column[:, 2:3] < 0.0, 1e6, column[:, 2:3])
        below = jnp.where(key_column < turned[2:3, :], 1.0, 0.0).astype(bf16)
        first = labels == turned[0:1, :]
        second = labels == turned[1:2, :]
        hot = jnp.concatenate([jnp.where(first, 1.0, 0.0), jnp.where(second, 1.0, 0.0)], 0)
        counts = mm(hot.astype(bf16), below)
        total_first = jnp.sum(hot[:experts], 1, keepdims=True)
        rank = jnp.where(
            first, counts[:experts], jnp.where(second, counts[experts:] + total_first, 1e6)
        )
        slot = jnp.where(rank < limit, rank, -1.0)
        slot_ref[block] = slot
        slotc_ref[block] = wide_transpose(slot, -1.0)[:, :experts]


def prepare(place, capacity, tokens, routes, priority):
    total, features = tokens.shape
    experts = capacity.shape[0]
    tall = 8 * ((total + PAD) // 8)
    priority = priority.reshape(total, 1)
    padded = (IMAGES, PAD, features)
    return pl.pallas_call(
        prepare_kernel,
        grid_spec=pltpu.PrefetchScalarGridSpec(
            num_scalar_prefetch=2,
            grid=(1,),
            in_specs=[whole(tokens.shape), whole(routes.shape), whole(priority.shape)],
            out_specs=(
                whole(padded),
                whole((MICRO, experts, ROWS)),
                whole((MICRO, ROWS, experts)),
            ),
            scratch_shapes=[pltpu.VMEM((tall, features), f32), pltpu.VMEM((tall, 128), f32)],
        ),
        out_shape=(
            jax.ShapeDtypeStruct(padded, bf16),
            jax.ShapeDtypeStruct((MICRO, experts, ROWS), f32),
            jax.ShapeDtypeStruct((MICRO, ROWS, experts), f32),
        ),
        compiler_params=params(60),
        cost_estimate=cost(0, 8_000_000),
        name="prepare",
    )(place, capacity, tokens, routes, priority)


def norm(values, gain, offset):
    center = values - jnp.mean(values, -1, keepdims=True)
    inverse = lax.rsqrt(jnp.mean(center * center, -1, keepdims=True) + EPSILON)
    normal = center * inverse
    return normal * gain + offset, normal, inverse


def load_dense(place_ref, two_ref, more_ref, w_s, sem):
    copies = [
        pltpu.make_async_copy((two_ref, more_ref)[j // 2].at[j % 2], w_s.at[place_ref[j]], sem.at[j])
        for j in range(4)
    ]
    for copy in copies:
        copy.start()
    return copies


def vectors(w_s):
    quarters = w_s.shape[0]
    width = w_s.shape[1] - 16
    row = [w_s[q, pl.ds(width, 1), :] for q in range(quarters)]

    def pick(index):
        return jnp.concatenate([r[:, index * width : (index + 1) * width] for r in row], 1)

    return pick


def dense_weights(w_s, features):
    width = w_s.shape[1] - 16
    qkv = w_s[:, :width, : 3 * features].reshape(features, 3 * features)
    out = w_s[:, :width, 3 * features :].reshape(features, features)
    return qkv, out


def router_rows(pick, place_ref, experts):
    table = jnp.concatenate([pick(4 + e) for e in range(experts)], 0)
    labels = label_column(place_ref, experts)
    order = labels == lax.broadcasted_iota(jnp.int32, (experts, experts), 1)
    return mm(jnp.where(order, 1.0, 0.0).astype(bf16), table).astype(bf16)


def half_mask(index, value):
    lane = lax.broadcasted_iota(jnp.int32, (1, 2 * HEAD_DIM), 1)
    return jnp.where((lane < HEAD_DIM) == (index == 0), value, 0.0).astype(bf16)


def forward_kernel(first, place_ref, tok_ref, two_ref, more_ref, proj_ref, prob_ref, att_ref, mid_ref, n2_ref, gate_ref, w_s, sem, in_sem, out_sem, tok_s, n1_s, proj_s, prob_s, att_s, mid_s, n2_s):
    features = tok_s.shape[1]
    copy_in = pltpu.make_async_copy(tok_ref.at[first // IMG_MB], tok_s, in_sem.at[0])
    copy_in.start()
    waits = load_dense(place_ref, two_ref, more_ref, w_s, sem)
    out_copies = [
        pltpu.make_async_copy(src, dst, out_sem.at[i])
        for i, (src, dst) in enumerate(
            ((proj_s, proj_ref), (prob_s, prob_ref), (att_s, att_ref), (mid_s, mid_ref), (n2_s, n2_ref))
        )
    ]
    copy_in.wait()
    for copy in waits:
        copy.wait()
    pick = vectors(w_s)
    qkv, out = dense_weights(w_s, features)
    gain, offset = pick(0).astype(f32), pick(1).astype(f32)

    @pl.loop(0, IMG_MB)
    def _(i):
        span = pl.ds(pl.multiple_of(i * PAD, PAD), PAD)
        pre, _, _ = norm(tok_s[span, :].astype(f32), gain, offset)
        n1_s[span, :] = pre.astype(bf16)

    proj_s[...] = mm(n1_s[...], qkv).astype(bf16)
    out_copies[0].start()
    column = lax.broadcasted_iota(jnp.int32, (1, PAD), 1)
    pair = 2 * HEAD_DIM

    @pl.loop(0, IMG_MB)
    def _(i):
        span = pl.ds(pl.multiple_of(i * PAD, PAD), PAD)
        for group in range(HEADS // 2):
            q2 = proj_s[span, group * pair : (group + 1) * pair]
            k2 = proj_s[span, features + group * pair : features + (group + 1) * pair]
            v2 = proj_s[span, 2 * features + group * pair : 2 * features + (group + 1) * pair]
            total = None
            for half in range(2):
                scores = mm(q2 * half_mask(half, SCALING), k2, NT)
                scores = jnp.where(column < SEQ, scores, -1e30)
                expos = jnp.exp(scores - jnp.max(scores, -1, keepdims=True))
                probs = (expos * (1.0 / jnp.sum(expos, -1, keepdims=True))).astype(bf16)
                prob_s[i, 2 * group + half] = probs
                piece = mm(probs, v2 * half_mask(half, 1.0))
                total = piece if total is None else total + piece
            att_s[span, group * pair : (group + 1) * pair] = total.astype(bf16)

    out_copies[1].start()
    out_copies[2].start()
    mid_s[...] = mm(att_s[...], out)
    gain_two, offset_two = pick(2).astype(f32), pick(3).astype(f32)

    @pl.loop(0, IMG_MB)
    def _(i):
        span = pl.ds(pl.multiple_of(i * PAD, PAD), PAD)
        middle = tok_s[span, :].astype(f32) + mid_s[span, :]
        mid_s[span, :] = middle
        pre, _, _ = norm(middle, gain_two, offset_two)
        n2_s[span, :] = pre.astype(bf16)

    out_copies[4].start()
    out_copies[3].start()
    router = router_rows(pick, place_ref, gate_ref.shape[0])
    logits = mm(router, n2_s[...], NT)
    expos = jnp.exp(logits - jnp.max(logits, 0, keepdims=True))
    gate_ref[...] = expos / jnp.sum(expos, 0, keepdims=True)
    for copy in out_copies:
        copy.wait()


def image(*tail):
    zeros = (0,) * len(tail)
    return pl.BlockSpec((1, *tail), lambda i, *_: (i, *zeros))


def forward_images(first, place, tokp, dense, experts):
    features = tokp.shape[2]
    count = IMG_MB
    flops = 2 * count * PAD * (4 * features * features + 2 * PAD * 256 * HEADS)
    shapes = (
        ((ROWS, 3 * features), bf16),
        ((count, HEADS, PAD, PAD), bf16),
        ((ROWS, features), bf16),
        ((ROWS, features), f32),
        ((ROWS, features), bf16),
    )
    scratch = [((ROWS, features), bf16), ((ROWS, features), bf16), *shapes]
    return pl.pallas_call(
        functools.partial(forward_kernel, first),
        grid_spec=pltpu.PrefetchScalarGridSpec(
            num_scalar_prefetch=1,
            grid=(1,),
            in_specs=[pl.BlockSpec(memory_space=pl.ANY)] * 3,
            out_specs=(*[pl.BlockSpec(memory_space=pl.ANY)] * 5, whole((experts, ROWS))),
            scratch_shapes=[
                pltpu.VMEM((4, *dense[0].shape[1:]), bf16),
                pltpu.SemaphoreType.DMA((4,)),
                pltpu.SemaphoreType.DMA((1,)),
                pltpu.SemaphoreType.DMA((5,)),
            ]
            + [pltpu.VMEM(*shape) for shape in scratch],
        ),
        out_shape=(
            *[pltpu.HBM(*shape) for shape in shapes],
            jax.ShapeDtypeStruct((experts, ROWS), f32),
        ),
        compiler_params=params(32),
        cost_estimate=cost(flops, count * 3_000_000),
        name="forward",
    )(place, tokp.reshape(MICRO, ROWS, features), *dense)


def gelu_pair(field):
    cdf = 0.5 * (1.0 + lax.erf(field * ROOT_HALF))
    return field * cdf, cdf + field * (jnp.exp(-0.5 * field * field) * INV_ROOT_TWO_PI)


def expert_kernel(index, own, part, place_ref, *refs):
    low, high = {"all": (0, 2 * MICRO), "own": (0, MICRO), "other": (MICRO, 2 * MICRO)}[part]
    blocks = high - low
    n2_refs = refs[:blocks]
    refs = refs[blocks:]
    cot_refs = refs[: blocks // MICRO]
    refs = refs[blocks // MICRO :]
    if low == 0:
        slot_ref, gate0_ref, gate1_ref = refs[:3]
        refs = refs[3:]
    if high > MICRO:
        other_ref = refs[0]
        refs = refs[1:]
    sources = 2 if own else 4
    w_refs = refs[:sources]
    refs = refs[sources:]
    if part == "other":
        keep_in_ref, send_in_ref = refs[:2]
        refs = refs[2:]
    res_ref, dx_ref, keep_ref, send_ref = refs[:4]
    refs = refs[4:]
    lines = {}
    for first in range(low, high, MICRO):
        lines[first] = refs[0]
        refs = refs[1:]
    w_s, sem, n2_s, cot_s, in_sem, x_s, g_s, raw_s, xt_s, gt_s, gs_s, r_acc, dx_acc, act_s, dh_s = refs
    step = pl.program_id(0)
    quarters, _, _, width = w_s.shape
    slots = x_s.shape[0] // blocks
    row = lax.broadcasted_iota(jnp.int32, (slots, ROWS), 0).astype(f32)

    def copies(j):
        if own:
            start = pl.multiple_of(place_ref[j] * width, width)
            return (
                pltpu.make_async_copy(w_refs[0].at[0, :, pl.ds(start, width)], w_s.at[j, 0], sem.at[2 * j]),
                pltpu.make_async_copy(w_refs[1].at[0, pl.ds(start, width), :], w_s.at[j, 1], sem.at[2 * j + 1]),
            )
        return (pltpu.make_async_copy(w_refs[j], w_s.at[j], sem.at[j]),)

    def slot_row(local):
        b = low + local
        if b < MICRO:
            return slot_ref[b, pl.ds(index, 1), :]
        return other_ref[b - MICRO, pl.ds(index + 4, 1), :]

    def gate_row(local):
        b = low + local
        if b < MICRO:
            return (gate0_ref, gate1_ref)[b][pl.ds(index, 1), :]
        return other_ref[b, pl.ds(index + 4, 1), :]

    def rows_in(b):
        return (
            pltpu.make_async_copy(n2_refs[b], n2_s.at[b], in_sem.at[2 * b]),
            pltpu.make_async_copy(cot_refs[b // MICRO].at[b % MICRO], cot_s.at[b], in_sem.at[2 * b + 1]),
        )

    @pl.when(step == 0)
    def _():
        for b in range(blocks):
            for copy in rows_in(b):
                copy.start()
        for j in range(quarters):
            for copy in copies(j):
                copy.start()
        r_acc[...] = jnp.zeros_like(r_acc)
        dx_acc[...] = jnp.zeros_like(dx_acc)
        for b in range(blocks):
            for copy in rows_in(b):
                copy.wait()
            span = pl.ds(b * slots, slots)
            hit = row == slot_row(b)
            pick = jnp.where(hit, 1.0, 0.0)
            gate = jnp.sum(jnp.where(hit, gate_row(b), 0.0), 1, keepdims=True)
            pick = pick.astype(bf16)
            x = mm(pick, n2_s[b])
            raw = mm(pick, cot_s[b])
            x_s[span, :] = x.astype(bf16)
            raw_s[span, :] = raw.astype(bf16)
            g = gate * raw
            g_s[span, :] = g.astype(bf16)
            gs_s[span, :] = jnp.broadcast_to(gate, (slots, 128))
        xt_s[...] = jnp.transpose(x_s[...])
        gt_s[...] = jnp.transpose(g_s[...])

    for j in range(quarters):

        @pl.when(step == j)
        def _():
            for copy in copies(j):
                copy.wait()

    w_in = w_s[step, 0]
    w_out = w_s[step, 1]
    rows = blocks * slots
    for r in range(1):
        span = pl.ds(r * rows, rows)
        act, slope = gelu_pair(mm(x_s[span, :], w_in))
        act = act.astype(bf16)
        dh = (mm(g_s[span, :], w_out, NT) * slope).astype(bf16)
        act_s[span, :] = act
        dh_s[span, :] = dh
        r_acc[span, :] += mm(act, w_out)
        dx_acc[span, :] += mm(dh, w_in, NT)
    grad_in = mm(xt_s[...], dh_s[...])
    grad_out = mm(gt_s[...], act_s[...])
    if part == "other":
        early = step < quarters // 2
        grad_in += jnp.where(early, keep_in_ref[0, 0].astype(f32), send_in_ref[0, 0].astype(f32))
        grad_out += jnp.where(early, keep_in_ref[0, 1].astype(f32), send_in_ref[0, 1].astype(f32))

    @pl.when(step < quarters // 2)
    def _():
        keep_ref[0, 0] = grad_in.astype(bf16)
        keep_ref[0, 1] = grad_out.astype(bf16)

    @pl.when(step >= quarters // 2)
    def _():
        send_ref[0, 0] = grad_in.astype(bf16)
        send_ref[0, 1] = grad_out.astype(bf16)

    @pl.when(step == quarters - 1)
    def _():
        dx_ref[...] = dx_acc[...].astype(bf16).reshape(dx_ref.shape)
        for b in range(blocks):
            span = pl.ds(b * slots, slots)
            res = r_acc[span, :].astype(bf16).astype(f32)
            dgate = jnp.sum(res * raw_s[span, :].astype(f32), 1, keepdims=True)
            res_ref[b] = (res * gs_s[span, 0:1]).astype(bf16)
            hit = row == slot_row(b)
            line = jnp.sum(jnp.where(hit, dgate, 0.0), 0, keepdims=True)
            lines[low + b - b % MICRO][pl.ds(b % MICRO, 1), :] = line


def expert_apply(index, place, n2, cot, tables, weights, slots, part="all", before=()):
    blocks = len(n2)
    features = n2[0].shape[1]
    own = len(weights) == 2
    quarters = 4
    width = weights[0].shape[2] // (4 if own else 1)
    rows = blocks * slots

    def fixed(shape):
        zeros = (0,) * len(shape)
        return pl.BlockSpec(shape, lambda *_: zeros)

    half = quarters // 2
    keep = pl.BlockSpec((1, 2, features, width), lambda i, _: (jnp.minimum(i, half - 1), 0, 0, 0))
    send = pl.BlockSpec((1, 2, features, width), lambda i, _: (jnp.maximum(i - half, 0), 0, 0, 0))
    groups = blocks // MICRO
    return pl.pallas_call(
        functools.partial(expert_kernel, index, own, part),
        grid_spec=pltpu.PrefetchScalarGridSpec(
            num_scalar_prefetch=1,
            grid=(quarters,),
            in_specs=[pl.BlockSpec(memory_space=pl.ANY)] * (blocks + len(cot))
            + [fixed(piece.shape) for piece in tables]
            + [pl.BlockSpec(memory_space=pl.ANY)] * len(weights)
            + [keep, send][: len(before)],
            out_specs=(
                fixed((blocks, slots, features)),
                fixed((blocks, slots, features)),
                keep,
                send,
                *[fixed((MICRO, ROWS))] * groups,
            ),
            scratch_shapes=[
                pltpu.VMEM((quarters, 2, features, width), bf16),
                pltpu.SemaphoreType.DMA((2 * quarters,)),
                pltpu.VMEM((blocks, ROWS, features), bf16),
                pltpu.VMEM((blocks, ROWS, features), bf16),
                pltpu.SemaphoreType.DMA((2 * blocks,)),
                pltpu.VMEM((rows, features), bf16),
                pltpu.VMEM((rows, features), bf16),
                pltpu.VMEM((rows, features), bf16),
                pltpu.VMEM((features, rows), bf16),
                pltpu.VMEM((features, rows), bf16),
                pltpu.VMEM((rows, 128), f32),
                pltpu.VMEM((rows, features), f32),
                pltpu.VMEM((rows, features), f32),
                pltpu.VMEM((rows, width), bf16),
                pltpu.VMEM((rows, width), bf16),
            ],
        ),
        out_shape=(
            pltpu.HBM((blocks, slots, features), bf16),
            pltpu.HBM((blocks, slots, features), bf16),
            pltpu.HBM((half, 2, features, width), bf16),
            pltpu.HBM((half, 2, features, width), bf16),
            *[jax.ShapeDtypeStruct((MICRO, ROWS), f32)] * groups,
        ),
        compiler_params=params(40),
        cost_estimate=cost(12 * rows * features * width * quarters, 4_000_000 + 3_000_000 * blocks),
        name="expert",
    )(place, *n2, *cot, *tables, *weights, *map(pinned, before))


def selector(columns, slots):
    count = columns.shape[1]
    lane = lax.broadcasted_iota(jnp.int32, (columns.shape[0], slots), 1).astype(f32)
    pieces = [jnp.where(columns[:, k : k + 1] == lane, 1.0, 0.0).astype(bf16) for k in range(count)]
    return jnp.concatenate(pieces, 1)


def combine_kernel(count, slot_ref, *refs):
    slots = refs[0].shape[1]
    pick = selector(wide_transpose(slot_ref[0, count:, :], -1.0)[:, :count], slots)
    refs[count][0] = mm(pick, jnp.concatenate([r[0] for r in refs[:count]], 0)).astype(bf16)


def combine(slot, pieces, block, blocks):
    count = len(pieces)
    _, slots, features = pieces[0].shape
    late = pl.BlockSpec((1, slots, features), lambda i: (i + block + MICRO, 0, 0))
    short = pl.BlockSpec((1, slots, features), lambda i: (i + block, 0, 0))
    return pl.pallas_call(
        functools.partial(combine_kernel, count),
        grid=(blocks,),
        in_specs=[pl.BlockSpec((1, 2 * count, ROWS), lambda i: (i + block, 0, 0))]
        + [late if piece.shape[0] > MICRO else short for piece in pieces],
        out_specs=image(ROWS, features),
        out_shape=jax.ShapeDtypeStruct((blocks, ROWS, features), bf16),
        compiler_params=params(24),
        cost_estimate=cost(2 * blocks * ROWS * features * slots * count, 5_000_000),
        name="combine",
    )(slot, *map(pinned, pieces))


def finish_kernel(count, mid0_ref, mid1_ref, part_ref, slotc_ref, dtok0_ref, dtok1_ref, *refs):
    out_ref, dout_ref, buf, dbuf = refs[count:]
    slots = refs[0].shape[1]
    step = pl.program_id(0)
    choose = selector(slotc_ref[0, :, :count], slots)
    mixed = mm(choose, jnp.concatenate([r[0] for r in refs[:count]], 0)) + part_ref[0].astype(f32)
    early = step < IMG_MB
    middle = jnp.where(early, mid0_ref[...], mid1_ref[...])
    value = middle + mixed
    grad = jnp.where(early, dtok0_ref[...].astype(f32), dtok1_ref[...].astype(f32))
    for i in range(IMAGES):

        @pl.when(step == i)
        def _():
            buf[pl.ds(i * SEQ, SEQ), :] = value[:SEQ]
            dbuf[pl.ds(i * SEQ, SEQ), :] = grad[:SEQ]

    @pl.when(step == IMAGES - 1)
    def _():
        out_ref[...] = buf[pl.ds(0, out_ref.shape[0]), :].astype(bf16)
        dout_ref[...] = dbuf[pl.ds(0, out_ref.shape[0]), :].astype(bf16)


def finish(middles, part, slotc, dtoks, results):
    count = len(results)
    _, slots, features = results[0].shape
    experts = slotc.shape[2]
    piece = pl.BlockSpec((1, slots, features), lambda i: (lax.div(i, IMG_MB), 0, 0))
    total = IMAGES * SEQ
    tall = 8 * ((total + 7) // 8)
    early = pl.BlockSpec((PAD, features), lambda i: (jnp.minimum(i, IMG_MB - 1), 0))
    later = pl.BlockSpec((PAD, features), lambda i: (jnp.maximum(i - IMG_MB, 0), 0))
    return pl.pallas_call(
        functools.partial(finish_kernel, count),
        grid=(IMAGES,),
        in_specs=[early, later, image(PAD, features), image(PAD, experts), early, later] + [piece] * count,
        out_specs=(whole((total, features)), whole((total, features))),
        out_shape=(jax.ShapeDtypeStruct((total, features), bf16),) * 2,
        scratch_shapes=[pltpu.VMEM((tall, features), f32)] * 2,
        compiler_params=params(24),
        cost_estimate=cost(4 * ROWS * features * slots * count, 15_000_000),
        name="finish",
    )(*middles, part, slotc, *dtoks, *results)


def norm_back(grad, normal, inverse, gain):
    scaled = grad * gain
    return inverse * (
        scaled
        - jnp.mean(scaled, -1, keepdims=True)
        - normal * jnp.mean(scaled * normal, -1, keepdims=True)
    )


def backward_kernel(first, count, place_ref, gate_ref, slotc_ref, dgo_ref, *refs):
    dg_refs = refs[:count]
    sources = refs[count : count + 8]
    refs = refs[count + 8 :]
    two_ref, more_ref = refs[:2]
    dx_refs = refs[2 : 2 + count]
    refs = refs[2 + count :]
    chained = first > 0
    if chained:
        before_ref, before_row_ref = refs[:2]
        dtok_ref, keep_ref, send_ref = refs[2:5]
        acc_s, acc_sem, row_ref = refs[5:8]
        refs = refs[8:]
    else:
        dtok_ref, acc_ref, row_ref = refs[:3]
        acc_s, acc_sem = refs[3:5]
        refs = refs[5:]
    w_s, sem, in_sem, dx_sem = refs[:4]
    tok_s, cot_s, proj_s, prob_s, att_s, mid_s, n2_s, dn2_s = stores = refs[4:12]
    dx_s, dbr_s, datt_s, dproj_s, n1_s, sum_s = refs[12:]
    micro = first // IMG_MB
    features = tok_s.shape[1]
    experts = 2 * count
    slots = dx_s.shape[0] // count
    copies = []
    for i, (src, dst) in enumerate(zip(sources, stores)):
        copies.append(pltpu.make_async_copy(src.at[micro] if i < 2 else src, dst, in_sem.at[i]))
    tok_in, cot_in, proj_in, prob_in, att_in, mid_in, n2_in, dn2_in = copies
    dx_in = [
        pltpu.make_async_copy(dx_refs[k].at[micro], dx_s.at[pl.ds(k * slots, slots), :], dx_sem.at[k])
        for k in range(count)
    ]
    for copy in (*dx_in, dn2_in, n2_in):
        copy.start()
    dense_in = load_dense(place_ref, two_ref, more_ref, w_s, sem)
    for copy in (mid_in, cot_in, att_in, proj_in, prob_in, tok_in):
        copy.start()
    if chained:
        acc_in = pltpu.make_async_copy(before_ref, acc_s, acc_sem.at[0])
        acc_in.start()
        row_ref[...] = before_row_ref[...]
    else:
        row_ref[...] = jnp.zeros_like(row_ref)
    choose = selector(slotc_ref[0, :, :count], slots)
    gates = gate_ref[...]
    dgates = [ref[pl.ds(micro, 1), :] for ref in dg_refs] + [dgo_ref[k, pl.ds(micro, 1), :] for k in range(count)]
    dgates = jnp.concatenate(dgates, 0)
    dlogits = (gates * (dgates - jnp.sum(gates * dgates, 0, keepdims=True))).astype(bf16)
    for copy in (*dx_in, dn2_in, n2_in, *dense_in):
        copy.wait()
    pick = vectors(w_s)
    qkv, out = dense_weights(w_s, features)
    router = router_rows(pick, place_ref, experts)
    row_ref[8 : 8 + experts, :] += mm(dlogits, n2_s[...])
    sum_s[...] = mm(choose, dx_s[...]) + mm(dlogits, router, TN)
    mid_in.wait()
    cot_in.wait()
    gain_two = pick(2).astype(f32)

    @pl.loop(0, IMG_MB)
    def _(i):
        span = pl.ds(pl.multiple_of(i * PAD, PAD), PAD)
        dn2 = sum_s[span, :] + dn2_s[span, :].astype(f32)
        _, normal_two, inverse_two = norm(mid_s[span, :], gain_two, 0.0)
        row_ref[2:3, :] += jnp.sum(dn2 * normal_two, 0, keepdims=True)
        row_ref[3:4, :] += jnp.sum(dn2, 0, keepdims=True)
        dmiddle = cot_s[span, :].astype(f32) + norm_back(dn2, normal_two, inverse_two, gain_two)
        mid_s[span, :] = dmiddle
        dbr_s[span, :] = dmiddle.astype(bf16)

    att_in.wait()
    if chained:
        acc_in.wait()
    grad_out = mm(att_s[...], dbr_s[...], TN)
    if chained:
        acc_s[:, 3 * features :] += grad_out
    else:
        acc_s[:, 3 * features :] = grad_out
    datt_s[...] = mm(dbr_s[...], out, NT).astype(bf16)
    proj_in.wait()
    prob_in.wait()
    tok_in.wait()
    pair = 2 * HEAD_DIM
    gain_one, offset_one = pick(0).astype(f32), pick(1).astype(f32)

    @pl.loop(0, IMG_MB)
    def _(i):
        span = pl.ds(pl.multiple_of(i * PAD, PAD), PAD)
        pre, _, _ = norm(tok_s[span, :].astype(f32), gain_one, offset_one)
        n1_s[span, :] = pre.astype(bf16)
        for group in range(HEADS // 2):
            at = [part * features + group * pair for part in range(3)]
            q2, k2, v2 = (proj_s[span, start : start + pair] for start in at)
            d2 = datt_s[span, group * pair : (group + 1) * pair]
            dq = dk = dv = None
            for half in range(2):
                probs = prob_s[i, 2 * group + half]
                wide = probs.astype(f32)
                dm = d2 * half_mask(half, 1.0)
                dweights = mm(dm, v2, NT)
                inner = jnp.sum(dweights * wide, -1, keepdims=True)
                dscores = (wide * (dweights - inner)).astype(bf16)
                part_q = mm(dscores, k2 * half_mask(half, SCALING))
                part_k = mm(dscores, q2 * half_mask(half, SCALING), TN)
                part_v = mm(probs, dm, TN)
                dq = part_q if dq is None else dq + part_q
                dk = part_k if dk is None else dk + part_k
                dv = part_v if dv is None else dv + part_v
            for start, value in zip(at, (dq, dk, dv)):
                dproj_s[span, start : start + pair] = value.astype(bf16)

    grad_qkv = mm(n1_s[...], dproj_s[...], TN)
    if chained:
        acc_s[:, : 3 * features] += grad_qkv
    else:
        acc_s[:, : 3 * features] = grad_qkv
        acc_out = pltpu.make_async_copy(acc_s, acc_ref, acc_sem.at[0])
        acc_out.start()
    sum_s[...] = mm(dproj_s[...], qkv, NT)

    @pl.loop(0, IMG_MB)
    def _(i):
        span = pl.ds(pl.multiple_of(i * PAD, PAD), PAD)
        dnormed = sum_s[span, :]
        _, normal_one, inverse_one = norm(tok_s[span, :].astype(f32), gain_one, offset_one)
        row_ref[0:1, :] += jnp.sum(dnormed * normal_one, 0, keepdims=True)
        row_ref[1:2, :] += jnp.sum(dnormed, 0, keepdims=True)
        dtok_ref[span, :] = (mid_s[span, :] + norm_back(dnormed, normal_one, inverse_one, gain_one)).astype(bf16)

    if not chained:
        acc_out.wait()
        return
    width = keep_ref.shape[1] - 16
    lines = [row_ref[i : i + 1, :] for i in range(4)]
    for e in range(experts):
        line = jnp.zeros((1, features), f32)
        for r in range(experts):
            line = jnp.where(expert_of(place_ref, r) == e, row_ref[8 + r : 9 + r, :], line)
        lines.append(line)
    blank = jnp.zeros((1, 4 * features - (4 + experts) * width), f32)
    tails = []
    for q in range(4):
        parts = [line[:, q * width : (q + 1) * width] for line in lines]
        tails.append(jnp.concatenate(parts + [blank], 1))
    for j in range(4):
        quarter = place_ref[j]
        to = (keep_ref, send_ref)[j // 2]
        to[j % 2, :width, :] = acc_s[pl.ds(pl.multiple_of(quarter * width, width), width), :].astype(bf16)
        tail = tails[0]
        for q in range(1, 4):
            tail = jnp.where(quarter == q, tails[q], tail)
        tail = jnp.concatenate([tail, jnp.zeros((15, tail.shape[1]), f32)], 0)
        to[j % 2, width:, :] = tail.astype(bf16)


def backward_images(first, place, tokp, cotp, saved, dgs, dg_other, slotc, dn2_part, dense, dxs, before):
    projected, probs, attended, middle, n2, gates = saved
    count = len(dxs)
    features = tokp.shape[2]
    experts = 2 * count
    slots = dxs[0].shape[1]
    totals = ((features, 4 * features), (8 + experts, features))
    packed = (2, *dense[0].shape[1:])
    anywhere = pl.BlockSpec(memory_space=pl.ANY)
    flat = (MICRO, ROWS, features)
    sources = (tokp.reshape(flat), cotp.reshape(flat), projected, probs, attended, middle, n2, dn2_part)
    out_specs = [whole((ROWS, features))]
    out_shape = [jax.ShapeDtypeStruct((ROWS, features), bf16)]
    scratch = [pltpu.VMEM(totals[0], f32), pltpu.SemaphoreType.DMA((1,))]
    if before:
        out_specs += [whole(packed)] * 2
        out_shape += [jax.ShapeDtypeStruct(packed, bf16)] * 2
        scratch.append(pltpu.VMEM(totals[1], f32))
        extra = [anywhere, whole(totals[1])]
    else:
        out_specs += [anywhere, whole(totals[1])]
        out_shape += [jax.ShapeDtypeStruct(shape, f32) for shape in totals]
        extra = []
    scratch += [
        pltpu.VMEM((4, *dense[0].shape[1:]), bf16),
        pltpu.SemaphoreType.DMA((4,)),
        pltpu.SemaphoreType.DMA((8,)),
        pltpu.SemaphoreType.DMA((count,)),
    ]
    scratch += [pltpu.VMEM((ROWS, features), bf16)] * 2
    scratch += [pltpu.VMEM(piece.shape, piece.dtype) for piece in sources[2:]]
    scratch += [
        pltpu.VMEM((count * slots, features), bf16),
        pltpu.VMEM((ROWS, features), bf16),
        pltpu.VMEM((ROWS, features), bf16),
        pltpu.VMEM((ROWS, 3 * features), bf16),
        pltpu.VMEM((ROWS, features), bf16),
        pltpu.VMEM((ROWS, features), f32),
    ]
    micro = first // IMG_MB
    return pl.pallas_call(
        functools.partial(backward_kernel, first, count),
        grid_spec=pltpu.PrefetchScalarGridSpec(
            num_scalar_prefetch=1,
            grid=(1,),
            in_specs=[
                whole(gates.shape),
                pl.BlockSpec((1, ROWS, experts), lambda i, _: (micro, 0, 0)),
                whole(dg_other.shape),
            ]
            + [whole(piece.shape) for piece in dgs]
            + [anywhere] * (10 + count)
            + extra,
            out_specs=tuple(out_specs),
            scratch_shapes=scratch,
        ),
        out_shape=tuple(out_shape),
        compiler_params=params(40),
        cost_estimate=cost(40 * ROWS * features * features, 15_000_000),
        name="backward",
    )(place, gates, slotc, dg_other, *dgs, *sources, *dense, *dxs, *before)


def settle_kernel(place_ref, far_ref, *refs):
    in_ref, back_ref = refs[-2:]
    z = place_ref[Z_AT]
    outer = jnp.where((z == 0) | (z == 3), 1.0, 0.0)

    def total(i):
        value = far_ref[i].astype(f32) * outer + refs[i - 4][...].astype(f32)
        for ref in refs[:-4]:
            piece = ref[0, i] if len(ref.shape) == 4 else ref[i]
            value = value + piece.astype(f32)
        return value

    in_ref[0] = total(0)
    back_ref[0] = jnp.transpose(total(1))


def settle(place, *pieces):
    features, span = pieces[-1].shape

    def spec(piece):
        shape = (1, *piece.shape[1:]) if len(piece.shape) == 4 else piece.shape
        return whole(shape)

    return pl.pallas_call(
        settle_kernel,
        grid_spec=pltpu.PrefetchScalarGridSpec(
            num_scalar_prefetch=1,
            grid=(1,),
            in_specs=[spec(piece) for piece in pieces],
            out_specs=(whole((1, features, span)), whole((1, span, features))),
        ),
        out_shape=(
            jax.ShapeDtypeStruct((1, features, span), f32),
            jax.ShapeDtypeStruct((1, span, features), f32),
        ),
        compiler_params=params(24),
        cost_estimate=cost(0, 5_000_000),
        name="settle",
    )(place, *map(pinned, pieces))


def unpack_kernel(part_ref, qkv_ref, out_ref, router_ref, g1_ref, b1_ref, g2_ref, b2_ref):
    width, columns = qkv_ref.shape
    pieces, _, lanes = part_ref.shape
    for i in range(pieces):
        value = part_ref[i, :width, :].astype(f32)
        at = i * lanes
        if at < columns:
            qkv_ref[:, at : at + lanes] = value
        else:
            out_ref[:, at - columns : at - columns + lanes] = value
    row = jnp.concatenate([part_ref[i, width:, :].astype(f32)[0:1] for i in range(pieces)], 1)
    for i, ref in enumerate((g1_ref, b1_ref, g2_ref, b2_ref)):
        ref[...] = row[:, i * width : (i + 1) * width]
    lines = [row[:, (4 + e) * width : (5 + e) * width] for e in range(router_ref.shape[0])]
    router_ref[...] = jnp.concatenate(lines, 0)


def unpack(part, columns, experts):
    pieces, height, lanes = part.shape
    width = height - 16
    line = (1, width)
    shapes = ((width, columns), (width, pieces * lanes - columns), (experts, width), line, line, line, line)
    return pl.pallas_call(
        unpack_kernel,
        grid=(1,),
        in_specs=[whole(part.shape)],
        out_specs=tuple(whole(shape) for shape in shapes),
        out_shape=tuple(jax.ShapeDtypeStruct(shape, f32) for shape in shapes),
        compiler_params=params(24),
        cost_estimate=cost(0, 3_000_000),
        name="unpack",
    )(part)


def norm_forward(values, gain, offset):
    center = values - jnp.mean(values, -1, keepdims=True)
    inverse = lax.rsqrt(jnp.mean(center * center, -1, keepdims=True) + EPSILON)
    normal = center * inverse
    return (normal * gain + offset, normal, inverse)


def norm_backward(grad, normal, inverse, gain):
    scaled = grad * gain
    return inverse * (
        scaled
        - jnp.mean(scaled, -1, keepdims=True)
        - normal * jnp.mean(scaled * normal, -1, keepdims=True)
    )


def gelu_value(field):
    return 0.5 * field * (1.0 + lax.erf(field * ROOT_HALF))


def gelu_slope(field):
    return (
        0.5 * (1.0 + lax.erf(field * ROOT_HALF))
        + field * jnp.exp(-0.5 * field * field) * INV_ROOT_TWO_PI
    )


def block_ranks(route_rows, order_keys, capacity):
    count = order_keys.shape[0]
    expert_count = capacity.shape[0]
    chosen = jnp.concatenate([route_rows[:, 0], route_rows[:, 1]])
    sort_keys = jnp.concatenate([order_keys, order_keys + count])
    positions = jnp.arange(2 * count, dtype=jnp.int32)
    inverse = jnp.zeros((2 * count,), jnp.int32).at[sort_keys].set(positions)
    ordered = chosen[inverse]
    labels = jnp.arange(expert_count, dtype=jnp.int32)
    onehot = (ordered[:, None] == labels[None, :]).astype(jnp.int32)
    before = jnp.cumsum(onehot, 0) - onehot
    rank_sorted = jnp.sum(before * onehot, 1)
    ranking = jnp.zeros((2 * count,), jnp.int32).at[inverse].set(rank_sorted)
    pair_onehot = chosen[:, None] == labels[None, :]
    limit = jnp.sum(pair_onehot.astype(jnp.int32) * capacity[None, :], 1)
    return (chosen, ranking, ranking < limit, pair_onehot.astype(jnp.float32))


def exchanged(
    tokens,
    ln1_gain,
    ln1_bias,
    qkv_weight,
    out_weight,
    ln2_gain,
    ln2_bias,
    router_weight,
    expert_in,
    expert_out,
    routes,
    priority,
    capacity,
    cotangent,
):
    f32 = jnp.float32
    bf16 = jnp.bfloat16
    gathered = (
        lax.all_gather(ln1_gain, "dp", axis=0, tiled=True),
        lax.all_gather(ln1_bias, "dp", axis=0, tiled=True),
        lax.all_gather(qkv_weight, "dp", axis=0, tiled=True),
        lax.all_gather(out_weight, "dp", axis=0, tiled=True),
        lax.all_gather(ln2_gain, "dp", axis=0, tiled=True),
        lax.all_gather(ln2_bias, "dp", axis=0, tiled=True),
        lax.all_gather(router_weight, "dp", axis=0, tiled=True),
    )
    gain_one = gathered[0].astype(f32)
    offset_one = gathered[1].astype(f32)
    weight_qkv = gathered[2]
    weight_out = gathered[3]
    gain_two = gathered[4].astype(f32)
    offset_two = gathered[5].astype(f32)
    weight_router = gathered[6]
    features = tokens.shape[1]
    owners = lax.axis_size("expert")
    per_owner = expert_in.shape[0]
    experts = owners * per_owner
    slots = 8 * (3 * TOP * IMG_MB * SEQ // (16 * experts) + 1)
    row_count = IMG_MB * SEQ
    sum_gain_one = jnp.zeros((features,), f32)
    sum_offset_one = jnp.zeros((features,), f32)
    sum_qkv = jnp.zeros(weight_qkv.shape, f32)
    sum_out = jnp.zeros(weight_out.shape, f32)
    sum_gain_two = jnp.zeros((features,), f32)
    sum_offset_two = jnp.zeros((features,), f32)
    sum_router = jnp.zeros(weight_router.shape, f32)
    sum_expert_in = jnp.zeros(expert_in.shape, f32)
    sum_expert_out = jnp.zeros(expert_out.shape, f32)
    outputs = []
    input_grads = []
    for micro in range(MICRO):
        start = micro * row_count
        inputs = tokens[start : start + row_count].astype(f32)
        pre_one, normal_one, inverse_one = norm_forward(inputs, gain_one, offset_one)
        normed = pre_one.astype(bf16)
        projected = jnp.dot(normed, weight_qkv, preferred_element_type=f32).astype(bf16)
        projected = projected.reshape(IMG_MB, SEQ, 3, HEADS, HEAD_DIM)
        queries = projected[:, :, 0]
        key_rows = projected[:, :, 1]
        values = projected[:, :, 2]
        scores = (
            jnp.einsum("gqhd,gkhd->ghqk", queries, key_rows, preferred_element_type=f32) * SCALING
        )
        highest = jnp.max(scores, -1, keepdims=True)
        expos = jnp.exp(scores - highest)
        totals = jnp.sum(expos, -1, keepdims=True)
        log_total = highest + jnp.log(totals)
        attn_weights = (expos / totals).astype(bf16)
        attended = jnp.einsum(
            "ghqk,gkhd->gqhd", attn_weights, values, preferred_element_type=f32
        ).astype(bf16)
        attended = attended.reshape(row_count, features)
        middle = inputs + jnp.dot(attended, weight_out, preferred_element_type=f32)
        pre_two, normal_two, inverse_two = norm_forward(middle, gain_two, offset_two)
        normed_two = pre_two.astype(bf16)
        logits = jnp.dot(normed_two, weight_router, preferred_element_type=f32)
        gates = jax.nn.softmax(logits, -1)
        route_rows = routes[start : start + row_count]
        chosen, ranking, kept, pair_onehot = block_ranks(
            route_rows, priority[start : start + row_count], capacity
        )
        keep_float = kept.astype(f32)
        slot_send = jnp.where(kept, ranking, slots)
        slot_read = jnp.where(kept, ranking, 0)
        doubled = jnp.concatenate([normed_two, normed_two], 0)
        send = (
            jnp.zeros((experts, slots, features), bf16)
            .at[chosen, slot_send]
            .set(doubled, mode="drop")
        )
        received = lax.all_to_all(
            send.reshape(owners, per_owner, slots, features),
            "expert",
            split_axis=0,
            concat_axis=0,
            tiled=True,
        )
        hidden = jnp.einsum("sjcd,jdf->sjcf", received, expert_in, preferred_element_type=f32)
        active = gelu_value(hidden).astype(bf16)
        result = jnp.einsum(
            "sjcf,jfd->sjcd", active, expert_out, preferred_element_type=f32
        ).astype(bf16)
        back = lax.all_to_all(result, "expert", split_axis=0, concat_axis=0, tiled=True).reshape(
            experts, slots, features
        )
        pieces = back[chosen, slot_read].astype(f32) * keep_float[:, None]
        picked = jnp.take_along_axis(gates, route_rows, 1)
        gate_pair = jnp.concatenate([picked[:, 0], picked[:, 1]])
        mixed = pieces[:row_count] * picked[:, 0:1] + pieces[row_count:] * picked[:, 1:2]
        outputs.append((middle + mixed).astype(bf16))
        grad_out = cotangent[start : start + row_count].astype(f32)
        grad_doubled = jnp.concatenate([grad_out, grad_out], 0)
        dgate = jnp.sum(grad_doubled * pieces, -1)
        dpieces = (grad_doubled * (gate_pair * keep_float)[:, None]).astype(bf16)
        dgates = (
            pair_onehot[:row_count] * dgate[:row_count, None]
            + pair_onehot[row_count:] * dgate[row_count:, None]
        )
        dlogits = (gates * (dgates - jnp.sum(gates * dgates, -1, keepdims=True))).astype(bf16)
        grad_send = (
            jnp.zeros((experts, slots, features), bf16)
            .at[chosen, slot_send]
            .set(dpieces, mode="drop")
        )
        grad_received = lax.all_to_all(
            grad_send.reshape(owners, per_owner, slots, features),
            "expert",
            split_axis=0,
            concat_axis=0,
            tiled=True,
        )
        dactive = jnp.einsum(
            "sjcd,jfd->sjcf", grad_received, expert_out, preferred_element_type=f32
        )
        dhidden = (dactive * gelu_slope(hidden)).astype(bf16)
        grad_w_out = jnp.einsum("sjcf,sjcd->jfd", active, grad_received, preferred_element_type=f32)
        grad_w_in = jnp.einsum("sjcd,sjcf->jdf", received, dhidden, preferred_element_type=f32)
        sum_expert_in = sum_expert_in + grad_w_in
        sum_expert_out = sum_expert_out + grad_w_out
        dsent = jnp.einsum("sjcf,jdf->sjcd", dhidden, expert_in, preferred_element_type=f32).astype(
            bf16
        )
        dreturn = lax.all_to_all(dsent, "expert", split_axis=0, concat_axis=0, tiled=True).reshape(
            experts, slots, features
        )
        dpair = dreturn[chosen, slot_read].astype(f32) * keep_float[:, None]
        dnormed_two = (
            jnp.dot(dlogits, weight_router.T, preferred_element_type=f32)
            + dpair[:row_count]
            + dpair[row_count:]
        )
        sum_router = sum_router + jnp.dot(normed_two.T, dlogits, preferred_element_type=f32)
        sum_gain_two = sum_gain_two + jnp.sum(dnormed_two * normal_two, 0)
        sum_offset_two = sum_offset_two + jnp.sum(dnormed_two, 0)
        dmiddle = grad_out + norm_backward(dnormed_two, normal_two, inverse_two, gain_two)
        dbranch = dmiddle.astype(bf16)
        sum_out = sum_out + jnp.dot(attended.T, dbranch, preferred_element_type=f32)
        dattended = jnp.dot(dbranch, weight_out.T, preferred_element_type=f32).astype(bf16)
        dattended = dattended.reshape(IMG_MB, SEQ, HEADS, HEAD_DIM)
        again = (
            jnp.einsum("gqhd,gkhd->ghqk", queries, key_rows, preferred_element_type=f32) * SCALING
        )
        probs_again = jnp.exp(again - log_total)
        dvalues = jnp.einsum(
            "ghqk,gqhd->gkhd", probs_again.astype(bf16), dattended, preferred_element_type=f32
        )
        dweights = jnp.einsum("gqhd,gkhd->ghqk", dattended, values, preferred_element_type=f32)
        inner = jnp.sum(dweights * probs_again, -1, keepdims=True)
        dscores = (probs_again * (dweights - inner)).astype(bf16)
        dqueries = (
            jnp.einsum("ghqk,gkhd->gqhd", dscores, key_rows, preferred_element_type=f32) * SCALING
        )
        dkeys = (
            jnp.einsum("ghqk,gqhd->gkhd", dscores, queries, preferred_element_type=f32) * SCALING
        )
        dprojected = (
            jnp.stack([dqueries, dkeys, dvalues], 2).astype(bf16).reshape(row_count, 3 * features)
        )
        sum_qkv = sum_qkv + jnp.dot(normed.T, dprojected, preferred_element_type=f32)
        dnormed = jnp.dot(dprojected, weight_qkv.T, preferred_element_type=f32)
        sum_gain_one = sum_gain_one + jnp.sum(dnormed * normal_one, 0)
        sum_offset_one = sum_offset_one + jnp.sum(dnormed, 0)
        input_grads.append(
            (dmiddle + norm_backward(dnormed, normal_one, inverse_one, gain_one)).astype(bf16)
        )
    grad_expert_in, grad_expert_out = (
        lax.psum_scatter(
            sum_expert_in.astype(jnp.bfloat16), "dp", scatter_dimension=2, tiled=True
        ).astype(jnp.float32),
        lax.psum_scatter(
            sum_expert_out.astype(jnp.bfloat16), "dp", scatter_dimension=1, tiled=True
        ).astype(jnp.float32),
    )
    dense = (
        sum_gain_one,
        sum_offset_one,
        sum_qkv,
        sum_out,
        sum_gain_two,
        sum_offset_two,
        sum_router,
    )
    totals_all = (
        lax.psum(dense[0].astype(jnp.bfloat16), "expert").astype(jnp.float32),
        lax.psum(dense[1].astype(jnp.bfloat16), "expert").astype(jnp.float32),
        lax.psum(dense[2].astype(jnp.bfloat16), "expert").astype(jnp.float32),
        lax.psum(dense[3].astype(jnp.bfloat16), "expert").astype(jnp.float32),
        lax.psum(dense[4].astype(jnp.bfloat16), "expert").astype(jnp.float32),
        lax.psum(dense[5].astype(jnp.bfloat16), "expert").astype(jnp.float32),
        lax.psum(dense[6].astype(jnp.bfloat16), "expert").astype(jnp.float32),
    )
    owned = (
        lax.psum_scatter(
            totals_all[0].astype(jnp.bfloat16), "dp", scatter_dimension=0, tiled=True
        ).astype(jnp.float32),
        lax.psum_scatter(
            totals_all[1].astype(jnp.bfloat16), "dp", scatter_dimension=0, tiled=True
        ).astype(jnp.float32),
        lax.psum_scatter(
            totals_all[2].astype(jnp.bfloat16), "dp", scatter_dimension=0, tiled=True
        ).astype(jnp.float32),
        lax.psum_scatter(
            totals_all[3].astype(jnp.bfloat16), "dp", scatter_dimension=0, tiled=True
        ).astype(jnp.float32),
        lax.psum_scatter(
            totals_all[4].astype(jnp.bfloat16), "dp", scatter_dimension=0, tiled=True
        ).astype(jnp.float32),
        lax.psum_scatter(
            totals_all[5].astype(jnp.bfloat16), "dp", scatter_dimension=0, tiled=True
        ).astype(jnp.float32),
        lax.psum_scatter(
            totals_all[6].astype(jnp.bfloat16), "dp", scatter_dimension=0, tiled=True
        ).astype(jnp.float32),
    )
    block_out = jnp.concatenate(outputs, 0)
    grad_tokens = jnp.concatenate(input_grads, 0)
    return (
        block_out,
        grad_tokens,
        owned[0],
        owned[1],
        owned[2],
        owned[3],
        owned[4],
        owned[5],
        owned[6],
        grad_expert_in,
        grad_expert_out,
    )


SWAP = [(0, 1), (1, 0)]
OUTWARD = [(1, 0), (2, 3)]
SECOND = [(0, 1), (3, 2), (1, 3), (2, 0)]
MIDDLE = [(1, 2), (2, 1)]


def flip(bit):
    return [(i, i ^ bit) for i in range(4)]


def add(*pieces):
    total = pieces[0].astype(f32)
    for piece in pieces[1:]:
        total = total + piece.astype(f32)
    return total.astype(bf16)


def stage(*values):
    return lax.optimization_barrier(values)


def after(value, *others):
    return lax.optimization_barrier((value, *others))[0]


def paired(
    tokens,
    ln1_gain,
    ln1_bias,
    qkv_weight,
    out_weight,
    ln2_gain,
    ln2_bias,
    router_weight,
    expert_in,
    expert_out,
    routes,
    priority,
    capacity,
    cotangent,
):
    y, core, z, x = (lax.axis_index(name) for name in ("y", "core", "z", "x"))
    features = tokens.shape[1]
    experts = capacity.shape[0]
    width = qkv_weight.shape[0]
    count = experts // 2
    slots = 8 * (3 * TOP * IMG_MB * SEQ // (16 * experts) + 1)
    lanes = 4 * features

    order = jnp.arange(8, dtype=jnp.int32)
    place = (((order & 1) ^ y) << 1) | (((order >> 1) & 1) ^ core)
    for at, value in ((Z_AT, z), (X_AT, x), (Y_AT, y), (CORE_AT, core)):
        place = jnp.where(order == at, value, place)

    def swap(value, axis, pairs=SWAP):
        return lax.ppermute(value, axis, pairs)

    gains = (ln1_gain, ln1_bias, ln2_gain, ln2_bias)
    packed = pack(gains, qkv_weight, out_weight, router_weight.T)
    from_y = swap(packed, "y")
    one = quarter_of(after(place, packed), expert_in, expert_out)
    near = swap(one, "z", flip(1))
    centre = swap(one, "z", MIDDLE)
    cotp = pad_images(after(cotangent, one))
    cot_other = swap(cotp, "x")
    place, cotp = stage(place, cotp)
    tokp, slot, slotc = prepare(place, capacity, tokens, routes, priority)
    place, from_y, tokp, slot = stage(place, from_y, tokp, slot)
    two = jnp.concatenate([packed, from_y], 0)
    dense = (two, swap(two, "core"))

    place, near, centre = stage(place, near, centre)
    second_mid = swap(near, "z", MIDDLE)
    second_out = swap(centre, "z", OUTWARD)
    across = [swap(near, "y")]
    saved = [forward_images(0, place, tokp, dense, experts)]
    place, cot_other, first_n2 = stage(place, cot_other, saved[0][4])
    n2_other = [swap(first_n2, "x")]
    saved.append(forward_images(IMG_MB, place, tokp, dense, experts))
    place, last_n2, last_gates, second_mid, second_out, across[0], n2_other[0] = stage(
        place, saved[1][4], saved[1][5], second_mid, second_out, across[0], n2_other[0]
    )
    n2_other.append(swap(last_n2, "x"))
    tables = jnp.concatenate([slot, saved[0][5][None], last_gates[None]], 0)
    other = swap(tables, "x")
    second = second_mid + second_out
    outer = swap(second, "z", OUTWARD)
    across.append(swap(second, "y"))
    corner = [swap(piece, "core") for piece in (near, across[0])]

    n2 = [piece[4] for piece in saved] + n2_other
    cot = [piece.reshape(MICRO, ROWS, features) for piece in (cotp, cot_other)]
    tables = (slot, saved[0][5], saved[1][5], other)
    place, *corner = stage(place, *corner)
    pieces = (near, across[0], *corner)
    half1 = expert_apply(1, place, n2[:MICRO], cot[:1], tables[:3], pieces, slots, "own")
    place, *half1 = stage(place, *half1)
    out1 = expert_apply(1, place, n2[MICRO:], cot[1:], tables[3:], pieces, slots, "other", half1[2:4])
    place, outer, across[1], *out1 = stage(place, outer, across[1], *out1)
    third = centre + outer
    across.append(swap(third, "y"))
    corner = [swap(piece, "core") for piece in (second, across[1])]
    core1 = swap(out1[3], "core")
    place, *corner = stage(place, *corner)
    pieces = (second, across[1], *corner)
    out2 = expert_apply(2, place, n2, cot, tables, pieces, slots)
    place, across[2], core1, *out2 = stage(place, across[2], core1, *out2)
    corner = [swap(piece, "core") for piece in (third, across[2])]
    core2 = swap(out2[3], "core")
    side1 = swap(add(out1[2][1], core1[1]), "y")
    place, *corner = stage(place, *corner)
    pieces = (third, across[2], *corner)
    out3 = expert_apply(3, place, n2, cot, tables, pieces, slots)
    place, core2, side1, *out3 = stage(place, core2, side1, *out3)
    core3 = swap(out3[3], "core")
    side2 = swap(add(out2[2][1], core2[1]), "y")
    first_swap = swap(add(out1[2][0], core1[0], side1), "z", flip(1))
    out0 = expert_apply(0, place, n2, cot, tables, (expert_in, expert_out), slots)
    place, core3, side2, first_swap, *out0 = stage(place, core3, side2, first_swap, *out0)

    outs = (out0, half1, out2, out3)
    results, dxs, _, _, dgs = ([piece[i] for piece in outs] for i in range(5))
    outs = (out0, out1, out2, out3)
    other_results, other_dxs, _, _ = ([piece[i] for piece in outs] for i in range(4))
    dgos = [piece[-1] for piece in outs]
    dn2_mine = [combine(other, other_dxs, 0, 1)]
    rest, core_send, dn2_send, *dgos = stage(other, out0[3], dn2_mine[0], *dgos)
    dn2 = [swap(dn2_send, "x")]
    dg_other = swap(jnp.stack(dgos), "x")
    side3 = swap(add(out3[2][1], core3[1]), "y")
    second_swap = swap(add(out2[2][0], core2[0], side2), "z", SECOND)
    core0 = swap(core_send, "core")
    dn2_mine.append(combine(rest, other_dxs, 1, 1))
    mixed_mine = combine(after(rest, dn2_mine[1]), other_results, 0, MICRO)
    place, mixed_mine, core0, dn2[0], last, dg_other = stage(
        place, mixed_mine, core0, dn2[0], dn2_mine[1], dg_other
    )
    dn2.append(swap(last, "x"))

    columns = slotc.reshape(IMAGES, PAD, experts)

    def back_images(micro, place, before):
        rows = dn2[micro].reshape(ROWS, features)
        return backward_images(
            micro * IMG_MB, place, tokp, cotp, saved[micro], dgs, dg_other, slotc, rows, dense, dxs, before
        )

    first = back_images(0, place, ())
    place, second_swap, side3, dn2[1], *first = stage(place, second_swap, side3, dn2[1], *first)
    inner = (z == 1) | (z == 2)
    third_sum = add(out3[2][0], core3[0], side3, jnp.where(inner, second_swap, 0.0))
    third_swap = [swap(third_sum[0], "z", flip(3))]
    side0 = swap(add(out0[2][1], core0[1]), "y")
    mixed = swap(mixed_mine, "x")
    keep_send = back_images(1, place, tuple(first[1:]))
    place, third_swap[0], side0, mixed, *keep_send = stage(place, third_swap[0], side0, mixed, *keep_send)
    third_swap.append(swap(third_sum[1], "z", flip(3)))
    mixed = mixed.reshape(IMAGES, PAD, features)
    dtok = [first[0], keep_send[0]]
    keep, send = keep_send[1:]

    from_near = swap(send, "core")
    part = swap(add(keep[1], from_near[1]), "y")
    block_out, grad_tokens = finish([piece[3] for piece in saved], mixed, columns, dtok, results)
    part, third_swap[1], block_out, grad_tokens = stage(part, third_swap[1], block_out, grad_tokens)
    part = add(keep[0], from_near[0], part)
    cut = part.reshape(width + 16, 8, lanes // 8).transpose(1, 0, 2)
    cut = lax.all_to_all(cut, ("z", "x"), split_axis=0, concat_axis=0, tiled=True)
    cut = jnp.sum(cut.astype(f32), 0).astype(bf16)
    part = jnp.broadcast_to(cut[None], (8, *cut.shape))
    part = lax.all_to_all(part, ("z", "x"), split_axis=0, concat_axis=0, tiled=True)
    gq, go, gr, *lines = unpack(part, 3 * features, experts)
    lines = [line.reshape(width) for line in lines]
    grad_in, grad_back = settle(place, second_swap, out0[2], core0, side0, first_swap, *third_swap)

    return (block_out, grad_tokens, lines[0], lines[1], gq, go, lines[2], lines[3], gr.T, grad_in, grad_back)


def solution(mesh):
    if mesh.shape["dp"] == 4 and mesh.shape["expert"] == 8:
        mesh = Mesh(mesh.devices.reshape(2, 2, 4, 2), ("y", "core", "z", "x"))
        body, dp, expert = paired, ("y", "core"), ("z", "x")
    else:
        body, dp, expert = exchanged, ("dp",), ("expert",)
    rows = P((*dp, *expert), None)
    return jax.shard_map(
        body,
        mesh=mesh,
        in_specs=(
            rows,
            P(dp),
            P(dp),
            P(dp, None),
            P(dp, None),
            P(dp),
            P(dp),
            P(dp, None),
            P(expert, None, None),
            P(expert, None, None),
            rows,
            P((*dp, *expert)),
            P(),
            rows,
        ),
        out_specs=(
            rows,
            rows,
            P(dp),
            P(dp),
            P(dp, None),
            P(dp, None),
            P(dp),
            P(dp),
            P(dp, None),
            P(expert, None, dp),
            P(expert, dp, None),
        ),
        check_vma=False,
    )
```

```python
import functools
import jax
import jax.numpy as jnp
from jax import lax
from jax.experimental import pallas as pl
from jax.experimental.pallas import tpu as pltpu
from jax.sharding import Mesh
from jax.sharding import PartitionSpec as P

HEADS = 8
HEAD_DIM = 64
TOP = 2
SEQ = 197
IMG_MB = 3
MICRO = 2
EPSILON = 1e-06
SCALING = 0.125
ROOT_HALF = 0.7071067811865476
INV_ROOT_TWO_PI = 0.3989422804014327
PAD = 16 * ((SEQ + 15) // 16)
ROWS = IMG_MB * PAD
IMAGES = MICRO * IMG_MB
f32 = jnp.float32
bf16 = jnp.bfloat16
NN = (((1,), (0,)), ((), ()))
NT = (((1,), (1,)), ((), ()))
TN = (((0,), (0,)), ((), ()))


def mm(a, b, dims=NN):
    return lax.dot_general(a, b, dims, preferred_element_type=f32)


def whole(shape):
    zeros = (0,) * len(shape)
    return pl.BlockSpec(shape, lambda *_: zeros)


def pinned(value):
    return pltpu.with_memory_space_constraint(value, pltpu.HBM)


def params(mb=60):
    return pltpu.CompilerParams(vmem_limit_bytes=mb << 20)


SHARE = 1.0


def cost(flops, moved):
    return pl.CostEstimate(flops=int(flops * SHARE), bytes_accessed=int(moved * SHARE), transcendentals=0)


Z_AT, X_AT, Y_AT, CORE_AT = 4, 5, 6, 7


def expert_of(place_ref, index):
    return 2 * (place_ref[Z_AT] ^ (index & 3)) + (place_ref[X_AT] ^ (index >> 2))


def label_column(place_ref, experts):
    index = lax.broadcasted_iota(jnp.int32, (experts, 1), 0)
    label = jnp.zeros((experts, 1), jnp.int32)
    for r in range(experts):
        label = jnp.where(index == r, expert_of(place_ref, r), label)
    return label


def wide_transpose(rows, fill):
    pad = jnp.full((128 - rows.shape[0], rows.shape[1]), fill, f32)
    return jnp.transpose(jnp.concatenate([rows, pad], 0))


def pack_kernel(g1_ref, b1_ref, g2_ref, b2_ref, qkv_ref, out_ref, router_ref, packed_ref):
    width, columns = qkv_ref.shape
    packed_ref[0, :width, :columns] = qkv_ref[...]
    packed_ref[0, :width, columns:] = out_ref[...]
    pieces = [ref[...].astype(f32) for ref in (g1_ref, b1_ref, g2_ref, b2_ref)]
    router = router_ref[...].astype(f32)
    pieces += [router[e : e + 1, :] for e in range(router.shape[0])]
    rest = packed_ref.shape[2] - width * len(pieces)
    row = jnp.concatenate(pieces + [jnp.zeros((1, rest), f32)], 1)
    row = jnp.concatenate([row, jnp.zeros((15, row.shape[1]), f32)], 0)
    packed_ref[0, width:, :] = row.astype(bf16)


def pack(vectors_in, qkv, out, router):
    width, columns = qkv.shape
    rows = [vector.reshape(1, width) for vector in vectors_in]
    packed = (1, width + 16, columns + out.shape[1])
    inputs = (*rows, qkv, out, router)
    return pl.pallas_call(
        pack_kernel,
        grid=(1,),
        in_specs=[whole(value.shape) for value in inputs],
        out_specs=whole(packed),
        out_shape=jax.ShapeDtypeStruct(packed, bf16),
        compiler_params=params(60),
        cost_estimate=cost(0, 2_000_000),
        name="pack",
    )(*inputs)


def quarter_kernel(place_ref, in_ref, back_ref, one_ref, sem):
    span = one_ref.shape[1]
    start = pl.multiple_of(place_ref[0] * span, span)
    copies = (
        pltpu.make_async_copy(in_ref.at[0, :, pl.ds(start, span)], one_ref.at[0], sem.at[0]),
        pltpu.make_async_copy(back_ref.at[0, pl.ds(start, span), :], one_ref.at[1], sem.at[1]),
    )
    for copy in copies:
        copy.start()
    for copy in copies:
        copy.wait()


def quarter_of(place, expert_in, expert_out):
    shape = (2, expert_in.shape[1], expert_in.shape[2] // 4)
    return pl.pallas_call(
        quarter_kernel,
        grid_spec=pltpu.PrefetchScalarGridSpec(
            num_scalar_prefetch=1,
            grid=(1,),
            in_specs=[pl.BlockSpec(memory_space=pl.ANY)] * 2,
            out_specs=whole(shape),
            scratch_shapes=[pltpu.SemaphoreType.DMA((2,))],
        ),
        out_shape=jax.ShapeDtypeStruct(shape, bf16),
        compiler_params=params(60),
        cost_estimate=cost(0, 2_000_000),
        name="quarter",
    )(place, expert_in, expert_out)


def pad_rows(src_ref, dst_ref, buf):
    buf[pl.ds(0, src_ref.shape[0]), :] = src_ref[...].astype(f32)
    for image in range(IMAGES):
        piece = buf[pl.ds(image * SEQ, PAD), :]
        row = lax.broadcasted_iota(jnp.int32, piece.shape, 0)
        dst_ref[image] = jnp.where(row < SEQ, piece, 0.0).astype(bf16)


def pad_images(values):
    total, features = values.shape
    padded = (IMAGES, PAD, features)
    return pl.pallas_call(
        pad_rows,
        grid=(1,),
        in_specs=[whole(values.shape)],
        out_specs=whole(padded),
        out_shape=jax.ShapeDtypeStruct(padded, bf16),
        scratch_shapes=[pltpu.VMEM((8 * ((total + PAD) // 8), features), f32)],
        compiler_params=params(60),
        cost_estimate=cost(0, 4_000_000),
        name="pad",
    )(values)


def prepare_kernel(place_ref, cap_ref, tok_ref, route_ref, prio_ref, tokp_ref, slot_ref, slotc_ref, buf, keys):
    total = tok_ref.shape[0]
    experts = slot_ref.shape[1]
    pad_rows(tok_ref, tokp_ref, buf)
    keys[...] = jnp.full_like(keys, -1.0)
    keys[pl.ds(0, total), 0:2] = route_ref[...].astype(f32)
    keys[pl.ds(0, total), 2:3] = prio_ref[...].astype(f32)
    labels = label_column(place_ref, experts)
    limit = jnp.zeros((experts, 1), f32)
    for e in range(experts):
        limit = jnp.where(labels == e, cap_ref[e].astype(f32), limit)
    labels = labels.astype(f32)
    for block in range(MICRO):
        columns = []
        for image in range(IMG_MB):
            piece = keys[pl.ds((block * IMG_MB + image) * SEQ, PAD), :]
            row = lax.broadcasted_iota(jnp.int32, piece.shape, 0)
            columns.append(jnp.where(row < SEQ, piece, -1.0))
        column = jnp.concatenate(columns, 0)
        turned = jnp.transpose(column)
        key_column = jnp.where(column[:, 2:3] < 0.0, 1e6, column[:, 2:3])
        below = jnp.where(key_column < turned[2:3, :], 1.0, 0.0).astype(bf16)
        first = labels == turned[0:1, :]
        second = labels == turned[1:2, :]
        hot = jnp.concatenate([jnp.where(first, 1.0, 0.0), jnp.where(second, 1.0, 0.0)], 0)
        counts = mm(hot.astype(bf16), below)
        total_first = jnp.sum(hot[:experts], 1, keepdims=True)
        rank = jnp.where(
            first, counts[:experts], jnp.where(second, counts[experts:] + total_first, 1e6)
        )
        slot = jnp.where(rank < limit, rank, -1.0)
        slot_ref[block] = slot
        slotc_ref[block] = wide_transpose(slot, -1.0)[:, :experts]


def prepare(place, capacity, tokens, routes, priority):
    total, features = tokens.shape
    experts = capacity.shape[0]
    tall = 8 * ((total + PAD) // 8)
    priority = priority.reshape(total, 1)
    padded = (IMAGES, PAD, features)
    return pl.pallas_call(
        prepare_kernel,
        grid_spec=pltpu.PrefetchScalarGridSpec(
            num_scalar_prefetch=2,
            grid=(1,),
            in_specs=[whole(tokens.shape), whole(routes.shape), whole(priority.shape)],
            out_specs=(
                whole(padded),
                whole((MICRO, experts, ROWS)),
                whole((MICRO, ROWS, experts)),
            ),
            scratch_shapes=[pltpu.VMEM((tall, features), f32), pltpu.VMEM((tall, 128), f32)],
        ),
        out_shape=(
            jax.ShapeDtypeStruct(padded, bf16),
            jax.ShapeDtypeStruct((MICRO, experts, ROWS), f32),
            jax.ShapeDtypeStruct((MICRO, ROWS, experts), f32),
        ),
        compiler_params=params(60),
        cost_estimate=cost(0, 8_000_000),
        name="prepare",
    )(place, capacity, tokens, routes, priority)


def norm(values, gain, offset):
    center = values - jnp.mean(values, -1, keepdims=True)
    inverse = lax.rsqrt(jnp.mean(center * center, -1, keepdims=True) + EPSILON)
    normal = center * inverse
    return normal * gain + offset, normal, inverse


def load_dense(place_ref, two_ref, more_ref, w_s, sem):
    copies = [
        pltpu.make_async_copy((two_ref, more_ref)[j // 2].at[j % 2], w_s.at[place_ref[j]], sem.at[j])
        for j in range(4)
    ]
    for copy in copies:
        copy.start()
    return copies


def vectors(w_s):
    quarters = w_s.shape[0]
    width = w_s.shape[1] - 16
    row = [w_s[q, pl.ds(width, 1), :] for q in range(quarters)]

    def pick(index):
        return jnp.concatenate([r[:, index * width : (index + 1) * width] for r in row], 1)

    return pick


def dense_weights(w_s, features):
    width = w_s.shape[1] - 16
    qkv = w_s[:, :width, : 3 * features].reshape(features, 3 * features)
    out = w_s[:, :width, 3 * features :].reshape(features, features)
    return qkv, out


def router_rows(pick, place_ref, experts):
    table = jnp.concatenate([pick(4 + e) for e in range(experts)], 0)
    labels = label_column(place_ref, experts)
    order = labels == lax.broadcasted_iota(jnp.int32, (experts, experts), 1)
    return mm(jnp.where(order, 1.0, 0.0).astype(bf16), table).astype(bf16)


def half_mask(index, value):
    lane = lax.broadcasted_iota(jnp.int32, (1, 2 * HEAD_DIM), 1)
    return jnp.where((lane < HEAD_DIM) == (index == 0), value, 0.0).astype(bf16)


def forward_kernel(first, place_ref, tok_ref, two_ref, more_ref, proj_ref, prob_ref, att_ref, mid_ref, n2_ref, gate_ref, w_s, sem, in_sem, out_sem, tok_s, n1_s, proj_s, prob_s, att_s, mid_s, n2_s):
    features = tok_s.shape[1]
    copy_in = pltpu.make_async_copy(tok_ref.at[first // IMG_MB], tok_s, in_sem.at[0])
    copy_in.start()
    waits = load_dense(place_ref, two_ref, more_ref, w_s, sem)
    out_copies = [
        pltpu.make_async_copy(src, dst, out_sem.at[i])
        for i, (src, dst) in enumerate(
            ((proj_s, proj_ref), (prob_s, prob_ref), (att_s, att_ref), (mid_s, mid_ref), (n2_s, n2_ref))
        )
    ]
    copy_in.wait()
    for copy in waits:
        copy.wait()
    pick = vectors(w_s)
    qkv, out = dense_weights(w_s, features)
    gain, offset = pick(0).astype(f32), pick(1).astype(f32)

    @pl.loop(0, IMG_MB)
    def _(i):
        span = pl.ds(pl.multiple_of(i * PAD, PAD), PAD)
        pre, _, _ = norm(tok_s[span, :].astype(f32), gain, offset)
        n1_s[span, :] = pre.astype(bf16)

    proj_s[...] = mm(n1_s[...], qkv).astype(bf16)
    out_copies[0].start()
    column = lax.broadcasted_iota(jnp.int32, (1, PAD), 1)
    pair = 2 * HEAD_DIM

    @pl.loop(0, IMG_MB)
    def _(i):
        span = pl.ds(pl.multiple_of(i * PAD, PAD), PAD)
        for group in range(HEADS // 2):
            q2 = proj_s[span, group * pair : (group + 1) * pair]
            k2 = proj_s[span, features + group * pair : features + (group + 1) * pair]
            v2 = proj_s[span, 2 * features + group * pair : 2 * features + (group + 1) * pair]
            total = None
            for half in range(2):
                scores = mm(q2 * half_mask(half, SCALING), k2, NT)
                scores = jnp.where(column < SEQ, scores, -1e30)
                expos = jnp.exp(scores - jnp.max(scores, -1, keepdims=True))
                probs = (expos * (1.0 / jnp.sum(expos, -1, keepdims=True))).astype(bf16)
                prob_s[i, 2 * group + half] = probs
                piece = mm(probs, v2 * half_mask(half, 1.0))
                total = piece if total is None else total + piece
            att_s[span, group * pair : (group + 1) * pair] = total.astype(bf16)

    out_copies[1].start()
    out_copies[2].start()
    mid_s[...] = mm(att_s[...], out)
    gain_two, offset_two = pick(2).astype(f32), pick(3).astype(f32)

    @pl.loop(0, IMG_MB)
    def _(i):
        span = pl.ds(pl.multiple_of(i * PAD, PAD), PAD)
        middle = tok_s[span, :].astype(f32) + mid_s[span, :]
        mid_s[span, :] = middle
        pre, _, _ = norm(middle, gain_two, offset_two)
        n2_s[span, :] = pre.astype(bf16)

    out_copies[4].start()
    out_copies[3].start()
    router = router_rows(pick, place_ref, gate_ref.shape[0])
    logits = mm(router, n2_s[...], NT)
    expos = jnp.exp(logits - jnp.max(logits, 0, keepdims=True))
    gate_ref[...] = expos / jnp.sum(expos, 0, keepdims=True)
    for copy in out_copies:
        copy.wait()


def image(*tail):
    zeros = (0,) * len(tail)
    return pl.BlockSpec((1, *tail), lambda i, *_: (i, *zeros))


def forward_images(first, place, tokp, dense, experts):
    features = tokp.shape[2]
    count = IMG_MB
    flops = 2 * count * PAD * (4 * features * features + 2 * PAD * 256 * HEADS)
    shapes = (
        ((ROWS, 3 * features), bf16),
        ((count, HEADS, PAD, PAD), bf16),
        ((ROWS, features), bf16),
        ((ROWS, features), f32),
        ((ROWS, features), bf16),
    )
    scratch = [((ROWS, features), bf16), ((ROWS, features), bf16), *shapes]
    return pl.pallas_call(
        functools.partial(forward_kernel, first),
        grid_spec=pltpu.PrefetchScalarGridSpec(
            num_scalar_prefetch=1,
            grid=(1,),
            in_specs=[pl.BlockSpec(memory_space=pl.ANY)] * 3,
            out_specs=(*[pl.BlockSpec(memory_space=pl.ANY)] * 5, whole((experts, ROWS))),
            scratch_shapes=[
                pltpu.VMEM((4, *dense[0].shape[1:]), bf16),
                pltpu.SemaphoreType.DMA((4,)),
                pltpu.SemaphoreType.DMA((1,)),
                pltpu.SemaphoreType.DMA((5,)),
            ]
            + [pltpu.VMEM(*shape) for shape in scratch],
        ),
        out_shape=(
            *[pltpu.HBM(*shape) for shape in shapes],
            jax.ShapeDtypeStruct((experts, ROWS), f32),
        ),
        compiler_params=params(32),
        cost_estimate=cost(flops, count * 3_000_000),
        name="forward",
    )(place, tokp.reshape(MICRO, ROWS, features), *dense)


def gelu_pair(field):
    cdf = 0.5 * (1.0 + lax.erf(field * ROOT_HALF))
    return field * cdf, cdf + field * (jnp.exp(-0.5 * field * field) * INV_ROOT_TWO_PI)


def expert_kernel(index, own, part, place_ref, *refs):
    low, high = {"all": (0, 2 * MICRO), "own": (0, MICRO), "other": (MICRO, 2 * MICRO)}[part]
    blocks = high - low
    n2_refs = refs[:blocks]
    refs = refs[blocks:]
    cot_refs = refs[: blocks // MICRO]
    refs = refs[blocks // MICRO :]
    if low == 0:
        slot_ref, gate0_ref, gate1_ref = refs[:3]
        refs = refs[3:]
    if high > MICRO:
        other_ref = refs[0]
        refs = refs[1:]
    sources = 2 if own else 4
    w_refs = refs[:sources]
    refs = refs[sources:]
    if part == "other":
        keep_in_ref, send_in_ref = refs[:2]
        refs = refs[2:]
    res_ref, dx_ref, keep_ref, send_ref = refs[:4]
    refs = refs[4:]
    lines = {}
    for first in range(low, high, MICRO):
        lines[first] = refs[0]
        refs = refs[1:]
    w_s, sem, n2_s, cot_s, in_sem, x_s, g_s, raw_s, xt_s, gt_s, gs_s, r_acc, dx_acc, act_s, dh_s = refs
    step = pl.program_id(0)
    quarters, _, _, width = w_s.shape
    slots = x_s.shape[0] // blocks
    row = lax.broadcasted_iota(jnp.int32, (slots, ROWS), 0).astype(f32)

    def copies(j):
        if own:
            start = pl.multiple_of(place_ref[j] * width, width)
            return (
                pltpu.make_async_copy(w_refs[0].at[0, :, pl.ds(start, width)], w_s.at[j, 0], sem.at[2 * j]),
                pltpu.make_async_copy(w_refs[1].at[0, pl.ds(start, width), :], w_s.at[j, 1], sem.at[2 * j + 1]),
            )
        return (pltpu.make_async_copy(w_refs[j], w_s.at[j], sem.at[j]),)

    def slot_row(local):
        b = low + local
        if b < MICRO:
            return slot_ref[b, pl.ds(index, 1), :]
        return other_ref[b - MICRO, pl.ds(index + 4, 1), :]

    def gate_row(local):
        b = low + local
        if b < MICRO:
            return (gate0_ref, gate1_ref)[b][pl.ds(index, 1), :]
        return other_ref[b, pl.ds(index + 4, 1), :]

    def rows_in(b):
        return (
            pltpu.make_async_copy(n2_refs[b], n2_s.at[b], in_sem.at[2 * b]),
            pltpu.make_async_copy(cot_refs[b // MICRO].at[b % MICRO], cot_s.at[b], in_sem.at[2 * b + 1]),
        )

    @pl.when(step == 0)
    def _():
        for b in range(blocks):
            for copy in rows_in(b):
                copy.start()
        for j in range(quarters):
            for copy in copies(j):
                copy.start()
        for b in range(blocks):
            for copy in rows_in(b):
                copy.wait()
            span = pl.ds(b * slots, slots)
            hit = row == slot_row(b)
            pick = jnp.where(hit, 1.0, 0.0)
            gate = jnp.sum(jnp.where(hit, gate_row(b), 0.0), 1, keepdims=True)
            pick = pick.astype(bf16)
            x = mm(pick, n2_s[b])
            raw = mm(pick, cot_s[b])
            x_s[span, :] = x.astype(bf16)
            raw_s[span, :] = raw.astype(bf16)
            g = gate * raw
            g_s[span, :] = g.astype(bf16)
            gs_s[span, :] = jnp.broadcast_to(gate, (slots, 128))
        xt_s[...] = jnp.transpose(x_s[...])
        gt_s[...] = jnp.transpose(g_s[...])

    for j in range(quarters):

        @pl.when(step == j)
        def _():
            for copy in copies(j):
                copy.wait()

    w_in = w_s[step, 0]
    w_out = w_s[step, 1]
    rows = blocks * slots
    for r in range(1):
        span = pl.ds(r * rows, rows)
        act, slope = gelu_pair(mm(x_s[span, :], w_in))
        act = act.astype(bf16)
        dh = (mm(g_s[span, :], w_out, NT) * slope).astype(bf16)
        act_s[span, :] = act
        dh_s[span, :] = dh
        r_acc[span, :] = jnp.where(step == 0, 0.0, r_acc[span, :]) + mm(act, w_out)
        dx_acc[span, :] = jnp.where(step == 0, 0.0, dx_acc[span, :]) + mm(dh, w_in, NT)
    grad_in = mm(xt_s[...], dh_s[...])
    grad_out = mm(gt_s[...], act_s[...])
    if part == "other":
        early = step < quarters // 2
        grad_in += jnp.where(early, keep_in_ref[0, 0].astype(f32), send_in_ref[0, 0].astype(f32))
        grad_out += jnp.where(early, keep_in_ref[0, 1].astype(f32), send_in_ref[0, 1].astype(f32))

    @pl.when(step < quarters // 2)
    def _():
        keep_ref[0, 0] = grad_in.astype(bf16)
        keep_ref[0, 1] = grad_out.astype(bf16)

    @pl.when(step >= quarters // 2)
    def _():
        send_ref[0, 0] = grad_in.astype(bf16)
        send_ref[0, 1] = grad_out.astype(bf16)

    @pl.when(step == quarters - 1)
    def _():
        dx_ref[...] = dx_acc[...].astype(bf16).reshape(dx_ref.shape)
        for b in range(blocks):
            span = pl.ds(b * slots, slots)
            res = r_acc[span, :].astype(bf16).astype(f32)
            dgate = jnp.sum(res * raw_s[span, :].astype(f32), 1, keepdims=True)
            res_ref[b] = (res * gs_s[span, 0:1]).astype(bf16)
            hit = row == slot_row(b)
            line = jnp.sum(jnp.where(hit, dgate, 0.0), 0, keepdims=True)
            lines[low + b - b % MICRO][pl.ds(b % MICRO, 1), :] = line


def expert_apply(index, place, n2, cot, tables, weights, slots, part="all", before=()):
    blocks = len(n2)
    features = n2[0].shape[1]
    own = len(weights) == 2
    quarters = 4
    width = weights[0].shape[2] // (4 if own else 1)
    rows = blocks * slots

    def fixed(shape):
        zeros = (0,) * len(shape)
        return pl.BlockSpec(shape, lambda *_: zeros)

    half = quarters // 2
    keep = pl.BlockSpec((1, 2, features, width), lambda i, _: (jnp.minimum(i, half - 1), 0, 0, 0))
    send = pl.BlockSpec((1, 2, features, width), lambda i, _: (jnp.maximum(i - half, 0), 0, 0, 0))
    groups = blocks // MICRO
    return pl.pallas_call(
        functools.partial(expert_kernel, index, own, part),
        grid_spec=pltpu.PrefetchScalarGridSpec(
            num_scalar_prefetch=1,
            grid=(quarters,),
            in_specs=[pl.BlockSpec(memory_space=pl.ANY)] * (blocks + len(cot))
            + [fixed(piece.shape) for piece in tables]
            + [pl.BlockSpec(memory_space=pl.ANY)] * len(weights)
            + [keep, send][: len(before)],
            out_specs=(
                fixed((blocks, slots, features)),
                fixed((blocks, slots, features)),
                keep,
                send,
                *[fixed((MICRO, ROWS))] * groups,
            ),
            scratch_shapes=[
                pltpu.VMEM((quarters, 2, features, width), bf16),
                pltpu.SemaphoreType.DMA((2 * quarters,)),
                pltpu.VMEM((blocks, ROWS, features), bf16),
                pltpu.VMEM((blocks, ROWS, features), bf16),
                pltpu.SemaphoreType.DMA((2 * blocks,)),
                pltpu.VMEM((rows, features), bf16),
                pltpu.VMEM((rows, features), bf16),
                pltpu.VMEM((rows, features), bf16),
                pltpu.VMEM((features, rows), bf16),
                pltpu.VMEM((features, rows), bf16),
                pltpu.VMEM((rows, 128), f32),
                pltpu.VMEM((rows, features), f32),
                pltpu.VMEM((rows, features), f32),
                pltpu.VMEM((rows, width), bf16),
                pltpu.VMEM((rows, width), bf16),
            ],
        ),
        out_shape=(
            pltpu.HBM((blocks, slots, features), bf16),
            pltpu.HBM((blocks, slots, features), bf16),
            pltpu.HBM((half, 2, features, width), bf16),
            pltpu.HBM((half, 2, features, width), bf16),
            *[jax.ShapeDtypeStruct((MICRO, ROWS), f32)] * groups,
        ),
        compiler_params=params(40),
        cost_estimate=cost(12 * rows * features * width * quarters, 4_000_000 + 3_000_000 * blocks),
        name="expert",
    )(place, *n2, *cot, *tables, *weights, *map(pinned, before))


def selector(columns, slots):
    count = columns.shape[1]
    lane = lax.broadcasted_iota(jnp.int32, (columns.shape[0], slots), 1).astype(f32)
    pieces = [jnp.where(columns[:, k : k + 1] == lane, 1.0, 0.0).astype(bf16) for k in range(count)]
    return jnp.concatenate(pieces, 1)


def combine_kernel(count, slot_ref, *refs):
    slots = refs[0].shape[1]
    pick = selector(wide_transpose(slot_ref[0, count:, :], -1.0)[:, :count], slots)
    refs[count][0] = mm(pick, jnp.concatenate([r[0] for r in refs[:count]], 0)).astype(bf16)


def combine(slot, pieces, block, blocks):
    count = len(pieces)
    _, slots, features = pieces[0].shape
    late = pl.BlockSpec((1, slots, features), lambda i: (i + block + MICRO, 0, 0))
    short = pl.BlockSpec((1, slots, features), lambda i: (i + block, 0, 0))
    return pl.pallas_call(
        functools.partial(combine_kernel, count),
        grid=(blocks,),
        in_specs=[pl.BlockSpec((1, 2 * count, ROWS), lambda i: (i + block, 0, 0))]
        + [late if piece.shape[0] > MICRO else short for piece in pieces],
        out_specs=image(ROWS, features),
        out_shape=jax.ShapeDtypeStruct((blocks, ROWS, features), bf16),
        compiler_params=params(24),
        cost_estimate=cost(2 * blocks * ROWS * features * slots * count, 5_000_000),
        name="combine",
    )(slot, *map(pinned, pieces))


def finish_kernel(count, mid0_ref, mid1_ref, part_ref, slotc_ref, dtok0_ref, dtok1_ref, *refs):
    out_ref, dout_ref, buf, dbuf = refs[count:]
    slots = refs[0].shape[1]
    step = pl.program_id(0)
    choose = selector(slotc_ref[0, :, :count], slots)
    mixed = mm(choose, jnp.concatenate([r[0] for r in refs[:count]], 0)) + part_ref[0].astype(f32)
    early = step < IMG_MB
    middle = jnp.where(early, mid0_ref[...], mid1_ref[...])
    value = middle + mixed
    grad = jnp.where(early, dtok0_ref[...].astype(f32), dtok1_ref[...].astype(f32))
    for i in range(IMAGES):

        @pl.when(step == i)
        def _():
            buf[pl.ds(i * SEQ, SEQ), :] = value[:SEQ]
            dbuf[pl.ds(i * SEQ, SEQ), :] = grad[:SEQ]

    @pl.when(step == IMAGES - 1)
    def _():
        out_ref[...] = buf[pl.ds(0, out_ref.shape[0]), :].astype(bf16)
        dout_ref[...] = dbuf[pl.ds(0, out_ref.shape[0]), :].astype(bf16)


def finish(middles, part, slotc, dtoks, results):
    count = len(results)
    _, slots, features = results[0].shape
    experts = slotc.shape[2]
    piece = pl.BlockSpec((1, slots, features), lambda i: (lax.div(i, IMG_MB), 0, 0))
    total = IMAGES * SEQ
    tall = 8 * ((total + 7) // 8)
    early = pl.BlockSpec((PAD, features), lambda i: (jnp.minimum(i, IMG_MB - 1), 0))
    later = pl.BlockSpec((PAD, features), lambda i: (jnp.maximum(i - IMG_MB, 0), 0))
    return pl.pallas_call(
        functools.partial(finish_kernel, count),
        grid=(IMAGES,),
        in_specs=[early, later, image(PAD, features), image(PAD, experts), early, later] + [piece] * count,
        out_specs=(whole((total, features)), whole((total, features))),
        out_shape=(jax.ShapeDtypeStruct((total, features), bf16),) * 2,
        scratch_shapes=[pltpu.VMEM((tall, features), f32)] * 2,
        compiler_params=params(24),
        cost_estimate=cost(4 * ROWS * features * slots * count, 15_000_000),
        name="finish",
    )(*middles, part, slotc, *dtoks, *results)


def norm_back(grad, normal, inverse, gain):
    scaled = grad * gain
    return inverse * (
        scaled
        - jnp.mean(scaled, -1, keepdims=True)
        - normal * jnp.mean(scaled * normal, -1, keepdims=True)
    )


def backward_kernel(first, count, place_ref, gate_ref, slotc_ref, dgo_ref, *refs):
    dg_refs = refs[:count]
    sources = refs[count : count + 8]
    refs = refs[count + 8 :]
    two_ref, more_ref = refs[:2]
    dx_refs = refs[2 : 2 + count]
    refs = refs[2 + count :]
    chained = first > 0
    if chained:
        before_ref, before_row_ref = refs[:2]
        dtok_ref, keep_ref, send_ref = refs[2:5]
        acc_s, acc_sem, row_ref = refs[5:8]
        refs = refs[8:]
    else:
        dtok_ref, acc_ref, row_ref = refs[:3]
        acc_s, acc_sem = refs[3:5]
        refs = refs[5:]
    w_s, sem, in_sem, dx_sem = refs[:4]
    tok_s, cot_s, proj_s, prob_s, att_s, mid_s, n2_s, dn2_s = stores = refs[4:12]
    dx_s, dbr_s, datt_s, dproj_s, n1_s, sum_s = refs[12:]
    micro = first // IMG_MB
    features = tok_s.shape[1]
    experts = 2 * count
    slots = dx_s.shape[0] // count
    copies = []
    for i, (src, dst) in enumerate(zip(sources, stores)):
        copies.append(pltpu.make_async_copy(src.at[micro] if i < 2 else src, dst, in_sem.at[i]))
    tok_in, cot_in, proj_in, prob_in, att_in, mid_in, n2_in, dn2_in = copies
    dx_in = [
        pltpu.make_async_copy(dx_refs[k].at[micro], dx_s.at[pl.ds(k * slots, slots), :], dx_sem.at[k])
        for k in range(count)
    ]
    for copy in (*dx_in, dn2_in, n2_in):
        copy.start()
    dense_in = load_dense(place_ref, two_ref, more_ref, w_s, sem)
    for copy in (mid_in, cot_in, att_in, proj_in, prob_in, tok_in):
        copy.start()
    if chained:
        acc_in = pltpu.make_async_copy(before_ref, acc_s, acc_sem.at[0])
        acc_in.start()
        row_ref[...] = before_row_ref[...]
    else:
        row_ref[...] = jnp.zeros_like(row_ref)
    choose = selector(slotc_ref[0, :, :count], slots)
    gates = gate_ref[...]
    dgates = [ref[pl.ds(micro, 1), :] for ref in dg_refs] + [dgo_ref[k, pl.ds(micro, 1), :] for k in range(count)]
    dgates = jnp.concatenate(dgates, 0)
    dlogits = (gates * (dgates - jnp.sum(gates * dgates, 0, keepdims=True))).astype(bf16)
    for copy in (*dx_in, dn2_in, n2_in, *dense_in):
        copy.wait()
    pick = vectors(w_s)
    qkv, out = dense_weights(w_s, features)
    router = router_rows(pick, place_ref, experts)
    row_ref[8 : 8 + experts, :] += mm(dlogits, n2_s[...])
    sum_s[...] = mm(choose, dx_s[...]) + mm(dlogits, router, TN)
    mid_in.wait()
    cot_in.wait()
    gain_two = pick(2).astype(f32)

    @pl.loop(0, IMG_MB)
    def _(i):
        span = pl.ds(pl.multiple_of(i * PAD, PAD), PAD)
        dn2 = sum_s[span, :] + dn2_s[span, :].astype(f32)
        _, normal_two, inverse_two = norm(mid_s[span, :], gain_two, 0.0)
        row_ref[2:3, :] += jnp.sum(dn2 * normal_two, 0, keepdims=True)
        row_ref[3:4, :] += jnp.sum(dn2, 0, keepdims=True)
        dmiddle = cot_s[span, :].astype(f32) + norm_back(dn2, normal_two, inverse_two, gain_two)
        mid_s[span, :] = dmiddle
        dbr_s[span, :] = dmiddle.astype(bf16)

    att_in.wait()
    if chained:
        acc_in.wait()
    grad_out = mm(att_s[...], dbr_s[...], TN)
    if chained:
        acc_s[:, 3 * features :] += grad_out
    else:
        acc_s[:, 3 * features :] = grad_out
    datt_s[...] = mm(dbr_s[...], out, NT).astype(bf16)
    proj_in.wait()
    prob_in.wait()
    tok_in.wait()
    pair = 2 * HEAD_DIM
    gain_one, offset_one = pick(0).astype(f32), pick(1).astype(f32)

    @pl.loop(0, IMG_MB)
    def _(i):
        span = pl.ds(pl.multiple_of(i * PAD, PAD), PAD)
        pre, _, _ = norm(tok_s[span, :].astype(f32), gain_one, offset_one)
        n1_s[span, :] = pre.astype(bf16)
        for group in range(HEADS // 2):
            at = [part * features + group * pair for part in range(3)]
            q2, k2, v2 = (proj_s[span, start : start + pair] for start in at)
            d2 = datt_s[span, group * pair : (group + 1) * pair]
            dq = dk = dv = None
            for half in range(2):
                probs = prob_s[i, 2 * group + half]
                wide = probs.astype(f32)
                dm = d2 * half_mask(half, 1.0)
                dweights = mm(dm, v2, NT)
                inner = jnp.sum(dweights * wide, -1, keepdims=True)
                dscores = (wide * (dweights - inner)).astype(bf16)
                part_q = mm(dscores, k2 * half_mask(half, SCALING))
                part_k = mm(dscores, q2 * half_mask(half, SCALING), TN)
                part_v = mm(probs, dm, TN)
                dq = part_q if dq is None else dq + part_q
                dk = part_k if dk is None else dk + part_k
                dv = part_v if dv is None else dv + part_v
            for start, value in zip(at, (dq, dk, dv)):
                dproj_s[span, start : start + pair] = value.astype(bf16)

    grad_qkv = mm(n1_s[...], dproj_s[...], TN)
    if chained:
        acc_s[:, : 3 * features] += grad_qkv
    else:
        acc_s[:, : 3 * features] = grad_qkv
        acc_out = pltpu.make_async_copy(acc_s, acc_ref, acc_sem.at[0])
        acc_out.start()
    sum_s[...] = mm(dproj_s[...], qkv, NT)

    @pl.loop(0, IMG_MB)
    def _(i):
        span = pl.ds(pl.multiple_of(i * PAD, PAD), PAD)
        dnormed = sum_s[span, :]
        _, normal_one, inverse_one = norm(tok_s[span, :].astype(f32), gain_one, offset_one)
        row_ref[0:1, :] += jnp.sum(dnormed * normal_one, 0, keepdims=True)
        row_ref[1:2, :] += jnp.sum(dnormed, 0, keepdims=True)
        dtok_ref[span, :] = (mid_s[span, :] + norm_back(dnormed, normal_one, inverse_one, gain_one)).astype(bf16)

    if not chained:
        acc_out.wait()
        return
    width = keep_ref.shape[1] - 16
    lines = [row_ref[i : i + 1, :] for i in range(4)]
    for e in range(experts):
        line = jnp.zeros((1, features), f32)
        for r in range(experts):
            line = jnp.where(expert_of(place_ref, r) == e, row_ref[8 + r : 9 + r, :], line)
        lines.append(line)
    blank = jnp.zeros((1, 4 * features - (4 + experts) * width), f32)
    tails = []
    for q in range(4):
        parts = [line[:, q * width : (q + 1) * width] for line in lines]
        tails.append(jnp.concatenate(parts + [blank], 1))
    for j in range(4):
        quarter = place_ref[j]
        to = (keep_ref, send_ref)[j // 2]
        to[j % 2, :width, :] = acc_s[pl.ds(pl.multiple_of(quarter * width, width), width), :].astype(bf16)
        tail = tails[0]
        for q in range(1, 4):
            tail = jnp.where(quarter == q, tails[q], tail)
        tail = jnp.concatenate([tail, jnp.zeros((15, tail.shape[1]), f32)], 0)
        to[j % 2, width:, :] = tail.astype(bf16)


def backward_images(first, place, tokp, cotp, saved, dgs, dg_other, slotc, dn2_part, dense, dxs, before):
    projected, probs, attended, middle, n2, gates = saved
    count = len(dxs)
    features = tokp.shape[2]
    experts = 2 * count
    slots = dxs[0].shape[1]
    totals = ((features, 4 * features), (8 + experts, features))
    packed = (2, *dense[0].shape[1:])
    anywhere = pl.BlockSpec(memory_space=pl.ANY)
    flat = (MICRO, ROWS, features)
    sources = (tokp.reshape(flat), cotp.reshape(flat), projected, probs, attended, middle, n2, dn2_part)
    out_specs = [whole((ROWS, features))]
    out_shape = [jax.ShapeDtypeStruct((ROWS, features), bf16)]
    scratch = [pltpu.VMEM(totals[0], f32), pltpu.SemaphoreType.DMA((1,))]
    if before:
        out_specs += [whole(packed)] * 2
        out_shape += [jax.ShapeDtypeStruct(packed, bf16)] * 2
        scratch.append(pltpu.VMEM(totals[1], f32))
        extra = [anywhere, whole(totals[1])]
    else:
        out_specs += [anywhere, whole(totals[1])]
        out_shape += [jax.ShapeDtypeStruct(shape, f32) for shape in totals]
        extra = []
    scratch += [
        pltpu.VMEM((4, *dense[0].shape[1:]), bf16),
        pltpu.SemaphoreType.DMA((4,)),
        pltpu.SemaphoreType.DMA((8,)),
        pltpu.SemaphoreType.DMA((count,)),
    ]
    scratch += [pltpu.VMEM((ROWS, features), bf16)] * 2
    scratch += [pltpu.VMEM(piece.shape, piece.dtype) for piece in sources[2:]]
    scratch += [
        pltpu.VMEM((count * slots, features), bf16),
        pltpu.VMEM((ROWS, features), bf16),
        pltpu.VMEM((ROWS, features), bf16),
        pltpu.VMEM((ROWS, 3 * features), bf16),
        pltpu.VMEM((ROWS, features), bf16),
        pltpu.VMEM((ROWS, features), f32),
    ]
    micro = first // IMG_MB
    return pl.pallas_call(
        functools.partial(backward_kernel, first, count),
        grid_spec=pltpu.PrefetchScalarGridSpec(
            num_scalar_prefetch=1,
            grid=(1,),
            in_specs=[
                whole(gates.shape),
                pl.BlockSpec((1, ROWS, experts), lambda i, _: (micro, 0, 0)),
                whole(dg_other.shape),
            ]
            + [whole(piece.shape) for piece in dgs]
            + [anywhere] * (10 + count)
            + extra,
            out_specs=tuple(out_specs),
            scratch_shapes=scratch,
        ),
        out_shape=tuple(out_shape),
        compiler_params=params(40),
        cost_estimate=cost(40 * ROWS * features * features, 15_000_000),
        name="backward",
    )(place, gates, slotc, dg_other, *dgs, *sources, *dense, *dxs, *before)


def settle_kernel(place_ref, far_ref, *refs):
    in_ref, back_ref = refs[-2:]
    z = place_ref[Z_AT]
    outer = jnp.where((z == 0) | (z == 3), 1.0, 0.0)

    def total(i):
        value = far_ref[i].astype(f32) * outer + refs[i - 4][...].astype(f32)
        for ref in refs[:-4]:
            piece = ref[0, i] if len(ref.shape) == 4 else ref[i]
            value = value + piece.astype(f32)
        return value

    in_ref[0] = total(0)
    back_ref[0] = jnp.transpose(total(1))


def settle(place, *pieces):
    features, span = pieces[-1].shape

    def spec(piece):
        shape = (1, *piece.shape[1:]) if len(piece.shape) == 4 else piece.shape
        return whole(shape)

    return pl.pallas_call(
        settle_kernel,
        grid_spec=pltpu.PrefetchScalarGridSpec(
            num_scalar_prefetch=1,
            grid=(1,),
            in_specs=[spec(piece) for piece in pieces],
            out_specs=(whole((1, features, span)), whole((1, span, features))),
        ),
        out_shape=(
            jax.ShapeDtypeStruct((1, features, span), f32),
            jax.ShapeDtypeStruct((1, span, features), f32),
        ),
        compiler_params=params(24),
        cost_estimate=cost(0, 5_000_000),
        name="settle",
    )(place, *map(pinned, pieces))


def unpack_kernel(part_ref, qkv_ref, out_ref, router_ref, g1_ref, b1_ref, g2_ref, b2_ref):
    width, columns = qkv_ref.shape
    pieces, _, lanes = part_ref.shape
    for i in range(pieces):
        value = part_ref[i, :width, :].astype(f32)
        at = i * lanes
        if at < columns:
            qkv_ref[:, at : at + lanes] = value
        else:
            out_ref[:, at - columns : at - columns + lanes] = value
    row = jnp.concatenate([part_ref[i, width:, :].astype(f32)[0:1] for i in range(pieces)], 1)
    for i, ref in enumerate((g1_ref, b1_ref, g2_ref, b2_ref)):
        ref[...] = row[:, i * width : (i + 1) * width]
    lines = [row[:, (4 + e) * width : (5 + e) * width] for e in range(router_ref.shape[0])]
    router_ref[...] = jnp.concatenate(lines, 0)


def unpack(part, columns, experts):
    pieces, height, lanes = part.shape
    width = height - 16
    line = (1, width)
    shapes = ((width, columns), (width, pieces * lanes - columns), (experts, width), line, line, line, line)
    return pl.pallas_call(
        unpack_kernel,
        grid=(1,),
        in_specs=[whole(part.shape)],
        out_specs=tuple(whole(shape) for shape in shapes),
        out_shape=tuple(jax.ShapeDtypeStruct(shape, f32) for shape in shapes),
        compiler_params=params(24),
        cost_estimate=cost(0, 3_000_000),
        name="unpack",
    )(part)


def norm_forward(values, gain, offset):
    center = values - jnp.mean(values, -1, keepdims=True)
    inverse = lax.rsqrt(jnp.mean(center * center, -1, keepdims=True) + EPSILON)
    normal = center * inverse
    return (normal * gain + offset, normal, inverse)


def norm_backward(grad, normal, inverse, gain):
    scaled = grad * gain
    return inverse * (
        scaled
        - jnp.mean(scaled, -1, keepdims=True)
        - normal * jnp.mean(scaled * normal, -1, keepdims=True)
    )


def gelu_value(field):
    return 0.5 * field * (1.0 + lax.erf(field * ROOT_HALF))


def gelu_slope(field):
    return (
        0.5 * (1.0 + lax.erf(field * ROOT_HALF))
        + field * jnp.exp(-0.5 * field * field) * INV_ROOT_TWO_PI
    )


def block_ranks(route_rows, order_keys, capacity):
    count = order_keys.shape[0]
    expert_count = capacity.shape[0]
    chosen = jnp.concatenate([route_rows[:, 0], route_rows[:, 1]])
    sort_keys = jnp.concatenate([order_keys, order_keys + count])
    positions = jnp.arange(2 * count, dtype=jnp.int32)
    inverse = jnp.zeros((2 * count,), jnp.int32).at[sort_keys].set(positions)
    ordered = chosen[inverse]
    labels = jnp.arange(expert_count, dtype=jnp.int32)
    onehot = (ordered[:, None] == labels[None, :]).astype(jnp.int32)
    before = jnp.cumsum(onehot, 0) - onehot
    rank_sorted = jnp.sum(before * onehot, 1)
    ranking = jnp.zeros((2 * count,), jnp.int32).at[inverse].set(rank_sorted)
    pair_onehot = chosen[:, None] == labels[None, :]
    limit = jnp.sum(pair_onehot.astype(jnp.int32) * capacity[None, :], 1)
    return (chosen, ranking, ranking < limit, pair_onehot.astype(jnp.float32))


def exchanged(
    tokens,
    ln1_gain,
    ln1_bias,
    qkv_weight,
    out_weight,
    ln2_gain,
    ln2_bias,
    router_weight,
    expert_in,
    expert_out,
    routes,
    priority,
    capacity,
    cotangent,
):
    f32 = jnp.float32
    bf16 = jnp.bfloat16
    gathered = (
        lax.all_gather(ln1_gain, "dp", axis=0, tiled=True),
        lax.all_gather(ln1_bias, "dp", axis=0, tiled=True),
        lax.all_gather(qkv_weight, "dp", axis=0, tiled=True),
        lax.all_gather(out_weight, "dp", axis=0, tiled=True),
        lax.all_gather(ln2_gain, "dp", axis=0, tiled=True),
        lax.all_gather(ln2_bias, "dp", axis=0, tiled=True),
        lax.all_gather(router_weight, "dp", axis=0, tiled=True),
    )
    gain_one = gathered[0].astype(f32)
    offset_one = gathered[1].astype(f32)
    weight_qkv = gathered[2]
    weight_out = gathered[3]
    gain_two = gathered[4].astype(f32)
    offset_two = gathered[5].astype(f32)
    weight_router = gathered[6]
    features = tokens.shape[1]
    owners = lax.axis_size("expert")
    per_owner = expert_in.shape[0]
    experts = owners * per_owner
    slots = 8 * (3 * TOP * IMG_MB * SEQ // (16 * experts) + 1)
    row_count = IMG_MB * SEQ
    sum_gain_one = jnp.zeros((features,), f32)
    sum_offset_one = jnp.zeros((features,), f32)
    sum_qkv = jnp.zeros(weight_qkv.shape, f32)
    sum_out = jnp.zeros(weight_out.shape, f32)
    sum_gain_two = jnp.zeros((features,), f32)
    sum_offset_two = jnp.zeros((features,), f32)
    sum_router = jnp.zeros(weight_router.shape, f32)
    sum_expert_in = jnp.zeros(expert_in.shape, f32)
    sum_expert_out = jnp.zeros(expert_out.shape, f32)
    outputs = []
    input_grads = []
    for micro in range(MICRO):
        start = micro * row_count
        inputs = tokens[start : start + row_count].astype(f32)
        pre_one, normal_one, inverse_one = norm_forward(inputs, gain_one, offset_one)
        normed = pre_one.astype(bf16)
        projected = jnp.dot(normed, weight_qkv, preferred_element_type=f32).astype(bf16)
        projected = projected.reshape(IMG_MB, SEQ, 3, HEADS, HEAD_DIM)
        queries = projected[:, :, 0]
        key_rows = projected[:, :, 1]
        values = projected[:, :, 2]
        scores = (
            jnp.einsum("gqhd,gkhd->ghqk", queries, key_rows, preferred_element_type=f32) * SCALING
        )
        highest = jnp.max(scores, -1, keepdims=True)
        expos = jnp.exp(scores - highest)
        totals = jnp.sum(expos, -1, keepdims=True)
        log_total = highest + jnp.log(totals)
        attn_weights = (expos / totals).astype(bf16)
        attended = jnp.einsum(
            "ghqk,gkhd->gqhd", attn_weights, values, preferred_element_type=f32
        ).astype(bf16)
        attended = attended.reshape(row_count, features)
        middle = inputs + jnp.dot(attended, weight_out, preferred_element_type=f32)
        pre_two, normal_two, inverse_two = norm_forward(middle, gain_two, offset_two)
        normed_two = pre_two.astype(bf16)
        logits = jnp.dot(normed_two, weight_router, preferred_element_type=f32)
        gates = jax.nn.softmax(logits, -1)
        route_rows = routes[start : start + row_count]
        chosen, ranking, kept, pair_onehot = block_ranks(
            route_rows, priority[start : start + row_count], capacity
        )
        keep_float = kept.astype(f32)
        slot_send = jnp.where(kept, ranking, slots)
        slot_read = jnp.where(kept, ranking, 0)
        doubled = jnp.concatenate([normed_two, normed_two], 0)
        send = (
            jnp.zeros((experts, slots, features), bf16)
            .at[chosen, slot_send]
            .set(doubled, mode="drop")
        )
        received = lax.all_to_all(
            send.reshape(owners, per_owner, slots, features),
            "expert",
            split_axis=0,
            concat_axis=0,
            tiled=True,
        )
        hidden = jnp.einsum("sjcd,jdf->sjcf", received, expert_in, preferred_element_type=f32)
        active = gelu_value(hidden).astype(bf16)
        result = jnp.einsum(
            "sjcf,jfd->sjcd", active, expert_out, preferred_element_type=f32
        ).astype(bf16)
        back = lax.all_to_all(result, "expert", split_axis=0, concat_axis=0, tiled=True).reshape(
            experts, slots, features
        )
        pieces = back[chosen, slot_read].astype(f32) * keep_float[:, None]
        picked = jnp.take_along_axis(gates, route_rows, 1)
        gate_pair = jnp.concatenate([picked[:, 0], picked[:, 1]])
        mixed = pieces[:row_count] * picked[:, 0:1] + pieces[row_count:] * picked[:, 1:2]
        outputs.append((middle + mixed).astype(bf16))
        grad_out = cotangent[start : start + row_count].astype(f32)
        grad_doubled = jnp.concatenate([grad_out, grad_out], 0)
        dgate = jnp.sum(grad_doubled * pieces, -1)
        dpieces = (grad_doubled * (gate_pair * keep_float)[:, None]).astype(bf16)
        dgates = (
            pair_onehot[:row_count] * dgate[:row_count, None]
            + pair_onehot[row_count:] * dgate[row_count:, None]
        )
        dlogits = (gates * (dgates - jnp.sum(gates * dgates, -1, keepdims=True))).astype(bf16)
        grad_send = (
            jnp.zeros((experts, slots, features), bf16)
            .at[chosen, slot_send]
            .set(dpieces, mode="drop")
        )
        grad_received = lax.all_to_all(
            grad_send.reshape(owners, per_owner, slots, features),
            "expert",
            split_axis=0,
            concat_axis=0,
            tiled=True,
        )
        dactive = jnp.einsum(
            "sjcd,jfd->sjcf", grad_received, expert_out, preferred_element_type=f32
        )
        dhidden = (dactive * gelu_slope(hidden)).astype(bf16)
        grad_w_out = jnp.einsum("sjcf,sjcd->jfd", active, grad_received, preferred_element_type=f32)
        grad_w_in = jnp.einsum("sjcd,sjcf->jdf", received, dhidden, preferred_element_type=f32)
        sum_expert_in = sum_expert_in + grad_w_in
        sum_expert_out = sum_expert_out + grad_w_out
        dsent = jnp.einsum("sjcf,jdf->sjcd", dhidden, expert_in, preferred_element_type=f32).astype(
            bf16
        )
        dreturn = lax.all_to_all(dsent, "expert", split_axis=0, concat_axis=0, tiled=True).reshape(
            experts, slots, features
        )
        dpair = dreturn[chosen, slot_read].astype(f32) * keep_float[:, None]
        dnormed_two = (
            jnp.dot(dlogits, weight_router.T, preferred_element_type=f32)
            + dpair[:row_count]
            + dpair[row_count:]
        )
        sum_router = sum_router + jnp.dot(normed_two.T, dlogits, preferred_element_type=f32)
        sum_gain_two = sum_gain_two + jnp.sum(dnormed_two * normal_two, 0)
        sum_offset_two = sum_offset_two + jnp.sum(dnormed_two, 0)
        dmiddle = grad_out + norm_backward(dnormed_two, normal_two, inverse_two, gain_two)
        dbranch = dmiddle.astype(bf16)
        sum_out = sum_out + jnp.dot(attended.T, dbranch, preferred_element_type=f32)
        dattended = jnp.dot(dbranch, weight_out.T, preferred_element_type=f32).astype(bf16)
        dattended = dattended.reshape(IMG_MB, SEQ, HEADS, HEAD_DIM)
        again = (
            jnp.einsum("gqhd,gkhd->ghqk", queries, key_rows, preferred_element_type=f32) * SCALING
        )
        probs_again = jnp.exp(again - log_total)
        dvalues = jnp.einsum(
            "ghqk,gqhd->gkhd", probs_again.astype(bf16), dattended, preferred_element_type=f32
        )
        dweights = jnp.einsum("gqhd,gkhd->ghqk", dattended, values, preferred_element_type=f32)
        inner = jnp.sum(dweights * probs_again, -1, keepdims=True)
        dscores = (probs_again * (dweights - inner)).astype(bf16)
        dqueries = (
            jnp.einsum("ghqk,gkhd->gqhd", dscores, key_rows, preferred_element_type=f32) * SCALING
        )
        dkeys = (
            jnp.einsum("ghqk,gqhd->gkhd", dscores, queries, preferred_element_type=f32) * SCALING
        )
        dprojected = (
            jnp.stack([dqueries, dkeys, dvalues], 2).astype(bf16).reshape(row_count, 3 * features)
        )
        sum_qkv = sum_qkv + jnp.dot(normed.T, dprojected, preferred_element_type=f32)
        dnormed = jnp.dot(dprojected, weight_qkv.T, preferred_element_type=f32)
        sum_gain_one = sum_gain_one + jnp.sum(dnormed * normal_one, 0)
        sum_offset_one = sum_offset_one + jnp.sum(dnormed, 0)
        input_grads.append(
            (dmiddle + norm_backward(dnormed, normal_one, inverse_one, gain_one)).astype(bf16)
        )
    grad_expert_in, grad_expert_out = (
        lax.psum_scatter(
            sum_expert_in.astype(jnp.bfloat16), "dp", scatter_dimension=2, tiled=True
        ).astype(jnp.float32),
        lax.psum_scatter(
            sum_expert_out.astype(jnp.bfloat16), "dp", scatter_dimension=1, tiled=True
        ).astype(jnp.float32),
    )
    dense = (
        sum_gain_one,
        sum_offset_one,
        sum_qkv,
        sum_out,
        sum_gain_two,
        sum_offset_two,
        sum_router,
    )
    totals_all = (
        lax.psum(dense[0].astype(jnp.bfloat16), "expert").astype(jnp.float32),
        lax.psum(dense[1].astype(jnp.bfloat16), "expert").astype(jnp.float32),
        lax.psum(dense[2].astype(jnp.bfloat16), "expert").astype(jnp.float32),
        lax.psum(dense[3].astype(jnp.bfloat16), "expert").astype(jnp.float32),
        lax.psum(dense[4].astype(jnp.bfloat16), "expert").astype(jnp.float32),
        lax.psum(dense[5].astype(jnp.bfloat16), "expert").astype(jnp.float32),
        lax.psum(dense[6].astype(jnp.bfloat16), "expert").astype(jnp.float32),
    )
    owned = (
        lax.psum_scatter(
            totals_all[0].astype(jnp.bfloat16), "dp", scatter_dimension=0, tiled=True
        ).astype(jnp.float32),
        lax.psum_scatter(
            totals_all[1].astype(jnp.bfloat16), "dp", scatter_dimension=0, tiled=True
        ).astype(jnp.float32),
        lax.psum_scatter(
            totals_all[2].astype(jnp.bfloat16), "dp", scatter_dimension=0, tiled=True
        ).astype(jnp.float32),
        lax.psum_scatter(
            totals_all[3].astype(jnp.bfloat16), "dp", scatter_dimension=0, tiled=True
        ).astype(jnp.float32),
        lax.psum_scatter(
            totals_all[4].astype(jnp.bfloat16), "dp", scatter_dimension=0, tiled=True
        ).astype(jnp.float32),
        lax.psum_scatter(
            totals_all[5].astype(jnp.bfloat16), "dp", scatter_dimension=0, tiled=True
        ).astype(jnp.float32),
        lax.psum_scatter(
            totals_all[6].astype(jnp.bfloat16), "dp", scatter_dimension=0, tiled=True
        ).astype(jnp.float32),
    )
    block_out = jnp.concatenate(outputs, 0)
    grad_tokens = jnp.concatenate(input_grads, 0)
    return (
        block_out,
        grad_tokens,
        owned[0],
        owned[1],
        owned[2],
        owned[3],
        owned[4],
        owned[5],
        owned[6],
        grad_expert_in,
        grad_expert_out,
    )


SWAP = [(0, 1), (1, 0)]
OUTWARD = [(1, 0), (2, 3)]
SECOND = [(0, 1), (3, 2), (1, 3), (2, 0)]
MIDDLE = [(1, 2), (2, 1)]


def flip(bit):
    return [(i, i ^ bit) for i in range(4)]


def add(*pieces):
    total = pieces[0].astype(f32)
    for piece in pieces[1:]:
        total = total + piece.astype(f32)
    return total.astype(bf16)


def stage(*values):
    return lax.optimization_barrier(values)


def after(value, *others):
    return lax.optimization_barrier((value, *others))[0]


def paired(
    tokens,
    ln1_gain,
    ln1_bias,
    qkv_weight,
    out_weight,
    ln2_gain,
    ln2_bias,
    router_weight,
    expert_in,
    expert_out,
    routes,
    priority,
    capacity,
    cotangent,
):
    y, core, z, x = (lax.axis_index(name) for name in ("y", "core", "z", "x"))
    features = tokens.shape[1]
    experts = capacity.shape[0]
    width = qkv_weight.shape[0]
    count = experts // 2
    slots = 8 * (3 * TOP * IMG_MB * SEQ // (16 * experts) + 1)
    lanes = 4 * features

    order = jnp.arange(8, dtype=jnp.int32)
    place = (((order & 1) ^ y) << 1) | (((order >> 1) & 1) ^ core)
    for at, value in ((Z_AT, z), (X_AT, x), (Y_AT, y), (CORE_AT, core)):
        place = jnp.where(order == at, value, place)

    def swap(value, axis, pairs=SWAP):
        return lax.ppermute(value, axis, pairs)

    gains = (ln1_gain, ln1_bias, ln2_gain, ln2_bias)
    packed = pack(gains, qkv_weight, out_weight, router_weight.T)
    from_y = swap(packed, "y")
    one = quarter_of(after(place, packed), expert_in, expert_out)
    near = swap(one, "z", flip(1))
    centre = swap(one, "z", MIDDLE)
    cotp = pad_images(after(cotangent, one))
    cot_other = swap(cotp, "x")
    place, cotp = stage(place, cotp)
    tokp, slot, slotc = prepare(place, capacity, tokens, routes, priority)
    place, from_y, tokp, slot = stage(place, from_y, tokp, slot)
    two = jnp.concatenate([packed, from_y], 0)
    dense = (two, swap(two, "core"))

    place, near, centre = stage(place, near, centre)
    second_mid = swap(near, "z", MIDDLE)
    second_out = swap(centre, "z", OUTWARD)
    across = [swap(near, "y")]
    saved = [forward_images(0, place, tokp, dense, experts)]
    place, cot_other, first_n2 = stage(place, cot_other, saved[0][4])
    n2_other = [swap(first_n2, "x")]
    saved.append(forward_images(IMG_MB, place, tokp, dense, experts))
    place, last_n2, last_gates, second_mid, second_out, across[0], n2_other[0] = stage(
        place, saved[1][4], saved[1][5], second_mid, second_out, across[0], n2_other[0]
    )
    n2_other.append(swap(last_n2, "x"))
    tables = jnp.concatenate([slot, saved[0][5][None], last_gates[None]], 0)
    other = swap(tables, "x")
    second = second_mid + second_out
    outer = swap(second, "z", OUTWARD)
    across.append(swap(second, "y"))
    corner = [swap(piece, "core") for piece in (near, across[0])]

    n2 = [piece[4] for piece in saved] + n2_other
    cot = [piece.reshape(MICRO, ROWS, features) for piece in (cotp, cot_other)]
    tables = (slot, saved[0][5], saved[1][5], other)
    place, *corner = stage(place, *corner)
    pieces = (near, across[0], *corner)
    half1 = expert_apply(1, place, n2[:MICRO], cot[:1], tables[:3], pieces, slots, "own")
    place, *half1 = stage(place, *half1)
    out1 = expert_apply(1, place, n2[MICRO:], cot[1:], tables[3:], pieces, slots, "other", half1[2:4])
    place, outer, across[1], *out1 = stage(place, outer, across[1], *out1)
    third = centre + outer
    across.append(swap(third, "y"))
    corner = [swap(piece, "core") for piece in (second, across[1])]
    core1 = swap(out1[3], "core")
    place, *corner = stage(place, *corner)
    pieces = (second, across[1], *corner)
    out2 = expert_apply(2, place, n2, cot, tables, pieces, slots)
    place, across[2], core1, *out2 = stage(place, across[2], core1, *out2)
    corner = [swap(piece, "core") for piece in (third, across[2])]
    core2 = swap(out2[3], "core")
    side1 = swap(add(out1[2][1], core1[1]), "y")
    place, *corner = stage(place, *corner)
    pieces = (third, across[2], *corner)
    out3 = expert_apply(3, place, n2, cot, tables, pieces, slots)
    place, core2, side1, *out3 = stage(place, core2, side1, *out3)
    core3 = swap(out3[3], "core")
    side2 = swap(add(out2[2][1], core2[1]), "y")
    first_swap = swap(add(out1[2][0], core1[0], side1), "z", flip(1))
    out0 = expert_apply(0, place, n2, cot, tables, (expert_in, expert_out), slots)
    place, core3, side2, first_swap, *out0 = stage(place, core3, side2, first_swap, *out0)

    outs = (out0, half1, out2, out3)
    results, dxs, _, _, dgs = ([piece[i] for piece in outs] for i in range(5))
    outs = (out0, out1, out2, out3)
    other_results, other_dxs, _, _ = ([piece[i] for piece in outs] for i in range(4))
    dgos = [piece[-1] for piece in outs]
    dn2_mine = [combine(other, other_dxs, 0, 1)]
    rest, core_send, dn2_send, *dgos = stage(other, out0[3], dn2_mine[0], *dgos)
    dn2 = [swap(dn2_send, "x")]
    dg_other = swap(jnp.stack(dgos), "x")
    side3 = swap(add(out3[2][1], core3[1]), "y")
    second_swap = swap(add(out2[2][0], core2[0], side2), "z", SECOND)
    core0 = swap(core_send, "core")
    dn2_mine.append(combine(rest, other_dxs, 1, 1))
    mixed_mine = combine(after(rest, dn2_mine[1]), other_results, 0, MICRO)
    place, mixed_mine, core0, dn2[0], last, dg_other = stage(
        place, mixed_mine, core0, dn2[0], dn2_mine[1], dg_other
    )
    dn2.append(swap(last, "x"))

    columns = slotc.reshape(IMAGES, PAD, experts)

    def back_images(micro, place, before):
        rows = dn2[micro].reshape(ROWS, features)
        return backward_images(
            micro * IMG_MB, place, tokp, cotp, saved[micro], dgs, dg_other, slotc, rows, dense, dxs, before
        )

    first = back_images(0, place, ())
    place, second_swap, side3, dn2[1], *first = stage(place, second_swap, side3, dn2[1], *first)
    inner = (z == 1) | (z == 2)
    third_sum = add(out3[2][0], core3[0], side3, jnp.where(inner, second_swap, 0.0))
    third_swap = [swap(third_sum[0], "z", flip(3))]
    side0 = swap(add(out0[2][1], core0[1]), "y")
    mixed = swap(mixed_mine, "x")
    keep_send = back_images(1, place, tuple(first[1:]))
    place, third_swap[0], side0, mixed, *keep_send = stage(place, third_swap[0], side0, mixed, *keep_send)
    third_swap.append(swap(third_sum[1], "z", flip(3)))
    mixed = mixed.reshape(IMAGES, PAD, features)
    dtok = [first[0], keep_send[0]]
    keep, send = keep_send[1:]

    from_near = swap(send, "core")
    part = swap(add(keep[1], from_near[1]), "y")
    block_out, grad_tokens = finish([piece[3] for piece in saved], mixed, columns, dtok, results)
    part, third_swap[1], block_out, grad_tokens = stage(part, third_swap[1], block_out, grad_tokens)
    part = add(keep[0], from_near[0], part)
    cut = part.reshape(width + 16, 8, lanes // 8).transpose(1, 0, 2)
    cut = lax.all_to_all(cut, ("z", "x"), split_axis=0, concat_axis=0, tiled=True)
    cut = jnp.sum(cut.astype(f32), 0).astype(bf16)
    part = jnp.broadcast_to(cut[None], (8, *cut.shape))
    part = lax.all_to_all(part, ("z", "x"), split_axis=0, concat_axis=0, tiled=True)
    gq, go, gr, *lines = unpack(part, 3 * features, experts)
    lines = [line.reshape(width) for line in lines]
    grad_in, grad_back = settle(place, second_swap, out0[2], core0, side0, first_swap, *third_swap)

    return (block_out, grad_tokens, lines[0], lines[1], gq, go, lines[2], lines[3], gr.T, grad_in, grad_back)


def solution(mesh):
    if mesh.shape["dp"] == 4 and mesh.shape["expert"] == 8:
        mesh = Mesh(mesh.devices.reshape(2, 2, 4, 2), ("y", "core", "z", "x"))
        body, dp, expert = paired, ("y", "core"), ("z", "x")
    else:
        body, dp, expert = exchanged, ("dp",), ("expert",)
    rows = P((*dp, *expert), None)
    return jax.shard_map(
        body,
        mesh=mesh,
        in_specs=(
            rows,
            P(dp),
            P(dp),
            P(dp, None),
            P(dp, None),
            P(dp),
            P(dp),
            P(dp, None),
            P(expert, None, None),
            P(expert, None, None),
            rows,
            P((*dp, *expert)),
            P(),
            rows,
        ),
        out_specs=(
            rows,
            rows,
            P(dp),
            P(dp),
            P(dp, None),
            P(dp, None),
            P(dp),
            P(dp),
            P(dp, None),
            P(expert, None, dp),
            P(expert, dp, None),
        ),
        check_vma=False,
    )
```
